32 devices in a mesh: section: 2 (over core), dp: 16 (over z, y, x).
Axes of the slice: x: 2, y: 2, z: 4, core: 2. Of those that a mesh axis runs over, the one named last changes fastest.
Arguments:
- pixels: bfloat16 [2, 16, 588, 1536], P(None, 'dp'), may hold values from -20 to 20
- keep_index: int32 [2, 16, 147], P(None, 'dp'), may hold values from 0 to 587, as said below
- clear_mask: int32 [2, 16, 588], P(None, 'dp'), may hold values from 0 to 1
- slot_tile: int32 [2, 384], P('section'), may hold values from 0 to 256, as said below
- master: float32 [2, 384, 128, 256], P('section', 'dp'), may hold values from -4 to 4, as said below
- moment_one: float32 [2, 384, 128, 256], P('section', 'dp'), as said below
- moment_two: float32 [2, 384, 128, 256], P('section', 'dp'), as said below
Outputs:
- new_master: float32 [2, 384, 128, 256], P('section', 'dp')
- new_moment_one: float32 [2, 384, 128, 256], P('section', 'dp')
- new_moment_two: float32 [2, 384, 128, 256], P('section', 'dp')
- loss: float32 [1], replicated
- grad_norm: float32 [1], replicated
The draws below stay inside these ranges and needn't reach their ends.
Inputs may be any that keep to these rules, and one draw needn't show every extreme that they name: `keep_index`: the 147 indices of an item are distinct and increasing. `slot_tile`: row s names each tile of 0 to 253 - 1 (s = 0) or 0 to 133 - 1 (s = 1) in exactly one slot, every other slot holds 256 (empty); slots d * 24 to (d + 1) * 24 - 1 belong to index d of dp, and in each row some index has no empty slot. `master`: entries of empty slots are zero. `moment_one`: entries of empty slots are zero. `moment_two`: entries of empty slots are zero, all others positive.
All inputs are finite; a program needn't handle non-finite values.
Results may differ from the reference program's by a relative error of at most 0.0005.
The reference program's roundings to bfloat16 on the way count: a program that leaves them out, or rounds other values in their place, can miss the bound.
Values may be sent and summed in bfloat16 or wider, within the bound.
A program may use at most 448 MiB of HBM per device.

```python
import math
import jax
import jax.numpy as jnp
import numpy as np
from jax import lax

D_ENC = 768
H_ENC = 12
FF_ENC = 3072
D_DEC = 512
H_DEC = 16
FF_DEC = 2048
BANDS = 6
PATCH_PIX = 256
PATCH_DIM = 1536
SEQ = 588
KEEP = 147
IT_DEV = 1
MICRO = 2
STEP = 5
TR = 128
TC = 256
TILES = 256
TILES_ENC = 253
TILES_DEC = 133
SLOTS = 24
N_DP = 16


def used_count(section_id):
    if section_id == 0:
        return TILES_ENC
    return TILES_DEC


def slot_rows(key):
    total_slots = N_DP * SLOTS
    owner_index = jnp.arange(total_slots) // SLOTS
    result = []
    for section_id in range(2):
        base_key = jax.random.fold_in(jax.random.fold_in(key, 7), section_id)
        pick_key, order_key = jax.random.split(base_key)
        full_owner = jax.random.randint(pick_key, (), 0, N_DP)
        shuffled = jax.random.permutation(order_key, total_slots)
        score_int = jnp.where(owner_index == full_owner, shuffled - total_slots, shuffled)
        slot_order = jnp.argsort(score_int)
        used_tiles = used_count(section_id)
        slot_row = jnp.full((total_slots,), TILES, jnp.int32).at[slot_order[:used_tiles]].set(jnp.arange(used_tiles, dtype=jnp.int32))
        result.append(slot_row)
    return jnp.stack(result)


def draw_slot_tile(key, part):
    return slot_rows(key).astype(jnp.int32)


def scale_tables(section_id):
    if section_id == 0:
        feature_width, hidden = (D_ENC, FF_ENC)
        matrices = [(PATCH_DIM, D_ENC, 1.0)]
        vectors = [(D_ENC, 0.0, 0.3)]
    else:
        feature_width, hidden = (D_DEC, FF_DEC)
        matrices = [(D_ENC, D_DEC, 1.0)]
        vectors = [(D_DEC, 0.0, 0.3), (D_DEC, 0.0, 1.0)]
    matrices = matrices + [(feature_width, 3 * feature_width, 1.0), (feature_width, feature_width, 2.0), (feature_width, hidden, 1.0), (hidden, feature_width, 1.0)]
    vectors = vectors + [(feature_width, 1.0, 0.25), (feature_width, 0.0, 0.3), (2 * feature_width, 0.0, 0.3), (feature_width, 0.0, 0.3), (feature_width, 1.0, 0.25), (feature_width, 0.0, 0.3), (hidden, 0.0, 0.3), (feature_width, 0.0, 0.3), (feature_width, 1.0, 0.25), (feature_width, 0.0, 0.3)]
    if section_id == 1:
        matrices = matrices + [(D_DEC, PATCH_DIM, 1.0)]
        vectors = vectors + [(PATCH_DIM, 0.0, 0.3)]
    tile_scale = np.zeros(TILES + 1, np.float32)
    tile_start = 0
    for row_count, col_count, factor in matrices:
        tiles_here = row_count * col_count // (TR * TC)
        tile_scale[tile_start:tile_start + tiles_here] = factor / np.sqrt(row_count)
        tile_start += tiles_here
    centre = np.zeros(TR * TC, np.float32)
    spread = np.zeros(TR * TC, np.float32)
    entry_start = 0
    for length, middle_val, width_val in vectors:
        centre[entry_start:entry_start + length] = middle_val
        spread[entry_start:entry_start + length] = width_val
        entry_start += length
    return (tile_scale, centre, spread, tile_start)


def unit_noise(key, dims):
    return jnp.clip(jax.random.normal(key, dims, jnp.float32), -4.0, 4.0)


def draw_master(key, part):
    slot_table = slot_rows(key)
    stacked = []
    for section_id in range(2):
        tile_scale, centre, spread, vec_index = scale_tables(section_id)
        noise_draw = unit_noise(jax.random.fold_in(key, 100 + section_id), (N_DP * SLOTS, TR * TC))
        slot_row = slot_table[section_id]
        is_vector = (slot_row == vec_index)[:, None]
        values = jnp.where(is_vector, jnp.asarray(centre) + jnp.asarray(spread) * noise_draw, jnp.asarray(tile_scale)[slot_row][:, None] * noise_draw)
        stacked.append(values.reshape(N_DP * SLOTS, TR, TC))
    return jnp.stack(stacked)


def moment_scale(slot_row, vec_index, vector_factor):
    grad_size = 0.001 * ((TILES_ENC + TILES_DEC) * TR * TC) ** (-0.5)
    used_slot = (slot_row < TILES).astype(jnp.float32)
    return (grad_size * used_slot * jnp.where(slot_row == vec_index, vector_factor, 1.0))[:, None]


def draw_moment_one(key, part):
    slot_table = slot_rows(key)
    stacked = []
    for section_id in range(2):
        vec_index = used_count(section_id) - 1
        noise_draw = unit_noise(jax.random.fold_in(key, 200 + section_id), (N_DP * SLOTS, TR * TC))
        values = moment_scale(slot_table[section_id], vec_index, 5.0) * noise_draw
        stacked.append(values.reshape(N_DP * SLOTS, TR, TC))
    return jnp.stack(stacked)


def draw_moment_two(key, part):
    slot_table = slot_rows(key)
    stacked = []
    for section_id in range(2):
        vec_index = used_count(section_id) - 1
        draw_key = jax.random.fold_in(key, 300 + section_id)
        factor = jnp.exp(jax.random.uniform(draw_key, (N_DP * SLOTS, TR * TC), jnp.float32, float(np.log(1.0 / 6.0)), float(np.log(8.0 / 3.0))))
        scale_rows = moment_scale(slot_table[section_id], vec_index, 5.0)
        stacked.append((scale_rows * scale_rows * factor).reshape(N_DP * SLOTS, TR, TC))
    return jnp.stack(stacked)


def draw_pixels(key, part):
    item_count = N_DP * IT_DEV
    item_index = jnp.arange(item_count, dtype=jnp.float32)
    item_scale = 1.0 + 2.0 * item_index / max(item_count - 1, 1)
    band_index = jnp.arange(BANDS, dtype=jnp.float32)
    dims = (MICRO, item_count, SEQ, BANDS, PATCH_PIX)
    noise_draw = jnp.clip(jax.random.normal(key, dims, jnp.float32), -6.0, 6.0)
    offset = 0.2 * band_index
    values = offset[:, None] + item_scale[None, :, None, None, None] * noise_draw
    return values.reshape(MICRO, item_count, SEQ, PATCH_DIM).astype(jnp.bfloat16)


def draw_keep_index(key, part):
    item_total = MICRO * N_DP * IT_DEV
    item_keys = jax.random.split(key, item_total)
    chosen = jax.vmap(lambda k: jax.random.permutation(k, SEQ)[:KEEP])(item_keys)
    return jnp.sort(chosen, axis=-1).reshape(MICRO, N_DP * IT_DEV, KEEP).astype(jnp.int32)


def draw_clear_mask(key, part):
    item_count = N_DP * IT_DEV
    heavy_key, cell_key = jax.random.split(key)
    cloud_level = 750 - 500 * jnp.arange(item_count, dtype=jnp.int32) // max(item_count - 1, 1)
    heavy_item = jax.random.randint(heavy_key, (MICRO, item_count), 0, 8) == 0
    cloud_level = jnp.where(heavy_item, 950, cloud_level[None, :])
    cell_draw = jax.random.randint(cell_key, (MICRO, item_count, SEQ), 0, 1000)
    return (cell_draw >= cloud_level[:, :, None]).astype(jnp.int32)


def setup_inputs(seed: int = 0) -> dict:
    seeds = jax.random.split(jax.random.key(seed), 8)
    return {
        "pixels": draw_pixels(jax.random.fold_in(seeds[7], 71), 0),
        "keep_index": draw_keep_index(jax.random.fold_in(seeds[7], 71), 0),
        "clear_mask": draw_clear_mask(jax.random.fold_in(seeds[7], 71), 0),
        "slot_tile": draw_slot_tile(jax.random.fold_in(seeds[7], 71), 0),
        "master": draw_master(jax.random.fold_in(seeds[7], 71), 0),
        "moment_one": draw_moment_one(jax.random.fold_in(seeds[7], 71), 0),
        "moment_two": draw_moment_two(jax.random.fold_in(seeds[7], 71), 0),
    }


@jax.custom_vjp
def low(v):
    return lax.optimization_barrier(v.astype(jnp.bfloat16)).astype(jnp.float32)

@jax.custom_vjp
def low_back(v):
    return v

def low_keep(v):
    return (low(v), None)

def low_pass(kept, grad):
    return (grad,)

def back_keep(v):
    return (v, None)

def back_low(kept, grad):
    return (low(grad),)
low.defvjp(low_keep, low_pass)
low_back.defvjp(back_keep, back_low)
EPS_NORM = 1e-06
EPS_BAND = 1e-05
CLIP_NORM = 0.001
RATE = 0.02
DECAY = 0.05
BETA_ONE = 0.5
BETA_TWO = 0.75
ADAM_EPS = 1e-08
HIGH = lax.Precision.HIGHEST

def layout(section_id):
    if section_id == 0:
        feature_width, hidden = (D_ENC, FF_ENC)
        matrices = [('first', PATCH_DIM, D_ENC)]
        vectors = [('first_bias', D_ENC)]
    else:
        feature_width, hidden = (D_DEC, FF_DEC)
        matrices = [('first', D_ENC, D_DEC)]
        vectors = [('first_bias', D_DEC), ('mask', D_DEC)]
    matrices = matrices + [('qkv', feature_width, 3 * feature_width), ('proj', feature_width, feature_width), ('fc1', feature_width, hidden), ('fc2', hidden, feature_width)]
    vectors = vectors + [('g1', feature_width), ('b1', feature_width), ('qv_bias', 2 * feature_width), ('proj_bias', feature_width), ('g2', feature_width), ('b2', feature_width), ('fc1_bias', hidden), ('fc2_bias', feature_width), ('gf', feature_width), ('bf', feature_width)]
    if section_id == 1:
        matrices = matrices + [('head', D_DEC, PATCH_DIM)]
        vectors = vectors + [('head_bias', PATCH_DIM)]
    return (matrices, vectors)

def unpack(flat_tiles, section_id):
    matrices, vectors = layout(section_id)
    flat_line = flat_tiles.reshape(-1)
    result = {}
    offset = 0
    for entry_name, row_count, col_count in matrices:
        result[entry_name] = flat_line[offset:offset + row_count * col_count].reshape(row_count, col_count)
        offset += row_count * col_count
    for entry_name, length in vectors:
        result[entry_name] = flat_line[offset:offset + length]
        offset += length
    return result

def positions(feature_width):
    token_place = jnp.arange(SEQ, dtype=jnp.float32)[:, None]
    frequency = jnp.exp(jnp.arange(feature_width // 2, dtype=jnp.float32) * (-2.0 * math.log(10000.0) / feature_width))
    return jnp.concatenate([jnp.sin(token_place * frequency), jnp.cos(token_place * frequency)], axis=1)

def matmul(a, b):
    return jnp.matmul(a, b, precision=HIGH)

def layer_norm(values, gain_vec, offset_vec):
    centre = values - lax.optimization_barrier(jnp.mean(values, -1, keepdims=True))
    return centre * lax.rsqrt(lax.optimization_barrier(jnp.mean(centre * centre, -1, keepdims=True)) + EPS_NORM) * gain_vec + offset_vec

def block(inputs, w, head_count):
    length, width_all = inputs.shape
    head_size = width_all // head_count
    normed_a = low(layer_norm(inputs, w['g1'], w['b1']))
    qv_bias = w['qv_bias']
    joined_bias = jnp.concatenate([qv_bias[:width_all], jnp.zeros((width_all,), inputs.dtype), qv_bias[width_all:]])
    qkv_all = low(low_back(matmul(normed_a, w['qkv']) + joined_bias))
    queries, key_rows, value_rows = [segment.reshape(length, head_count, head_size) for segment in jnp.split(qkv_all, 3, axis=1)]
    scores = low_back(jnp.einsum('qhd,khd->hqk', queries, key_rows, precision=HIGH) * head_size ** (-0.5))
    probs = low(jax.nn.softmax(scores, axis=-1))
    attended = low(low_back(jnp.einsum('hqk,khd->qhd', probs, value_rows, precision=HIGH).reshape(length, width_all)))
    middle = inputs + low_back(matmul(attended, w['proj']) + w['proj_bias'])
    normed_c = low(layer_norm(middle, w['g2'], w['b2']))
    pre_act = low_back(matmul(normed_c, w['fc1']) + w['fc1_bias'])
    activated = low(jax.nn.gelu(pre_act, approximate=False))
    return middle + low_back(matmul(activated, w['fc2']) + w['fc2_bias'])

def item_loss(weights_enc, weights_dec, band_mean, band_scale, pix_item, keep_item, valid_item, valid_count):
    visible = pix_item[keep_item].reshape(KEEP, BANDS, PATCH_PIX)
    normed_in = low(((visible - band_mean[:, None]) * band_scale[:, None]).reshape(KEEP, PATCH_DIM))
    embedded = low_back(matmul(normed_in, weights_enc['first'])) + weights_enc['first_bias'] + positions(D_ENC)[keep_item]
    encoded = block(embedded, weights_enc, H_ENC)
    sent = low(low_back(layer_norm(encoded, weights_enc['gf'], weights_enc['bf'])))
    placed = low_back(matmul(sent, weights_dec['first'])) + weights_dec['first_bias']
    canvas = jnp.broadcast_to(weights_dec['mask'], (SEQ, D_DEC)).at[keep_item].set(placed) + positions(D_DEC)
    decoded = block(canvas, weights_dec, H_DEC)
    final_norm = low(layer_norm(decoded, weights_dec['gf'], weights_dec['bf']))
    predicted = low_back(matmul(final_norm, weights_dec['head'])) + weights_dec['head_bias']
    patches = pix_item.reshape(SEQ, BANDS, PATCH_PIX)
    centre = patches - lax.optimization_barrier(jnp.mean(patches, -1, keepdims=True))
    target = centre * lax.rsqrt(lax.optimization_barrier(jnp.mean(centre * centre, -1, keepdims=True)) + EPS_NORM)
    misfit = predicted.reshape(SEQ, BANDS, PATCH_PIX) - target
    return jnp.sum(valid_item[:, None] * lax.optimization_barrier(jnp.mean(misfit * misfit, -1))) / (BANDS * valid_count)

def reference(pixels, keep_index, clear_mask, slot_tile, master, moment_one, moment_two):
    item_total = pixels.shape[0] * pixels.shape[1]
    pixel_items = pixels.astype(jnp.float32).reshape(item_total, SEQ, PATCH_DIM)
    keep_items = keep_index.reshape(item_total, KEEP)
    clear_items = clear_mask.reshape(item_total, SEQ).astype(jnp.float32)
    band_view = pixel_items.reshape(item_total, SEQ, BANDS, PATCH_PIX)
    pixel_count = item_total * SEQ * PATCH_PIX
    band_mean = lax.optimization_barrier(jnp.sum(band_view, (0, 1, 3))) / pixel_count
    band_scale = lax.rsqrt(lax.optimization_barrier(jnp.sum(band_view * band_view, (0, 1, 3))) / pixel_count - band_mean * band_mean + EPS_BAND)
    kept_rows = jnp.zeros((item_total, SEQ), jnp.float32).at[jnp.arange(item_total)[:, None], keep_items].set(1.0)
    valid_rows = clear_items * (1.0 - kept_rows)
    valid_count = jnp.maximum(jnp.sum(valid_rows), 1.0)
    tile_shape = master.shape[2:]
    flat_list = []
    for section_id in range(2):
        holder = jnp.zeros((TILES + 1,) + tile_shape, master.dtype).at[slot_tile[section_id]].set(master[section_id])
        flat_list.append(holder[:TILES])

    def total_loss(flat_enc, flat_dec):
        weights_enc = unpack(low(flat_enc), 0)
        weights_dec = unpack(low(flat_dec), 1)

        def one_item(running, scan_input):
            pix_item, keep_item, valid_item = scan_input
            term = jax.checkpoint(item_loss)(weights_enc, weights_dec, band_mean, band_scale, pix_item, keep_item, valid_item, valid_count)
            return (running + term, None)
        return lax.scan(one_item, jnp.zeros((), jnp.float32), (pixel_items, keep_items, valid_rows))[0]
    loss_value, pull_back = jax.vjp(total_loss, flat_list[0], flat_list[1])
    grad_list = pull_back(jnp.ones((), loss_value.dtype))
    total_square = jnp.sum(grad_list[0] * grad_list[0]) + jnp.sum(grad_list[1] * grad_list[1])
    grad_norm = jnp.sqrt(total_square)
    factor = jnp.minimum(1.0, CLIP_NORM / (grad_norm + 1e-06))
    step_value = float(STEP)
    masters, firsts, seconds = ([], [], [])
    for section_id in range(2):
        padded = jnp.concatenate([grad_list[section_id], jnp.zeros((1,) + tile_shape, master.dtype)])
        clipped = padded[slot_tile[section_id]] * factor
        first_new = BETA_ONE * moment_one[section_id] + (1.0 - BETA_ONE) * clipped
        second_new = BETA_TWO * moment_two[section_id] + (1.0 - BETA_TWO) * clipped * clipped
        ratio = first_new / (1.0 - BETA_ONE ** step_value) / (jnp.sqrt(second_new / (1.0 - BETA_TWO ** step_value)) + ADAM_EPS)
        masters.append(master[section_id] - RATE * (ratio + DECAY * master[section_id]))
        firsts.append(first_new)
        seconds.append(second_new)
    return (jnp.stack(masters), jnp.stack(firsts), jnp.stack(seconds), loss_value[None], grad_norm[None])
```

```python
import functools
import math

import jax
import jax.numpy as jnp
import numpy as np
from jax import lax
from jax.experimental import pallas as pl
from jax.experimental.pallas import tpu as pltpu
from jax.sharding import PartitionSpec as P

D_ENC = 768
H_ENC = 12
FF_ENC = 3072
D_DEC = 512
H_DEC = 16
FF_DEC = 2048
BANDS = 6
PATCH_PIX = 256
PATCH_DIM = 1536
SEQ = 588
KEEP = 147
STEP = 5
TILES = 256
USED = (253, 133)

EPS_NORM = 1e-06
EPS_BAND = 1e-05
CLIP_NORM = 0.001
RATE = 0.02
DECAY = 0.05
BETA_ONE = 0.5
BETA_TWO = 0.75
ADAM_EPS = 1e-08

MESH = pl.DeviceIdType.MESH
TR, TC = 128, 256
PARTS = ((0, 5), (5, 10), (10, 13))


def exchange(name, cid, n_dp, dealt, shared):
    n_dev = 2 * n_dp
    n_a, n_s = len(dealt), len(shared)
    n_all = n_a + n_s

    def kernel(*refs):
        sources, targets = refs[:n_all], refs[n_all : 2 * n_all]
        send_sem, recv_sem, own_sem = refs[2 * n_all :]
        section, place = lax.axis_index("section"), lax.axis_index("dp")
        me = section * n_dp + place

        def who(step):
            other = lax.rem(me + step, n_dev)
            return other, (lax.div(other, n_dp), lax.rem(other, n_dp))

        barrier = pltpu.get_barrier_semaphore()

        def greet(step, carry):
            pl.semaphore_signal(barrier, inc=1, device_id=who(step)[1], device_id_type=MESH)
            return carry

        lax.fori_loop(1, n_dev, greet, 0)
        own = []
        for which in range(n_all):
            source = sources[which].at[me] if which < n_a else sources[which]
            copy = pltpu.make_async_copy(source, targets[which].at[me], own_sem.at[which])
            copy.start()
            own.append(copy)
        pl.semaphore_wait(barrier, n_dev - 1)

        def made(which, step):
            other, place_of = who(step)
            source = sources[which].at[other] if which < n_a else sources[which]
            return pltpu.make_async_remote_copy(
                src_ref=source,
                dst_ref=targets[which].at[me],
                send_sem=send_sem.at[which, step],
                recv_sem=recv_sem.at[which, step],
                device_id=place_of,
                device_id_type=MESH,
            )

        def begin(step, carry):
            for which in reversed(range(n_all)):
                made(which, step).start()
            return carry

        def end(step, carry):
            for which in range(n_all):
                made(which, step).wait()
            return carry

        lax.fori_loop(1, n_dev, begin, 0)
        for copy in own:
            copy.wait()
        lax.fori_loop(1, n_dev, end, 0)

    arrays = list(dealt) + list(shared)
    shapes = [jax.ShapeDtypeStruct(a.shape, a.dtype) for a in dealt] + [
        jax.ShapeDtypeStruct((n_dev,) + a.shape, a.dtype) for a in shared
    ]
    any_spec = pl.BlockSpec(memory_space=pltpu.HBM)
    return pl.pallas_call(
        kernel,
        out_shape=shapes,
        in_specs=[any_spec] * n_all,
        out_specs=[any_spec] * n_all,
        scratch_shapes=[
            pltpu.SemaphoreType.DMA((n_all, n_dev)),
            pltpu.SemaphoreType.DMA((n_all, n_dev)),
            pltpu.SemaphoreType.DMA((n_all,)),
        ],
        compiler_params=pltpu.CompilerParams(collective_id=cid, has_side_effects=True),
        name=name,
    )(*arrays)


def code(values):
    top = jnp.max(jnp.abs(values), axis=0, keepdims=True)
    up = jnp.where(top > 0.0, 32766.0 / top, 0.0)
    scaled = values * up
    return (scaled + jnp.where(scaled >= 0.0, 0.5, -0.5)).astype(jnp.int32).astype(jnp.int16), top * (1.0 / 32766.0)


def gather_all(block, cid):
    per = block.shape[0]
    cut = [0, 3, 6, 9, per] if per == 13 else [0, per // 4, per // 2, 3 * per // 4, per]
    ways = (("z", "y", "x"), ("z", "x", "y"), ("y", "z", "x"), ("x", "z", "y"))

    def kernel(block_ref, all_ref, send_sem, recv_sem, side_send, side_recv, own_sem):
        section, place = lax.axis_index("section"), lax.axis_index("dp")
        x, y, z = lax.rem(place, 2), lax.rem(lax.div(place, 2), 2), lax.div(place, 4)

        def at(dz, dy, dx):
            return lax.rem(z + dz, 4) * 4 + lax.rem(y + dy, 2) * 2 + lax.rem(x + dx, 2)

        barrier = pltpu.get_barrier_semaphore()
        peers = [(1 - section, place)] + [
            (section, at(*d)) for d in ((0, 0, 1), (0, 1, 0), (1, 0, 0), (2, 0, 0), (3, 0, 0))
        ]
        for peer in peers:
            pl.semaphore_signal(barrier, inc=1, device_id=peer, device_id_type=MESH)
        own = pltpu.make_async_copy(block_ref, all_ref.at[section, place], own_sem)
        own.start()
        pl.semaphore_wait(barrier, len(peers))
        copies = {}
        sides = {}
        count = [0]

        def rows(way):
            return pl.ds(cut[way], cut[way + 1] - cut[way])

        def send(way, origin, move):
            target = at(*move)
            holder = at(*origin)
            arrived = tuple((o - m) % s for o, m, s in zip(origin, move, (4, 2, 2)))
            source = block_ref.at[rows(way)] if origin == (0, 0, 0) else all_ref.at[section, holder, rows(way)]
            index = count[0]
            count[0] += 1
            copy = pltpu.make_async_remote_copy(
                src_ref=source,
                dst_ref=all_ref.at[section, holder, rows(way)],
                send_sem=send_sem.at[index],
                recv_sem=recv_sem.at[index],
                device_id=(section, target),
                device_id_type=MESH,
            )
            copy.start()
            copies[way, arrived] = (copy, index)

        def arrive(way, origin):
            holder = at(*origin)
            copy, index = copies[way, origin]
            pltpu.make_async_remote_copy(
                src_ref=block_ref.at[rows(way)],
                dst_ref=all_ref.at[section, holder, rows(way)],
                send_sem=send_sem.at[index],
                recv_sem=recv_sem.at[index],
                device_id=(section, place),
                device_id_type=MESH,
            ).wait_recv()

        side_count = [0]

        def side(way, origin):
            holder = at(*origin)
            source = block_ref.at[rows(way)] if origin == (0, 0, 0) else all_ref.at[section, holder, rows(way)]
            index = side_count[0]
            side_count[0] += 1
            copy = pltpu.make_async_remote_copy(
                src_ref=source,
                dst_ref=all_ref.at[section, holder, rows(way)],
                send_sem=side_send.at[index],
                recv_sem=side_recv.at[index],
                device_id=(1 - section, place),
                device_id_type=MESH,
            )
            copy.start()
            sides[way, origin] = (copy, index)

        unit = {
            "x": [(0, 0, 1)],
            "y": [(0, 1, 0)],
            "z": [(1, 0, 0), (2, 0, 0), (3, 0, 0)],
        }

        def moved(origin, move):
            return tuple((o - m) % s for o, m, s in zip(origin, move, (4, 2, 2)))

        zero = (0, 0, 0)
        held = {way: [zero] for way in range(4)}
        for way, dims in enumerate(ways):
            for move in unit[dims[0]]:
                send(way, zero, move)
        for way, dims in enumerate(ways):
            for move in unit[dims[1]]:
                send(way, zero, move)
            for move in unit[dims[2]]:
                send(way, zero, move)
        for way in range(4):
            side(way, zero)
        first = {way: [moved(zero, m) for m in unit[ways[way][0]]] for way in range(4)}
        for way in (2, 3, 0, 1):
            dims = ways[way]
            for origin in first[way]:
                arrive(way, origin)
                for move in unit[dims[1]]:
                    send(way, origin, move)
                for move in unit[dims[2]]:
                    send(way, origin, move)
                side(way, origin)
        second = {}
        for way in range(4):
            have = [zero] + first[way]
            second[way] = [moved(o, m) for m in unit[ways[way][1]] for o in have]
        longest = max(len(v) for v in second.values())
        for i in range(longest):
            for way in (0, 1, 2, 3):
                if i < len(second[way]):
                    origin = second[way][i]
                    arrive(way, origin)
                    for move in unit[ways[way][2]]:
                        send(way, origin, move)
                    side(way, origin)
        third = {}
        for way in range(4):
            have = [zero] + first[way] + second[way]
            third[way] = [moved(o, m) for m in unit[ways[way][2]] for o in have]
        for i in range(8):
            for way in range(4):
                arrive(way, third[way][i])
                side(way, third[way][i])
        own.wait()
        for (way, origin), (copy, index) in copies.items():
            copy.wait_send()
        for (way, origin), (copy, index) in sides.items():
            copy.wait_send()
            holder = at(*origin)
            pltpu.make_async_remote_copy(
                src_ref=block_ref.at[rows(way)],
                dst_ref=all_ref.at[1 - section, holder, rows(way)],
                send_sem=side_send.at[index],
                recv_sem=side_recv.at[index],
                device_id=(1 - section, place),
                device_id_type=MESH,
            ).wait_recv()

    spec = pl.BlockSpec(memory_space=pltpu.HBM)
    return pl.pallas_call(
        kernel,
        out_shape=jax.ShapeDtypeStruct((2, 16, per, TR, TC), block.dtype),
        in_specs=[spec],
        out_specs=spec,
        scratch_shapes=[
            pltpu.SemaphoreType.DMA((60,)),
            pltpu.SemaphoreType.DMA((60,)),
            pltpu.SemaphoreType.DMA((64,)),
            pltpu.SemaphoreType.DMA((64,)),
            pltpu.SemaphoreType.DMA,
        ],
        compiler_params=pltpu.CompilerParams(collective_id=cid, has_side_effects=True),
        name="gather_tiles",
    )(block)


def reduce_all(codes, scales, cid):
    per = codes.shape[2]

    def kernel(codes_ref, scales_ref, out_ref, outs_ref, acc, accs, rc, rcs, r_code, r_scale,
               own_sem, owns_sem, c_send, c_recv, p_send, p_recv):
        section, place = lax.axis_index("section"), lax.axis_index("dp")
        x, y, z = lax.rem(place, 2), lax.rem(lax.div(place, 2), 2), lax.div(place, 4)

        def at(dz, dy, dx):
            return lax.rem(z + dz, 4) * 4 + lax.rem(y + dy, 2) * 2 + lax.rem(x + dx, 2)

        sibling = (1 - section, place)
        barrier = pltpu.get_barrier_semaphore()
        peers = [sibling] + [(section, at(*d)) for d in ((0, 0, 1), (0, 1, 0), (1, 0, 0), (2, 0, 0), (3, 0, 0))]
        for peer in peers:
            pl.semaphore_signal(barrier, inc=1, device_id=peer, device_id_type=MESH)
        order = [(dz, dy, dx) for dz in (2, 1, 3, 0) for dy in (1, 0) for dx in (1, 0)]
        loads = {}
        for n, d in enumerate(order):
            b = at(*d)
            loads[d] = (
                pltpu.make_async_copy(codes_ref.at[section, b], acc.at[b], own_sem.at[n]),
                pltpu.make_async_copy(scales_ref.at[section, b], accs.at[b], owns_sem.at[n]),
            )
            for copy in loads[d]:
                copy.start()
        pl.semaphore_wait(barrier, len(peers))
        crossing = {}
        for n, d in enumerate(order):
            b = at(*d)
            pair = []
            for k, (source, target) in enumerate(((codes_ref, rc), (scales_ref, rcs))):
                copy = pltpu.make_async_remote_copy(
                    src_ref=source.at[1 - section, b], dst_ref=target.at[b],
                    send_sem=c_send.at[k, n], recv_sem=c_recv.at[k, n],
                    device_id=sibling, device_id_type=MESH)
                copy.start()
                pair.append(copy)
            crossing[d] = pair

        def add(b, first, count, scale_row, from_code, from_first, from_scale, from_row):
            def one(t, carry):
                mine = acc[b, first + t].astype(jnp.float32) * accs[b, pl.ds(scale_row + t, 1), :]
                theirs = from_code[from_first + t].astype(jnp.float32) * from_scale[pl.ds(from_row + t, 1), :]
                value, scale = code(mine + theirs)
                acc[b, first + t] = value
                accs[b, pl.ds(scale_row + t, 1), :] = scale
                return carry
            lax.fori_loop(0, count, one, 0)

        sends = {}
        slots = {}
        used = [0, 0]

        def send(part, key, b, peer):
            t0, t1 = PARTS[part]
            slot, index = used
            used[0] += t1 - t0
            used[1] += 1
            pair = []
            for k, (source, target) in enumerate((
                (acc.at[b, pl.ds(t0, t1 - t0)], r_code.at[pl.ds(slot, t1 - t0)]),
                (accs.at[b, pl.ds(8 * part, 8)], r_scale.at[index]),
            )):
                copy = pltpu.make_async_remote_copy(
                    src_ref=source, dst_ref=target, send_sem=p_send.at[k, index], recv_sem=p_recv.at[k, index],
                    device_id=peer, device_id_type=MESH)
                copy.start()
                pair.append(copy)
            sends[part, key] = pair
            slots[part, key] = (slot, index)

        def take(part, key, b):
            t0, t1 = PARTS[part]
            slot, index = slots[part, key]
            for copy in sends[part, key]:
                copy.wait_recv()
            add(b, t0, t1 - t0, 8 * part, r_code, slot, r_scale.at[index], 0)

        to_x, to_y = (section, at(0, 0, 1)), (section, at(0, 1, 0))

        def to_z(dz):
            return (section, at(dz, 0, 0))

        for d in order:
            dz, dy, dx = d
            b = at(*d)
            for copy in loads[d]:
                copy.wait()
            for copy in crossing[d]:
                copy.wait_recv()
            for part, (t0, t1) in enumerate(PARTS):
                add(b, t0, t1 - t0, 8 * part, rc.at[b], t0, rcs.at[b], 8 * part)
            if dz:
                send(2, ("1", dz, dy, dx), b, to_z(dz))
            if dx:
                send(0, ("1", dz, dy), b, to_x)
            if dy:
                send(1, ("1", dz, dx), b, to_y)
        steps = []
        a_list = [("A", dz, 1) for dz in (2, 1, 3, 0)] + [("A", dz, 0) for dz in (2, 1, 3, 0)]
        b_list = [("B", dz, dx) for dz in (2, 1, 3) for dx in (1, 0)] + [("B", 0, 1), ("B", 0, 0)]
        c_list = [("C", dy, 1) for dy in (1, 0)] + [("C", dy, 0) for dy in (1, 0)]
        for i in range(8):
            steps.append(a_list[i])
            steps.append(b_list[i])
            if i % 2 == 1:
                steps.append(c_list[i // 2])
        for kind, one, two in steps:
            if kind == "A":
                b = at(one, two, 0)
                take(0, ("1", one, two), b)
                if two:
                    send(0, ("2", one), b, to_y)
            elif kind == "B":
                b = at(one, 0, two)
                take(1, ("1", one, two), b)
                if one:
                    send(1, ("2", one, two), b, to_z(one))
            else:
                b = at(0, one, two)
                for dz in (1, 3, 2):
                    take(2, ("1", dz, one, two), b)
                if two:
                    send(2, ("2", one), b, to_x)
        for dz in (2, 1, 3, 0):
            b = at(dz, 0, 0)
            take(0, ("2", dz), b)
            if dz:
                send(0, ("3", dz), b, to_z(dz))
        take(2, ("2", 1), at(0, 1, 0))
        send(2, ("3",), at(0, 1, 0), to_y)
        for dx in (1, 0):
            b = at(0, 0, dx)
            for dz in (1, 3, 2):
                take(1, ("2", dz, dx), b)
            if dx:
                send(1, ("3",), b, to_x)
        take(2, ("2", 0), place)
        for dz in (1, 3, 2):
            take(0, ("3", dz), place)
        take(2, ("3",), place)
        take(1, ("3",), place)
        out_ref[...] = acc[place]
        outs_ref[...] = accs[place]
        for pair in crossing.values():
            for copy in pair:
                copy.wait_send()
        for pair in sends.values():
            for copy in pair:
                copy.wait_send()

    n_tiles = 195
    n_copies = 45
    hbm = pl.BlockSpec(memory_space=pltpu.HBM)
    vmem = pl.BlockSpec(memory_space=pltpu.VMEM)
    return pl.pallas_call(
        kernel,
        out_shape=(
            jax.ShapeDtypeStruct((per, TR, TC), jnp.int16),
            jax.ShapeDtypeStruct((24, TC), jnp.float32),
        ),
        in_specs=[hbm, hbm],
        out_specs=(vmem, vmem),
        scratch_shapes=[
            pltpu.VMEM((16, per, TR, TC), jnp.int16),
            pltpu.VMEM((16, 24, TC), jnp.float32),
            pltpu.VMEM((16, per, TR, TC), jnp.int16),
            pltpu.VMEM((16, 24, TC), jnp.float32),
            pltpu.VMEM((n_tiles, TR, TC), jnp.int16),
            pltpu.VMEM((n_copies, 8, TC), jnp.float32),
            pltpu.SemaphoreType.DMA((16,)),
            pltpu.SemaphoreType.DMA((16,)),
            pltpu.SemaphoreType.DMA((2, 16)),
            pltpu.SemaphoreType.DMA((2, 16)),
            pltpu.SemaphoreType.DMA((2, n_copies)),
            pltpu.SemaphoreType.DMA((2, n_copies)),
        ],
        compiler_params=pltpu.CompilerParams(
            collective_id=cid, has_side_effects=True, vmem_limit_bytes=60 * 2**20
        ),
        name="reduce_tiles",
    )(codes, scales)


def layout(section_id):
    if section_id == 0:
        width, hidden = D_ENC, FF_ENC
        matrices = [("first", PATCH_DIM, D_ENC)]
        vectors = [("first_bias", D_ENC)]
    else:
        width, hidden = D_DEC, FF_DEC
        matrices = [("first", D_ENC, D_DEC)]
        vectors = [("first_bias", D_DEC), ("mask", D_DEC)]
    matrices = matrices + [
        ("qkv", width, 3 * width),
        ("proj", width, width),
        ("fc1", width, hidden),
        ("fc2", hidden, width),
    ]
    vectors = vectors + [
        ("g1", width),
        ("b1", width),
        ("qv_bias", 2 * width),
        ("proj_bias", width),
        ("g2", width),
        ("b2", width),
        ("fc1_bias", hidden),
        ("fc2_bias", width),
        ("gf", width),
        ("bf", width),
    ]
    if section_id == 1:
        matrices = matrices + [("head", D_DEC, PATCH_DIM)]
        vectors = vectors + [("head_bias", PATCH_DIM)]
    return matrices, vectors


def positions(width):
    place = np.arange(SEQ, dtype=np.float32)[:, None]
    rate = np.exp(np.arange(width // 2, dtype=np.float32) * np.float32(-2.0 * math.log(10000.0) / width))
    angle = (place * rate).astype(np.float32)
    return np.concatenate([np.sin(angle), np.cos(angle)], axis=1).astype(np.float32)


LANES = 128


def pick_tiles(tiles, index, dtype, name):
    count = index.shape[0]

    def kernel(index_ref, tiles_ref, out_ref):
        def one(t, carry):
            out_ref[t] = tiles_ref[index_ref[t]].astype(dtype)
            return carry

        lax.fori_loop(0, count, one, 0)

    return pl.pallas_call(
        kernel,
        out_shape=jax.ShapeDtypeStruct((count, TR, TC), dtype),
        in_specs=[pl.BlockSpec(memory_space=pltpu.SMEM), pl.BlockSpec(memory_space=pltpu.VMEM)],
        out_specs=pl.BlockSpec(memory_space=pltpu.VMEM),
        compiler_params=pltpu.CompilerParams(vmem_limit_bytes=40 * 2**20),
        name=name,
    )(index, tiles)


def unpack_matrix(tiles, place, base, rows, columns, name):
    wide = columns // TC

    def kernel(place_ref, *refs):
        sources, out_ref, lines = refs[:wide], refs[wide], refs[wide + 1 :]
        for j in range(wide):
            for h in range(2):
                lines[h][j * TR : (j + 1) * TR, :] = sources[j][0, :, h * LANES : (h + 1) * LANES].astype(jnp.float32)
        for j in range(wide):
            for h in range(2):
                start = j * TC + h * LANES
                out_ref[:, start : start + LANES] = lines[h][pl.ds(j, TR, stride=wide), :].astype(tiles.dtype)

    def spec(j):
        return pl.BlockSpec((1, TR, TC), lambda g, place_ref: (place_ref[base + g * wide + j], 0, 0))

    return pl.pallas_call(
        kernel,
        out_shape=jax.ShapeDtypeStruct((rows, columns), tiles.dtype),
        grid_spec=pltpu.PrefetchScalarGridSpec(
            num_scalar_prefetch=1,
            grid=(rows // TR,),
            in_specs=[spec(j) for j in range(wide)],
            out_specs=pl.BlockSpec((TR, columns), lambda g, place_ref: (g, 0)),
            scratch_shapes=[pltpu.VMEM((wide * TR, LANES), jnp.float32)] * 2,
        ),
        compiler_params=pltpu.CompilerParams(vmem_limit_bytes=32 * 2**20),
        name="unpack_" + name,
    )(place, *([tiles] * wide))


def pack_matrix(grad, place, line, base, codes, scales, total, name):
    rows, columns = grad.shape
    wide = columns // TC
    steps = rows // TR
    fresh = codes is None

    def kernel(place_ref, line_ref, grad_ref, *refs):
        scales_in = refs[0]
        codes_ref, scales_ref, left, right, ready, sem = refs[-6:]
        step = pl.program_id(0)
        slot = lax.rem(step, 2)

        @pl.when(step == 0)
        def _():
            scales_ref[...] = scales_in[...]

        def copies(at_step, at_slot):
            return [
                pltpu.make_async_copy(
                    ready.at[at_slot, j], codes_ref.at[place_ref[base + at_step * wide + j]], sem.at[at_slot, j]
                )
                for j in range(wide)
            ]

        @pl.when(step >= 2)
        def _():
            for copy in copies(step - 2, slot):
                copy.wait()

        for j in range(wide):
            for h, lines in enumerate((left, right)):
                start = j * TC + h * LANES
                lines[pl.ds(j, TR, stride=wide), :] = grad_ref[:, start : start + LANES]
        for j in range(wide):
            line = line_ref[base + step * wide + j]
            pair = []
            for h, lines in enumerate((left, right)):
                value, scale = code(lines[j * TR : (j + 1) * TR, :])
                ready[slot, j, :, h * LANES : (h + 1) * LANES] = value
                pair.append(scale)
            scales_ref[pl.ds(line, 1), :] = jnp.concatenate(pair, axis=1)
        for copy in copies(step, slot):
            copy.start()

        @pl.when(step == steps - 1)
        def _():
            if steps > 1:
                for copy in copies(step - 1, 1 - slot):
                    copy.wait()
            for copy in copies(step, slot):
                copy.wait()

    whole = pl.BlockSpec(scales.shape, lambda g, a, b: (0, 0))
    hbm = pl.BlockSpec(memory_space=pltpu.HBM)
    return pl.pallas_call(
        kernel,
        out_shape=(
            jax.ShapeDtypeStruct((total, TR, TC), jnp.int16),
            jax.ShapeDtypeStruct(scales.shape, jnp.float32),
        ),
        grid_spec=pltpu.PrefetchScalarGridSpec(
            num_scalar_prefetch=2,
            grid=(steps,),
            in_specs=[pl.BlockSpec((TR, columns), lambda g, a, b: (g, 0)), whole] + ([] if fresh else [hbm]),
            out_specs=(hbm, whole),
            scratch_shapes=[
                pltpu.VMEM((wide * TR, LANES), jnp.float32),
                pltpu.VMEM((wide * TR, LANES), jnp.float32),
                pltpu.VMEM((2, wide, TR, TC), jnp.int16),
                pltpu.SemaphoreType.DMA((2, wide)),
            ],
        ),
        input_output_aliases={3: 1} if fresh else {3: 1, 4: 0},
        compiler_params=pltpu.CompilerParams(vmem_limit_bytes=40 * 2**20),
        name="pack_" + name,
    )(place, line, grad, scales, *([] if fresh else [codes]))


def adam(codes, scales, index, used, factor, master, first, second):
    slots = master.shape[0]
    per = 3 if slots % 3 == 0 else 1

    def kernel(index_ref, used_ref, factor_ref, codes_ref, scales_ref, w_ref, m_ref, v_ref, w_out, m_out, v_out):
        for t in range(per):
            slot = pl.program_id(0) * per + t
            source = index_ref[slot]
            grad = codes_ref[source].astype(jnp.float32) * scales_ref[source]
            grad = jnp.where(used_ref[slot] > 0, grad * factor_ref[0], 0.0)
            first_new = BETA_ONE * m_ref[t] + (1.0 - BETA_ONE) * grad
            second_new = BETA_TWO * v_ref[t] + (1.0 - BETA_TWO) * grad * grad
            ratio = (
                first_new
                / (1.0 - BETA_ONE ** float(STEP))
                / (jnp.sqrt(second_new / (1.0 - BETA_TWO ** float(STEP))) + ADAM_EPS)
            )
            w_out[t] = w_ref[t] - RATE * (ratio + DECAY * w_ref[t])
            m_out[t] = first_new
            v_out[t] = second_new

    smem = pl.BlockSpec(memory_space=pltpu.SMEM)
    block = pl.BlockSpec((per, TR, TC), lambda g: (g, 0, 0))
    return pl.pallas_call(
        kernel,
        out_shape=[jax.ShapeDtypeStruct(master.shape, jnp.float32)] * 3,
        grid=(slots // per,),
        in_specs=[
            smem,
            smem,
            smem,
            pl.BlockSpec(codes.shape, lambda g: (0, 0, 0)),
            pl.BlockSpec(scales.shape, lambda g: (0, 0, 0)),
            block,
            block,
            block,
        ],
        out_specs=[block] * 3,
        compiler_params=pltpu.CompilerParams(vmem_limit_bytes=40 * 2**20),
        name="adam",
    )(index, used, factor, codes, scales, master, first, second)


def project(a, w):
    return jnp.dot(a, w, preferred_element_type=jnp.float32)


def project_back(d, w):
    return lax.dot_general(d, w, (((1,), (1,)), ((), ())), preferred_element_type=jnp.float32)


def weight_grad(a, d):
    return lax.dot_general(a, d, (((0,), (0,)), ((), ())), preferred_element_type=jnp.float32)


def layer_norm(values, gain, offset):
    centre = values - jnp.mean(values, -1, keepdims=True)
    return centre * lax.rsqrt(jnp.mean(centre * centre, -1, keepdims=True) + EPS_NORM) * gain + offset


def norm_back(upstream, values, gain):
    centre = values - jnp.mean(values, -1, keepdims=True)
    spread = lax.rsqrt(jnp.mean(centre * centre, -1, keepdims=True) + EPS_NORM)
    normed = centre * spread
    scaled = upstream * gain
    downstream = spread * (
        scaled - jnp.mean(scaled, -1, keepdims=True) - normed * jnp.mean(scaled * normed, -1, keepdims=True)
    )
    return downstream, jnp.sum(upstream * normed, 0), jnp.sum(upstream, 0)


def gelu_slope(pre):
    return 0.5 * (1.0 + lax.erf(pre * (1.0 / math.sqrt(2.0)))) + pre * jnp.exp(-0.5 * pre * pre) * (
        1.0 / math.sqrt(2.0 * math.pi)
    )


def column_sums(values):
    return jnp.sum(values.astype(jnp.float32), 0)


def attention(qkv, heads):
    length, width = qkv.shape[0], qkv.shape[1] // 3
    size = width // heads
    q, k, v = [part.reshape(length, heads, size) for part in jnp.split(qkv, 3, axis=-1)]
    scores = jnp.einsum("qhd,khd->hqk", q, k, preferred_element_type=jnp.float32) * size ** (-0.5)
    top = jnp.max(scores, -1, keepdims=True)
    log_total = top + jnp.log(jnp.sum(jnp.exp(scores - top), -1, keepdims=True))
    low = jnp.exp(scores - log_total).astype(jnp.bfloat16)
    out = jnp.einsum("hqk,khd->qhd", low, v, preferred_element_type=jnp.float32)
    return out.reshape(length, width).astype(jnp.bfloat16), log_total


def attention_back(qkv, log_total, grad, heads):
    length, width = grad.shape
    size = width // heads
    factor = size ** (-0.5)
    q, k, v = [part.reshape(length, heads, size) for part in jnp.split(qkv, 3, axis=-1)]
    grad = grad.reshape(length, heads, size)
    scores = jnp.einsum("qhd,khd->hqk", q, k, preferred_element_type=jnp.float32) * factor
    probs = jnp.exp(scores - log_total)
    dv = jnp.einsum("hqk,qhd->khd", probs.astype(jnp.bfloat16), grad, preferred_element_type=jnp.float32)
    dp = jnp.einsum("qhd,khd->hqk", grad, v, preferred_element_type=jnp.float32)
    ds = (probs * (dp - jnp.sum(dp * probs, -1, keepdims=True))).astype(jnp.bfloat16)
    dq = jnp.einsum("hqk,khd->qhd", ds, k, preferred_element_type=jnp.float32) * factor
    dk = jnp.einsum("hqk,qhd->khd", ds, q, preferred_element_type=jnp.float32) * factor
    return jnp.concatenate([part.reshape(length, width) for part in (dq, dk, dv)], -1).astype(jnp.bfloat16)


def block_forward(x, w, heads):
    width = x.shape[-1]
    a = layer_norm(x, w["g1"], w["b1"]).astype(jnp.bfloat16)
    bias = jnp.concatenate([w["qv_bias"][:width], jnp.zeros((width,), jnp.float32), w["qv_bias"][width:]])
    qkv = (project(a, w["qkv"]) + bias).astype(jnp.bfloat16)
    attended, log_total = attention(qkv, heads)
    middle = x + project(attended, w["proj"]) + w["proj_bias"]
    c = layer_norm(middle, w["g2"], w["b2"]).astype(jnp.bfloat16)
    pre = project(c, w["fc1"]) + w["fc1_bias"]
    z = jax.nn.gelu(pre, approximate=False).astype(jnp.bfloat16)
    out = middle + project(z, w["fc2"]) + w["fc2_bias"]
    return out, (x, a, qkv, log_total, attended, middle, c, pre, z)


def block_backward(grad_out, stored, w, heads):
    x, a, qkv, log_total, attended, middle, c, pre, z = stored
    width = x.shape[-1]
    grads = {}
    two = grad_out.astype(jnp.bfloat16)
    grads["fc2"] = weight_grad(z, two)
    grads["fc2_bias"] = column_sums(two)
    grad_pre = (project_back(two, w["fc2"]) * gelu_slope(pre)).astype(jnp.bfloat16)
    grads["fc1"] = weight_grad(c, grad_pre)
    grads["fc1_bias"] = column_sums(grad_pre)
    grad_c, grads["g2"], grads["b2"] = norm_back(project_back(grad_pre, w["fc1"]), middle, w["g2"])
    grad_middle = grad_out + grad_c
    one = grad_middle.astype(jnp.bfloat16)
    grads["proj"] = weight_grad(attended, one)
    grads["proj_bias"] = column_sums(one)
    grad_att = project_back(one, w["proj"]).astype(jnp.bfloat16)
    grad_qkv = attention_back(qkv, log_total, grad_att, heads)
    grads["qkv"] = weight_grad(a, grad_qkv)
    sums = column_sums(grad_qkv)
    grads["qv_bias"] = jnp.concatenate([sums[:width], sums[2 * width :]])
    grad_a, grads["g1"], grads["b1"] = norm_back(project_back(grad_qkv, w["qkv"]), x, w["g1"])
    return grad_middle + grad_a, grads


def item_step(enc, dec, pix, keep, kept, valid, band_mean, band_scale, valid_count):
    chosen = (keep[:, None] == jnp.arange(SEQ)).astype(jnp.bfloat16)
    seen = project(chosen, pix).reshape(KEEP, BANDS, PATCH_PIX)
    xin = ((seen - band_mean[:, None]) * band_scale[:, None]).reshape(KEEP, PATCH_DIM).astype(jnp.bfloat16)
    place_enc = jnp.dot(chosen.astype(jnp.float32), jnp.asarray(positions(D_ENC)), precision=lax.Precision.HIGHEST)
    embedded = project(xin, enc["first"]) + enc["first_bias"] + place_enc
    y_enc, stored_enc = block_forward(embedded, enc, H_ENC)
    sent = layer_norm(y_enc, enc["gf"], enc["bf"]).astype(jnp.bfloat16)

    spread = weight_grad(chosen, sent).astype(jnp.bfloat16)
    placed = project(spread, dec["first"]) + dec["first_bias"]
    grid = jnp.where(kept[:, None] > 0.0, placed, dec["mask"]) + jnp.asarray(positions(D_DEC))
    y_dec, stored_dec = block_forward(grid, dec, H_DEC)
    final = layer_norm(y_dec, dec["gf"], dec["bf"]).astype(jnp.bfloat16)
    predicted = project(final, dec["head"]) + dec["head_bias"]
    patches = pix.astype(jnp.float32).reshape(SEQ, BANDS, PATCH_PIX)
    centre = patches - jnp.mean(patches, -1, keepdims=True)
    target = centre * lax.rsqrt(jnp.mean(centre * centre, -1, keepdims=True) + EPS_NORM)
    misfit = predicted.reshape(SEQ, BANDS, PATCH_PIX) - target
    loss = jnp.sum(valid[:, None] * jnp.mean(misfit * misfit, -1)) / (BANDS * valid_count)
    grad_pred = (valid[:, None, None] * misfit * (2.0 / (BANDS * PATCH_PIX * valid_count))).reshape(SEQ, PATCH_DIM)
    pred_low = grad_pred.astype(jnp.bfloat16)
    grad_head = weight_grad(final, pred_low)
    head_bias = jnp.sum(grad_pred, 0)
    grad_y, gain, shift = norm_back(project_back(pred_low, dec["head"]), y_dec, dec["gf"])
    grad_grid, grads_dec = block_backward(grad_y, stored_dec, dec, H_DEC)
    grads_dec["head"] = grad_head
    grads_dec["head_bias"] = head_bias
    grads_dec["gf"] = gain
    grads_dec["bf"] = shift
    grads_dec["mask"] = jnp.sum(grad_grid * (1.0 - kept)[:, None], 0)
    grads_dec["first_bias"] = jnp.sum(grad_grid * kept[:, None], 0)
    embed_low = project(chosen, grad_grid.astype(jnp.bfloat16)).astype(jnp.bfloat16)
    grads_dec["first"] = weight_grad(sent, embed_low)

    grad_sent = project_back(embed_low, dec["first"]).astype(jnp.bfloat16).astype(jnp.float32)
    grad_y, gain, shift = norm_back(grad_sent, y_enc, enc["gf"])
    grad_embed, grads_enc = block_backward(grad_y, stored_enc, enc, H_ENC)
    grads_enc["gf"] = gain
    grads_enc["bf"] = shift
    grads_enc["first"] = weight_grad(xin, grad_embed.astype(jnp.bfloat16))
    grads_enc["first_bias"] = jnp.sum(grad_embed, 0)
    return grads_enc, grads_dec, loss


def local(pixels, keep_index, clear_mask, slot_tile, master, moment_one, moment_two):
    n_dp = lax.axis_size("dp")
    n_dev = 2 * n_dp
    section, place = lax.axis_index("section"), lax.axis_index("dp")
    me = section * n_dp + place
    slots = master.shape[1]
    per = -(-sum(USED) // n_dev)
    rows_each = PARTS_ROWS if n_dp == 16 else 8 * (-(-per // 8))

    pix = lax.dynamic_index_in_dim(pixels, section, 0, keepdims=False)[0]
    keep = lax.dynamic_index_in_dim(keep_index, section, 0, keepdims=False)[0]
    clear = lax.dynamic_index_in_dim(clear_mask, section, 0, keepdims=False)[0]
    kept = jnp.any(keep[:, None] == jnp.arange(SEQ), axis=0).astype(jnp.float32)
    valid = clear.astype(jnp.float32) * (1.0 - kept)
    band_view = pix.reshape(SEQ, BANDS, PATCH_PIX).astype(jnp.float32)
    sums = jnp.concatenate(
        [jnp.sum(band_view, (0, 2)), jnp.sum(band_view * band_view, (0, 2)), jnp.sum(valid)[None]]
    )
    sums = jnp.pad(sums, (0, 1024 - sums.shape[0])).reshape(8, 128)

    def order(table, start):
        used = (table < TILES).astype(jnp.int32)
        count = table.shape[0]
        before = (jnp.arange(count)[:, None] > jnp.arange(count)[None]).astype(jnp.int32)
        return used, jnp.sum(before * used[None], 1) + start

    table_own = slot_tile[0]
    used_own, order_own = order(table_own, USED[0] * section)
    used_mine = lax.dynamic_slice_in_dim(used_own, place * slots, slots)
    order_mine = lax.dynamic_slice_in_dim(order_own, place * slots, slots)
    goes = lax.rem(order_mine, n_dev)
    slot_for = jnp.sum(
        jnp.arange(slots)[None] * used_mine[None] * (goes[None] == jnp.arange(n_dev)[:, None]), 1
    ).astype(jnp.int32)
    dealt = pick_tiles(master[0], slot_for, jnp.bfloat16, "deal_weights")
    table_out = jnp.pad(table_own, (0, 1024 - table_own.shape[0])).reshape(8, 128)
    arrived, all_sums, all_tables = exchange("deal", 1, n_dp, [dealt], [sums, table_out])

    totals = jnp.sum(all_sums, 0).reshape(-1)
    pixel_count = n_dev * SEQ * PATCH_PIX
    band_mean = totals[:BANDS] / pixel_count
    band_scale = lax.rsqrt(totals[BANDS : 2 * BANDS] / pixel_count - band_mean * band_mean + EPS_BAND)
    valid_count = jnp.maximum(totals[2 * BANDS], 1.0)

    n_slots = table_own.shape[0]
    tables = jnp.stack([all_tables[s * n_dp].reshape(-1)[:n_slots] for s in range(2)])
    both = [order(tables[s], USED[0] * s) for s in range(2)]
    used_all = jnp.concatenate([b[0] for b in both])
    order_all = jnp.concatenate([b[1] for b in both])
    owner_all = jnp.arange(2 * n_slots) // slots
    held = jnp.arange(per) * n_dev + me
    match = used_all[None] * (order_all[None] == held[:, None])
    from_owner = jnp.sum(match * owner_all[None], 1).astype(jnp.int32)
    is_held = jnp.sum(match, 1)
    block = pick_tiles(arrived, from_owner, jnp.bfloat16, "hold_weights")
    if n_dp == 16:
        tiles = gather_all(block, 2).reshape(n_dev * per, TR, TC)
    else:
        tiles = lax.all_gather(lax.all_gather(block, "dp"), "section").reshape(n_dev * per, TR, TC)

    where_tile = []
    line_tile = []
    for s in range(2):
        hit = tables[s][None] == jnp.arange(TILES)[:, None]
        rank = jnp.sum(hit * both[s][1][None], 1)
        device, turn = lax.rem(rank, n_dev), lax.div(rank, n_dev)
        where_tile.append((device * per + turn).astype(jnp.int32))
        line_tile.append((device * rows_each + line_of(turn, n_dp)).astype(jnp.int32))

    weights = []
    for s in range(2):
        matrices, vectors = layout(s)
        found, base = {}, 0
        for name, rows, columns in matrices:
            found[name] = unpack_matrix(tiles, where_tile[s], base, rows, columns, f"{name}_{s}")
            base += rows * columns // (TR * TC)
        flat = lax.dynamic_index_in_dim(tiles, where_tile[s][base], 0, keepdims=False).reshape(-1)
        offset = 0
        for name, length in vectors:
            found[name] = flat[offset : offset + length].astype(jnp.float32)
            offset += length
        weights.append(found)

    grads_enc, grads_dec, loss = item_step(
        weights[0], weights[1], pix, keep, kept, valid, band_mean, band_scale, valid_count
    )

    codes = None
    scales = jnp.zeros((n_dev * rows_each, TC), jnp.float32)
    for s, grads in ((1, grads_dec), (0, grads_enc)):
        matrices, vectors = layout(s)
        base = 0
        for name, rows, columns in matrices:
            codes, scales = pack_matrix(
                grads[name], where_tile[s], line_tile[s], base, codes, scales, n_dev * per, f"{name}_{s}"
            )
            base += rows * columns // (TR * TC)
        line = jnp.concatenate([grads[name] for name, length in vectors])
        line = jnp.pad(line, (0, TR * TC - line.shape[0])).reshape(TR, TC)
        codes, scales = pack_matrix(line, where_tile[s], line_tile[s], base, codes, scales, n_dev * per, f"vectors_{s}")

    if n_dp == 16:
        own_codes, own_scales = reduce_all(
            codes.reshape(2, n_dp, per, TR, TC), scales.reshape(2, n_dp, rows_each, TC), 3
        )
    else:
        wide = scales.reshape(n_dev, rows_each, TC)[:, :per]
        values = jnp.where(wide[:, :, None] > 0.0, codes.reshape(n_dev, per, TR, TC).astype(jnp.float32), 0.0)
        values = values * wide[:, :, None]
        values = lax.psum_scatter(values, ("section", "dp"), scatter_dimension=0, tiled=True)[0]
        top = jnp.max(jnp.abs(values), 1, keepdims=True)
        up = jnp.where(top > 0.0, 32766.0 / top, 0.0)
        own_codes = jnp.round(values * up).astype(jnp.int16)
        own_scales = jnp.pad(top[:, 0] * (1.0 / 32766.0), ((0, rows_each - per), (0, 0)))
    own_scale = own_scales[line_of(jnp.arange(per), n_dp)]
    own = jnp.where(is_held[:, None, None] > 0, own_codes.astype(jnp.float32) * own_scale[:, None], 0.0)
    tail = jnp.stack([jnp.sum(own * own), loss])
    tail = jnp.pad(tail, (0, 1022)).reshape(8, 128)

    turn_for = jnp.sum(
        jnp.arange(per)[None] * is_held[None] * (from_owner[None] == jnp.arange(n_dev)[:, None]), 1
    ).astype(jnp.int32)
    codes_back = pick_tiles(own_codes, turn_for, jnp.int16, "deal_gradients")
    scales_back = own_scale[turn_for][:, None]
    codes_mine, scales_mine, tails = exchange("return", 4, n_dp, [codes_back, scales_back], [tail])
    totals = jnp.sum(tails, 0)[0]
    grad_norm = jnp.sqrt(totals[0])
    factor = jnp.minimum(1.0, CLIP_NORM / (grad_norm + 1e-06))
    master_new, first_new, second_new = adam(
        codes_mine, scales_mine, goes, used_mine, factor[None], master[0], moment_one[0], moment_two[0]
    )
    return master_new[None], first_new[None], second_new[None], totals[1][None], grad_norm[None]


PARTS_ROWS = 24


def line_of(turn, n_dp):
    if n_dp != 16:
        return turn
    return turn + 3 * (turn >= 5) + 3 * (turn >= 10)


def solution(mesh):
    return jax.shard_map(
        local,
        mesh=mesh,
        in_specs=(
            P(None, "dp", None, None),
            P(None, "dp", None),
            P(None, "dp", None),
            P("section", None),
            P("section", "dp", None, None),
            P("section", "dp", None, None),
            P("section", "dp", None, None),
        ),
        out_specs=(
            P("section", "dp", None, None),
            P("section", "dp", None, None),
            P("section", "dp", None, None),
            P(),
            P(),
        ),
        check_vma=False,
    )
```

```python
import functools
import math

import jax
import jax.numpy as jnp
import numpy as np
from jax import lax
from jax.experimental import pallas as pl
from jax.experimental.pallas import tpu as pltpu
from jax.sharding import PartitionSpec as P

D_ENC = 768
H_ENC = 12
FF_ENC = 3072
D_DEC = 512
H_DEC = 16
FF_DEC = 2048
BANDS = 6
PATCH_PIX = 256
PATCH_DIM = 1536
SEQ = 588
KEEP = 147
STEP = 5
TILES = 256
USED = (253, 133)

EPS_NORM = 1e-06
EPS_BAND = 1e-05
CLIP_NORM = 0.001
RATE = 0.02
DECAY = 0.05
BETA_ONE = 0.5
BETA_TWO = 0.75
ADAM_EPS = 1e-08

MESH = pl.DeviceIdType.MESH
TR, TC = 128, 256
PARTS = ((0, 8), (8, 13))
PARTS_ROWS = 16


def neighbours(section, place):
    x, y, z = lax.rem(place, 2), lax.rem(lax.div(place, 2), 2), lax.div(place, 4)

    def at(dz, dv, du):
        dx = (1 - section) * du + section * dv
        dy = (1 - section) * dv + section * du
        return lax.rem(z + dz, 4) * 4 + lax.rem(y + dy, 2) * 2 + lax.rem(x + dx, 2)

    return at


def exchange(name, cid, n_dp, dealt, shared):
    n_dev = 2 * n_dp
    n_a, n_s = len(dealt), len(shared)
    n_all = n_a + n_s

    def kernel(*refs):
        sources, targets = refs[:n_all], refs[n_all : 2 * n_all]
        send_sem, recv_sem, own_sem = refs[2 * n_all :]
        section, place = lax.axis_index("section"), lax.axis_index("dp")
        me = section * n_dp + place

        def who(step):
            other = lax.rem(me + step, n_dev)
            return other, (lax.div(other, n_dp), lax.rem(other, n_dp))

        barrier = pltpu.get_barrier_semaphore()

        def greet(step, carry):
            pl.semaphore_signal(barrier, inc=1, device_id=who(step)[1], device_id_type=MESH)
            return carry

        lax.fori_loop(1, n_dev, greet, 0)
        own = []
        for which in range(n_all):
            source = sources[which].at[me] if which < n_a else sources[which]
            copy = pltpu.make_async_copy(source, targets[which].at[me], own_sem.at[which])
            copy.start()
            own.append(copy)
        pl.semaphore_wait(barrier, n_dev - 1)

        def made(which, step):
            other, place_of = who(step)
            source = sources[which].at[other] if which < n_a else sources[which]
            return pltpu.make_async_remote_copy(
                src_ref=source,
                dst_ref=targets[which].at[me],
                send_sem=send_sem.at[which, step],
                recv_sem=recv_sem.at[which, step],
                device_id=place_of,
                device_id_type=MESH,
            )

        def begin(step, carry):
            for which in reversed(range(n_all)):
                made(which, step).start()
            return carry

        def end(step, carry):
            for which in range(n_all):
                made(which, step).wait()
            return carry

        lax.fori_loop(1, n_dev, begin, 0)
        for copy in own:
            copy.wait()
        lax.fori_loop(1, n_dev, end, 0)

    arrays = list(dealt) + list(shared)
    shapes = [jax.ShapeDtypeStruct(a.shape, a.dtype) for a in dealt] + [
        jax.ShapeDtypeStruct((n_dev,) + a.shape, a.dtype) for a in shared
    ]
    any_spec = pl.BlockSpec(memory_space=pltpu.HBM)
    return pl.pallas_call(
        kernel,
        out_shape=shapes,
        in_specs=[any_spec] * n_all,
        out_specs=[any_spec] * n_all,
        scratch_shapes=[
            pltpu.SemaphoreType.DMA((n_all, n_dev)),
            pltpu.SemaphoreType.DMA((n_all, n_dev)),
            pltpu.SemaphoreType.DMA((n_all,)),
        ],
        compiler_params=pltpu.CompilerParams(collective_id=cid, has_side_effects=True),
        name=name,
    )(*arrays)


def code(values):
    top = jnp.max(jnp.abs(values), axis=0, keepdims=True)
    up = jnp.where(top > 0.0, 32766.0 / top, 0.0)
    scaled = values * up
    return (scaled + jnp.where(scaled >= 0.0, 0.5, -0.5)).astype(jnp.int32).astype(jnp.int16), top * (1.0 / 32766.0)


def gather_all(block, cid):
    per = block.shape[0]
    cut = [0, 4, 8, 11, per]
    ways = (("z", "y", "x"), ("z", "x", "y"), ("y", "z", "x"), ("x", "z", "y"))

    def kernel(block_ref, all_ref, send_sem, recv_sem, side_send, side_recv, own_sem):
        section, place = lax.axis_index("section"), lax.axis_index("dp")
        at = neighbours(section, place)

        barrier = pltpu.get_barrier_semaphore()
        peers = [(1 - section, place)] + [
            (section, at(*d)) for d in ((0, 0, 1), (0, 1, 0), (1, 0, 0), (2, 0, 0), (3, 0, 0))
        ]
        for peer in peers:
            pl.semaphore_signal(barrier, inc=1, device_id=peer, device_id_type=MESH)
        own = pltpu.make_async_copy(block_ref, all_ref.at[section, place], own_sem)
        own.start()
        pl.semaphore_wait(barrier, len(peers))
        copies = {}
        sides = {}
        count = [0]

        def rows(way):
            return pl.ds(cut[way], cut[way + 1] - cut[way])

        def send(way, origin, move):
            target = at(*move)
            holder = at(*origin)
            arrived = tuple((o - m) % s for o, m, s in zip(origin, move, (4, 2, 2)))
            source = block_ref.at[rows(way)] if origin == (0, 0, 0) else all_ref.at[section, holder, rows(way)]
            index = count[0]
            count[0] += 1
            copy = pltpu.make_async_remote_copy(
                src_ref=source,
                dst_ref=all_ref.at[section, holder, rows(way)],
                send_sem=send_sem.at[index],
                recv_sem=recv_sem.at[index],
                device_id=(section, target),
                device_id_type=MESH,
            )
            copy.start()
            copies[way, arrived] = (copy, index)

        def arrive(way, origin):
            holder = at(*origin)
            copy, index = copies[way, origin]
            pltpu.make_async_remote_copy(
                src_ref=block_ref.at[rows(way)],
                dst_ref=all_ref.at[section, holder, rows(way)],
                send_sem=send_sem.at[index],
                recv_sem=recv_sem.at[index],
                device_id=(section, place),
                device_id_type=MESH,
            ).wait_recv()

        side_count = [0]

        def side(way, origin):
            holder = at(*origin)
            source = block_ref.at[rows(way)] if origin == (0, 0, 0) else all_ref.at[section, holder, rows(way)]
            index = side_count[0]
            side_count[0] += 1
            copy = pltpu.make_async_remote_copy(
                src_ref=source,
                dst_ref=all_ref.at[section, holder, rows(way)],
                send_sem=side_send.at[index],
                recv_sem=side_recv.at[index],
                device_id=(1 - section, place),
                device_id_type=MESH,
            )
            copy.start()
            sides[way, origin] = (copy, index)

        unit = {
            "x": [(0, 0, 1)],
            "y": [(0, 1, 0)],
            "z": [(1, 0, 0), (2, 0, 0), (3, 0, 0)],
        }

        def moved(origin, move):
            return tuple((o - m) % s for o, m, s in zip(origin, move, (4, 2, 2)))

        zero = (0, 0, 0)
        held = {way: [zero] for way in range(4)}
        for way, dims in enumerate(ways):
            for move in unit[dims[0]]:
                send(way, zero, move)
        for way, dims in enumerate(ways):
            for move in unit[dims[1]]:
                send(way, zero, move)
            for move in unit[dims[2]]:
                send(way, zero, move)
        for way in range(4):
            side(way, zero)
        first = {way: [moved(zero, m) for m in unit[ways[way][0]]] for way in range(4)}
        for way in (2, 3, 0, 1):
            dims = ways[way]
            for origin in first[way]:
                arrive(way, origin)
                for move in unit[dims[1]]:
                    send(way, origin, move)
                for move in unit[dims[2]]:
                    send(way, origin, move)
                side(way, origin)
        second = {}
        for way in range(4):
            have = [zero] + first[way]
            second[way] = [moved(o, m) for m in unit[ways[way][1]] for o in have]
        longest = max(len(v) for v in second.values())
        for i in range(longest):
            for way in (0, 1, 2, 3):
                if i < len(second[way]):
                    origin = second[way][i]
                    arrive(way, origin)
                    for move in unit[ways[way][2]]:
                        send(way, origin, move)
                    side(way, origin)
        third = {}
        for way in range(4):
            have = [zero] + first[way] + second[way]
            third[way] = [moved(o, m) for m in unit[ways[way][2]] for o in have]
        for i in range(8):
            for way in range(4):
                arrive(way, third[way][i])
                side(way, third[way][i])
        own.wait()
        for (way, origin), (copy, index) in copies.items():
            copy.wait_send()
        for (way, origin), (copy, index) in sides.items():
            copy.wait_send()
            holder = at(*origin)
            pltpu.make_async_remote_copy(
                src_ref=block_ref.at[rows(way)],
                dst_ref=all_ref.at[1 - section, holder, rows(way)],
                send_sem=side_send.at[index],
                recv_sem=side_recv.at[index],
                device_id=(1 - section, place),
                device_id_type=MESH,
            ).wait_recv()

    spec = pl.BlockSpec(memory_space=pltpu.HBM)
    return pl.pallas_call(
        kernel,
        out_shape=jax.ShapeDtypeStruct((2, 16, per, TR, TC), block.dtype),
        in_specs=[spec],
        out_specs=spec,
        scratch_shapes=[
            pltpu.SemaphoreType.DMA((60,)),
            pltpu.SemaphoreType.DMA((60,)),
            pltpu.SemaphoreType.DMA((64,)),
            pltpu.SemaphoreType.DMA((64,)),
            pltpu.SemaphoreType.DMA,
        ],
        compiler_params=pltpu.CompilerParams(collective_id=cid, has_side_effects=True),
        name="gather_tiles",
    )(block)


def reduce_all(codes, scales, cid, SUMS=True):
    per = codes.shape[2]

    def kernel(codes_ref, scales_ref, out_ref, outs_ref, acc, accs, rc, rcs, r_code, r_scale,
               own_sem, owns_sem, c_send, c_recv, p_send, p_recv):
        section, place = lax.axis_index("section"), lax.axis_index("dp")
        at, at_other = neighbours(section, place), neighbours(1 - section, place)
        sibling = (1 - section, place)
        to_u, to_v = (section, at(0, 0, 1)), (section, at(0, 1, 0))

        def to_z(dz):
            return (section, at(dz, 0, 0))

        barrier = pltpu.get_barrier_semaphore()
        peers = [sibling, to_u, to_v, to_z(1), to_z(2), to_z(3)]
        for peer in peers:
            pl.semaphore_signal(barrier, inc=1, device_id=peer, device_id_type=MESH)
        order = [(dz, dv, du) for dz in (2, 1, 3, 0) for dv in (1, 0) for du in (1, 0)]
        loads = {}
        for n, d in enumerate(order):
            b = at(*d)
            loads[d] = (
                pltpu.make_async_copy(codes_ref.at[section, b], acc.at[b], own_sem.at[n]),
                pltpu.make_async_copy(scales_ref.at[section, b], accs.at[b], owns_sem.at[n]),
            )
            for copy in loads[d]:
                copy.start()
        pl.semaphore_wait(barrier, len(peers))
        crossing = {}
        for n, d in enumerate(order):
            b = at_other(*d)
            pair = []
            for k, (source, target) in enumerate(((codes_ref, rc), (scales_ref, rcs))):
                copy = pltpu.make_async_remote_copy(
                    src_ref=source.at[1 - section, b],
                    dst_ref=target.at[b],
                    send_sem=c_send.at[k, n],
                    recv_sem=c_recv.at[k, n],
                    device_id=sibling,
                    device_id_type=MESH,
                )
                copy.start()
                pair.append(copy)
            crossing[d] = pair

        def add(b, part, from_code, from_first, from_scale, from_row):
            first, count = PARTS[part][0], PARTS[part][1] - PARTS[part][0]

            def one(t, carry):
                line = pl.ds(8 * part + t, 1)
                mine = acc[b, first + t].astype(jnp.float32) * accs[b, line, :]
                theirs = from_code[from_first + t].astype(jnp.float32) * from_scale[pl.ds(from_row + t, 1), :]
                value, scale = code(mine + theirs)
                acc[b, first + t] = value
                accs[b, line, :] = scale
                return carry

            if SUMS:
                lax.fori_loop(0, count, one, 0)

        sends = {}
        used = [0, 0]

        def send(part, key, b, peer):
            t0, t1 = PARTS[part]
            slot, index = used
            used[0] += t1 - t0
            used[1] += 1
            pair = []
            for k, (source, target) in enumerate(
                (
                    (acc.at[b, pl.ds(t0, t1 - t0)], r_code.at[pl.ds(slot, t1 - t0)]),
                    (accs.at[b, pl.ds(8 * part, 8)], r_scale.at[index]),
                )
            ):
                copy = pltpu.make_async_remote_copy(
                    src_ref=source,
                    dst_ref=target,
                    send_sem=p_send.at[k, index],
                    recv_sem=p_recv.at[k, index],
                    device_id=peer,
                    device_id_type=MESH,
                )
                copy.start()
                pair.append(copy)
            sends[part, key] = (pair, slot, index)

        def take(part, key, b):
            pair, slot, index = sends[part, key]
            for copy in pair:
                copy.wait_recv()
            add(b, part, r_code, slot, r_scale.at[index], 0)

        def first(d):
            dz, dv, du = d
            b = at(*d)
            for copy in loads[d]:
                copy.wait()
            for copy in crossing[d]:
                copy.wait_recv()
            for part in range(2):
                add(b, part, rc.at[b], PARTS[part][0], rcs.at[b], 8 * part)
            if du:
                send(0, ("1", dz, dv), b, to_u)
            if dv:
                send(1, ("1", dz, du), b, to_v)

        def second(dz):
            for du in (1, 0):
                b = at(dz, 0, du)
                take(1, ("1", dz, du), b)
                if dz:
                    send(1, ("2", dz, du), b, to_z(dz))
            for dv in (1, 0):
                b = at(dz, dv, 0)
                take(0, ("1", dz, dv), b)
                if dv:
                    send(0, ("2", dz), b, to_v)

        def third(dz):
            b = at(dz, 0, 0)
            take(0, ("2", dz), b)
            if dz:
                send(0, ("3", dz), b, to_z(dz))

        for d in order:
            first(d)
        for n, dz in enumerate((2, 1, 3, 0)):
            second(dz)
            if n:
                third((2, 1, 3)[n - 1])
        third(0)
        for du in (1, 0):
            b = at(0, 0, du)
            for dz in (1, 3, 2):
                take(1, ("2", dz, du), b)
            if du:
                send(1, ("3",), b, to_u)
        for dz in (1, 3, 2):
            take(0, ("3", dz), place)
        take(1, ("3",), place)
        out_ref[...] = acc[place]
        outs_ref[...] = accs[place]
        for pair in crossing.values():
            for copy in pair:
                copy.wait_send()
        for pair, slot, index in sends.values():
            for copy in pair:
                copy.wait_send()

    sizes = [t1 - t0 for t0, t1 in PARTS]
    n_tiles = 15 * sizes[0] + 15 * sizes[1]
    n_copies = 30
    hbm = pl.BlockSpec(memory_space=pltpu.HBM)
    vmem = pl.BlockSpec(memory_space=pltpu.VMEM)
    return pl.pallas_call(
        kernel,
        out_shape=(
            jax.ShapeDtypeStruct((per, TR, TC), jnp.int16),
            jax.ShapeDtypeStruct((PARTS_ROWS, TC), jnp.float32),
        ),
        in_specs=[hbm, hbm],
        out_specs=(vmem, vmem),
        scratch_shapes=[
            pltpu.VMEM((16, per, TR, TC), jnp.int16),
            pltpu.VMEM((16, PARTS_ROWS, TC), jnp.float32),
            pltpu.VMEM((16, per, TR, TC), jnp.int16),
            pltpu.VMEM((16, PARTS_ROWS, TC), jnp.float32),
            pltpu.VMEM((n_tiles, TR, TC), jnp.int16),
            pltpu.VMEM((n_copies, 8, TC), jnp.float32),
            pltpu.SemaphoreType.DMA((16,)),
            pltpu.SemaphoreType.DMA((16,)),
            pltpu.SemaphoreType.DMA((2, 16)),
            pltpu.SemaphoreType.DMA((2, 16)),
            pltpu.SemaphoreType.DMA((2, n_copies)),
            pltpu.SemaphoreType.DMA((2, n_copies)),
        ],
        compiler_params=pltpu.CompilerParams(
            collective_id=cid, has_side_effects=True, vmem_limit_bytes=60 * 2**20
        ),
        name="reduce_tiles",
    )(codes, scales)


def layout(section_id):
    if section_id == 0:
        width, hidden = D_ENC, FF_ENC
        matrices = [("first", PATCH_DIM, D_ENC)]
        vectors = [("first_bias", D_ENC)]
    else:
        width, hidden = D_DEC, FF_DEC
        matrices = [("first", D_ENC, D_DEC)]
        vectors = [("first_bias", D_DEC), ("mask", D_DEC)]
    matrices = matrices + [
        ("qkv", width, 3 * width),
        ("proj", width, width),
        ("fc1", width, hidden),
        ("fc2", hidden, width),
    ]
    vectors = vectors + [
        ("g1", width),
        ("b1", width),
        ("qv_bias", 2 * width),
        ("proj_bias", width),
        ("g2", width),
        ("b2", width),
        ("fc1_bias", hidden),
        ("fc2_bias", width),
        ("gf", width),
        ("bf", width),
    ]
    if section_id == 1:
        matrices = matrices + [("head", D_DEC, PATCH_DIM)]
        vectors = vectors + [("head_bias", PATCH_DIM)]
    return matrices, vectors


def positions(width):
    place = np.arange(SEQ, dtype=np.float32)[:, None]
    rate = np.exp(np.arange(width // 2, dtype=np.float32) * np.float32(-2.0 * math.log(10000.0) / width))
    angle = (place * rate).astype(np.float32)
    return np.concatenate([np.sin(angle), np.cos(angle)], axis=1).astype(np.float32)


LANES = 128


def pick_tiles(tiles, index, dtype, name):
    count = index.shape[0]

    def kernel(index_ref, tiles_ref, out_ref):
        def one(t, carry):
            out_ref[t] = tiles_ref[index_ref[t]].astype(dtype)
            return carry

        lax.fori_loop(0, count, one, 0)

    return pl.pallas_call(
        kernel,
        out_shape=jax.ShapeDtypeStruct((count, TR, TC), dtype),
        in_specs=[pl.BlockSpec(memory_space=pltpu.SMEM), pl.BlockSpec(memory_space=pltpu.VMEM)],
        out_specs=pl.BlockSpec(memory_space=pltpu.VMEM),
        compiler_params=pltpu.CompilerParams(vmem_limit_bytes=40 * 2**20),
        name=name,
    )(index, tiles)


def groups_of(rows, wide):
    groups = rows // TR
    return max(m for m in range(1, groups + 1) if groups % m == 0 and (m == 1 or m * wide <= 12))


def unpack_matrix(tiles, place, base, rows, columns, name):
    wide = columns // TC
    many = groups_of(rows, wide)
    count = many * wide

    def kernel(place_ref, *refs):
        sources, out_ref, lines = refs[:count], refs[count], refs[count + 1 :]
        for j in range(count):
            for h in range(2):
                lines[h][j * TR : (j + 1) * TR, :] = sources[j][0, :, h * LANES : (h + 1) * LANES].astype(jnp.float32)
        for j in range(wide):
            for h in range(2):
                start = j * TC + h * LANES
                out_ref[:, start : start + LANES] = lines[h][pl.ds(j, many * TR, stride=wide), :].astype(tiles.dtype)

    def spec(j):
        return pl.BlockSpec((1, TR, TC), lambda g, place_ref: (place_ref[base + g * count + j], 0, 0))

    return pl.pallas_call(
        kernel,
        out_shape=jax.ShapeDtypeStruct((rows, columns), tiles.dtype),
        grid_spec=pltpu.PrefetchScalarGridSpec(
            num_scalar_prefetch=1,
            grid=(rows // (many * TR),),
            in_specs=[spec(j) for j in range(count)],
            out_specs=pl.BlockSpec((many * TR, columns), lambda g, place_ref: (g, 0)),
            scratch_shapes=[pltpu.VMEM((count * TR, LANES), jnp.float32)] * 2,
        ),
        compiler_params=pltpu.CompilerParams(vmem_limit_bytes=32 * 2**20),
        name="unpack_" + name,
    )(place, *([tiles] * count))


def pack_matrix(grad, place, line, base, codes, scales, total, name):
    rows, columns = grad.shape
    wide = columns // TC
    many = groups_of(rows, wide)
    count = many * wide
    steps = rows // (many * TR)
    fresh = codes is None

    def kernel(place_ref, line_ref, grad_ref, *refs):
        scales_in = refs[0]
        codes_ref, scales_ref, left, right, ready, sem = refs[-6:]
        step = pl.program_id(0)
        slot = lax.rem(step, 2)

        @pl.when(step == 0)
        def _():
            scales_ref[...] = scales_in[...]

        def copies(at_step, at_slot):
            return [
                pltpu.make_async_copy(
                    ready.at[at_slot, j], codes_ref.at[place_ref[base + at_step * count + j]], sem.at[at_slot, j]
                )
                for j in range(count)
            ]

        @pl.when(step >= 2)
        def _():
            for copy in copies(step - 2, slot):
                copy.wait()

        for j in range(wide):
            for h, lines in enumerate((left, right)):
                start = j * TC + h * LANES
                lines[pl.ds(j, many * TR, stride=wide), :] = grad_ref[:, start : start + LANES]
        for j in range(count):
            at = line_ref[base + step * count + j]
            pair = []
            for h, lines in enumerate((left, right)):
                value, scale = code(lines[j * TR : (j + 1) * TR, :])
                ready[slot, j, :, h * LANES : (h + 1) * LANES] = value
                pair.append(scale)
            scales_ref[pl.ds(at, 1), :] = jnp.concatenate(pair, axis=1)
        for copy in copies(step, slot):
            copy.start()

        @pl.when(step == steps - 1)
        def _():
            if steps > 1:
                for copy in copies(step - 1, 1 - slot):
                    copy.wait()
            for copy in copies(step, slot):
                copy.wait()

    whole = pl.BlockSpec(scales.shape, lambda g, a, b: (0, 0))
    hbm = pl.BlockSpec(memory_space=pltpu.HBM)
    return pl.pallas_call(
        kernel,
        out_shape=(
            jax.ShapeDtypeStruct((total, TR, TC), jnp.int16),
            jax.ShapeDtypeStruct(scales.shape, jnp.float32),
        ),
        grid_spec=pltpu.PrefetchScalarGridSpec(
            num_scalar_prefetch=2,
            grid=(steps,),
            in_specs=[pl.BlockSpec((many * TR, columns), lambda g, a, b: (g, 0)), whole] + ([] if fresh else [hbm]),
            out_specs=(hbm, whole),
            scratch_shapes=[
                pltpu.VMEM((count * TR, LANES), jnp.float32),
                pltpu.VMEM((count * TR, LANES), jnp.float32),
                pltpu.VMEM((2, count, TR, TC), jnp.int16),
                pltpu.SemaphoreType.DMA((2, count)),
            ],
        ),
        input_output_aliases={3: 1} if fresh else {3: 1, 4: 0},
        compiler_params=pltpu.CompilerParams(vmem_limit_bytes=40 * 2**20),
        name="pack_" + name,
    )(place, line, grad, scales, *([] if fresh else [codes]))


def adam(codes, scales, index, used, factor, master, first, second):
    slots = master.shape[0]
    per = 3 if slots % 3 == 0 else 1

    def kernel(index_ref, used_ref, factor_ref, codes_ref, scales_ref, w_ref, m_ref, v_ref, w_out, m_out, v_out):
        for t in range(per):
            slot = pl.program_id(0) * per + t
            source = index_ref[slot]
            grad = codes_ref[source].astype(jnp.float32) * scales_ref[source]
            grad = jnp.where(used_ref[slot] > 0, grad * factor_ref[0], 0.0)
            first_new = BETA_ONE * m_ref[t] + (1.0 - BETA_ONE) * grad
            second_new = BETA_TWO * v_ref[t] + (1.0 - BETA_TWO) * grad * grad
            ratio = (
                first_new
                / (1.0 - BETA_ONE ** float(STEP))
                / (jnp.sqrt(second_new / (1.0 - BETA_TWO ** float(STEP))) + ADAM_EPS)
            )
            w_out[t] = w_ref[t] - RATE * (ratio + DECAY * w_ref[t])
            m_out[t] = first_new
            v_out[t] = second_new

    smem = pl.BlockSpec(memory_space=pltpu.SMEM)
    block = pl.BlockSpec((per, TR, TC), lambda g: (g, 0, 0))
    return pl.pallas_call(
        kernel,
        out_shape=[jax.ShapeDtypeStruct(master.shape, jnp.float32)] * 3,
        grid=(slots // per,),
        in_specs=[
            smem,
            smem,
            smem,
            pl.BlockSpec(codes.shape, lambda g: (0, 0, 0)),
            pl.BlockSpec(scales.shape, lambda g: (0, 0, 0)),
            block,
            block,
            block,
        ],
        out_specs=[block] * 3,
        compiler_params=pltpu.CompilerParams(vmem_limit_bytes=40 * 2**20),
        name="adam",
    )(index, used, factor, codes, scales, master, first, second)


def project(a, w):
    return jnp.dot(a, w, preferred_element_type=jnp.float32)


def project_back(d, w):
    return lax.dot_general(d, w, (((1,), (1,)), ((), ())), preferred_element_type=jnp.float32)


def weight_grad(a, d):
    return lax.dot_general(a, d, (((0,), (0,)), ((), ())), preferred_element_type=jnp.float32)


def layer_norm(values, gain, offset):
    centre = values - jnp.mean(values, -1, keepdims=True)
    return centre * lax.rsqrt(jnp.mean(centre * centre, -1, keepdims=True) + EPS_NORM) * gain + offset


def norm_back(upstream, values, gain):
    centre = values - jnp.mean(values, -1, keepdims=True)
    spread = lax.rsqrt(jnp.mean(centre * centre, -1, keepdims=True) + EPS_NORM)
    normed = centre * spread
    scaled = upstream * gain
    downstream = spread * (
        scaled - jnp.mean(scaled, -1, keepdims=True) - normed * jnp.mean(scaled * normed, -1, keepdims=True)
    )
    return downstream, jnp.sum(upstream * normed, 0), jnp.sum(upstream, 0)


def gelu_slope(pre):
    return 0.5 * (1.0 + lax.erf(pre * (1.0 / math.sqrt(2.0)))) + pre * jnp.exp(-0.5 * pre * pre) * (
        1.0 / math.sqrt(2.0 * math.pi)
    )


def column_sums(values):
    return jnp.sum(values.astype(jnp.float32), 0)


def head_mask(size, h):
    lane = lax.broadcasted_iota(jnp.int32, (1, LANES), 1)
    return (lane >= h * size) & (lane < (h + 1) * size)


def attention(qkv, heads):
    length, width = qkv.shape[0], qkv.shape[1] // 3
    size = width // heads
    groups = width // LANES
    factor = size ** (-0.5)
    cuts = row_cuts(length)

    def kernel(q_ref, k_ref, v_ref, out_ref):
        keys, values = k_ref[...], v_ref[...]
        for lo, hi in cuts:
            total = jnp.zeros((hi - lo, LANES), jnp.float32)
            for h in range(LANES // size):
                mask = head_mask(size, h)
                query = jnp.where(mask, q_ref[lo:hi, :], jnp.zeros((), jnp.bfloat16))
                scores = project_back(query, keys) * factor
                top = jnp.max(scores, -1, keepdims=True)
                power = jnp.exp(scores - top)
                probs = power / jnp.sum(power, -1, keepdims=True)
                mixed = project(probs.astype(jnp.bfloat16), values)
                total = jnp.where(mask, mixed, total)
            out_ref[lo:hi, :] = total.astype(jnp.bfloat16)

    def spec(offset):
        return pl.BlockSpec((length, LANES), lambda g: (0, g + offset))

    return pl.pallas_call(
        kernel,
        out_shape=jax.ShapeDtypeStruct((length, width), jnp.bfloat16),
        grid=(groups,),
        in_specs=[spec(0), spec(groups), spec(2 * groups)],
        out_specs=spec(0),
        compiler_params=pltpu.CompilerParams(vmem_limit_bytes=40 * 2**20),
        name=f"attention_{heads}",
    )(qkv, qkv, qkv)


def row_cuts(length):
    step = 160
    return [(lo, min(lo + step, length)) for lo in range(0, length, step)]


def attention_back(qkv, grad, heads):
    length, width = grad.shape
    size = width // heads
    groups = width // LANES
    factor = size ** (-0.5)
    cuts = row_cuts(length)

    def kernel(q_ref, k_ref, v_ref, g_ref, dq_ref, dk_ref, dv_ref, dk_sum, dv_sum):
        zero = jnp.zeros((), jnp.bfloat16)
        dk_sum[...] = jnp.zeros_like(dk_sum)
        dv_sum[...] = jnp.zeros_like(dv_sum)
        for lo, hi in cuts:
            query_all, grad_all = q_ref[lo:hi, :], g_ref[lo:hi, :]
            dq = jnp.zeros((hi - lo, LANES), jnp.float32)
            for h in range(LANES // size):
                mask = head_mask(size, h)
                query = jnp.where(mask, query_all, zero)
                upstream = jnp.where(mask, grad_all, zero)
                scores = project_back(k_ref[...], query) * factor
                power = jnp.exp(scores - jnp.max(scores, 0, keepdims=True))
                probs = power / jnp.sum(power, 0, keepdims=True)
                d_probs = project_back(v_ref[...], upstream)
                inner = jnp.sum(d_probs * probs, 0, keepdims=True)
                d_scores = (probs * (d_probs - inner)).astype(jnp.bfloat16)
                dv_sum[...] += project(probs.astype(jnp.bfloat16), upstream)
                dk_sum[...] += project(d_scores, query)
                dq = jnp.where(mask, weight_grad(d_scores, k_ref[...]), dq)
            dq_ref[lo:hi, :] = (dq * factor).astype(jnp.bfloat16)
        dk_ref[...] = (dk_sum[...] * factor).astype(jnp.bfloat16)
        dv_ref[...] = dv_sum[...].astype(jnp.bfloat16)

    def spec(offset):
        return pl.BlockSpec((length, LANES), lambda g: (0, g + offset))

    return pl.pallas_call(
        kernel,
        out_shape=[jax.ShapeDtypeStruct((length, width), jnp.bfloat16)] * 3,
        grid=(groups,),
        in_specs=[spec(0), spec(groups), spec(2 * groups), spec(0)],
        out_specs=[spec(0)] * 3,
        scratch_shapes=[pltpu.VMEM((length, LANES), jnp.float32)] * 2,
        compiler_params=pltpu.CompilerParams(vmem_limit_bytes=40 * 2**20),
        name=f"attention_back_{heads}",
    )(qkv, qkv, qkv, grad)


def head_step(final, w, bias, pix, valid, inverse):
    def kernel(inverse_ref, final_ref, w_ref, bias_ref, pix_ref, valid_ref, low_ref, sums_ref, loss_ref, back_ref):
        one = inverse_ref[0]
        for band in range(BANDS):
            columns = slice(band * PATCH_PIX, (band + 1) * PATCH_PIX)
            predicted = jnp.dot(final_ref[...], w_ref[:, columns], preferred_element_type=jnp.float32)
            predicted = predicted + bias_ref[:, columns]
            values = pix_ref[:, columns].astype(jnp.float32)
            centre = values - jnp.mean(values, -1, keepdims=True)
            target = centre * lax.rsqrt(jnp.mean(centre * centre, -1, keepdims=True) + EPS_NORM)
            misfit = predicted - target
            valid_misfit = valid_ref[...] * misfit
            part = jnp.sum(valid_misfit * misfit, 0, keepdims=True) * (one / (BANDS * PATCH_PIX))
            if band:
                loss_ref[...] += part
            else:
                loss_ref[...] = part
            grad = valid_misfit * (one * (2.0 / (BANDS * PATCH_PIX)))
            low = grad.astype(jnp.bfloat16)
            low_ref[:, columns] = low
            sums_ref[:, columns] = jnp.sum(grad, 0, keepdims=True)
            back = lax.dot_general(low, w_ref[:, columns], (((1,), (1,)), ((), ())), preferred_element_type=jnp.float32)
            if band:
                back_ref[...] += back
            else:
                back_ref[...] = back

    vmem = pl.BlockSpec(memory_space=pltpu.VMEM)
    return pl.pallas_call(
        kernel,
        out_shape=[
            jax.ShapeDtypeStruct((SEQ, PATCH_DIM), jnp.bfloat16),
            jax.ShapeDtypeStruct((1, PATCH_DIM), jnp.float32),
            jax.ShapeDtypeStruct((1, PATCH_PIX), jnp.float32),
            jax.ShapeDtypeStruct((SEQ, D_DEC), jnp.float32),
        ],
        in_specs=[pl.BlockSpec(memory_space=pltpu.SMEM)] + [vmem] * 5,
        out_specs=[vmem] * 4,
        compiler_params=pltpu.CompilerParams(vmem_limit_bytes=40 * 2**20),
        name="head_step",
    )(inverse, final, w, bias, pix, valid)


def block_forward(x, w, heads):
    width = x.shape[-1]
    a = layer_norm(x, w["g1"], w["b1"]).astype(jnp.bfloat16)
    bias = jnp.concatenate([w["qv_bias"][:width], jnp.zeros((width,), jnp.float32), w["qv_bias"][width:]])
    qkv = (project(a, w["qkv"]) + bias).astype(jnp.bfloat16)
    attended = attention(qkv, heads)
    middle = x + project(attended, w["proj"]) + w["proj_bias"]
    c = layer_norm(middle, w["g2"], w["b2"]).astype(jnp.bfloat16)
    pre = project(c, w["fc1"]) + w["fc1_bias"]
    z = jax.nn.gelu(pre, approximate=False).astype(jnp.bfloat16)
    out = middle + project(z, w["fc2"]) + w["fc2_bias"]
    return out, (x, a, qkv, attended, middle, c, pre, z)


def block_backward(grad_out, stored, w, heads):
    x, a, qkv, attended, middle, c, pre, z = stored
    width = x.shape[-1]
    grads = {}
    two = grad_out.astype(jnp.bfloat16)
    grads["fc2"] = weight_grad(z, two)
    grads["fc2_bias"] = column_sums(two)
    grad_pre = (project_back(two, w["fc2"]) * gelu_slope(pre)).astype(jnp.bfloat16)
    grads["fc1"] = weight_grad(c, grad_pre)
    grads["fc1_bias"] = column_sums(grad_pre)
    grad_c, grads["g2"], grads["b2"] = norm_back(project_back(grad_pre, w["fc1"]), middle, w["g2"])
    grad_middle = grad_out + grad_c
    one = grad_middle.astype(jnp.bfloat16)
    grads["proj"] = weight_grad(attended, one)
    grads["proj_bias"] = column_sums(one)
    grad_att = project_back(one, w["proj"]).astype(jnp.bfloat16)
    grad_qkv = jnp.concatenate(attention_back(qkv, grad_att, heads), -1)
    grads["qkv"] = weight_grad(a, grad_qkv)
    sums = column_sums(grad_qkv)
    grads["qv_bias"] = jnp.concatenate([sums[:width], sums[2 * width :]])
    grad_a, grads["g1"], grads["b1"] = norm_back(project_back(grad_qkv, w["qkv"]), x, w["g1"])
    return grad_middle + grad_a, grads


def item_step(enc, dec, pix, keep, kept, valid, band_mean, band_scale, valid_count):
    chosen = (keep[:, None] == jnp.arange(SEQ)).astype(jnp.bfloat16)
    mean_line = jnp.repeat(band_mean, PATCH_PIX, total_repeat_length=PATCH_DIM)
    scale_line = jnp.repeat(band_scale, PATCH_PIX, total_repeat_length=PATCH_DIM)
    xin = ((project(chosen, pix) - mean_line) * scale_line).astype(jnp.bfloat16)
    place_enc = jnp.dot(chosen.astype(jnp.float32), jnp.asarray(positions(D_ENC)), precision=lax.Precision.HIGHEST)
    embedded = project(xin, enc["first"]) + enc["first_bias"] + place_enc
    y_enc, stored_enc = block_forward(embedded, enc, H_ENC)
    sent = layer_norm(y_enc, enc["gf"], enc["bf"]).astype(jnp.bfloat16)

    spread = weight_grad(chosen, sent).astype(jnp.bfloat16)
    placed = project(spread, dec["first"]) + dec["first_bias"]
    grid = jnp.where(kept[:, None] > 0.0, placed, dec["mask"]) + jnp.asarray(positions(D_DEC))
    y_dec, stored_dec = block_forward(grid, dec, H_DEC)
    final = layer_norm(y_dec, dec["gf"], dec["bf"]).astype(jnp.bfloat16)
    pred_low, head_bias, loss_terms, grad_final = head_step(
        final, dec["head"], dec["head_bias"][None], pix, valid[:, None], (1.0 / valid_count)[None]
    )
    loss = jnp.sum(loss_terms)
    grad_head = weight_grad(final, pred_low)
    grad_y, gain, shift = norm_back(grad_final, y_dec, dec["gf"])
    grad_grid, grads_dec = block_backward(grad_y, stored_dec, dec, H_DEC)
    grads_dec["head"] = grad_head
    grads_dec["head_bias"] = head_bias[0]
    grads_dec["gf"] = gain
    grads_dec["bf"] = shift
    grads_dec["mask"] = jnp.sum(grad_grid * (1.0 - kept)[:, None], 0)
    grads_dec["first_bias"] = jnp.sum(grad_grid * kept[:, None], 0)
    embed_low = project(chosen, grad_grid.astype(jnp.bfloat16)).astype(jnp.bfloat16)
    grads_dec["first"] = weight_grad(sent, embed_low)

    grad_sent = project_back(embed_low, dec["first"]).astype(jnp.bfloat16).astype(jnp.float32)
    grad_y, gain, shift = norm_back(grad_sent, y_enc, enc["gf"])
    grad_embed, grads_enc = block_backward(grad_y, stored_enc, enc, H_ENC)
    grads_enc["gf"] = gain
    grads_enc["bf"] = shift
    grads_enc["first"] = weight_grad(xin, grad_embed.astype(jnp.bfloat16))
    grads_enc["first_bias"] = jnp.sum(grad_embed, 0)
    return grads_enc, grads_dec, loss


def local(pixels, keep_index, clear_mask, slot_tile, master, moment_one, moment_two):
    n_dp = lax.axis_size("dp")
    n_dev = 2 * n_dp
    section, place = lax.axis_index("section"), lax.axis_index("dp")
    me = section * n_dp + place
    slots = master.shape[1]
    per = -(-sum(USED) // n_dev)
    rows_each = 8 * (-(-per // 8))

    pix = lax.dynamic_index_in_dim(pixels, section, 0, keepdims=False)[0]
    keep = lax.dynamic_index_in_dim(keep_index, section, 0, keepdims=False)[0]
    clear = lax.dynamic_index_in_dim(clear_mask, section, 0, keepdims=False)[0]
    kept = jnp.any(keep[:, None] == jnp.arange(SEQ), axis=0).astype(jnp.float32)
    valid = clear.astype(jnp.float32) * (1.0 - kept)
    wide_pix = pix.astype(jnp.float32)
    sums = jnp.concatenate(
        [
            jnp.sum(jnp.sum(wide_pix, 0).reshape(BANDS, PATCH_PIX), 1),
            jnp.sum(jnp.sum(wide_pix * wide_pix, 0).reshape(BANDS, PATCH_PIX), 1),
            jnp.sum(valid)[None],
        ]
    )
    sums = jnp.pad(sums, (0, 1024 - sums.shape[0])).reshape(8, 128)

    def order(table, start):
        used = (table < TILES).astype(jnp.int32)
        count = table.shape[0]
        before = (jnp.arange(count)[:, None] > jnp.arange(count)[None]).astype(jnp.int32)
        return used, jnp.sum(before * used[None], 1) + start

    table_own = slot_tile[0]
    used_own, order_own = order(table_own, USED[0] * section)
    used_mine = lax.dynamic_slice_in_dim(used_own, place * slots, slots)
    order_mine = lax.dynamic_slice_in_dim(order_own, place * slots, slots)
    goes = lax.rem(order_mine, n_dev)
    slot_for = jnp.sum(
        jnp.arange(slots)[None] * used_mine[None] * (goes[None] == jnp.arange(n_dev)[:, None]), 1
    ).astype(jnp.int32)
    dealt = pick_tiles(master[0], slot_for, jnp.bfloat16, "deal_weights")
    table_out = jnp.pad(table_own, (0, 1024 - table_own.shape[0])).reshape(8, 128)
    arrived, all_sums, all_tables = exchange("deal", 1, n_dp, [dealt], [sums, table_out])

    totals = jnp.sum(all_sums, 0).reshape(-1)
    pixel_count = n_dev * SEQ * PATCH_PIX
    band_mean = totals[:BANDS] / pixel_count
    band_scale = lax.rsqrt(totals[BANDS : 2 * BANDS] / pixel_count - band_mean * band_mean + EPS_BAND)
    valid_count = jnp.maximum(totals[2 * BANDS], 1.0)

    n_slots = table_own.shape[0]
    tables = jnp.stack([all_tables[s * n_dp].reshape(-1)[:n_slots] for s in range(2)])
    both = [order(tables[s], USED[0] * s) for s in range(2)]
    used_all = jnp.concatenate([b[0] for b in both])
    order_all = jnp.concatenate([b[1] for b in both])
    owner_all = jnp.arange(2 * n_slots) // slots
    held = jnp.arange(per) * n_dev + me
    match = used_all[None] * (order_all[None] == held[:, None])
    from_owner = jnp.sum(match * owner_all[None], 1).astype(jnp.int32)
    is_held = jnp.sum(match, 1)
    block = pick_tiles(arrived, from_owner, jnp.bfloat16, "hold_weights")
    if n_dp == 16:
        tiles = gather_all(block, 2).reshape(n_dev * per, TR, TC)
    else:
        tiles = lax.all_gather(lax.all_gather(block, "dp"), "section").reshape(n_dev * per, TR, TC)

    where_tile = []
    line_tile = []
    for s in range(2):
        hit = tables[s][None] == jnp.arange(TILES)[:, None]
        rank = jnp.sum(hit * both[s][1][None], 1)
        device, turn = lax.rem(rank, n_dev), lax.div(rank, n_dev)
        where_tile.append((device * per + turn).astype(jnp.int32))
        line_tile.append((device * rows_each + turn).astype(jnp.int32))

    weights = []
    for s in range(2):
        matrices, vectors = layout(s)
        found, base = {}, 0
        for name, rows, columns in matrices:
            found[name] = unpack_matrix(tiles, where_tile[s], base, rows, columns, f"{name}_{s}")
            base += rows * columns // (TR * TC)
        flat = lax.dynamic_index_in_dim(tiles, where_tile[s][base], 0, keepdims=False).reshape(-1)
        offset = 0
        for name, length in vectors:
            found[name] = flat[offset : offset + length].astype(jnp.float32)
            offset += length
        weights.append(found)

    grads_enc, grads_dec, loss = item_step(
        weights[0], weights[1], pix, keep, kept, valid, band_mean, band_scale, valid_count
    )

    codes = None
    scales = jnp.zeros((n_dev * rows_each, TC), jnp.float32)
    for s, grads in ((1, grads_dec), (0, grads_enc)):
        matrices, vectors = layout(s)
        base = 0
        for name, rows, columns in matrices:
            codes, scales = pack_matrix(
                grads[name], where_tile[s], line_tile[s], base, codes, scales, n_dev * per, f"{name}_{s}"
            )
            base += rows * columns // (TR * TC)
        line = jnp.concatenate([grads[name] for name, length in vectors])
        line = jnp.pad(line, (0, TR * TC - line.shape[0])).reshape(TR, TC)
        codes, scales = pack_matrix(line, where_tile[s], line_tile[s], base, codes, scales, n_dev * per, f"vectors_{s}")

    if n_dp == 16:
        own_codes, own_scales = reduce_all(
            codes.reshape(2, n_dp, per, TR, TC), scales.reshape(2, n_dp, rows_each, TC), 3
        )
    else:
        wide = scales.reshape(n_dev, rows_each, TC)[:, :per]
        values = jnp.where(wide[:, :, None] > 0.0, codes.reshape(n_dev, per, TR, TC).astype(jnp.float32), 0.0)
        values = values * wide[:, :, None]
        values = lax.psum_scatter(values, ("section", "dp"), scatter_dimension=0, tiled=True)[0]
        top = jnp.max(jnp.abs(values), 1, keepdims=True)
        up = jnp.where(top > 0.0, 32766.0 / top, 0.0)
        own_codes = jnp.round(values * up).astype(jnp.int16)
        own_scales = jnp.pad(top[:, 0] * (1.0 / 32766.0), ((0, rows_each - per), (0, 0)))
    own_scale = own_scales[:per]
    own = jnp.where(is_held[:, None, None] > 0, own_codes.astype(jnp.float32) * own_scale[:, None], 0.0)
    tail = jnp.stack([jnp.sum(own * own), loss])
    tail = jnp.pad(tail, (0, 1022)).reshape(8, 128)

    turn_for = jnp.sum(
        jnp.arange(per)[None] * is_held[None] * (from_owner[None] == jnp.arange(n_dev)[:, None]), 1
    ).astype(jnp.int32)
    codes_back = pick_tiles(own_codes, turn_for, jnp.int16, "deal_gradients")
    scales_back = own_scale[turn_for][:, None]
    codes_mine, scales_mine, tails = exchange("return", 4, n_dp, [codes_back, scales_back], [tail])
    totals = jnp.sum(tails, 0)[0]
    grad_norm = jnp.sqrt(totals[0])
    factor = jnp.minimum(1.0, CLIP_NORM / (grad_norm + 1e-06))
    master_new, first_new, second_new = adam(
        codes_mine, scales_mine, goes, used_mine, factor[None], master[0], moment_one[0], moment_two[0]
    )
    return master_new[None], first_new[None], second_new[None], totals[1][None], grad_norm[None]


def solution(mesh):
    return jax.shard_map(
        local,
        mesh=mesh,
        in_specs=(
            P(None, "dp", None, None),
            P(None, "dp", None),
            P(None, "dp", None),
            P("section", None),
            P("section", "dp", None, None),
            P("section", "dp", None, None),
            P("section", "dp", None, None),
        ),
        out_specs=(
            P("section", "dp", None, None),
            P("section", "dp", None, None),
            P("section", "dp", None, None),
            P(),
            P(),
        ),
        check_vma=False,
    )
```

```python
import functools
import math

import jax
import jax.numpy as jnp
import numpy as np
from jax import lax
from jax.experimental import pallas as pl
from jax.experimental.pallas import tpu as pltpu
from jax.sharding import PartitionSpec as P

D_ENC = 768
H_ENC = 12
FF_ENC = 3072
D_DEC = 512
H_DEC = 16
FF_DEC = 2048
BANDS = 6
PATCH_PIX = 256
PATCH_DIM = 1536
SEQ = 588
KEEP = 147
STEP = 5
TILES = 256
USED = (253, 133)

EPS_NORM = 1e-06
EPS_BAND = 1e-05
CLIP_NORM = 0.001
RATE = 0.02
DECAY = 0.05
BETA_ONE = 0.5
BETA_TWO = 0.75
ADAM_EPS = 1e-08

MESH = pl.DeviceIdType.MESH
TR, TC = 128, 256
PARTS = ((0, 8), (8, 13))
PARTS_ROWS = 16


def neighbours(section, place):
    x, y, z = lax.rem(place, 2), lax.rem(lax.div(place, 2), 2), lax.div(place, 4)

    def at(dz, dv, du):
        dx = (1 - section) * du + section * dv
        dy = (1 - section) * dv + section * du
        return lax.rem(z + dz, 4) * 4 + lax.rem(y + dy, 2) * 2 + lax.rem(x + dx, 2)

    return at


def exchange(name, cid, n_dp, dealt, shared):
    n_dev = 2 * n_dp
    n_a, n_s = len(dealt), len(shared)
    n_all = n_a + n_s

    def kernel(*refs):
        sources, targets = refs[:n_all], refs[n_all : 2 * n_all]
        send_sem, recv_sem, own_sem = refs[2 * n_all :]
        section, place = lax.axis_index("section"), lax.axis_index("dp")
        me = section * n_dp + place

        def who(step):
            other = lax.rem(me + step, n_dev)
            return other, (lax.div(other, n_dp), lax.rem(other, n_dp))

        barrier = pltpu.get_barrier_semaphore()

        def greet(step, carry):
            pl.semaphore_signal(barrier, inc=1, device_id=who(step)[1], device_id_type=MESH)
            return carry

        lax.fori_loop(1, n_dev, greet, 0)
        own = []
        for which in range(n_all):
            source = sources[which].at[me] if which < n_a else sources[which]
            copy = pltpu.make_async_copy(source, targets[which].at[me], own_sem.at[which])
            copy.start()
            own.append(copy)
        pl.semaphore_wait(barrier, n_dev - 1)

        def made(which, step):
            other, place_of = who(step)
            source = sources[which].at[other] if which < n_a else sources[which]
            return pltpu.make_async_remote_copy(
                src_ref=source,
                dst_ref=targets[which].at[me],
                send_sem=send_sem.at[which, step],
                recv_sem=recv_sem.at[which, step],
                device_id=place_of,
                device_id_type=MESH,
            )

        def begin(step, carry):
            for which in reversed(range(n_all)):
                made(which, step).start()
            return carry

        def end(step, carry):
            for which in range(n_all):
                made(which, step).wait()
            return carry

        lax.fori_loop(1, n_dev, begin, 0)
        for copy in own:
            copy.wait()
        lax.fori_loop(1, n_dev, end, 0)

    arrays = list(dealt) + list(shared)
    shapes = [jax.ShapeDtypeStruct(a.shape, a.dtype) for a in dealt] + [
        jax.ShapeDtypeStruct((n_dev,) + a.shape, a.dtype) for a in shared
    ]
    any_spec = pl.BlockSpec(memory_space=pltpu.HBM)
    return pl.pallas_call(
        kernel,
        out_shape=shapes,
        in_specs=[any_spec] * n_all,
        out_specs=[any_spec] * n_all,
        scratch_shapes=[
            pltpu.SemaphoreType.DMA((n_all, n_dev)),
            pltpu.SemaphoreType.DMA((n_all, n_dev)),
            pltpu.SemaphoreType.DMA((n_all,)),
        ],
        compiler_params=pltpu.CompilerParams(collective_id=cid, has_side_effects=True),
        name=name,
    )(*arrays)


def code(values):
    top = jnp.max(jnp.abs(values), axis=0, keepdims=True)
    up = jnp.where(top > 0.0, 32766.0 / top, 0.0)
    scaled = values * up
    return (scaled + jnp.where(scaled >= 0.0, 0.5, -0.5)).astype(jnp.int32).astype(jnp.int16), top * (1.0 / 32766.0)


def gather_all(block, cid):
    per = block.shape[0]
    cut = [0, 4, 8, 11, per] if per == 13 else [0, 3, 5, 7, per]
    ways = (("z", "y", "x"), ("z", "x", "y"), ("y", "z", "x"), ("x", "z", "y"))

    def kernel(block_ref, all_ref, send_sem, recv_sem, side_send, side_recv, own_sem):
        section, place = lax.axis_index("section"), lax.axis_index("dp")
        at = neighbours(section, place)

        barrier = pltpu.get_barrier_semaphore()
        peers = [(1 - section, place)] + [
            (section, at(*d)) for d in ((0, 0, 1), (0, 1, 0), (1, 0, 0), (2, 0, 0), (3, 0, 0))
        ]
        for peer in peers:
            pl.semaphore_signal(barrier, inc=1, device_id=peer, device_id_type=MESH)
        own = pltpu.make_async_copy(block_ref, all_ref.at[section, place], own_sem)
        own.start()
        pl.semaphore_wait(barrier, len(peers))
        copies = {}
        sides = {}
        count = [0]

        def rows(way):
            return pl.ds(cut[way], cut[way + 1] - cut[way])

        def send(way, origin, move):
            target = at(*move)
            holder = at(*origin)
            arrived = tuple((o - m) % s for o, m, s in zip(origin, move, (4, 2, 2)))
            source = block_ref.at[rows(way)] if origin == (0, 0, 0) else all_ref.at[section, holder, rows(way)]
            index = count[0]
            count[0] += 1
            copy = pltpu.make_async_remote_copy(
                src_ref=source,
                dst_ref=all_ref.at[section, holder, rows(way)],
                send_sem=send_sem.at[index],
                recv_sem=recv_sem.at[index],
                device_id=(section, target),
                device_id_type=MESH,
            )
            copy.start()
            copies[way, arrived] = (copy, index)

        def arrive(way, origin):
            holder = at(*origin)
            copy, index = copies[way, origin]
            pltpu.make_async_remote_copy(
                src_ref=block_ref.at[rows(way)],
                dst_ref=all_ref.at[section, holder, rows(way)],
                send_sem=send_sem.at[index],
                recv_sem=recv_sem.at[index],
                device_id=(section, place),
                device_id_type=MESH,
            ).wait_recv()

        side_count = [0]

        def side(way, origin):
            holder = at(*origin)
            source = block_ref.at[rows(way)] if origin == (0, 0, 0) else all_ref.at[section, holder, rows(way)]
            index = side_count[0]
            side_count[0] += 1
            copy = pltpu.make_async_remote_copy(
                src_ref=source,
                dst_ref=all_ref.at[section, holder, rows(way)],
                send_sem=side_send.at[index],
                recv_sem=side_recv.at[index],
                device_id=(1 - section, place),
                device_id_type=MESH,
            )
            copy.start()
            sides[way, origin] = (copy, index)

        unit = {
            "x": [(0, 0, 1)],
            "y": [(0, 1, 0)],
            "z": [(1, 0, 0), (2, 0, 0), (3, 0, 0)],
        }

        def moved(origin, move):
            return tuple((o - m) % s for o, m, s in zip(origin, move, (4, 2, 2)))

        zero = (0, 0, 0)
        held = {way: [zero] for way in range(4)}
        for way, dims in enumerate(ways):
            for move in unit[dims[0]]:
                send(way, zero, move)
        for way, dims in enumerate(ways):
            for move in unit[dims[1]]:
                send(way, zero, move)
            for move in unit[dims[2]]:
                send(way, zero, move)
        for way in range(4):
            side(way, zero)
        first = {way: [moved(zero, m) for m in unit[ways[way][0]]] for way in range(4)}
        for way in (2, 3, 0, 1):
            dims = ways[way]
            for origin in first[way]:
                arrive(way, origin)
                for move in unit[dims[1]]:
                    send(way, origin, move)
                for move in unit[dims[2]]:
                    send(way, origin, move)
                side(way, origin)
        second = {}
        for way in range(4):
            have = [zero] + first[way]
            second[way] = [moved(o, m) for m in unit[ways[way][1]] for o in have]
        longest = max(len(v) for v in second.values())
        for i in range(longest):
            for way in (0, 1, 2, 3):
                if i < len(second[way]):
                    origin = second[way][i]
                    arrive(way, origin)
                    for move in unit[ways[way][2]]:
                        send(way, origin, move)
                    side(way, origin)
        third = {}
        for way in range(4):
            have = [zero] + first[way] + second[way]
            third[way] = [moved(o, m) for m in unit[ways[way][2]] for o in have]
        for i in range(8):
            for way in range(4):
                arrive(way, third[way][i])
                side(way, third[way][i])
        own.wait()
        for (way, origin), (copy, index) in copies.items():
            copy.wait_send()
        for (way, origin), (copy, index) in sides.items():
            copy.wait_send()
            holder = at(*origin)
            pltpu.make_async_remote_copy(
                src_ref=block_ref.at[rows(way)],
                dst_ref=all_ref.at[1 - section, holder, rows(way)],
                send_sem=side_send.at[index],
                recv_sem=side_recv.at[index],
                device_id=(1 - section, place),
                device_id_type=MESH,
            ).wait_recv()

    spec = pl.BlockSpec(memory_space=pltpu.HBM)
    return pl.pallas_call(
        kernel,
        out_shape=jax.ShapeDtypeStruct((2, 16, per, TR, TC), block.dtype),
        in_specs=[spec],
        out_specs=spec,
        scratch_shapes=[
            pltpu.SemaphoreType.DMA((60,)),
            pltpu.SemaphoreType.DMA((60,)),
            pltpu.SemaphoreType.DMA((64,)),
            pltpu.SemaphoreType.DMA((64,)),
            pltpu.SemaphoreType.DMA,
        ],
        compiler_params=pltpu.CompilerParams(collective_id=cid, has_side_effects=True),
        name="gather_tiles",
    )(block)


def reduce_all(codes, scales, cid, SUMS=True):
    per = codes.shape[2]

    def kernel(codes_ref, scales_ref, out_ref, outs_ref, acc, accs, rc, rcs, r_code, r_scale,
               own_sem, owns_sem, c_send, c_recv, p_send, p_recv):
        section, place = lax.axis_index("section"), lax.axis_index("dp")
        at, at_other = neighbours(section, place), neighbours(1 - section, place)
        sibling = (1 - section, place)
        to_u, to_v = (section, at(0, 0, 1)), (section, at(0, 1, 0))

        def to_z(dz):
            return (section, at(dz, 0, 0))

        barrier = pltpu.get_barrier_semaphore()
        peers = [sibling, to_u, to_v, to_z(1), to_z(2), to_z(3)]
        for peer in peers:
            pl.semaphore_signal(barrier, inc=1, device_id=peer, device_id_type=MESH)
        order = [(dz, dv, du) for dz in (2, 1, 3, 0) for dv in (1, 0) for du in (1, 0)]
        loads = {}
        for n, d in enumerate(order):
            b = at(*d)
            loads[d] = (
                pltpu.make_async_copy(codes_ref.at[section, b], acc.at[b], own_sem.at[n]),
                pltpu.make_async_copy(scales_ref.at[section, b], accs.at[b], owns_sem.at[n]),
            )
            for copy in loads[d]:
                copy.start()
        pl.semaphore_wait(barrier, len(peers))
        crossing = {}
        for n, d in enumerate(order):
            b = at_other(*d)
            pair = []
            for k, (source, target) in enumerate(((codes_ref, rc), (scales_ref, rcs))):
                copy = pltpu.make_async_remote_copy(
                    src_ref=source.at[1 - section, b],
                    dst_ref=target.at[b],
                    send_sem=c_send.at[k, n],
                    recv_sem=c_recv.at[k, n],
                    device_id=sibling,
                    device_id_type=MESH,
                )
                copy.start()
                pair.append(copy)
            crossing[d] = pair

        def add(b, part, from_code, from_first, from_scale, from_row):
            first, count = PARTS[part][0], PARTS[part][1] - PARTS[part][0]

            def one(t, carry):
                line = pl.ds(8 * part + t, 1)
                mine = acc[b, first + t].astype(jnp.float32) * accs[b, line, :]
                theirs = from_code[from_first + t].astype(jnp.float32) * from_scale[pl.ds(from_row + t, 1), :]
                value, scale = code(mine + theirs)
                acc[b, first + t] = value
                accs[b, line, :] = scale
                return carry

            if SUMS:
                lax.fori_loop(0, count, one, 0)

        sends = {}
        used = [0, 0]

        def send(part, key, b, peer):
            t0, t1 = PARTS[part]
            slot, index = used
            used[0] += t1 - t0
            used[1] += 1
            pair = []
            for k, (source, target) in enumerate(
                (
                    (acc.at[b, pl.ds(t0, t1 - t0)], r_code.at[pl.ds(slot, t1 - t0)]),
                    (accs.at[b, pl.ds(8 * part, 8)], r_scale.at[index]),
                )
            ):
                copy = pltpu.make_async_remote_copy(
                    src_ref=source,
                    dst_ref=target,
                    send_sem=p_send.at[k, index],
                    recv_sem=p_recv.at[k, index],
                    device_id=peer,
                    device_id_type=MESH,
                )
                copy.start()
                pair.append(copy)
            sends[part, key] = (pair, slot, index)

        def take(part, key, b):
            pair, slot, index = sends[part, key]
            for copy in pair:
                copy.wait_recv()
            add(b, part, r_code, slot, r_scale.at[index], 0)

        far = (2, 1, 3, 0)

        def first(dz):
            for dv in (1, 0):
                for du in (1, 0):
                    d = (dz, dv, du)
                    b = at(*d)
                    for copy in loads[d]:
                        copy.wait()
                    for copy in crossing[d]:
                        copy.wait_recv()
                    for part in range(2):
                        add(b, part, rc.at[b], PARTS[part][0], rcs.at[b], 8 * part)
                        if du:
                            send(part, ("1", dz, dv), b, to_u)

        def second(dz):
            for dv in (1, 0):
                for part in range(2):
                    b = at(dz, dv, 0)
                    take(part, ("1", dz, dv), b)
                    if dv:
                        send(part, ("2", dz), b, to_v)

        def third(dz):
            for part in range(2):
                b = at(dz, 0, 0)
                take(part, ("2", dz), b)
                if dz:
                    send(part, ("3", dz), b, to_z(dz))

        first(2)
        first(1)
        second(2)
        first(3)
        second(1)
        third(2)
        second(3)
        first(0)
        third(1)
        third(3)
        second(0)
        third(0)
        for dz in (2, 1, 3):
            for part in range(2):
                take(part, ("3", dz), place)
        out_ref[...] = acc[place]
        outs_ref[...] = accs[place]
        for pair in crossing.values():
            for copy in pair:
                copy.wait_send()
        for pair, slot, index in sends.values():
            for copy in pair:
                copy.wait_send()

    sizes = [t1 - t0 for t0, t1 in PARTS]
    n_tiles = 15 * sizes[0] + 15 * sizes[1]
    n_copies = 30
    hbm = pl.BlockSpec(memory_space=pltpu.HBM)
    vmem = pl.BlockSpec(memory_space=pltpu.VMEM)
    return pl.pallas_call(
        kernel,
        out_shape=(
            jax.ShapeDtypeStruct((per, TR, TC), jnp.int16),
            jax.ShapeDtypeStruct((PARTS_ROWS, TC), jnp.float32),
        ),
        in_specs=[hbm, hbm],
        out_specs=(vmem, vmem),
        scratch_shapes=[
            pltpu.VMEM((16, per, TR, TC), jnp.int16),
            pltpu.VMEM((16, PARTS_ROWS, TC), jnp.float32),
            pltpu.VMEM((16, per, TR, TC), jnp.int16),
            pltpu.VMEM((16, PARTS_ROWS, TC), jnp.float32),
            pltpu.VMEM((n_tiles, TR, TC), jnp.int16),
            pltpu.VMEM((n_copies, 8, TC), jnp.float32),
            pltpu.SemaphoreType.DMA((16,)),
            pltpu.SemaphoreType.DMA((16,)),
            pltpu.SemaphoreType.DMA((2, 16)),
            pltpu.SemaphoreType.DMA((2, 16)),
            pltpu.SemaphoreType.DMA((2, n_copies)),
            pltpu.SemaphoreType.DMA((2, n_copies)),
        ],
        compiler_params=pltpu.CompilerParams(
            collective_id=cid, has_side_effects=True, vmem_limit_bytes=60 * 2**20
        ),
        name="reduce_tiles",
    )(codes, scales)


def layout(section_id):
    if section_id == 0:
        width, hidden = D_ENC, FF_ENC
        matrices = [("first", PATCH_DIM, D_ENC)]
        vectors = [("first_bias", D_ENC)]
    else:
        width, hidden = D_DEC, FF_DEC
        matrices = [("first", D_ENC, D_DEC)]
        vectors = [("first_bias", D_DEC), ("mask", D_DEC)]
    matrices = matrices + [
        ("qkv", width, 3 * width),
        ("proj", width, width),
        ("fc1", width, hidden),
        ("fc2", hidden, width),
    ]
    vectors = vectors + [
        ("g1", width),
        ("b1", width),
        ("qv_bias", 2 * width),
        ("proj_bias", width),
        ("g2", width),
        ("b2", width),
        ("fc1_bias", hidden),
        ("fc2_bias", width),
        ("gf", width),
        ("bf", width),
    ]
    if section_id == 1:
        matrices = matrices + [("head", D_DEC, PATCH_DIM)]
        vectors = vectors + [("head_bias", PATCH_DIM)]
    return matrices, vectors


def positions(width):
    place = np.arange(SEQ, dtype=np.float32)[:, None]
    rate = np.exp(np.arange(width // 2, dtype=np.float32) * np.float32(-2.0 * math.log(10000.0) / width))
    angle = (place * rate).astype(np.float32)
    return np.concatenate([np.sin(angle), np.cos(angle)], axis=1).astype(np.float32)


LANES = 128
LOG2E = math.log2(math.e)


def pick_tiles(tiles, index, dtype, name):
    count = index.shape[0]

    def kernel(index_ref, tiles_ref, out_ref):
        def one(t, carry):
            out_ref[t] = tiles_ref[index_ref[t]].astype(dtype)
            return carry

        lax.fori_loop(0, count, one, 0)

    return pl.pallas_call(
        kernel,
        out_shape=jax.ShapeDtypeStruct((count, TR, TC), dtype),
        in_specs=[pl.BlockSpec(memory_space=pltpu.SMEM), pl.BlockSpec(memory_space=pltpu.VMEM)],
        out_specs=pl.BlockSpec(memory_space=pltpu.VMEM),
        compiler_params=pltpu.CompilerParams(vmem_limit_bytes=40 * 2**20),
        name=name,
    )(index, tiles)


def groups_of(rows, wide):
    groups = rows // TR
    return max(m for m in range(1, groups + 1) if groups % m == 0 and (m == 1 or m * wide <= 12))


def unpack_matrix(tiles, place, base, rows, columns, name):
    wide = columns // TC
    many = groups_of(rows, wide)
    count = many * wide

    def kernel(place_ref, *refs):
        sources, out_ref, lines = refs[:count], refs[count], refs[count + 1 :]
        for j in range(count):
            for h in range(2):
                lines[h][j * TR : (j + 1) * TR, :] = sources[j][0, :, h * LANES : (h + 1) * LANES].astype(jnp.float32)
        for j in range(wide):
            for h in range(2):
                start = j * TC + h * LANES
                out_ref[:, start : start + LANES] = lines[h][pl.ds(j, many * TR, stride=wide), :].astype(tiles.dtype)

    def spec(j):
        return pl.BlockSpec((1, TR, TC), lambda g, place_ref: (place_ref[base + g * count + j], 0, 0))

    return pl.pallas_call(
        kernel,
        out_shape=jax.ShapeDtypeStruct((rows, columns), tiles.dtype),
        grid_spec=pltpu.PrefetchScalarGridSpec(
            num_scalar_prefetch=1,
            grid=(rows // (many * TR),),
            in_specs=[spec(j) for j in range(count)],
            out_specs=pl.BlockSpec((many * TR, columns), lambda g, place_ref: (g, 0)),
            scratch_shapes=[pltpu.VMEM((count * TR, LANES), jnp.float32)] * 2,
        ),
        compiler_params=pltpu.CompilerParams(vmem_limit_bytes=32 * 2**20),
        name="unpack_" + name,
    )(place, *([tiles] * count))


def unpack_vectors(tiles, place, base, lengths, name):
    def kernel(place_ref, tile_ref, *refs):
        row = 0
        for out_ref, length in zip(refs, lengths):
            for r in range(length // TC):
                out_ref[:, r * TC : (r + 1) * TC] = tile_ref[0, row : row + 1, :].astype(jnp.float32)
                row += 1

    return pl.pallas_call(
        kernel,
        out_shape=[jax.ShapeDtypeStruct((1, length), jnp.float32) for length in lengths],
        grid_spec=pltpu.PrefetchScalarGridSpec(
            num_scalar_prefetch=1,
            grid=(1,),
            in_specs=[pl.BlockSpec((1, TR, TC), lambda g, place_ref: (place_ref[base], 0, 0))],
            out_specs=[pl.BlockSpec((1, length), lambda g, place_ref: (0, 0)) for length in lengths],
        ),
        name="unpack_vectors_" + name,
    )(place, tiles)


def join_vectors(vectors, name):
    def kernel(*refs):
        out_ref = refs[-1]
        row = 0
        for source in refs[:-1]:
            for r in range(source.shape[1] // TC):
                out_ref[row : row + 1, :] = source[:, r * TC : (r + 1) * TC]
                row += 1
        out_ref[row:, :] = jnp.zeros((TR - row, TC), jnp.float32)

    return pl.pallas_call(
        kernel,
        out_shape=jax.ShapeDtypeStruct((TR, TC), jnp.float32),
        name="join_vectors_" + name,
    )(*vectors)


def weight_codes(a, d, place, line, base, codes, scales, total, name):
    length = a.shape[0]
    rows, columns = a.shape if d is None else (a.shape[1], d.shape[1])
    wide = columns // TC
    many = groups_of(rows, wide)
    count = many * wide
    steps = rows // (many * TR)
    fresh = codes is None
    n_in = 1 if d is None else 2

    def kernel(place_ref, line_ref, *refs):
        scales_in = refs[n_in]
        codes_ref, scales_ref, left, right, ready, sem = refs[-6:]
        step = pl.program_id(0)
        slot = lax.rem(step, 2)

        @pl.when(step == 0)
        def _():
            scales_ref[...] = scales_in[...]

        def copies(at_step, at_slot):
            return [
                pltpu.make_async_copy(
                    ready.at[at_slot, j], codes_ref.at[place_ref[base + at_step * count + j]], sem.at[at_slot, j]
                )
                for j in range(count)
            ]

        @pl.when(step >= 2)
        def _():
            for copy in copies(step - 2, slot):
                copy.wait()

        for j in range(wide):
            columns_j = slice(j * TC, (j + 1) * TC)
            if d is None:
                part = refs[0][:, columns_j]
            else:
                part = weight_grad(refs[0][...], refs[1][:, columns_j])
            for h, lines in enumerate((left, right)):
                lines[pl.ds(j, many * TR, stride=wide), :] = part[:, h * LANES : (h + 1) * LANES]
        for j in range(count):
            at = line_ref[base + step * count + j]
            pair = []
            for h, lines in enumerate((left, right)):
                value, scale = code(lines[j * TR : (j + 1) * TR, :])
                ready[slot, j, :, h * LANES : (h + 1) * LANES] = value
                pair.append(scale)
            scales_ref[pl.ds(at, 1), :] = jnp.concatenate(pair, axis=1)
        for copy in copies(step, slot):
            copy.start()

        @pl.when(step == steps - 1)
        def _():
            if steps > 1:
                for copy in copies(step - 1, 1 - slot):
                    copy.wait()
            for copy in copies(step, slot):
                copy.wait()

    whole = pl.BlockSpec(scales.shape, lambda g, a, b: (0, 0))
    hbm = pl.BlockSpec(memory_space=pltpu.HBM)
    if d is None:
        operands, specs = [a], [pl.BlockSpec((many * TR, columns), lambda g, a, b: (g, 0))]
    else:
        operands = [a, d]
        specs = [
            pl.BlockSpec((length, many * TR), lambda g, a, b: (0, g)),
            pl.BlockSpec((length, columns), lambda g, a, b: (0, 0)),
        ]
    aliases = {2 + n_in: 1}
    if not fresh:
        aliases[3 + n_in] = 0
    return pl.pallas_call(
        kernel,
        out_shape=(
            jax.ShapeDtypeStruct((total, TR, TC), jnp.int16),
            jax.ShapeDtypeStruct(scales.shape, jnp.float32),
        ),
        grid_spec=pltpu.PrefetchScalarGridSpec(
            num_scalar_prefetch=2,
            grid=(steps,),
            in_specs=specs + [whole] + ([] if fresh else [hbm]),
            out_specs=(hbm, whole),
            scratch_shapes=[
                pltpu.VMEM((count * TR, LANES), jnp.float32),
                pltpu.VMEM((count * TR, LANES), jnp.float32),
                pltpu.VMEM((2, count, TR, TC), jnp.int16),
                pltpu.SemaphoreType.DMA((2, count)),
            ],
        ),
        input_output_aliases=aliases,
        compiler_params=pltpu.CompilerParams(vmem_limit_bytes=40 * 2**20),
        name="weight_codes_" + name,
    )(place, line, *operands, scales, *([] if fresh else [codes]))


def adam(codes, scales, index, used, factor, master, first, second):
    slots = master.shape[0]
    per = 3 if slots % 3 == 0 else 1

    def kernel(index_ref, used_ref, factor_ref, codes_ref, scales_ref, w_ref, m_ref, v_ref, w_out, m_out, v_out):
        for t in range(per):
            slot = pl.program_id(0) * per + t
            source = index_ref[slot]
            grad = codes_ref[source].astype(jnp.float32) * scales_ref[source]
            grad = jnp.where(used_ref[slot] > 0, grad * factor_ref[0], 0.0)
            first_new = BETA_ONE * m_ref[t] + (1.0 - BETA_ONE) * grad
            second_new = BETA_TWO * v_ref[t] + (1.0 - BETA_TWO) * grad * grad
            ratio = (
                first_new
                / (1.0 - BETA_ONE ** float(STEP))
                / (jnp.sqrt(second_new / (1.0 - BETA_TWO ** float(STEP))) + ADAM_EPS)
            )
            w_out[t] = w_ref[t] - RATE * (ratio + DECAY * w_ref[t])
            m_out[t] = first_new
            v_out[t] = second_new

    smem = pl.BlockSpec(memory_space=pltpu.SMEM)
    block = pl.BlockSpec((per, TR, TC), lambda g: (g, 0, 0))
    return pl.pallas_call(
        kernel,
        out_shape=[jax.ShapeDtypeStruct(master.shape, jnp.float32)] * 3,
        grid=(slots // per,),
        in_specs=[
            smem,
            smem,
            smem,
            pl.BlockSpec(codes.shape, lambda g: (0, 0, 0)),
            pl.BlockSpec(scales.shape, lambda g: (0, 0, 0)),
            block,
            block,
            block,
        ],
        out_specs=[block] * 3,
        compiler_params=pltpu.CompilerParams(vmem_limit_bytes=40 * 2**20),
        name="adam",
    )(index, used, factor, codes, scales, master, first, second)


def project(a, w):
    return jnp.dot(a, w, preferred_element_type=jnp.float32)


def project_back(d, w):
    return lax.dot_general(d, w, (((1,), (1,)), ((), ())), preferred_element_type=jnp.float32)


def weight_grad(a, d):
    return lax.dot_general(a, d, (((0,), (0,)), ((), ())), preferred_element_type=jnp.float32)


def layer_norm(values, gain, offset):
    centre = values - jnp.mean(values, -1, keepdims=True)
    return centre * lax.rsqrt(jnp.mean(centre * centre, -1, keepdims=True) + EPS_NORM) * gain + offset


def norm_back(upstream, values, gain):
    centre = values - jnp.mean(values, -1, keepdims=True)
    spread = lax.rsqrt(jnp.mean(centre * centre, -1, keepdims=True) + EPS_NORM)
    normed = centre * spread
    scaled = upstream * gain
    downstream = spread * (
        scaled - jnp.mean(scaled, -1, keepdims=True) - normed * jnp.mean(scaled * normed, -1, keepdims=True)
    )
    return downstream, jnp.sum(upstream * normed, 0, keepdims=True), jnp.sum(upstream, 0, keepdims=True)


def gelu_slope(pre):
    return 0.5 * (1.0 + lax.erf(pre * (1.0 / math.sqrt(2.0)))) + pre * jnp.exp(-0.5 * pre * pre) * (
        1.0 / math.sqrt(2.0 * math.pi)
    )


def column_sums(values):
    return jnp.sum(values.astype(jnp.float32), 0, keepdims=True)


def head_mask(size, h):
    lane = lax.broadcasted_iota(jnp.int32, (1, LANES), 1)
    return (lane >= h * size) & (lane < (h + 1) * size)


def head_mask(size, h):
    lane = lax.broadcasted_iota(jnp.int32, (1, LANES), 1)
    return (lane >= h * size) & (lane < (h + 1) * size)


def row_cuts(length, step):
    return [(lo, min(lo + step, length)) for lo in range(0, length, step)]


def attention(qkv, heads):
    length, width = qkv.shape[0], qkv.shape[1] // 3
    size = width // heads
    groups = width // LANES
    factor = size ** (-0.5)

    def kernel(q_ref, k_ref, v_ref, out_ref):
        keys, values = k_ref[...].T, v_ref[...]
        for lo, hi in row_cuts(length, 304):
            total = jnp.zeros((hi - lo, LANES), jnp.float32)
            for h in range(LANES // size):
                mask = head_mask(size, h)
                query = jnp.where(mask, q_ref[lo:hi, :], jnp.zeros((), jnp.bfloat16))
                scores = project(query, keys)
                power = jnp.exp2((scores - jnp.max(scores, -1, keepdims=True)) * (factor * LOG2E))
                probs = power * (1.0 / jnp.sum(power, -1, keepdims=True))
                mixed = project(probs.astype(jnp.bfloat16), values)
                total = jnp.where(mask, mixed, total)
            out_ref[lo:hi, :] = total.astype(jnp.bfloat16)

    def spec(offset):
        return pl.BlockSpec((length, LANES), lambda g: (0, g + offset))

    return pl.pallas_call(
        kernel,
        out_shape=jax.ShapeDtypeStruct((length, width), jnp.bfloat16),
        grid=(groups,),
        in_specs=[spec(0), spec(groups), spec(2 * groups)],
        out_specs=spec(0),
        compiler_params=pltpu.CompilerParams(vmem_limit_bytes=40 * 2**20),
        name=f"attention_{heads}",
    )(qkv, qkv, qkv)


def attention_back(qkv, grad, heads):
    length, width = grad.shape
    size = width // heads
    groups = width // LANES
    factor = size ** (-0.5)

    def kernel(q_ref, k_ref, v_ref, g_ref, dq_ref, dk_ref, dv_ref, dq_turned):
        zero = jnp.zeros((), jnp.bfloat16)
        keys, values = k_ref[...], v_ref[...]
        keys_turned = keys.T
        cuts = row_cuts(length, 256)
        for n, (lo, hi) in enumerate(cuts):
            query_all, grad_all = q_ref[lo:hi, :], g_ref[lo:hi, :]
            query_turned, grad_turned = query_all.T, grad_all.T
            dk = dv = None
            for h in range(LANES // size):
                own = slice(h * size, (h + 1) * size)
                row = lax.broadcasted_iota(jnp.int32, (LANES, 1), 0)
                rows = (row >= h * size) & (row < (h + 1) * size)
                mask = head_mask(size, h)
                scores = project(keys, jnp.where(rows, query_turned, zero))
                power = jnp.exp2((scores - jnp.max(scores, 0, keepdims=True)) * (factor * LOG2E))
                probs = power * (1.0 / jnp.sum(power, 0, keepdims=True))
                d_probs = project(values, jnp.where(rows, grad_turned, zero))
                inner = jnp.sum(d_probs * probs, 0, keepdims=True)
                d_scores = (probs * (d_probs - inner)).astype(jnp.bfloat16)
                dv_h = project(probs.astype(jnp.bfloat16), jnp.where(mask, grad_all, zero))
                dk_h = project(d_scores, jnp.where(mask, query_all, zero))
                dv = dv_h if dv is None else dv + dv_h
                dk = dk_h if dk is None else dk + dk_h
                dq_turned[own, lo:hi] = project(keys_turned[own, :], d_scores)
            if n:
                dk_sum, dv_sum = dk_sum + dk, dv_sum + dv
            else:
                dk_sum, dv_sum = dk, dv
        dq_ref[...] = (dq_turned[...].T * factor).astype(jnp.bfloat16)
        dk_ref[...] = (dk_sum * factor).astype(jnp.bfloat16)
        dv_ref[...] = dv_sum.astype(jnp.bfloat16)

    def spec(offset):
        return pl.BlockSpec((length, LANES), lambda g: (0, g + offset))

    return pl.pallas_call(
        kernel,
        out_shape=[jax.ShapeDtypeStruct((length, width), jnp.bfloat16)] * 3,
        grid=(groups,),
        in_specs=[spec(0), spec(groups), spec(2 * groups), spec(0)],
        out_specs=[spec(0)] * 3,
        scratch_shapes=[pltpu.VMEM((LANES, length), jnp.float32)],
        compiler_params=pltpu.CompilerParams(vmem_limit_bytes=40 * 2**20),
        name=f"attention_back_{heads}",
    )(qkv, qkv, qkv, grad)


def head_step(final, w, bias, pix, valid, inverse):
    def kernel(inverse_ref, final_ref, w_ref, bias_ref, pix_ref, valid_ref, low_ref, sums_ref, loss_ref, back_ref):
        one = inverse_ref[0]
        for band in range(BANDS):
            columns = slice(band * PATCH_PIX, (band + 1) * PATCH_PIX)
            predicted = jnp.dot(final_ref[...], w_ref[:, columns], preferred_element_type=jnp.float32)
            predicted = predicted + bias_ref[:, columns]
            values = pix_ref[:, columns].astype(jnp.float32)
            centre = values - jnp.mean(values, -1, keepdims=True)
            target = centre * lax.rsqrt(jnp.mean(centre * centre, -1, keepdims=True) + EPS_NORM)
            misfit = predicted - target
            valid_misfit = valid_ref[...] * misfit
            part = jnp.sum(valid_misfit * misfit, 0, keepdims=True) * (one / (BANDS * PATCH_PIX))
            if band:
                loss_ref[...] += part
            else:
                loss_ref[...] = part
            grad = valid_misfit * (one * (2.0 / (BANDS * PATCH_PIX)))
            low = grad.astype(jnp.bfloat16)
            low_ref[:, columns] = low
            sums_ref[:, columns] = jnp.sum(grad, 0, keepdims=True)
            back = lax.dot_general(low, w_ref[:, columns], (((1,), (1,)), ((), ())), preferred_element_type=jnp.float32)
            if band:
                back_ref[...] += back
            else:
                back_ref[...] = back

    vmem = pl.BlockSpec(memory_space=pltpu.VMEM)
    return pl.pallas_call(
        kernel,
        out_shape=[
            jax.ShapeDtypeStruct((SEQ, PATCH_DIM), jnp.bfloat16),
            jax.ShapeDtypeStruct((1, PATCH_DIM), jnp.float32),
            jax.ShapeDtypeStruct((1, PATCH_PIX), jnp.float32),
            jax.ShapeDtypeStruct((SEQ, D_DEC), jnp.float32),
        ],
        in_specs=[pl.BlockSpec(memory_space=pltpu.SMEM)] + [vmem] * 5,
        out_specs=[vmem] * 4,
        compiler_params=pltpu.CompilerParams(vmem_limit_bytes=40 * 2**20),
        name="head_step",
    )(inverse, final, w, bias, pix, valid)


def block_forward(x, w, heads):
    width = x.shape[-1]
    a = layer_norm(x, w["g1"], w["b1"]).astype(jnp.bfloat16)
    bias = jnp.concatenate([w["qv_bias"][:, :width], jnp.zeros((1, width), jnp.float32), w["qv_bias"][:, width:]], 1)
    qkv = (project(a, w["qkv"]) + bias).astype(jnp.bfloat16)
    attended = attention(qkv, heads)
    middle = x + project(attended, w["proj"]) + w["proj_bias"]
    c = layer_norm(middle, w["g2"], w["b2"]).astype(jnp.bfloat16)
    pre = project(c, w["fc1"]) + w["fc1_bias"]
    z = jax.nn.gelu(pre, approximate=False).astype(jnp.bfloat16)
    out = middle + project(z, w["fc2"]) + w["fc2_bias"]
    return out, (x, a, qkv, attended, middle, c, pre, z)


def block_backward(grad_out, stored, w, heads):
    x, a, qkv, attended, middle, c, pre, z = stored
    width = x.shape[-1]
    grads = {}
    two = grad_out.astype(jnp.bfloat16)
    grads["fc2"] = (z, two)
    grads["fc2_bias"] = column_sums(two)
    grad_pre = (project_back(two, w["fc2"]) * gelu_slope(pre)).astype(jnp.bfloat16)
    grads["fc1"] = (c, grad_pre)
    grads["fc1_bias"] = column_sums(grad_pre)
    grad_c, grads["g2"], grads["b2"] = norm_back(project_back(grad_pre, w["fc1"]), middle, w["g2"])
    grad_middle = grad_out + grad_c
    one = grad_middle.astype(jnp.bfloat16)
    grads["proj"] = (attended, one)
    grads["proj_bias"] = column_sums(one)
    grad_att = project_back(one, w["proj"]).astype(jnp.bfloat16)
    grad_qkv = jnp.concatenate(attention_back(qkv, grad_att, heads), -1)
    grads["qkv"] = (a, grad_qkv)
    sums = column_sums(grad_qkv)
    grads["qv_bias"] = jnp.concatenate([sums[:, :width], sums[:, 2 * width :]], 1)
    grad_a, grads["g1"], grads["b1"] = norm_back(project_back(grad_qkv, w["qkv"]), x, w["g1"])
    return grad_middle + grad_a, grads


def item_step(enc, dec, pix, keep, kept, valid, band_mean, band_scale, valid_count):
    chosen = (keep[:, None] == jnp.arange(SEQ)).astype(jnp.bfloat16)
    mean_line = jnp.broadcast_to(band_mean[:, None], (BANDS, PATCH_PIX)).reshape(PATCH_DIM)
    scale_line = jnp.broadcast_to(band_scale[:, None], (BANDS, PATCH_PIX)).reshape(PATCH_DIM)
    xin = ((project(chosen, pix) - mean_line) * scale_line).astype(jnp.bfloat16)
    place_enc = jnp.dot(chosen.astype(jnp.float32), jnp.asarray(positions(D_ENC)), precision=lax.Precision.HIGHEST)
    embedded = project(xin, enc["first"]) + enc["first_bias"] + place_enc
    y_enc, stored_enc = block_forward(embedded, enc, H_ENC)
    sent = layer_norm(y_enc, enc["gf"], enc["bf"]).astype(jnp.bfloat16)

    spread = weight_grad(chosen, sent).astype(jnp.bfloat16)
    placed = project(spread, dec["first"]) + dec["first_bias"]
    grid = jnp.where(kept[:, None] > 0.0, placed, dec["mask"]) + jnp.asarray(positions(D_DEC))
    y_dec, stored_dec = block_forward(grid, dec, H_DEC)
    final = layer_norm(y_dec, dec["gf"], dec["bf"]).astype(jnp.bfloat16)
    pred_low, head_bias, loss_terms, grad_final = head_step(
        final, dec["head"], dec["head_bias"], pix, valid[:, None], (1.0 / valid_count)[None]
    )
    loss = jnp.sum(loss_terms)
    grad_head = (final, pred_low)
    grad_y, gain, shift = norm_back(grad_final, y_dec, dec["gf"])
    grad_grid, grads_dec = block_backward(grad_y, stored_dec, dec, H_DEC)
    grads_dec["head"] = grad_head
    grads_dec["head_bias"] = head_bias
    grads_dec["gf"] = gain
    grads_dec["bf"] = shift
    grads_dec["mask"] = jnp.sum(grad_grid * (1.0 - kept)[:, None], 0, keepdims=True)
    grads_dec["first_bias"] = jnp.sum(grad_grid * kept[:, None], 0, keepdims=True)
    embed_low = project(chosen, grad_grid.astype(jnp.bfloat16)).astype(jnp.bfloat16)
    grads_dec["first"] = (sent, embed_low)

    grad_sent = project_back(embed_low, dec["first"]).astype(jnp.bfloat16).astype(jnp.float32)
    grad_y, gain, shift = norm_back(grad_sent, y_enc, enc["gf"])
    grad_embed, grads_enc = block_backward(grad_y, stored_enc, enc, H_ENC)
    grads_enc["gf"] = gain
    grads_enc["bf"] = shift
    grads_enc["first"] = (xin, grad_embed.astype(jnp.bfloat16))
    grads_enc["first_bias"] = jnp.sum(grad_embed, 0, keepdims=True)
    return grads_enc, grads_dec, loss


def local(pixels, keep_index, clear_mask, slot_tile, master, moment_one, moment_two):
    n_dp = lax.axis_size("dp")
    n_dev = 2 * n_dp
    section, place = lax.axis_index("section"), lax.axis_index("dp")
    me = section * n_dp + place
    slots = master.shape[1]
    turns = [-(-count // n_dev) for count in USED]
    per = sum(turns)
    starts = [0, turns[0] * n_dev]
    rows_each = 8 * (-(-per // 8))

    pix = lax.dynamic_index_in_dim(pixels, section, 0, keepdims=False)[0]
    keep = lax.dynamic_index_in_dim(keep_index, section, 0, keepdims=False)[0]
    clear = lax.dynamic_index_in_dim(clear_mask, section, 0, keepdims=False)[0]
    kept = jnp.any(keep[:, None] == jnp.arange(SEQ), axis=0).astype(jnp.float32)
    valid = clear.astype(jnp.float32) * (1.0 - kept)
    wide_pix = pix.astype(jnp.float32)
    sums = jnp.concatenate(
        [
            jnp.sum(jnp.sum(wide_pix, 0).reshape(BANDS, PATCH_PIX), 1),
            jnp.sum(jnp.sum(wide_pix * wide_pix, 0).reshape(BANDS, PATCH_PIX), 1),
            jnp.sum(valid)[None],
        ]
    )
    sums = jnp.pad(sums, (0, 1024 - sums.shape[0])).reshape(8, 128)

    def order(table, start):
        used = (table < TILES).astype(jnp.int32)
        count = table.shape[0]
        before = (jnp.arange(count)[:, None] > jnp.arange(count)[None]).astype(jnp.int32)
        return used, jnp.sum(before * used[None], 1) + start

    table_own = slot_tile[0]
    used_own, order_own = order(table_own, starts[1] * section)
    used_mine = lax.dynamic_slice_in_dim(used_own, place * slots, slots)
    order_mine = lax.dynamic_slice_in_dim(order_own, place * slots, slots)
    goes = lax.rem(order_mine, n_dev)
    slot_for = jnp.sum(
        jnp.arange(slots)[None] * used_mine[None] * (goes[None] == jnp.arange(n_dev)[:, None]), 1
    ).astype(jnp.int32)
    dealt = pick_tiles(master[0], slot_for, jnp.bfloat16, "deal_weights")
    table_out = jnp.pad(table_own, (0, 1024 - table_own.shape[0])).reshape(8, 128)
    arrived, all_sums, all_tables = exchange("deal", 1, n_dp, [dealt], [sums, table_out])

    totals = jnp.sum(all_sums, 0).reshape(-1)
    pixel_count = n_dev * SEQ * PATCH_PIX
    band_mean = totals[:BANDS] / pixel_count
    band_scale = lax.rsqrt(totals[BANDS : 2 * BANDS] / pixel_count - band_mean * band_mean + EPS_BAND)
    valid_count = jnp.maximum(totals[2 * BANDS], 1.0)

    n_slots = table_own.shape[0]
    tables = jnp.stack([all_tables[s * n_dp].reshape(-1)[:n_slots] for s in range(2)])
    both = [order(tables[s], starts[s]) for s in range(2)]
    used_all = jnp.concatenate([b[0] for b in both])
    order_all = jnp.concatenate([b[1] for b in both])
    owner_all = jnp.arange(2 * n_slots) // slots
    held = jnp.arange(per) * n_dev + me
    match = used_all[None] * (order_all[None] == held[:, None])
    from_owner = jnp.sum(match * owner_all[None], 1).astype(jnp.int32)
    is_held = jnp.sum(match, 1)
    block = pick_tiles(arrived, from_owner, jnp.bfloat16, "hold_weights")
    if n_dp == 16:
        tiles = gather_all(block, 2).reshape(n_dev * per, TR, TC)
    else:
        tiles = lax.all_gather(lax.all_gather(block, "dp"), "section").reshape(n_dev * per, TR, TC)

    where_tile = []
    line_tile = []
    for s in range(2):
        hit = tables[s][None] == jnp.arange(TILES)[:, None]
        rank = jnp.sum(hit * both[s][1][None], 1)
        device, turn = lax.rem(rank, n_dev), lax.div(rank, n_dev)
        where_tile.append((device * per + turn).astype(jnp.int32))
        line_tile.append((device * rows_each + turn).astype(jnp.int32))

    weights = []
    for s in range(2):
        matrices, vectors = layout(s)
        found, base = {}, 0
        for name, rows, columns in matrices:
            found[name] = unpack_matrix(tiles, where_tile[s], base, rows, columns, f"{name}_{s}")
            base += rows * columns // (TR * TC)
        lines = unpack_vectors(tiles, where_tile[s], base, [length for name, length in vectors], str(s))
        found.update({name: line for (name, length), line in zip(vectors, lines)})
        weights.append(found)

    grads_enc, grads_dec, loss = item_step(
        weights[0], weights[1], pix, keep, kept, valid, band_mean, band_scale, valid_count
    )

    codes = None
    scales = jnp.zeros((n_dev * rows_each, TC), jnp.float32)
    for s, grads in ((1, grads_dec), (0, grads_enc)):
        matrices, vectors = layout(s)
        base = 0
        for name, rows, columns in matrices:
            codes, scales = weight_codes(
                *grads[name], where_tile[s], line_tile[s], base, codes, scales, n_dev * per, f"{name}_{s}"
            )
            base += rows * columns // (TR * TC)
        line = join_vectors([grads[name] for name, length in vectors], str(s))
        codes, scales = weight_codes(
            line, None, where_tile[s], line_tile[s], base, codes, scales, n_dev * per, f"vectors_{s}"
        )

    if n_dp == 16:
        own_codes, own_scales = reduce_all(
            codes.reshape(2, n_dp, per, TR, TC), scales.reshape(2, n_dp, rows_each, TC), 3
        )
    else:
        wide = scales.reshape(n_dev, rows_each, TC)[:, :per]
        values = jnp.where(wide[:, :, None] > 0.0, codes.reshape(n_dev, per, TR, TC).astype(jnp.float32), 0.0)
        values = values * wide[:, :, None]
        values = lax.psum_scatter(values, ("section", "dp"), scatter_dimension=0, tiled=True)[0]
        top = jnp.max(jnp.abs(values), 1, keepdims=True)
        up = jnp.where(top > 0.0, 32766.0 / top, 0.0)
        own_codes = jnp.round(values * up).astype(jnp.int16)
        own_scales = jnp.pad(top[:, 0] * (1.0 / 32766.0), ((0, rows_each - per), (0, 0)))
    own_scale = own_scales[:per]
    own = jnp.where(is_held[:, None, None] > 0, own_codes.astype(jnp.float32) * own_scale[:, None], 0.0)
    tail = jnp.stack([jnp.sum(own * own), loss])
    tail = jnp.pad(tail, (0, 1022)).reshape(8, 128)

    turn_for = jnp.sum(
        jnp.arange(per)[None] * is_held[None] * (from_owner[None] == jnp.arange(n_dev)[:, None]), 1
    ).astype(jnp.int32)
    codes_back = pick_tiles(own_codes, turn_for, jnp.int16, "deal_gradients")
    scales_back = own_scale[turn_for][:, None]
    codes_mine, scales_mine, tails = exchange("return", 4, n_dp, [codes_back, scales_back], [tail])
    totals = jnp.sum(tails, 0)[0]
    grad_norm = jnp.sqrt(totals[0])
    factor = jnp.minimum(1.0, CLIP_NORM / (grad_norm + 1e-06))
    master_new, first_new, second_new = adam(
        codes_mine, scales_mine, goes, used_mine, factor[None], master[0], moment_one[0], moment_two[0]
    )
    return master_new[None], first_new[None], second_new[None], totals[1][None], grad_norm[None]


def solution(mesh):
    return jax.shard_map(
        local,
        mesh=mesh,
        in_specs=(
            P(None, "dp", None, None),
            P(None, "dp", None),
            P(None, "dp", None),
            P("section", None),
            P("section", "dp", None, None),
            P("section", "dp", None, None),
            P("section", "dp", None, None),
        ),
        out_specs=(
            P("section", "dp", None, None),
            P("section", "dp", None, None),
            P("section", "dp", None, None),
            P(),
            P(),
        ),
        check_vma=False,
    )
```

```python
import functools
import math

import jax
import jax.numpy as jnp
import numpy as np
from jax import lax
from jax.experimental import pallas as pl
from jax.experimental.pallas import tpu as pltpu
from jax.sharding import PartitionSpec as P

D_ENC = 768
H_ENC = 12
FF_ENC = 3072
D_DEC = 512
H_DEC = 16
FF_DEC = 2048
BANDS = 6
PATCH_PIX = 256
PATCH_DIM = 1536
SEQ = 588
KEEP = 147
STEP = 5
TILES = 256
USED = (253, 133)

EPS_NORM = 1e-06
EPS_BAND = 1e-05
CLIP_NORM = 0.001
RATE = 0.02
DECAY = 0.05
BETA_ONE = 0.5
BETA_TWO = 0.75
ADAM_EPS = 1e-08

MESH = pl.DeviceIdType.MESH
TR, TC = 128, 256
PARTS = ((0, 6), (6, 11), (11, 13))
PARTS_ROWS = 24


def neighbours(section, place):
    x, y, z = lax.rem(place, 2), lax.rem(lax.div(place, 2), 2), lax.div(place, 4)

    def at(dz, dv, du):
        dx = (1 - section) * du + section * dv
        dy = (1 - section) * dv + section * du
        return lax.rem(z + dz, 4) * 4 + lax.rem(y + dy, 2) * 2 + lax.rem(x + dx, 2)

    return at


def exchange(name, cid, n_dp, dealt, shared):
    n_dev = 2 * n_dp
    n_a, n_s = len(dealt), len(shared)
    n_all = n_a + n_s

    def kernel(*refs):
        sources, targets = refs[:n_all], refs[n_all : 2 * n_all]
        send_sem, recv_sem, own_sem = refs[2 * n_all :]
        section, place = lax.axis_index("section"), lax.axis_index("dp")
        me = section * n_dp + place

        def who(step):
            other = lax.rem(me + step, n_dev)
            return other, (lax.div(other, n_dp), lax.rem(other, n_dp))

        barrier = pltpu.get_barrier_semaphore()

        def greet(step, carry):
            pl.semaphore_signal(barrier, inc=1, device_id=who(step)[1], device_id_type=MESH)
            return carry

        lax.fori_loop(1, n_dev, greet, 0)
        own = []
        for which in range(n_all):
            source = sources[which].at[me] if which < n_a else sources[which]
            copy = pltpu.make_async_copy(source, targets[which].at[me], own_sem.at[which])
            copy.start()
            own.append(copy)
        pl.semaphore_wait(barrier, n_dev - 1)

        def made(which, step):
            other, place_of = who(step)
            source = sources[which].at[other] if which < n_a else sources[which]
            return pltpu.make_async_remote_copy(
                src_ref=source,
                dst_ref=targets[which].at[me],
                send_sem=send_sem.at[which, step],
                recv_sem=recv_sem.at[which, step],
                device_id=place_of,
                device_id_type=MESH,
            )

        def begin(step, carry):
            for which in reversed(range(n_all)):
                made(which, step).start()
            return carry

        def end(step, carry):
            for which in range(n_all):
                made(which, step).wait()
            return carry

        lax.fori_loop(1, n_dev, begin, 0)
        for copy in own:
            copy.wait()
        lax.fori_loop(1, n_dev, end, 0)

    arrays = list(dealt) + list(shared)
    shapes = [jax.ShapeDtypeStruct(a.shape, a.dtype) for a in dealt] + [
        jax.ShapeDtypeStruct((n_dev,) + a.shape, a.dtype) for a in shared
    ]
    any_spec = pl.BlockSpec(memory_space=pltpu.HBM)
    return pl.pallas_call(
        kernel,
        out_shape=shapes,
        in_specs=[any_spec] * n_all,
        out_specs=[any_spec] * n_all,
        scratch_shapes=[
            pltpu.SemaphoreType.DMA((n_all, n_dev)),
            pltpu.SemaphoreType.DMA((n_all, n_dev)),
            pltpu.SemaphoreType.DMA((n_all,)),
        ],
        compiler_params=pltpu.CompilerParams(collective_id=cid, has_side_effects=True),
        name=name,
    )(*arrays)


def line_of(turn, n_dp):
    if n_dp != 16:
        return turn
    return turn + 2 * (turn >= PARTS[0][1]) + 3 * (turn >= PARTS[1][1])


def code(values):
    top = jnp.max(jnp.abs(values), axis=0, keepdims=True)
    up = jnp.where(top > 0.0, 32766.0 / top, 0.0)
    scaled = values * up
    return (scaled + jnp.where(scaled >= 0.0, 0.5, -0.5)).astype(jnp.int32).astype(jnp.int16), top * (1.0 / 32766.0)


def gather_all(block, cid):
    per = block.shape[0]
    cut = [0, 4, 8, 11, per] if per == 13 else [0, 3, 5, 7, per]
    ways = (("z", "y", "x"), ("z", "x", "y"), ("y", "z", "x"), ("x", "z", "y"))

    def kernel(block_ref, all_ref, send_sem, recv_sem, side_send, side_recv, own_sem):
        section, place = lax.axis_index("section"), lax.axis_index("dp")
        at = neighbours(section, place)

        barrier = pltpu.get_barrier_semaphore()
        peers = [(1 - section, place)] + [
            (section, at(*d)) for d in ((0, 0, 1), (0, 1, 0), (1, 0, 0), (2, 0, 0), (3, 0, 0))
        ]
        for peer in peers:
            pl.semaphore_signal(barrier, inc=1, device_id=peer, device_id_type=MESH)
        own = pltpu.make_async_copy(block_ref, all_ref.at[section, place], own_sem)
        own.start()
        pl.semaphore_wait(barrier, len(peers))
        copies = {}
        sides = {}
        count = [0]

        def rows(way):
            return pl.ds(cut[way], cut[way + 1] - cut[way])

        def send(way, origin, move):
            target = at(*move)
            holder = at(*origin)
            arrived = tuple((o - m) % s for o, m, s in zip(origin, move, (4, 2, 2)))
            source = block_ref.at[rows(way)] if origin == (0, 0, 0) else all_ref.at[section, holder, rows(way)]
            index = count[0]
            count[0] += 1
            copy = pltpu.make_async_remote_copy(
                src_ref=source,
                dst_ref=all_ref.at[section, holder, rows(way)],
                send_sem=send_sem.at[index],
                recv_sem=recv_sem.at[index],
                device_id=(section, target),
                device_id_type=MESH,
            )
            copy.start()
            copies[way, arrived] = (copy, index)

        def arrive(way, origin):
            holder = at(*origin)
            copy, index = copies[way, origin]
            pltpu.make_async_remote_copy(
                src_ref=block_ref.at[rows(way)],
                dst_ref=all_ref.at[section, holder, rows(way)],
                send_sem=send_sem.at[index],
                recv_sem=recv_sem.at[index],
                device_id=(section, place),
                device_id_type=MESH,
            ).wait_recv()

        side_count = [0]

        def side(way, origin):
            holder = at(*origin)
            source = block_ref.at[rows(way)] if origin == (0, 0, 0) else all_ref.at[section, holder, rows(way)]
            index = side_count[0]
            side_count[0] += 1
            copy = pltpu.make_async_remote_copy(
                src_ref=source,
                dst_ref=all_ref.at[section, holder, rows(way)],
                send_sem=side_send.at[index],
                recv_sem=side_recv.at[index],
                device_id=(1 - section, place),
                device_id_type=MESH,
            )
            copy.start()
            sides[way, origin] = (copy, index)

        unit = {
            "x": [(0, 0, 1)],
            "y": [(0, 1, 0)],
            "z": [(1, 0, 0), (2, 0, 0), (3, 0, 0)],
        }

        def moved(origin, move):
            return tuple((o - m) % s for o, m, s in zip(origin, move, (4, 2, 2)))

        zero = (0, 0, 0)
        held = {way: [zero] for way in range(4)}
        for way, dims in enumerate(ways):
            for move in unit[dims[0]]:
                send(way, zero, move)
        for way, dims in enumerate(ways):
            for move in unit[dims[1]]:
                send(way, zero, move)
            for move in unit[dims[2]]:
                send(way, zero, move)
        for way in range(4):
            side(way, zero)
        first = {way: [moved(zero, m) for m in unit[ways[way][0]]] for way in range(4)}
        for way in (2, 3, 0, 1):
            dims = ways[way]
            for origin in first[way]:
                arrive(way, origin)
                for move in unit[dims[1]]:
                    send(way, origin, move)
                for move in unit[dims[2]]:
                    send(way, origin, move)
                side(way, origin)
        second = {}
        for way in range(4):
            have = [zero] + first[way]
            second[way] = [moved(o, m) for m in unit[ways[way][1]] for o in have]
        longest = max(len(v) for v in second.values())
        for i in range(longest):
            for way in (0, 1, 2, 3):
                if i < len(second[way]):
                    origin = second[way][i]
                    arrive(way, origin)
                    for move in unit[ways[way][2]]:
                        send(way, origin, move)
                    side(way, origin)
        third = {}
        for way in range(4):
            have = [zero] + first[way] + second[way]
            third[way] = [moved(o, m) for m in unit[ways[way][2]] for o in have]
        for i in range(8):
            for way in range(4):
                arrive(way, third[way][i])
                side(way, third[way][i])
        own.wait()
        for (way, origin), (copy, index) in copies.items():
            copy.wait_send()
        for (way, origin), (copy, index) in sides.items():
            copy.wait_send()
            holder = at(*origin)
            pltpu.make_async_remote_copy(
                src_ref=block_ref.at[rows(way)],
                dst_ref=all_ref.at[1 - section, holder, rows(way)],
                send_sem=side_send.at[index],
                recv_sem=side_recv.at[index],
                device_id=(1 - section, place),
                device_id_type=MESH,
            ).wait_recv()

    spec = pl.BlockSpec(memory_space=pltpu.HBM)
    return pl.pallas_call(
        kernel,
        out_shape=jax.ShapeDtypeStruct((2, 16, per, TR, TC), block.dtype),
        in_specs=[spec],
        out_specs=spec,
        scratch_shapes=[
            pltpu.SemaphoreType.DMA((60,)),
            pltpu.SemaphoreType.DMA((60,)),
            pltpu.SemaphoreType.DMA((64,)),
            pltpu.SemaphoreType.DMA((64,)),
            pltpu.SemaphoreType.DMA,
        ],
        compiler_params=pltpu.CompilerParams(collective_id=cid, has_side_effects=True),
        name="gather_tiles",
    )(block)


def reduce_all(codes, scales, cid, SUMS=True):
    per = codes.shape[2]

    def kernel(codes_ref, scales_ref, out_ref, outs_ref, acc, accs, rc, rcs, r_code, r_scale,
               own_sem, owns_sem, c_send, c_recv, p_send, p_recv):
        section, place = lax.axis_index("section"), lax.axis_index("dp")
        at, at_other = neighbours(section, place), neighbours(1 - section, place)
        sibling = (1 - section, place)
        to_u, to_v = (section, at(0, 0, 1)), (section, at(0, 1, 0))

        def to_z(dz):
            return (section, at(dz, 0, 0))

        barrier = pltpu.get_barrier_semaphore()
        peers = [sibling, to_u, to_v, to_z(1), to_z(2), to_z(3)]
        for peer in peers:
            pl.semaphore_signal(barrier, inc=1, device_id=peer, device_id_type=MESH)
        order = [(dz, dv, du) for dz in (2, 1, 3, 0) for dv in (1, 0) for du in (1, 0)]
        loads = {}
        for n, d in enumerate(order):
            b = at(*d)
            loads[d] = (
                pltpu.make_async_copy(codes_ref.at[section, b], acc.at[b], own_sem.at[n]),
                pltpu.make_async_copy(scales_ref.at[section, b], accs.at[b], owns_sem.at[n]),
            )
            for copy in loads[d]:
                copy.start()
        pl.semaphore_wait(barrier, len(peers))
        crossing = {}
        for n, d in enumerate(order):
            b = at_other(*d)
            pair = []
            for k, (source, target) in enumerate(((codes_ref, rc), (scales_ref, rcs))):
                copy = pltpu.make_async_remote_copy(
                    src_ref=source.at[1 - section, b],
                    dst_ref=target.at[b],
                    send_sem=c_send.at[k, n],
                    recv_sem=c_recv.at[k, n],
                    device_id=sibling,
                    device_id_type=MESH,
                )
                copy.start()
                pair.append(copy)
            crossing[d] = pair

        def add(b, part, from_code, from_first, from_scale, from_row):
            first, count = PARTS[part][0], PARTS[part][1] - PARTS[part][0]

            def one(t, carry):
                line = pl.ds(8 * part + t, 1)
                mine = acc[b, first + t].astype(jnp.float32) * accs[b, line, :]
                theirs = from_code[from_first + t].astype(jnp.float32) * from_scale[pl.ds(from_row + t, 1), :]
                value, scale = code(mine + theirs)
                acc[b, first + t] = value
                accs[b, line, :] = scale
                return carry

            if SUMS:
                lax.fori_loop(0, count, one, 0)

        sends = {}
        used = [0, 0]

        def send(part, key, b, peer):
            t0, t1 = PARTS[part]
            slot, index = used
            used[0] += t1 - t0
            used[1] += 1
            pair = []
            for k, (source, target) in enumerate(
                (
                    (acc.at[b, pl.ds(t0, t1 - t0)], r_code.at[pl.ds(slot, t1 - t0)]),
                    (accs.at[b, pl.ds(8 * part, 8)], r_scale.at[index]),
                )
            ):
                copy = pltpu.make_async_remote_copy(
                    src_ref=source,
                    dst_ref=target,
                    send_sem=p_send.at[k, index],
                    recv_sem=p_recv.at[k, index],
                    device_id=peer,
                    device_id_type=MESH,
                )
                copy.start()
                pair.append(copy)
            sends[part, key] = (pair, slot, index)

        def take(part, key, b):
            pair, slot, index = sends[part, key]
            for copy in pair:
                copy.wait_recv()
            add(b, part, r_code, slot, r_scale.at[index], 0)

        seen = set()

        def ready(d):
            if d not in seen:
                seen.add(d)
                for copy in loads[d]:
                    copy.wait()
                for copy in crossing[d]:
                    copy.wait_recv()

        def first(dz, parts=(0, 1, 2)):
            for dv in (1, 0):
                for du in (1, 0):
                    b = at(dz, dv, du)
                    ready((dz, dv, du))
                    for part in parts:
                        add(b, part, rc.at[b], PARTS[part][0], rcs.at[b], 8 * part)
                        if part == 2 and dz:
                            send(2, ("1", dz, dv, du), b, to_z(dz))
                        if part < 2 and du:
                            send(part, ("1", dz, dv), b, to_u)

        def second(dz):
            for dv in (1, 0):
                for part in (0, 1):
                    b = at(dz, dv, 0)
                    take(part, ("1", dz, dv), b)
                    if dv:
                        send(part, ("2", dz), b, to_v)

        def third(dz):
            for part in (0, 1):
                b = at(dz, 0, 0)
                take(part, ("2", dz), b)
                if dz:
                    send(part, ("3", dz), b, to_z(dz))

        first(2)
        first(1)
        first(3, (2,))
        second(2)
        first(3, (0, 1))
        second(1)
        third(2)
        first(0, (2,))
        second(3)
        first(0, (0, 1))
        third(1)
        for du in (1, 0):
            for dv in (1, 0):
                b = at(0, dv, du)
                for dz in (1, 3, 2):
                    take(2, ("1", dz, dv, du), b)
                if du:
                    send(2, ("2", dv), b, to_u)
        third(3)
        second(0)
        for dv in (1, 0):
            b = at(0, dv, 0)
            take(2, ("2", dv), b)
            if dv:
                send(2, ("3",), b, to_v)
        third(0)
        for dz in (2, 1, 3):
            for part in (0, 1):
                take(part, ("3", dz), place)
        take(2, ("3",), place)
        out_ref[...] = acc[place]
        outs_ref[...] = accs[place]
        for pair in crossing.values():
            for copy in pair:
                copy.wait_send()
        for pair, slot, index in sends.values():
            for copy in pair:
                copy.wait_send()

    n_tiles = 15 * per
    n_copies = 45
    hbm = pl.BlockSpec(memory_space=pltpu.HBM)
    vmem = pl.BlockSpec(memory_space=pltpu.VMEM)
    return pl.pallas_call(
        kernel,
        out_shape=(
            jax.ShapeDtypeStruct((per, TR, TC), jnp.int16),
            jax.ShapeDtypeStruct((PARTS_ROWS, TC), jnp.float32),
        ),
        in_specs=[hbm, hbm],
        out_specs=(vmem, vmem),
        scratch_shapes=[
            pltpu.VMEM((16, per, TR, TC), jnp.int16),
            pltpu.VMEM((16, PARTS_ROWS, TC), jnp.float32),
            pltpu.VMEM((16, per, TR, TC), jnp.int16),
            pltpu.VMEM((16, PARTS_ROWS, TC), jnp.float32),
            pltpu.VMEM((n_tiles, TR, TC), jnp.int16),
            pltpu.VMEM((n_copies, 8, TC), jnp.float32),
            pltpu.SemaphoreType.DMA((16,)),
            pltpu.SemaphoreType.DMA((16,)),
            pltpu.SemaphoreType.DMA((2, 16)),
            pltpu.SemaphoreType.DMA((2, 16)),
            pltpu.SemaphoreType.DMA((2, n_copies)),
            pltpu.SemaphoreType.DMA((2, n_copies)),
        ],
        compiler_params=pltpu.CompilerParams(
            collective_id=cid, has_side_effects=True, vmem_limit_bytes=60 * 2**20
        ),
        name="reduce_tiles",
    )(codes, scales)


def layout(section_id):
    if section_id == 0:
        width, hidden = D_ENC, FF_ENC
        matrices = [("first", PATCH_DIM, D_ENC)]
        vectors = [("first_bias", D_ENC)]
    else:
        width, hidden = D_DEC, FF_DEC
        matrices = [("first", D_ENC, D_DEC)]
        vectors = [("first_bias", D_DEC), ("mask", D_DEC)]
    matrices = matrices + [
        ("qkv", width, 3 * width),
        ("proj", width, width),
        ("fc1", width, hidden),
        ("fc2", hidden, width),
    ]
    vectors = vectors + [
        ("g1", width),
        ("b1", width),
        ("qv_bias", 2 * width),
        ("proj_bias", width),
        ("g2", width),
        ("b2", width),
        ("fc1_bias", hidden),
        ("fc2_bias", width),
        ("gf", width),
        ("bf", width),
    ]
    if section_id == 1:
        matrices = matrices + [("head", D_DEC, PATCH_DIM)]
        vectors = vectors + [("head_bias", PATCH_DIM)]
    return matrices, vectors


def positions(width):
    place = np.arange(SEQ, dtype=np.float32)[:, None]
    rate = np.exp(np.arange(width // 2, dtype=np.float32) * np.float32(-2.0 * math.log(10000.0) / width))
    angle = (place * rate).astype(np.float32)
    return np.concatenate([np.sin(angle), np.cos(angle)], axis=1).astype(np.float32)


LANES = 128
LOG2E = math.log2(math.e)


def pick_tiles(tiles, index, dtype, name):
    count = index.shape[0]

    def kernel(index_ref, tiles_ref, out_ref):
        def one(t, carry):
            out_ref[t] = tiles_ref[index_ref[t]].astype(dtype)
            return carry

        lax.fori_loop(0, count, one, 0)

    return pl.pallas_call(
        kernel,
        out_shape=jax.ShapeDtypeStruct((count, TR, TC), dtype),
        in_specs=[pl.BlockSpec(memory_space=pltpu.SMEM), pl.BlockSpec(memory_space=pltpu.VMEM)],
        out_specs=pl.BlockSpec(memory_space=pltpu.VMEM),
        compiler_params=pltpu.CompilerParams(vmem_limit_bytes=40 * 2**20),
        name=name,
    )(index, tiles)


def groups_of(rows, wide):
    groups = rows // TR
    return max(m for m in range(1, groups + 1) if groups % m == 0 and (m == 1 or m * wide <= 12))


def unpack_matrix(tiles, place, base, rows, columns, name):
    wide = columns // TC
    many = groups_of(rows, wide)
    count = many * wide

    def kernel(place_ref, *refs):
        sources, out_ref, lines = refs[:count], refs[count], refs[count + 1 :]
        for j in range(count):
            for h in range(2):
                lines[h][j * TR : (j + 1) * TR, :] = sources[j][0, :, h * LANES : (h + 1) * LANES].astype(jnp.float32)
        for j in range(wide):
            for h in range(2):
                start = j * TC + h * LANES
                out_ref[:, start : start + LANES] = lines[h][pl.ds(j, many * TR, stride=wide), :].astype(tiles.dtype)

    def spec(j):
        return pl.BlockSpec((1, TR, TC), lambda g, place_ref: (place_ref[base + g * count + j], 0, 0))

    return pl.pallas_call(
        kernel,
        out_shape=jax.ShapeDtypeStruct((rows, columns), tiles.dtype),
        grid_spec=pltpu.PrefetchScalarGridSpec(
            num_scalar_prefetch=1,
            grid=(rows // (many * TR),),
            in_specs=[spec(j) for j in range(count)],
            out_specs=pl.BlockSpec((many * TR, columns), lambda g, place_ref: (g, 0)),
            scratch_shapes=[pltpu.VMEM((count * TR, LANES), jnp.float32)] * 2,
        ),
        compiler_params=pltpu.CompilerParams(vmem_limit_bytes=32 * 2**20),
        name="unpack_" + name,
    )(place, *([tiles] * count))


def unpack_vectors(tiles, place, base, lengths, name):
    def kernel(place_ref, tile_ref, *refs):
        row = 0
        for out_ref, length in zip(refs, lengths):
            for r in range(length // TC):
                out_ref[:, r * TC : (r + 1) * TC] = tile_ref[0, row : row + 1, :].astype(jnp.float32)
                row += 1

    return pl.pallas_call(
        kernel,
        out_shape=[jax.ShapeDtypeStruct((1, length), jnp.float32) for length in lengths],
        grid_spec=pltpu.PrefetchScalarGridSpec(
            num_scalar_prefetch=1,
            grid=(1,),
            in_specs=[pl.BlockSpec((1, TR, TC), lambda g, place_ref: (place_ref[base], 0, 0))],
            out_specs=[pl.BlockSpec((1, length), lambda g, place_ref: (0, 0)) for length in lengths],
        ),
        name="unpack_vectors_" + name,
    )(place, tiles)


def join_vectors(vectors, name):
    def kernel(*refs):
        out_ref = refs[-1]
        row = 0
        for source in refs[:-1]:
            for r in range(source.shape[1] // TC):
                out_ref[row : row + 1, :] = source[:, r * TC : (r + 1) * TC]
                row += 1
        out_ref[row:, :] = jnp.zeros((TR - row, TC), jnp.float32)

    return pl.pallas_call(
        kernel,
        out_shape=jax.ShapeDtypeStruct((TR, TC), jnp.float32),
        name="join_vectors_" + name,
    )(*vectors)


def weight_codes(a, d, place, line, base, codes, scales, total, name):
    length = a.shape[0]
    rows, columns = a.shape if d is None else (a.shape[1], d.shape[1])
    wide = columns // TC
    many = groups_of(rows, wide)
    count = many * wide
    steps = rows // (many * TR)
    fresh = codes is None
    n_in = 1 if d is None else 2

    def kernel(place_ref, line_ref, *refs):
        scales_in = refs[n_in]
        codes_ref, scales_ref, left, right, ready, sem = refs[-6:]
        step = pl.program_id(0)
        slot = lax.rem(step, 2)

        @pl.when(step == 0)
        def _():
            scales_ref[...] = scales_in[...]

        def copies(at_step, at_slot):
            return [
                pltpu.make_async_copy(
                    ready.at[at_slot, j], codes_ref.at[place_ref[base + at_step * count + j]], sem.at[at_slot, j]
                )
                for j in range(count)
            ]

        @pl.when(step >= 2)
        def _():
            for copy in copies(step - 2, slot):
                copy.wait()

        for j in range(wide):
            columns_j = slice(j * TC, (j + 1) * TC)
            if d is None:
                part = refs[0][:, columns_j]
            else:
                part = weight_grad(refs[0][...], refs[1][:, columns_j])
            for h, lines in enumerate((left, right)):
                lines[pl.ds(j, many * TR, stride=wide), :] = part[:, h * LANES : (h + 1) * LANES]
        for j in range(count):
            at = line_ref[base + step * count + j]
            pair = []
            for h, lines in enumerate((left, right)):
                value, scale = code(lines[j * TR : (j + 1) * TR, :])
                ready[slot, j, :, h * LANES : (h + 1) * LANES] = value
                pair.append(scale)
            scales_ref[pl.ds(at, 1), :] = jnp.concatenate(pair, axis=1)
        for copy in copies(step, slot):
            copy.start()

        @pl.when(step == steps - 1)
        def _():
            if steps > 1:
                for copy in copies(step - 1, 1 - slot):
                    copy.wait()
            for copy in copies(step, slot):
                copy.wait()

    whole = pl.BlockSpec(scales.shape, lambda g, a, b: (0, 0))
    hbm = pl.BlockSpec(memory_space=pltpu.HBM)
    if d is None:
        operands, specs = [a], [pl.BlockSpec((many * TR, columns), lambda g, a, b: (g, 0))]
    else:
        operands = [a, d]
        specs = [
            pl.BlockSpec((length, many * TR), lambda g, a, b: (0, g)),
            pl.BlockSpec((length, columns), lambda g, a, b: (0, 0)),
        ]
    aliases = {2 + n_in: 1}
    if not fresh:
        aliases[3 + n_in] = 0
    return pl.pallas_call(
        kernel,
        out_shape=(
            jax.ShapeDtypeStruct((total, TR, TC), jnp.int16),
            jax.ShapeDtypeStruct(scales.shape, jnp.float32),
        ),
        grid_spec=pltpu.PrefetchScalarGridSpec(
            num_scalar_prefetch=2,
            grid=(steps,),
            in_specs=specs + [whole] + ([] if fresh else [hbm]),
            out_specs=(hbm, whole),
            scratch_shapes=[
                pltpu.VMEM((count * TR, LANES), jnp.float32),
                pltpu.VMEM((count * TR, LANES), jnp.float32),
                pltpu.VMEM((2, count, TR, TC), jnp.int16),
                pltpu.SemaphoreType.DMA((2, count)),
            ],
        ),
        input_output_aliases=aliases,
        compiler_params=pltpu.CompilerParams(vmem_limit_bytes=40 * 2**20),
        name="weight_codes_" + name,
    )(place, line, *operands, scales, *([] if fresh else [codes]))


def adam(codes, scales, index, used, factor, master, first, second):
    slots = master.shape[0]
    per = 3 if slots % 3 == 0 else 1

    def kernel(index_ref, used_ref, factor_ref, codes_ref, scales_ref, w_ref, m_ref, v_ref, w_out, m_out, v_out):
        for t in range(per):
            slot = pl.program_id(0) * per + t
            source = index_ref[slot]
            grad = codes_ref[source].astype(jnp.float32) * scales_ref[source]
            grad = jnp.where(used_ref[slot] > 0, grad * factor_ref[0], 0.0)
            first_new = BETA_ONE * m_ref[t] + (1.0 - BETA_ONE) * grad
            second_new = BETA_TWO * v_ref[t] + (1.0 - BETA_TWO) * grad * grad
            ratio = (
                first_new
                / (1.0 - BETA_ONE ** float(STEP))
                / (jnp.sqrt(second_new / (1.0 - BETA_TWO ** float(STEP))) + ADAM_EPS)
            )
            w_out[t] = w_ref[t] - RATE * (ratio + DECAY * w_ref[t])
            m_out[t] = first_new
            v_out[t] = second_new

    smem = pl.BlockSpec(memory_space=pltpu.SMEM)
    block = pl.BlockSpec((per, TR, TC), lambda g: (g, 0, 0))
    return pl.pallas_call(
        kernel,
        out_shape=[jax.ShapeDtypeStruct(master.shape, jnp.float32)] * 3,
        grid=(slots // per,),
        in_specs=[
            smem,
            smem,
            smem,
            pl.BlockSpec(codes.shape, lambda g: (0, 0, 0)),
            pl.BlockSpec(scales.shape, lambda g: (0, 0, 0)),
            block,
            block,
            block,
        ],
        out_specs=[block] * 3,
        compiler_params=pltpu.CompilerParams(vmem_limit_bytes=40 * 2**20),
        name="adam",
    )(index, used, factor, codes, scales, master, first, second)


def project(a, w):
    return jnp.dot(a, w, preferred_element_type=jnp.float32)


def project_back(d, w):
    return lax.dot_general(d, w, (((1,), (1,)), ((), ())), preferred_element_type=jnp.float32)


def weight_grad(a, d):
    return lax.dot_general(a, d, (((0,), (0,)), ((), ())), preferred_element_type=jnp.float32)


def layer_norm(values, gain, offset):
    centre = values - jnp.mean(values, -1, keepdims=True)
    return centre * lax.rsqrt(jnp.mean(centre * centre, -1, keepdims=True) + EPS_NORM) * gain + offset


def norm_back(upstream, values, gain):
    centre = values - jnp.mean(values, -1, keepdims=True)
    spread = lax.rsqrt(jnp.mean(centre * centre, -1, keepdims=True) + EPS_NORM)
    normed = centre * spread
    scaled = upstream * gain
    downstream = spread * (
        scaled - jnp.mean(scaled, -1, keepdims=True) - normed * jnp.mean(scaled * normed, -1, keepdims=True)
    )
    return downstream, line_sum(upstream * normed), line_sum(upstream)


def line_sum(values):
    return jnp.sum(values.astype(jnp.float32), 0, keepdims=True)


ERF_TOP = (
    -2.72614225801306e-10,
    2.77068142495902e-08,
    -2.10102402082508e-06,
    -5.69250639462346e-05,
    -7.34990630326855e-04,
    -2.95459980854025e-03,
    -1.60960333262415e-02,
)
ERF_BOTTOM = (
    -1.45660718464996e-05,
    -2.13374055278905e-04,
    -1.68282697438203e-03,
    -7.37332916720468e-03,
    -1.42647390514189e-02,
)


def erf(x):
    x = jnp.clip(x, -4.0, 4.0)
    square = x * x
    top, bottom = jnp.full_like(x, ERF_TOP[0]), jnp.full_like(x, ERF_BOTTOM[0])
    for coefficient in ERF_TOP[1:]:
        top = top * square + coefficient
    for coefficient in ERF_BOTTOM[1:]:
        bottom = bottom * square + coefficient
    return x * top / bottom


def whole_kernel(kernel, shapes, operands, name, scratch=(), smem=0):
    vmem = pl.BlockSpec(memory_space=pltpu.VMEM)
    return pl.pallas_call(
        kernel,
        out_shape=[jax.ShapeDtypeStruct(shape, dtype) for shape, dtype in shapes],
        in_specs=[pl.BlockSpec(memory_space=pltpu.SMEM)] * smem + [vmem] * (len(operands) - smem),
        out_specs=[vmem] * len(shapes),
        scratch_shapes=scratch,
        compiler_params=pltpu.CompilerParams(vmem_limit_bytes=56 * 2**20),
        name=name,
    )(*operands)


F32, BF16 = jnp.float32, jnp.bfloat16


def start_block(x_ref, rows, w, a_ref, qkv_ref):
    g1, b1, weight, bias = w
    width = x_ref.shape[1]
    a = layer_norm(x_ref[rows, :], g1[...], b1[...]).astype(BF16)
    a_ref[rows, :] = a
    for part in range(3):
        columns = slice(part * width, (part + 1) * width)
        value = project(a, weight[:, columns])
        if part != 1:
            value = value + bias[:, (part // 2) * width : (part // 2 + 1) * width]
        qkv_ref[rows, columns] = value.astype(BF16)


def enter_encoder(xin, place, w):
    def kernel(xin_ref, place_ref, first, bias, g1, b1, weight, qv_bias, x_ref, a_ref, qkv_ref):
        x_ref[...] = project(xin_ref[...], first[...]) + bias[...] + place_ref[...]
        start_block(x_ref, slice(None), (g1, b1, weight, qv_bias), a_ref, qkv_ref)

    shapes = [((KEEP, D_ENC), F32), ((KEEP, D_ENC), BF16), ((KEEP, 3 * D_ENC), BF16)]
    operands = [xin, place] + [w[k] for k in ("first", "first_bias", "g1", "b1", "qkv", "qv_bias")]
    return whole_kernel(kernel, shapes, operands, "enter_encoder")


def enter_decoder(chosen_turned, sent, kept, place, w):
    def kernel(chosen_ref, sent_ref, kept_ref, place_ref, first, bias, mask, g1, b1, weight, qv_bias,
               x_ref, a_ref, qkv_ref):
        for lo, hi in row_cuts(SEQ, 304):
            rows = slice(lo, hi)
            spread = project(chosen_ref[rows, :], sent_ref[...]).astype(BF16)
            placed = project(spread, first[...]) + bias[...]
            x_ref[rows, :] = jnp.where(kept_ref[rows, :] > 0.0, placed, mask[...]) + place_ref[rows, :]
            start_block(x_ref, rows, (g1, b1, weight, qv_bias), a_ref, qkv_ref)

    shapes = [((SEQ, D_DEC), F32), ((SEQ, D_DEC), BF16), ((SEQ, 3 * D_DEC), BF16)]
    names = ("first", "first_bias", "mask", "g1", "b1", "qkv", "qv_bias")
    operands = [chosen_turned, sent, kept, place] + [w[k] for k in names]
    return whole_kernel(kernel, shapes, operands, "enter_decoder")


def finish_block(x, attended, w, name):
    length, width = x.shape
    hidden = w["fc1"].shape[1]

    def kernel(x_ref, o_ref, proj, proj_bias, g2, b2, fc1, fc1_bias, fc2, fc2_bias, gf, bf,
               h_ref, c_ref, z_ref, slope_ref, y_ref, out_ref):
        for lo, hi in row_cuts(length, 304):
            rows = slice(lo, hi)
            h = x_ref[rows, :] + project(o_ref[rows, :], proj[...]) + proj_bias[...]
            h_ref[rows, :] = h
            c_ref[rows, :] = layer_norm(h, g2[...], b2[...]).astype(BF16)
        for lo in range(0, hidden, 256):
            columns = slice(lo, lo + 256)
            u = project(c_ref[...], fc1[:, columns]) + fc1_bias[:, columns]
            below = 0.5 * (1.0 + erf(u * (1.0 / math.sqrt(2.0))))
            z = (u * below).astype(BF16)
            z_ref[:, columns] = z
            slope_ref[:, columns] = below + u * jnp.exp(-0.5 * u * u) * (1.0 / math.sqrt(2.0 * math.pi))
            y = project(z, fc2[columns, :])
            if lo:
                y_ref[...] += y
            else:
                y_ref[...] = y
        for lo, hi in row_cuts(length, 304):
            rows = slice(lo, hi)
            y = h_ref[rows, :] + y_ref[rows, :] + fc2_bias[...]
            y_ref[rows, :] = y
            out_ref[rows, :] = layer_norm(y, gf[...], bf[...]).astype(BF16)

    line = (length, width)
    shapes = [(line, F32), (line, BF16), ((length, hidden), BF16), ((length, hidden), F32), (line, F32), (line, BF16)]
    names = ("proj", "proj_bias", "g2", "b2", "fc1", "fc1_bias", "fc2", "fc2_bias", "gf", "bf")
    return whole_kernel(kernel, shapes, [x, attended] + [w[k] for k in names], "finish_" + name)


def back_finish(d_out, y, slope, h, w, name):
    length, width = y.shape
    hidden = slope.shape[1]

    def kernel(d_ref, y_ref, slope_ref, h_ref, gf, fc2, fc1, g2, proj,
               two_ref, du_ref, dh_ref, one_ref, do_ref, s_gf, s_bf, s_fc2, s_fc1, s_g2, s_b2, s_proj, dc_ref):
        for n, (lo, hi) in enumerate(row_cuts(length, 304)):
            rows = slice(lo, hi)
            dy, gain, shift = norm_back(d_ref[rows, :].astype(F32), y_ref[rows, :], gf[...])
            dh_ref[rows, :] = dy
            two = dy.astype(BF16)
            two_ref[rows, :] = two
            collect(n, (s_gf, gain), (s_bf, shift), (s_fc2, line_sum(two)))
        for lo in range(0, hidden, 256):
            columns = slice(lo, lo + 256)
            du = (project_back(two_ref[...], fc2[columns, :]) * slope_ref[:, columns]).astype(BF16)
            du_ref[:, columns] = du
            s_fc1[:, columns] = line_sum(du)
            dc = project_back(du, fc1[:, columns])
            if lo:
                dc_ref[...] += dc
            else:
                dc_ref[...] = dc
        for n, (lo, hi) in enumerate(row_cuts(length, 304)):
            rows = slice(lo, hi)
            part, gain, shift = norm_back(dc_ref[rows, :], h_ref[rows, :], g2[...])
            dh = dh_ref[rows, :] + part
            dh_ref[rows, :] = dh
            one = dh.astype(BF16)
            one_ref[rows, :] = one
            collect(n, (s_g2, gain), (s_b2, shift), (s_proj, line_sum(one)))
        do_ref[...] = project_back(one_ref[...], proj[...]).astype(BF16)

    line = (length, width)
    shapes = [(line, BF16), ((length, hidden), BF16), (line, F32), (line, BF16), (line, BF16)]
    shapes += [((1, n), F32) for n in (width, width, width, hidden, width, width, width)]
    operands = [d_out, y, slope, h] + [w[k] for k in ("gf", "fc2", "fc1", "g2", "proj")]
    return whole_kernel(kernel, shapes, operands, "back_finish_" + name, [pltpu.VMEM(line, F32)])


def collect(n, *pairs):
    for ref, value in pairs:
        ref[...] = ref[...] + value if n else value


def leave_encoder(dqkv, x, dh, w):
    def kernel(d_ref, x_ref, dh_ref, g1, weight, low_ref, s_qv, s_g1, s_b1, s_first):
        d = d_ref[...]
        part, gain, shift = norm_back(project_back(d, weight[...]), x_ref[...], g1[...])
        dx = dh_ref[...] + part
        low_ref[...] = dx.astype(BF16)
        s_qv[:, :D_ENC] = line_sum(d[:, :D_ENC])
        s_qv[:, D_ENC:] = line_sum(d[:, 2 * D_ENC :])
        s_g1[...] = gain
        s_b1[...] = shift
        s_first[...] = line_sum(dx)

    shapes = [((KEEP, D_ENC), BF16)] + [((1, n), F32) for n in (2 * D_ENC, D_ENC, D_ENC, D_ENC)]
    return whole_kernel(kernel, shapes, [dqkv, x, dh, w["g1"], w["qkv"]], "leave_encoder")


def leave_decoder(dqkv, x, dh, chosen, kept, w):
    def kernel(d_ref, x_ref, dh_ref, chosen_ref, kept_ref, g1, weight, first,
               low_ref, sent_ref, s_qv, s_g1, s_b1, s_mask, s_first, da_ref, dx_ref):
        da_ref[...] = project_back(d_ref[...], weight[...])
        for n, (lo, hi) in enumerate(row_cuts(SEQ, 304)):
            rows = slice(lo, hi)
            part, gain, shift = norm_back(da_ref[rows, :], x_ref[rows, :], g1[...])
            dx = dh_ref[rows, :] + part
            dx_ref[rows, :] = dx.astype(BF16)
            kept_rows = kept_ref[rows, :]
            collect(
                n,
                (s_g1, gain),
                (s_b1, shift),
                (s_mask, line_sum(dx * (1.0 - kept_rows))),
                (s_first, line_sum(dx * kept_rows)),
            )
        s_qv[:, :D_DEC] = line_sum(d_ref[:, :D_DEC])
        s_qv[:, D_DEC:] = line_sum(d_ref[:, 2 * D_DEC :])
        low = project(chosen_ref[...], dx_ref[...]).astype(BF16)
        low_ref[...] = low
        sent_ref[...] = project_back(low, first[...]).astype(BF16)

    shapes = [((KEEP, D_DEC), BF16), ((KEEP, D_ENC), BF16)]
    shapes += [((1, n), F32) for n in (2 * D_DEC, D_DEC, D_DEC, D_DEC, D_DEC)]
    return whole_kernel(
        kernel,
        shapes,
        [dqkv, x, dh, chosen, kept, w["g1"], w["qkv"], w["first"]],
        "leave_decoder",
        [pltpu.VMEM((SEQ, D_DEC), F32), pltpu.VMEM((SEQ, D_DEC), BF16)],
    )


def head_mask(size, h):
    lane = lax.broadcasted_iota(jnp.int32, (1, LANES), 1)
    return (lane >= h * size) & (lane < (h + 1) * size)


def head_mask(size, h):
    lane = lax.broadcasted_iota(jnp.int32, (1, LANES), 1)
    return (lane >= h * size) & (lane < (h + 1) * size)


def row_cuts(length, step):
    return [(lo, min(lo + step, length)) for lo in range(0, length, step)]


def attention(qkv, heads):
    length, width = qkv.shape[0], qkv.shape[1] // 3
    size = width // heads
    groups = width // LANES
    factor = size ** (-0.5)

    def kernel(q_ref, k_ref, v_ref, out_ref):
        keys, values = k_ref[...].T, v_ref[...]
        for lo, hi in row_cuts(length, 304):
            total = jnp.zeros((hi - lo, LANES), jnp.float32)
            for h in range(LANES // size):
                mask = head_mask(size, h)
                query = jnp.where(mask, q_ref[lo:hi, :], jnp.zeros((), jnp.bfloat16))
                scores = project(query, keys)
                power = jnp.exp2((scores - jnp.max(scores, -1, keepdims=True)) * (factor * LOG2E))
                probs = power * (1.0 / jnp.sum(power, -1, keepdims=True))
                mixed = project(probs.astype(jnp.bfloat16), values)
                total = jnp.where(mask, mixed, total)
            out_ref[lo:hi, :] = total.astype(jnp.bfloat16)

    def spec(offset):
        return pl.BlockSpec((length, LANES), lambda g: (0, g + offset))

    return pl.pallas_call(
        kernel,
        out_shape=jax.ShapeDtypeStruct((length, width), jnp.bfloat16),
        grid=(groups,),
        in_specs=[spec(0), spec(groups), spec(2 * groups)],
        out_specs=spec(0),
        compiler_params=pltpu.CompilerParams(vmem_limit_bytes=40 * 2**20),
        name=f"attention_{heads}",
    )(qkv, qkv, qkv)


def attention_back(qkv, grad, heads):
    length, width = grad.shape
    size = width // heads
    groups = width // LANES
    factor = size ** (-0.5)

    def kernel(q_ref, k_ref, v_ref, g_ref, out_ref, dq_turned):
        zero = jnp.zeros((), jnp.bfloat16)
        keys, values = k_ref[...], v_ref[...]
        keys_turned = keys.T
        cuts = row_cuts(length, 256)
        for n, (lo, hi) in enumerate(cuts):
            query_all, grad_all = q_ref[lo:hi, :], g_ref[lo:hi, :]
            query_turned, grad_turned = query_all.T, grad_all.T
            dk = dv = None
            for h in range(LANES // size):
                own = slice(h * size, (h + 1) * size)
                row = lax.broadcasted_iota(jnp.int32, (LANES, 1), 0)
                rows = (row >= h * size) & (row < (h + 1) * size)
                mask = head_mask(size, h)
                scores = project(keys, jnp.where(rows, query_turned, zero))
                power = jnp.exp2((scores - jnp.max(scores, 0, keepdims=True)) * (factor * LOG2E))
                probs = power * (1.0 / jnp.sum(power, 0, keepdims=True))
                d_probs = project(values, jnp.where(rows, grad_turned, zero))
                inner = jnp.sum(d_probs * probs, 0, keepdims=True)
                d_scores = (probs * (d_probs - inner)).astype(jnp.bfloat16)
                dv_h = project(probs.astype(jnp.bfloat16), jnp.where(mask, grad_all, zero))
                dk_h = project(d_scores, jnp.where(mask, query_all, zero))
                dv = dv_h if dv is None else dv + dv_h
                dk = dk_h if dk is None else dk + dk_h
                dq_turned[own, lo:hi] = project(keys_turned[own, :], d_scores)
            if n:
                dk_sum, dv_sum = dk_sum + dk, dv_sum + dv
            else:
                dk_sum, dv_sum = dk, dv
        dq = dq_turned[...].T * factor
        for part, value in enumerate((dq, dk_sum * factor, dv_sum)):
            start = pl.multiple_of(part * width + pl.program_id(0) * LANES, LANES)
            out_ref[:, pl.ds(start, LANES)] = value.astype(jnp.bfloat16)

    def spec(offset):
        return pl.BlockSpec((length, LANES), lambda g: (0, g + offset))

    return pl.pallas_call(
        kernel,
        out_shape=jax.ShapeDtypeStruct((length, 3 * width), jnp.bfloat16),
        grid=(groups,),
        in_specs=[spec(0), spec(groups), spec(2 * groups), spec(0)],
        out_specs=pl.BlockSpec((length, 3 * width), lambda g: (0, 0)),
        scratch_shapes=[pltpu.VMEM((LANES, length), jnp.float32)],
        compiler_params=pltpu.CompilerParams(vmem_limit_bytes=40 * 2**20),
        name=f"attention_back_{heads}",
    )(qkv, qkv, qkv, grad)


def head_step(final, w, bias, pix, valid, inverse):
    def kernel(inverse_ref, final_ref, w_ref, bias_ref, pix_ref, valid_ref, low_ref, sums_ref, loss_ref, back_ref):
        one = inverse_ref[0]
        for band in range(BANDS):
            columns = slice(band * PATCH_PIX, (band + 1) * PATCH_PIX)
            predicted = jnp.dot(final_ref[...], w_ref[:, columns], preferred_element_type=jnp.float32)
            predicted = predicted + bias_ref[:, columns]
            values = pix_ref[:, columns].astype(jnp.float32)
            centre = values - jnp.mean(values, -1, keepdims=True)
            target = centre * lax.rsqrt(jnp.mean(centre * centre, -1, keepdims=True) + EPS_NORM)
            misfit = predicted - target
            valid_misfit = valid_ref[...] * misfit
            part = jnp.sum(valid_misfit * misfit, 0, keepdims=True) * (one / (BANDS * PATCH_PIX))
            if band:
                loss_ref[...] += part
            else:
                loss_ref[...] = part
            grad = valid_misfit * (one * (2.0 / (BANDS * PATCH_PIX)))
            low = grad.astype(jnp.bfloat16)
            low_ref[:, columns] = low
            sums_ref[:, columns] = jnp.sum(grad, 0, keepdims=True)
            back = lax.dot_general(low, w_ref[:, columns], (((1,), (1,)), ((), ())), preferred_element_type=jnp.float32)
            if band:
                back_ref[...] += back
            else:
                back_ref[...] = back

    vmem = pl.BlockSpec(memory_space=pltpu.VMEM)
    return pl.pallas_call(
        kernel,
        out_shape=[
            jax.ShapeDtypeStruct((SEQ, PATCH_DIM), jnp.bfloat16),
            jax.ShapeDtypeStruct((1, PATCH_DIM), jnp.float32),
            jax.ShapeDtypeStruct((1, PATCH_PIX), jnp.float32),
            jax.ShapeDtypeStruct((SEQ, D_DEC), jnp.float32),
        ],
        in_specs=[pl.BlockSpec(memory_space=pltpu.SMEM)] + [vmem] * 5,
        out_specs=[vmem] * 4,
        compiler_params=pltpu.CompilerParams(vmem_limit_bytes=40 * 2**20),
        name="head_step",
    )(inverse, final, w, bias, pix, valid)


def item_step(enc, dec, pix, keep, kept, valid, xin, chosen, inverse):
    place_enc = jnp.dot(chosen.astype(F32), jnp.asarray(positions(D_ENC)), precision=lax.Precision.HIGHEST)
    x0, a0, qkv0 = enter_encoder(xin, place_enc, enc)
    o0 = attention(qkv0, H_ENC)
    h0, c0, z0, slope0, y0, sent = finish_block(x0, o0, enc, "encoder")
    x1, a1, qkv1 = enter_decoder(chosen.T, sent, kept, jnp.asarray(positions(D_DEC)), dec)
    o1 = attention(qkv1, H_DEC)
    h1, c1, z1, slope1, y1, final = finish_block(x1, o1, dec, "decoder")
    pred_low, head_bias, loss_terms, d_final = head_step(
        final, dec["head"], dec["head_bias"], pix, valid, inverse
    )
    two, du, dh, one, do, *sums = back_finish(d_final, y1, slope1, h1, dec, "decoder")
    names = ("gf", "bf", "fc2_bias", "fc1_bias", "g2", "b2", "proj_bias")
    grads_dec = dict(zip(names, sums))
    dqkv = attention_back(qkv1, do, H_DEC)
    low, d_sent, *sums = leave_decoder(dqkv, x1, dh, chosen, kept, dec)
    grads_dec.update(zip(("qv_bias", "g1", "b1", "mask", "first_bias"), sums))
    grads_dec.update(
        head=(final, pred_low),
        head_bias=head_bias,
        fc2=(z1, two),
        fc1=(c1, du),
        proj=(o1, one),
        qkv=(a1, dqkv),
        first=(sent, low),
    )
    two, du, dh, one, do, *sums = back_finish(d_sent, y0, slope0, h0, enc, "encoder")
    grads_enc = dict(zip(names, sums))
    dqkv = attention_back(qkv0, do, H_ENC)
    low, *sums = leave_encoder(dqkv, x0, dh, enc)
    grads_enc.update(zip(("qv_bias", "g1", "b1", "first_bias"), sums))
    grads_enc.update(fc2=(z0, two), fc1=(c0, du), proj=(o0, one), qkv=(a0, dqkv), first=(xin, low))
    return grads_enc, grads_dec, jnp.sum(loss_terms)


def local(pixels, keep_index, clear_mask, slot_tile, master, moment_one, moment_two):
    n_dp = lax.axis_size("dp")
    n_dev = 2 * n_dp
    section, place = lax.axis_index("section"), lax.axis_index("dp")
    me = section * n_dp + place
    slots = master.shape[1]
    turns = [-(-count // n_dev) for count in USED]
    per = sum(turns)
    starts = [0, turns[0] * n_dev]
    rows_each = PARTS_ROWS if n_dp == 16 else 8 * (-(-per // 8))

    pix = lax.dynamic_index_in_dim(pixels, section, 0, keepdims=False)[0]
    keep = lax.dynamic_index_in_dim(keep_index, section, 0, keepdims=False)[0]
    clear = lax.dynamic_index_in_dim(clear_mask, section, 0, keepdims=False)[0]
    kept = jnp.any(keep[:, None] == jnp.arange(SEQ), axis=0).astype(jnp.float32)
    valid = clear.astype(jnp.float32) * (1.0 - kept)
    wide_pix = pix.astype(jnp.float32)
    sums = jnp.concatenate(
        [
            jnp.sum(jnp.sum(wide_pix, 0).reshape(BANDS, PATCH_PIX), 1),
            jnp.sum(jnp.sum(wide_pix * wide_pix, 0).reshape(BANDS, PATCH_PIX), 1),
            jnp.sum(valid)[None],
        ]
    )
    sums = jnp.pad(sums, (0, 1024 - sums.shape[0])).reshape(8, 128)

    def order(table, start):
        used = (table < TILES).astype(jnp.int32)
        count = table.shape[0]
        before = (jnp.arange(count)[:, None] > jnp.arange(count)[None]).astype(jnp.int32)
        return used, jnp.sum(before * used[None], 1) + start

    table_own = slot_tile[0]
    used_own, order_own = order(table_own, starts[1] * section)
    used_mine = lax.dynamic_slice_in_dim(used_own, place * slots, slots)
    order_mine = lax.dynamic_slice_in_dim(order_own, place * slots, slots)
    goes = lax.rem(order_mine, n_dev)
    slot_for = jnp.sum(
        jnp.arange(slots)[None] * used_mine[None] * (goes[None] == jnp.arange(n_dev)[:, None]), 1
    ).astype(jnp.int32)
    dealt = pick_tiles(master[0], slot_for, jnp.bfloat16, "deal_weights")
    table_out = jnp.pad(table_own, (0, 1024 - table_own.shape[0])).reshape(8, 128)
    arrived, all_sums, all_tables = exchange("deal", 1, n_dp, [dealt], [sums, table_out])

    totals = jnp.sum(all_sums, 0).reshape(-1)
    pixel_count = n_dev * SEQ * PATCH_PIX
    band_mean = totals[:BANDS] / pixel_count
    band_scale = lax.rsqrt(totals[BANDS : 2 * BANDS] / pixel_count - band_mean * band_mean + EPS_BAND)
    valid_count = jnp.maximum(totals[2 * BANDS], 1.0)

    chosen = (keep[:, None] == jnp.arange(SEQ)).astype(BF16)
    mean_line = jnp.broadcast_to(band_mean[:, None], (BANDS, PATCH_PIX)).reshape(PATCH_DIM)
    scale_line = jnp.broadcast_to(band_scale[:, None], (BANDS, PATCH_PIX)).reshape(PATCH_DIM)
    xin = ((project(chosen, pix) - mean_line) * scale_line).astype(BF16)

    n_slots = table_own.shape[0]
    tables = jnp.stack([all_tables[s * n_dp].reshape(-1)[:n_slots] for s in range(2)])
    both = [order(tables[s], starts[s]) for s in range(2)]
    used_all = jnp.concatenate([b[0] for b in both])
    order_all = jnp.concatenate([b[1] for b in both])
    owner_all = jnp.arange(2 * n_slots) // slots
    held = jnp.arange(per) * n_dev + me
    match = used_all[None] * (order_all[None] == held[:, None])
    from_owner = jnp.sum(match * owner_all[None], 1).astype(jnp.int32)
    is_held = jnp.sum(match, 1)
    block = pick_tiles(arrived, from_owner, jnp.bfloat16, "hold_weights")
    if n_dp == 16:
        tiles = gather_all(block, 2).reshape(n_dev * per, TR, TC)
    else:
        tiles = lax.all_gather(lax.all_gather(block, "dp"), "section").reshape(n_dev * per, TR, TC)

    where_tile = []
    line_tile = []
    for s in range(2):
        hit = tables[s][None] == jnp.arange(TILES)[:, None]
        rank = jnp.sum(hit * both[s][1][None], 1)
        device, turn = lax.rem(rank, n_dev), lax.div(rank, n_dev)
        where_tile.append((device * per + turn).astype(jnp.int32))
        line_tile.append((device * rows_each + line_of(turn, n_dp)).astype(jnp.int32))

    weights = []
    for s in range(2):
        matrices, vectors = layout(s)
        found, base = {}, 0
        for name, rows, columns in matrices:
            found[name] = unpack_matrix(tiles, where_tile[s], base, rows, columns, f"{name}_{s}")
            base += rows * columns // (TR * TC)
        lines = unpack_vectors(tiles, where_tile[s], base, [length for name, length in vectors], str(s))
        found.update({name: line for (name, length), line in zip(vectors, lines)})
        weights.append(found)

    grads_enc, grads_dec, loss = item_step(
        weights[0], weights[1], pix, keep, kept[:, None], valid[:, None], xin, chosen, (1.0 / valid_count)[None]
    )

    codes = None
    scales = jnp.zeros((n_dev * rows_each, TC), jnp.float32)
    for s, grads in ((1, grads_dec), (0, grads_enc)):
        matrices, vectors = layout(s)
        base = 0
        for name, rows, columns in matrices:
            codes, scales = weight_codes(
                *grads[name], where_tile[s], line_tile[s], base, codes, scales, n_dev * per, f"{name}_{s}"
            )
            base += rows * columns // (TR * TC)
        line = join_vectors([grads[name] for name, length in vectors], str(s))
        codes, scales = weight_codes(
            line, None, where_tile[s], line_tile[s], base, codes, scales, n_dev * per, f"vectors_{s}"
        )

    if n_dp == 16:
        own_codes, own_scales = reduce_all(
            codes.reshape(2, n_dp, per, TR, TC), scales.reshape(2, n_dp, rows_each, TC), 3
        )
    else:
        wide = scales.reshape(n_dev, rows_each, TC)[:, :per]
        values = jnp.where(wide[:, :, None] > 0.0, codes.reshape(n_dev, per, TR, TC).astype(jnp.float32), 0.0)
        values = values * wide[:, :, None]
        values = lax.psum_scatter(values, ("section", "dp"), scatter_dimension=0, tiled=True)[0]
        top = jnp.max(jnp.abs(values), 1, keepdims=True)
        up = jnp.where(top > 0.0, 32766.0 / top, 0.0)
        own_codes = jnp.round(values * up).astype(jnp.int16)
        own_scales = jnp.pad(top[:, 0] * (1.0 / 32766.0), ((0, rows_each - per), (0, 0)))
    own_scale = own_scales[np.array([line_of(t, n_dp) for t in range(per)])]
    own = jnp.where(is_held[:, None, None] > 0, own_codes.astype(jnp.float32) * own_scale[:, None], 0.0)
    tail = jnp.stack([jnp.sum(own * own), loss])
    tail = jnp.pad(tail, (0, 1022)).reshape(8, 128)

    turn_for = jnp.sum(
        jnp.arange(per)[None] * is_held[None] * (from_owner[None] == jnp.arange(n_dev)[:, None]), 1
    ).astype(jnp.int32)
    codes_back = pick_tiles(own_codes, turn_for, jnp.int16, "deal_gradients")
    scales_back = own_scale[turn_for][:, None]
    codes_mine, scales_mine, tails = exchange("return", 4, n_dp, [codes_back, scales_back], [tail])
    totals = jnp.sum(tails, 0)[0]
    grad_norm = jnp.sqrt(totals[0])
    factor = jnp.minimum(1.0, CLIP_NORM / (grad_norm + 1e-06))
    master_new, first_new, second_new = adam(
        codes_mine, scales_mine, goes, used_mine, factor[None], master[0], moment_one[0], moment_two[0]
    )
    return master_new[None], first_new[None], second_new[None], totals[1][None], grad_norm[None]


def solution(mesh):
    return jax.shard_map(
        local,
        mesh=mesh,
        in_specs=(
            P(None, "dp", None, None),
            P(None, "dp", None),
            P(None, "dp", None),
            P("section", None),
            P("section", "dp", None, None),
            P("section", "dp", None, None),
            P("section", "dp", None, None),
        ),
        out_specs=(
            P("section", "dp", None, None),
            P("section", "dp", None, None),
            P("section", "dp", None, None),
            P(),
            P(),
        ),
        check_vma=False,
    )
```

```python
import functools
import math

import jax
import jax.numpy as jnp
import numpy as np
from jax import lax
from jax.experimental import pallas as pl
from jax.experimental.pallas import tpu as pltpu
from jax.sharding import PartitionSpec as P

D_ENC = 768
H_ENC = 12
FF_ENC = 3072
D_DEC = 512
H_DEC = 16
FF_DEC = 2048
BANDS = 6
PATCH_PIX = 256
PATCH_DIM = 1536
SEQ = 588
KEEP = 147
STEP = 5
TILES = 256
USED = (253, 133)

EPS_NORM = 1e-06
EPS_BAND = 1e-05
CLIP_NORM = 0.001
RATE = 0.02
DECAY = 0.05
BETA_ONE = 0.5
BETA_TWO = 0.75
ADAM_EPS = 1e-08

MESH = pl.DeviceIdType.MESH
TR, TC = 128, 256
PARTS = ((0, 6), (6, 11), (11, 13))
PARTS_ROWS = 24


def neighbours(section, place):
    x, y, z = lax.rem(place, 2), lax.rem(lax.div(place, 2), 2), lax.div(place, 4)

    def at(dz, dv, du):
        dx = (1 - section) * du + section * dv
        dy = (1 - section) * dv + section * du
        return lax.rem(z + dz, 4) * 4 + lax.rem(y + dy, 2) * 2 + lax.rem(x + dx, 2)

    return at


def exchange(name, cid, n_dp, dealt, shared):
    n_dev = 2 * n_dp
    n_a, n_s = len(dealt), len(shared)
    n_all = n_a + n_s

    def kernel(*refs):
        sources, targets = refs[:n_all], refs[n_all : 2 * n_all]
        send_sem, recv_sem, own_sem = refs[2 * n_all :]
        section, place = lax.axis_index("section"), lax.axis_index("dp")
        me = section * n_dp + place

        def who(step):
            other = lax.rem(me + step, n_dev)
            return other, (lax.div(other, n_dp), lax.rem(other, n_dp))

        barrier = pltpu.get_barrier_semaphore()

        def greet(step, carry):
            pl.semaphore_signal(barrier, inc=1, device_id=who(step)[1], device_id_type=MESH)
            return carry

        lax.fori_loop(1, n_dev, greet, 0)
        own = []
        for which in range(n_all):
            source = sources[which].at[me] if which < n_a else sources[which]
            copy = pltpu.make_async_copy(source, targets[which].at[me], own_sem.at[which])
            copy.start()
            own.append(copy)
        pl.semaphore_wait(barrier, n_dev - 1)

        def made(which, step):
            other, place_of = who(step)
            source = sources[which].at[other] if which < n_a else sources[which]
            return pltpu.make_async_remote_copy(
                src_ref=source,
                dst_ref=targets[which].at[me],
                send_sem=send_sem.at[which, step],
                recv_sem=recv_sem.at[which, step],
                device_id=place_of,
                device_id_type=MESH,
            )

        def begin(step, carry):
            for which in reversed(range(n_all)):
                made(which, step).start()
            return carry

        def end(step, carry):
            for which in range(n_all):
                made(which, step).wait()
            return carry

        lax.fori_loop(1, n_dev, begin, 0)
        for copy in own:
            copy.wait()
        lax.fori_loop(1, n_dev, end, 0)

    arrays = list(dealt) + list(shared)
    shapes = [jax.ShapeDtypeStruct(a.shape, a.dtype) for a in dealt] + [
        jax.ShapeDtypeStruct((n_dev,) + a.shape, a.dtype) for a in shared
    ]
    any_spec = pl.BlockSpec(memory_space=pltpu.HBM)
    return pl.pallas_call(
        kernel,
        out_shape=shapes,
        in_specs=[any_spec] * n_all,
        out_specs=[any_spec] * n_all,
        scratch_shapes=[
            pltpu.SemaphoreType.DMA((n_all, n_dev)),
            pltpu.SemaphoreType.DMA((n_all, n_dev)),
            pltpu.SemaphoreType.DMA((n_all,)),
        ],
        compiler_params=pltpu.CompilerParams(collective_id=cid, has_side_effects=True),
        name=name,
    )(*arrays)


def line_of(turn, n_dp):
    if n_dp != 16:
        return turn
    return turn + 2 * (turn >= PARTS[0][1]) + 3 * (turn >= PARTS[1][1])


def code(values):
    top = jnp.max(jnp.abs(values), axis=0, keepdims=True)
    up = jnp.where(top > 0.0, 32766.0 / top, 0.0)
    scaled = values * up
    return (scaled + jnp.where(scaled >= 0.0, 0.5, -0.5)).astype(jnp.int32).astype(jnp.int16), top * (1.0 / 32766.0)


def reduce_all(codes, scales, cid, SUMS=True):
    per = codes.shape[2]

    def kernel(codes_ref, scales_ref, out_ref, outs_ref, acc, accs, rc, rcs, r_code, r_scale,
               own_sem, owns_sem, c_send, c_recv, p_send, p_recv):
        section, place = lax.axis_index("section"), lax.axis_index("dp")
        at, at_other = neighbours(section, place), neighbours(1 - section, place)
        sibling = (1 - section, place)
        to_u, to_v = (section, at(0, 0, 1)), (section, at(0, 1, 0))

        def to_z(dz):
            return (section, at(dz, 0, 0))

        barrier = pltpu.get_barrier_semaphore()
        peers = [sibling, to_u, to_v, to_z(1), to_z(2), to_z(3)]
        for peer in peers:
            pl.semaphore_signal(barrier, inc=1, device_id=peer, device_id_type=MESH)
        order = [(dz, dv, du) for dz in (2, 1, 3, 0) for dv in (1, 0) for du in (1, 0)]
        loads = {}
        for n, d in enumerate(order):
            b = at(*d)
            loads[d] = (
                pltpu.make_async_copy(codes_ref.at[section, b], acc.at[b], own_sem.at[n]),
                pltpu.make_async_copy(scales_ref.at[section, b], accs.at[b], owns_sem.at[n]),
            )
            for copy in loads[d]:
                copy.start()
        pl.semaphore_wait(barrier, len(peers))
        crossing = {}
        for n, d in enumerate(order):
            b = at_other(*d)
            pair = []
            for k, (source, target) in enumerate(((codes_ref, rc), (scales_ref, rcs))):
                copy = pltpu.make_async_remote_copy(
                    src_ref=source.at[1 - section, b],
                    dst_ref=target.at[b],
                    send_sem=c_send.at[k, n],
                    recv_sem=c_recv.at[k, n],
                    device_id=sibling,
                    device_id_type=MESH,
                )
                copy.start()
                pair.append(copy)
            crossing[d] = pair

        def add(b, part, from_code, from_first, from_scale, from_row):
            first, count = PARTS[part][0], PARTS[part][1] - PARTS[part][0]

            def one(t, carry):
                line = pl.ds(8 * part + t, 1)
                mine = acc[b, first + t].astype(jnp.float32) * accs[b, line, :]
                theirs = from_code[from_first + t].astype(jnp.float32) * from_scale[pl.ds(from_row + t, 1), :]
                value, scale = code(mine + theirs)
                acc[b, first + t] = value
                accs[b, line, :] = scale
                return carry

            if SUMS:
                lax.fori_loop(0, count, one, 0)

        sends = {}
        used = [0, 0]

        def send(part, key, b, peer):
            t0, t1 = PARTS[part]
            slot, index = used
            used[0] += t1 - t0
            used[1] += 1
            pair = []
            for k, (source, target) in enumerate(
                (
                    (acc.at[b, pl.ds(t0, t1 - t0)], r_code.at[pl.ds(slot, t1 - t0)]),
                    (accs.at[b, pl.ds(8 * part, 8)], r_scale.at[index]),
                )
            ):
                copy = pltpu.make_async_remote_copy(
                    src_ref=source,
                    dst_ref=target,
                    send_sem=p_send.at[k, index],
                    recv_sem=p_recv.at[k, index],
                    device_id=peer,
                    device_id_type=MESH,
                )
                copy.start()
                pair.append(copy)
            sends[part, key] = (pair, slot, index)

        def take(part, key, b):
            pair, slot, index = sends[part, key]
            for copy in pair:
                copy.wait_recv()
            add(b, part, r_code, slot, r_scale.at[index], 0)

        seen = set()

        def ready(d):
            if d not in seen:
                seen.add(d)
                for copy in loads[d]:
                    copy.wait()
                for copy in crossing[d]:
                    copy.wait_recv()

        def first(dz, parts=(0, 1, 2)):
            for dv in (1, 0):
                for du in (1, 0):
                    b = at(dz, dv, du)
                    ready((dz, dv, du))
                    for part in parts:
                        add(b, part, rc.at[b], PARTS[part][0], rcs.at[b], 8 * part)
                        if part == 2 and dz:
                            send(2, ("1", dz, dv, du), b, to_z(dz))
                        if part < 2 and du:
                            send(part, ("1", dz, dv), b, to_u)

        def second(dz):
            for dv in (1, 0):
                for part in (0, 1):
                    b = at(dz, dv, 0)
                    take(part, ("1", dz, dv), b)
                    if dv:
                        send(part, ("2", dz), b, to_v)

        def third(dz):
            for part in (0, 1):
                b = at(dz, 0, 0)
                take(part, ("2", dz), b)
                if dz:
                    send(part, ("3", dz), b, to_z(dz))

        first(2)
        first(1)
        first(3, (2,))
        second(2)
        first(3, (0, 1))
        second(1)
        third(2)
        first(0, (2,))
        second(3)
        first(0, (0, 1))
        third(1)
        for du in (1, 0):
            for dv in (1, 0):
                b = at(0, dv, du)
                for dz in (1, 3, 2):
                    take(2, ("1", dz, dv, du), b)
                if du:
                    send(2, ("2", dv), b, to_u)
        third(3)
        second(0)
        for dv in (1, 0):
            b = at(0, dv, 0)
            take(2, ("2", dv), b)
            if dv:
                send(2, ("3",), b, to_v)
        third(0)
        for dz in (2, 1, 3):
            for part in (0, 1):
                take(part, ("3", dz), place)
        take(2, ("3",), place)
        out_ref[...] = acc[place]
        outs_ref[...] = accs[place]
        for pair in crossing.values():
            for copy in pair:
                copy.wait_send()
        for pair, slot, index in sends.values():
            for copy in pair:
                copy.wait_send()

    n_tiles = 15 * per
    n_copies = 45
    hbm = pl.BlockSpec(memory_space=pltpu.HBM)
    vmem = pl.BlockSpec(memory_space=pltpu.VMEM)
    return pl.pallas_call(
        kernel,
        out_shape=(
            jax.ShapeDtypeStruct((per, TR, TC), jnp.int16),
            jax.ShapeDtypeStruct((PARTS_ROWS, TC), jnp.float32),
        ),
        in_specs=[hbm, hbm],
        out_specs=(vmem, vmem),
        scratch_shapes=[
            pltpu.VMEM((16, per, TR, TC), jnp.int16),
            pltpu.VMEM((16, PARTS_ROWS, TC), jnp.float32),
            pltpu.VMEM((16, per, TR, TC), jnp.int16),
            pltpu.VMEM((16, PARTS_ROWS, TC), jnp.float32),
            pltpu.VMEM((n_tiles, TR, TC), jnp.int16),
            pltpu.VMEM((n_copies, 8, TC), jnp.float32),
            pltpu.SemaphoreType.DMA((16,)),
            pltpu.SemaphoreType.DMA((16,)),
            pltpu.SemaphoreType.DMA((2, 16)),
            pltpu.SemaphoreType.DMA((2, 16)),
            pltpu.SemaphoreType.DMA((2, n_copies)),
            pltpu.SemaphoreType.DMA((2, n_copies)),
        ],
        compiler_params=pltpu.CompilerParams(
            collective_id=cid, has_side_effects=True, vmem_limit_bytes=60 * 2**20
        ),
        name="reduce_tiles",
    )(codes, scales)


def layout(section_id):
    if section_id == 0:
        width, hidden = D_ENC, FF_ENC
        matrices = [("first", PATCH_DIM, D_ENC)]
        vectors = [("first_bias", D_ENC)]
    else:
        width, hidden = D_DEC, FF_DEC
        matrices = [("first", D_ENC, D_DEC)]
        vectors = [("first_bias", D_DEC), ("mask", D_DEC)]
    matrices = matrices + [
        ("qkv", width, 3 * width),
        ("proj", width, width),
        ("fc1", width, hidden),
        ("fc2", hidden, width),
    ]
    vectors = vectors + [
        ("g1", width),
        ("b1", width),
        ("qv_bias", 2 * width),
        ("proj_bias", width),
        ("g2", width),
        ("b2", width),
        ("fc1_bias", hidden),
        ("fc2_bias", width),
        ("gf", width),
        ("bf", width),
    ]
    if section_id == 1:
        matrices = matrices + [("head", D_DEC, PATCH_DIM)]
        vectors = vectors + [("head_bias", PATCH_DIM)]
    return matrices, vectors


def positions(width):
    place = np.arange(SEQ, dtype=np.float32)[:, None]
    rate = np.exp(np.arange(width // 2, dtype=np.float32) * np.float32(-2.0 * math.log(10000.0) / width))
    angle = (place * rate).astype(np.float32)
    return np.concatenate([np.sin(angle), np.cos(angle)], axis=1).astype(np.float32)


LANES = 128
LOG2E = math.log2(math.e)


def pick_tiles(tiles, index, dtype, name):
    count = index.shape[0]

    def kernel(index_ref, tiles_ref, out_ref):
        def one(t, carry):
            out_ref[t] = tiles_ref[index_ref[t]].astype(dtype)
            return carry

        lax.fori_loop(0, count, one, 0)

    return pl.pallas_call(
        kernel,
        out_shape=jax.ShapeDtypeStruct((count, TR, TC), dtype),
        in_specs=[pl.BlockSpec(memory_space=pltpu.SMEM), pl.BlockSpec(memory_space=pltpu.VMEM)],
        out_specs=pl.BlockSpec(memory_space=pltpu.VMEM),
        compiler_params=pltpu.CompilerParams(vmem_limit_bytes=40 * 2**20),
        name=name,
    )(index, tiles)


def groups_of(rows, wide):
    groups = rows // TR
    return max(m for m in range(1, groups + 1) if groups % m == 0 and (m == 1 or m * wide <= 12))


def unpack_matrix(tiles, place, base, rows, columns, name):
    wide = columns // TC
    many = groups_of(rows, wide)
    count = many * wide

    def kernel(place_ref, *refs):
        sources, out_ref, lines = refs[:count], refs[count], refs[count + 1 :]
        for j in range(count):
            for h in range(2):
                lines[h][j * TR : (j + 1) * TR, :] = sources[j][0, :, h * LANES : (h + 1) * LANES].astype(jnp.float32)
        for j in range(wide):
            for h in range(2):
                start = j * TC + h * LANES
                out_ref[:, start : start + LANES] = lines[h][pl.ds(j, many * TR, stride=wide), :].astype(tiles.dtype)

    def spec(j):
        return pl.BlockSpec((1, TR, TC), lambda g, place_ref: (place_ref[base + g * count + j], 0, 0))

    return pl.pallas_call(
        kernel,
        out_shape=jax.ShapeDtypeStruct((rows, columns), tiles.dtype),
        grid_spec=pltpu.PrefetchScalarGridSpec(
            num_scalar_prefetch=1,
            grid=(rows // (many * TR),),
            in_specs=[spec(j) for j in range(count)],
            out_specs=pl.BlockSpec((many * TR, columns), lambda g, place_ref: (g, 0)),
            scratch_shapes=[pltpu.VMEM((count * TR, LANES), jnp.float32)] * 2,
        ),
        compiler_params=pltpu.CompilerParams(vmem_limit_bytes=32 * 2**20),
        name="unpack_" + name,
    )(place, *([tiles] * count))


def unpack_vectors(tiles, place, base, lengths, name):
    def kernel(place_ref, tile_ref, *refs):
        row = 0
        for out_ref, length in zip(refs, lengths):
            for r in range(length // TC):
                out_ref[:, r * TC : (r + 1) * TC] = tile_ref[0, row : row + 1, :].astype(jnp.float32)
                row += 1

    return pl.pallas_call(
        kernel,
        out_shape=[jax.ShapeDtypeStruct((1, length), jnp.float32) for length in lengths],
        grid_spec=pltpu.PrefetchScalarGridSpec(
            num_scalar_prefetch=1,
            grid=(1,),
            in_specs=[pl.BlockSpec((1, TR, TC), lambda g, place_ref: (place_ref[base], 0, 0))],
            out_specs=[pl.BlockSpec((1, length), lambda g, place_ref: (0, 0)) for length in lengths],
        ),
        name="unpack_vectors_" + name,
    )(place, tiles)


def join_vectors(vectors, name):
    def kernel(*refs):
        out_ref = refs[-1]
        row = 0
        for source in refs[:-1]:
            for r in range(source.shape[1] // TC):
                out_ref[row : row + 1, :] = source[:, r * TC : (r + 1) * TC]
                row += 1
        out_ref[row:, :] = jnp.zeros((TR - row, TC), jnp.float32)

    return pl.pallas_call(
        kernel,
        out_shape=jax.ShapeDtypeStruct((TR, TC), jnp.float32),
        name="join_vectors_" + name,
    )(*vectors)


def unpack_section(tiles, place, section_id):
    matrices, vectors = layout(section_id)
    found, base = {}, 0
    for name, rows, columns in matrices:
        found[name] = unpack_matrix(tiles, place, base, rows, columns, f"{name}_{section_id}")
        base += rows * columns // (TR * TC)
    lines = unpack_vectors(tiles, place, base, [length for name, length in vectors], str(section_id))
    found.update({name: line for (name, length), line in zip(vectors, lines)})
    return found


def weight_codes(a, d, place, line, base, codes, scales, total, name):
    length = a.shape[0]
    rows, columns = a.shape if d is None else (a.shape[1], d.shape[1])
    wide = columns // TC
    many = groups_of(rows, wide)
    count = many * wide
    steps = rows // (many * TR)
    fresh = codes is None
    n_in = 1 if d is None else 2

    def kernel(place_ref, line_ref, *refs):
        scales_in = refs[n_in]
        codes_ref, scales_ref, left, right, ready, sem = refs[-6:]
        step = pl.program_id(0)
        slot = lax.rem(step, 2)

        @pl.when(step == 0)
        def _():
            scales_ref[...] = scales_in[...]

        def copies(at_step, at_slot):
            return [
                pltpu.make_async_copy(
                    ready.at[at_slot, j], codes_ref.at[place_ref[base + at_step * count + j]], sem.at[at_slot, j]
                )
                for j in range(count)
            ]

        @pl.when(step >= 2)
        def _():
            for copy in copies(step - 2, slot):
                copy.wait()

        for j in range(wide):
            columns_j = slice(j * TC, (j + 1) * TC)
            if d is None:
                part = refs[0][:, columns_j]
            else:
                part = weight_grad(refs[0][...], refs[1][:, columns_j])
            for h, lines in enumerate((left, right)):
                lines[pl.ds(j, many * TR, stride=wide), :] = part[:, h * LANES : (h + 1) * LANES]
        for j in range(count):
            at = line_ref[base + step * count + j]
            pair = []
            for h, lines in enumerate((left, right)):
                value, scale = code(lines[j * TR : (j + 1) * TR, :])
                ready[slot, j, :, h * LANES : (h + 1) * LANES] = value
                pair.append(scale)
            scales_ref[pl.ds(at, 1), :] = jnp.concatenate(pair, axis=1)
        for copy in copies(step, slot):
            copy.start()

        @pl.when(step == steps - 1)
        def _():
            if steps > 1:
                for copy in copies(step - 1, 1 - slot):
                    copy.wait()
            for copy in copies(step, slot):
                copy.wait()

    whole = pl.BlockSpec(scales.shape, lambda g, a, b: (0, 0))
    hbm = pl.BlockSpec(memory_space=pltpu.HBM)
    if d is None:
        operands, specs = [a], [pl.BlockSpec((many * TR, columns), lambda g, a, b: (g, 0))]
    else:
        operands = [a, d]
        specs = [
            pl.BlockSpec((length, many * TR), lambda g, a, b: (0, g)),
            pl.BlockSpec((length, columns), lambda g, a, b: (0, 0)),
        ]
    aliases = {2 + n_in: 1}
    if not fresh:
        aliases[3 + n_in] = 0
    return pl.pallas_call(
        kernel,
        out_shape=(
            jax.ShapeDtypeStruct((total, TR, TC), jnp.int16),
            jax.ShapeDtypeStruct(scales.shape, jnp.float32),
        ),
        grid_spec=pltpu.PrefetchScalarGridSpec(
            num_scalar_prefetch=2,
            grid=(steps,),
            in_specs=specs + [whole] + ([] if fresh else [hbm]),
            out_specs=(hbm, whole),
            scratch_shapes=[
                pltpu.VMEM((count * TR, LANES), jnp.float32),
                pltpu.VMEM((count * TR, LANES), jnp.float32),
                pltpu.VMEM((2, count, TR, TC), jnp.int16),
                pltpu.SemaphoreType.DMA((2, count)),
            ],
        ),
        input_output_aliases=aliases,
        compiler_params=pltpu.CompilerParams(vmem_limit_bytes=40 * 2**20),
        name="weight_codes_" + name,
    )(place, line, *operands, scales, *([] if fresh else [codes]))


def adam(codes, scales, index, used, factor, master, first, second):
    slots = master.shape[0]
    per = 3 if slots % 3 == 0 else 1

    def kernel(index_ref, used_ref, factor_ref, codes_ref, scales_ref, w_ref, m_ref, v_ref, w_out, m_out, v_out):
        for t in range(per):
            slot = pl.program_id(0) * per + t
            source = index_ref[slot]
            grad = codes_ref[source].astype(jnp.float32) * scales_ref[source]
            grad = jnp.where(used_ref[slot] > 0, grad * factor_ref[0], 0.0)
            first_new = BETA_ONE * m_ref[t] + (1.0 - BETA_ONE) * grad
            second_new = BETA_TWO * v_ref[t] + (1.0 - BETA_TWO) * grad * grad
            ratio = (
                first_new
                / (1.0 - BETA_ONE ** float(STEP))
                / (jnp.sqrt(second_new / (1.0 - BETA_TWO ** float(STEP))) + ADAM_EPS)
            )
            w_out[t] = w_ref[t] - RATE * (ratio + DECAY * w_ref[t])
            m_out[t] = first_new
            v_out[t] = second_new

    smem = pl.BlockSpec(memory_space=pltpu.SMEM)
    block = pl.BlockSpec((per, TR, TC), lambda g: (g, 0, 0))
    return pl.pallas_call(
        kernel,
        out_shape=[jax.ShapeDtypeStruct(master.shape, jnp.float32)] * 3,
        grid=(slots // per,),
        in_specs=[
            smem,
            smem,
            smem,
            pl.BlockSpec(codes.shape, lambda g: (0, 0, 0)),
            pl.BlockSpec(scales.shape, lambda g: (0, 0, 0)),
            block,
            block,
            block,
        ],
        out_specs=[block] * 3,
        compiler_params=pltpu.CompilerParams(vmem_limit_bytes=40 * 2**20),
        name="adam",
    )(index, used, factor, codes, scales, master, first, second)


def project(a, w):
    return jnp.dot(a, w, preferred_element_type=jnp.float32)


def project_back(d, w):
    return lax.dot_general(d, w, (((1,), (1,)), ((), ())), preferred_element_type=jnp.float32)


def weight_grad(a, d):
    return lax.dot_general(a, d, (((0,), (0,)), ((), ())), preferred_element_type=jnp.float32)


def layer_norm(values, gain, offset):
    centre = values - jnp.mean(values, -1, keepdims=True)
    return centre * lax.rsqrt(jnp.mean(centre * centre, -1, keepdims=True) + EPS_NORM) * gain + offset


def norm_back(upstream, values, gain):
    centre = values - jnp.mean(values, -1, keepdims=True)
    spread = lax.rsqrt(jnp.mean(centre * centre, -1, keepdims=True) + EPS_NORM)
    normed = centre * spread
    scaled = upstream * gain
    downstream = spread * (
        scaled - jnp.mean(scaled, -1, keepdims=True) - normed * jnp.mean(scaled * normed, -1, keepdims=True)
    )
    return downstream, line_sum(upstream * normed), line_sum(upstream)


def line_sum(values):
    return jnp.sum(values.astype(jnp.float32), 0, keepdims=True)


ERF_TOP = (
    -2.72614225801306e-10,
    2.77068142495902e-08,
    -2.10102402082508e-06,
    -5.69250639462346e-05,
    -7.34990630326855e-04,
    -2.95459980854025e-03,
    -1.60960333262415e-02,
)
ERF_BOTTOM = (
    -1.45660718464996e-05,
    -2.13374055278905e-04,
    -1.68282697438203e-03,
    -7.37332916720468e-03,
    -1.42647390514189e-02,
)


def erf(x):
    x = jnp.clip(x, -4.0, 4.0)
    square = x * x
    top, bottom = jnp.full_like(x, ERF_TOP[0]), jnp.full_like(x, ERF_BOTTOM[0])
    for coefficient in ERF_TOP[1:]:
        top = top * square + coefficient
    for coefficient in ERF_BOTTOM[1:]:
        bottom = bottom * square + coefficient
    return x * top / bottom


def whole_kernel(kernel, shapes, operands, name, scratch=(), smem=0):
    vmem = pl.BlockSpec(memory_space=pltpu.VMEM)
    return pl.pallas_call(
        kernel,
        out_shape=[jax.ShapeDtypeStruct(shape, dtype) for shape, dtype in shapes],
        in_specs=[pl.BlockSpec(memory_space=pltpu.SMEM)] * smem + [vmem] * (len(operands) - smem),
        out_specs=[vmem] * len(shapes),
        scratch_shapes=scratch,
        compiler_params=pltpu.CompilerParams(vmem_limit_bytes=56 * 2**20),
        name=name,
    )(*operands)


F32, BF16 = jnp.float32, jnp.bfloat16


def start_block(x_ref, rows, w, a_ref, qkv_ref):
    g1, b1, weight, bias = w
    width = x_ref.shape[1]
    a = layer_norm(x_ref[rows, :], g1[...], b1[...]).astype(BF16)
    a_ref[rows, :] = a
    for part in range(3):
        columns = slice(part * width, (part + 1) * width)
        value = project(a, weight[:, columns])
        if part != 1:
            value = value + bias[:, (part // 2) * width : (part // 2 + 1) * width]
        qkv_ref[rows, columns] = value.astype(BF16)


def enter_encoder(xin, place, w):
    def kernel(xin_ref, place_ref, first, bias, g1, b1, weight, qv_bias, x_ref, a_ref, qkv_ref):
        x_ref[...] = project(xin_ref[...], first[...]) + bias[...] + place_ref[...]
        start_block(x_ref, slice(None), (g1, b1, weight, qv_bias), a_ref, qkv_ref)

    shapes = [((KEEP, D_ENC), F32), ((KEEP, D_ENC), BF16), ((KEEP, 3 * D_ENC), BF16)]
    operands = [xin, place] + [w[k] for k in ("first", "first_bias", "g1", "b1", "qkv", "qv_bias")]
    return whole_kernel(kernel, shapes, operands, "enter_encoder")


def enter_decoder(chosen_turned, sent, kept, place, w):
    def kernel(chosen_ref, sent_ref, kept_ref, place_ref, first, bias, mask, g1, b1, weight, qv_bias,
               x_ref, a_ref, qkv_ref):
        for lo, hi in row_cuts(SEQ, 304):
            rows = slice(lo, hi)
            spread = project(chosen_ref[rows, :], sent_ref[...]).astype(BF16)
            placed = project(spread, first[...]) + bias[...]
            x_ref[rows, :] = jnp.where(kept_ref[rows, :] > 0.0, placed, mask[...]) + place_ref[rows, :]
            start_block(x_ref, rows, (g1, b1, weight, qv_bias), a_ref, qkv_ref)

    shapes = [((SEQ, D_DEC), F32), ((SEQ, D_DEC), BF16), ((SEQ, 3 * D_DEC), BF16)]
    names = ("first", "first_bias", "mask", "g1", "b1", "qkv", "qv_bias")
    operands = [chosen_turned, sent, kept, place] + [w[k] for k in names]
    return whole_kernel(kernel, shapes, operands, "enter_decoder")


def finish_block(x, attended, w, name):
    length, width = x.shape
    hidden = w["fc1"].shape[1]

    line = (length, width)
    shapes = [(line, F32), (line, BF16), ((length, hidden), BF16), ((length, hidden), F32), (line, F32), (line, BF16)]
    names = ("proj", "proj_bias", "g2", "b2", "fc1", "fc1_bias", "fc2", "fc2_bias", "gf", "bf")
    return whole_kernel(finish_body, shapes, [x, attended] + [w[k] for k in names], "finish_" + name)


def finish_body(x_ref, o_ref, proj, proj_bias, g2, b2, fc1, fc1_bias, fc2, fc2_bias, gf, bf,
                h_ref, c_ref, z_ref, slope_ref, y_ref, out_ref, pump=None):
    length, hidden = z_ref.shape
    for lo, hi in row_cuts(length, 304):
        rows = slice(lo, hi)
        h = x_ref[rows, :] + project(o_ref[rows, :], proj[...]) + proj_bias[...]
        h_ref[rows, :] = h
        c_ref[rows, :] = layer_norm(h, g2[...], b2[...]).astype(BF16)
    for lo in range(0, hidden, 256):
        columns = slice(lo, lo + 256)
        u = project(c_ref[...], fc1[:, columns]) + fc1_bias[:, columns]
        below = 0.5 * (1.0 + erf(u * (1.0 / math.sqrt(2.0))))
        z = (u * below).astype(BF16)
        z_ref[:, columns] = z
        slope_ref[:, columns] = below + u * jnp.exp(-0.5 * u * u) * (1.0 / math.sqrt(2.0 * math.pi))
        y = project(z, fc2[columns, :])
        if lo:
            y_ref[...] += y
        else:
            y_ref[...] = y
        if pump is not None and lo % 512 == 256:
            pump(1)
    for lo, hi in row_cuts(length, 304):
        rows = slice(lo, hi)
        y = h_ref[rows, :] + y_ref[rows, :] + fc2_bias[...]
        y_ref[rows, :] = y
        out_ref[rows, :] = layer_norm(y, gf[...], bf[...]).astype(BF16)


def back_finish(d_out, y, slope, h, w, name):
    length, width = y.shape
    hidden = slope.shape[1]

    def kernel(d_ref, y_ref, slope_ref, h_ref, gf, fc2, fc1, g2, proj,
               two_ref, du_ref, dh_ref, one_ref, do_ref, s_gf, s_bf, s_fc2, s_fc1, s_g2, s_b2, s_proj, dc_ref):
        for n, (lo, hi) in enumerate(row_cuts(length, 304)):
            rows = slice(lo, hi)
            dy, gain, shift = norm_back(d_ref[rows, :].astype(F32), y_ref[rows, :], gf[...])
            dh_ref[rows, :] = dy
            two = dy.astype(BF16)
            two_ref[rows, :] = two
            collect(n, (s_gf, gain), (s_bf, shift), (s_fc2, line_sum(two)))
        for lo in range(0, hidden, 256):
            columns = slice(lo, lo + 256)
            du = (project_back(two_ref[...], fc2[columns, :]) * slope_ref[:, columns]).astype(BF16)
            du_ref[:, columns] = du
            s_fc1[:, columns] = line_sum(du)
            dc = project_back(du, fc1[:, columns])
            if lo:
                dc_ref[...] += dc
            else:
                dc_ref[...] = dc
        for n, (lo, hi) in enumerate(row_cuts(length, 304)):
            rows = slice(lo, hi)
            part, gain, shift = norm_back(dc_ref[rows, :], h_ref[rows, :], g2[...])
            dh = dh_ref[rows, :] + part
            dh_ref[rows, :] = dh
            one = dh.astype(BF16)
            one_ref[rows, :] = one
            collect(n, (s_g2, gain), (s_b2, shift), (s_proj, line_sum(one)))
        do_ref[...] = project_back(one_ref[...], proj[...]).astype(BF16)

    line = (length, width)
    shapes = [(line, BF16), ((length, hidden), BF16), (line, F32), (line, BF16), (line, BF16)]
    shapes += [((1, n), F32) for n in (width, width, width, hidden, width, width, width)]
    operands = [d_out, y, slope, h] + [w[k] for k in ("gf", "fc2", "fc1", "g2", "proj")]
    return whole_kernel(kernel, shapes, operands, "back_finish_" + name, [pltpu.VMEM(line, F32)])


def collect(n, *pairs):
    for ref, value in pairs:
        ref[...] = ref[...] + value if n else value


def leave_encoder(dqkv, x, dh, w):
    def kernel(d_ref, x_ref, dh_ref, g1, weight, low_ref, s_qv, s_g1, s_b1, s_first):
        d = d_ref[...]
        part, gain, shift = norm_back(project_back(d, weight[...]), x_ref[...], g1[...])
        dx = dh_ref[...] + part
        low_ref[...] = dx.astype(BF16)
        s_qv[:, :D_ENC] = line_sum(d[:, :D_ENC])
        s_qv[:, D_ENC:] = line_sum(d[:, 2 * D_ENC :])
        s_g1[...] = gain
        s_b1[...] = shift
        s_first[...] = line_sum(dx)

    shapes = [((KEEP, D_ENC), BF16)] + [((1, n), F32) for n in (2 * D_ENC, D_ENC, D_ENC, D_ENC)]
    return whole_kernel(kernel, shapes, [dqkv, x, dh, w["g1"], w["qkv"]], "leave_encoder")


def leave_decoder(dqkv, x, dh, chosen, kept, w):
    def kernel(d_ref, x_ref, dh_ref, chosen_ref, kept_ref, g1, weight, first,
               low_ref, sent_ref, s_qv, s_g1, s_b1, s_mask, s_first, da_ref, dx_ref):
        da_ref[...] = project_back(d_ref[...], weight[...])
        for n, (lo, hi) in enumerate(row_cuts(SEQ, 304)):
            rows = slice(lo, hi)
            part, gain, shift = norm_back(da_ref[rows, :], x_ref[rows, :], g1[...])
            dx = dh_ref[rows, :] + part
            dx_ref[rows, :] = dx.astype(BF16)
            kept_rows = kept_ref[rows, :]
            collect(
                n,
                (s_g1, gain),
                (s_b1, shift),
                (s_mask, line_sum(dx * (1.0 - kept_rows))),
                (s_first, line_sum(dx * kept_rows)),
            )
        s_qv[:, :D_DEC] = line_sum(d_ref[:, :D_DEC])
        s_qv[:, D_DEC:] = line_sum(d_ref[:, 2 * D_DEC :])
        low = project(chosen_ref[...], dx_ref[...]).astype(BF16)
        low_ref[...] = low
        sent_ref[...] = project_back(low, first[...]).astype(BF16)

    shapes = [((KEEP, D_DEC), BF16), ((KEEP, D_ENC), BF16)]
    shapes += [((1, n), F32) for n in (2 * D_DEC, D_DEC, D_DEC, D_DEC, D_DEC)]
    return whole_kernel(
        kernel,
        shapes,
        [dqkv, x, dh, chosen, kept, w["g1"], w["qkv"], w["first"]],
        "leave_decoder",
        [pltpu.VMEM((SEQ, D_DEC), F32), pltpu.VMEM((SEQ, D_DEC), BF16)],
    )


def head_mask(size, h):
    lane = lax.broadcasted_iota(jnp.int32, (1, LANES), 1)
    return (lane >= h * size) & (lane < (h + 1) * size)


def head_mask(size, h):
    lane = lax.broadcasted_iota(jnp.int32, (1, LANES), 1)
    return (lane >= h * size) & (lane < (h + 1) * size)


def row_cuts(length, step):
    return [(lo, min(lo + step, length)) for lo in range(0, length, step)]


def mix_heads(q_ref, k_ref, v_ref, out_ref, size):
    keys, values = k_ref[...].T, v_ref[...]
    for lo, hi in row_cuts(q_ref.shape[0], 304):
        total = jnp.zeros((hi - lo, LANES), F32)
        for h in range(LANES // size):
            mask = head_mask(size, h)
            query = jnp.where(mask, q_ref[lo:hi, :], jnp.zeros((), BF16))
            scores = project(query, keys)
            power = jnp.exp2((scores - jnp.max(scores, -1, keepdims=True)) * (size ** (-0.5) * LOG2E))
            probs = power * (1.0 / jnp.sum(power, -1, keepdims=True))
            mixed = project(probs.astype(BF16), values)
            total = jnp.where(mask, mixed, total)
        out_ref[lo:hi, :] = total.astype(BF16)


def attention(qkv, heads):
    length, width = qkv.shape[0], qkv.shape[1] // 3
    size = width // heads
    groups = width // LANES

    def kernel(q_ref, k_ref, v_ref, out_ref):
        mix_heads(q_ref, k_ref, v_ref, out_ref, size)

    def spec(offset):
        return pl.BlockSpec((length, LANES), lambda g: (0, g + offset))

    return pl.pallas_call(
        kernel,
        out_shape=jax.ShapeDtypeStruct((length, width), jnp.bfloat16),
        grid=(groups,),
        in_specs=[spec(0), spec(groups), spec(2 * groups)],
        out_specs=spec(0),
        compiler_params=pltpu.CompilerParams(vmem_limit_bytes=40 * 2**20),
        name=f"attention_{heads}",
    )(qkv, qkv, qkv)


def attention_back(qkv, grad, heads):
    length, width = grad.shape
    size = width // heads
    groups = width // LANES
    factor = size ** (-0.5)

    def kernel(q_ref, k_ref, v_ref, g_ref, out_ref, dq_turned):
        zero = jnp.zeros((), jnp.bfloat16)
        keys, values = k_ref[...], v_ref[...]
        keys_turned = keys.T
        cuts = row_cuts(length, 256)
        for n, (lo, hi) in enumerate(cuts):
            query_all, grad_all = q_ref[lo:hi, :], g_ref[lo:hi, :]
            query_turned, grad_turned = query_all.T, grad_all.T
            dk = dv = None
            for h in range(LANES // size):
                own = slice(h * size, (h + 1) * size)
                row = lax.broadcasted_iota(jnp.int32, (LANES, 1), 0)
                rows = (row >= h * size) & (row < (h + 1) * size)
                mask = head_mask(size, h)
                scores = project(keys, jnp.where(rows, query_turned, zero))
                power = jnp.exp2((scores - jnp.max(scores, 0, keepdims=True)) * (factor * LOG2E))
                probs = power * (1.0 / jnp.sum(power, 0, keepdims=True))
                d_probs = project(values, jnp.where(rows, grad_turned, zero))
                inner = jnp.sum(d_probs * probs, 0, keepdims=True)
                d_scores = (probs * (d_probs - inner)).astype(jnp.bfloat16)
                dv_h = project(probs.astype(jnp.bfloat16), jnp.where(mask, grad_all, zero))
                dk_h = project(d_scores, jnp.where(mask, query_all, zero))
                dv = dv_h if dv is None else dv + dv_h
                dk = dk_h if dk is None else dk + dk_h
                dq_turned[own, lo:hi] = project(keys_turned[own, :], d_scores)
            if n:
                dk_sum, dv_sum = dk_sum + dk, dv_sum + dv
            else:
                dk_sum, dv_sum = dk, dv
        dq = dq_turned[...].T * factor
        for part, value in enumerate((dq, dk_sum * factor, dv_sum)):
            start = pl.multiple_of(part * width + pl.program_id(0) * LANES, LANES)
            out_ref[:, pl.ds(start, LANES)] = value.astype(jnp.bfloat16)

    def spec(offset):
        return pl.BlockSpec((length, LANES), lambda g: (0, g + offset))

    return pl.pallas_call(
        kernel,
        out_shape=jax.ShapeDtypeStruct((length, 3 * width), jnp.bfloat16),
        grid=(groups,),
        in_specs=[spec(0), spec(groups), spec(2 * groups), spec(0)],
        out_specs=pl.BlockSpec((length, 3 * width), lambda g: (0, 0)),
        scratch_shapes=[pltpu.VMEM((LANES, length), jnp.float32)],
        compiler_params=pltpu.CompilerParams(vmem_limit_bytes=40 * 2**20),
        name=f"attention_back_{heads}",
    )(qkv, qkv, qkv, grad)


def head_step(final, w, bias, pix, valid, inverse):
    def kernel(inverse_ref, final_ref, w_ref, bias_ref, pix_ref, valid_ref, low_ref, sums_ref, loss_ref, back_ref):
        one = inverse_ref[0]
        for band in range(BANDS):
            columns = slice(band * PATCH_PIX, (band + 1) * PATCH_PIX)
            predicted = jnp.dot(final_ref[...], w_ref[:, columns], preferred_element_type=jnp.float32)
            predicted = predicted + bias_ref[:, columns]
            values = pix_ref[:, columns].astype(jnp.float32)
            centre = values - jnp.mean(values, -1, keepdims=True)
            target = centre * lax.rsqrt(jnp.mean(centre * centre, -1, keepdims=True) + EPS_NORM)
            misfit = predicted - target
            valid_misfit = valid_ref[...] * misfit
            part = jnp.sum(valid_misfit * misfit, 0, keepdims=True) * (one / (BANDS * PATCH_PIX))
            if band:
                loss_ref[...] += part
            else:
                loss_ref[...] = part
            grad = valid_misfit * (one * (2.0 / (BANDS * PATCH_PIX)))
            low = grad.astype(jnp.bfloat16)
            low_ref[:, columns] = low
            sums_ref[:, columns] = jnp.sum(grad, 0, keepdims=True)
            back = lax.dot_general(low, w_ref[:, columns], (((1,), (1,)), ((), ())), preferred_element_type=jnp.float32)
            if band:
                back_ref[...] += back
            else:
                back_ref[...] = back

    vmem = pl.BlockSpec(memory_space=pltpu.VMEM)
    return pl.pallas_call(
        kernel,
        out_shape=[
            jax.ShapeDtypeStruct((SEQ, PATCH_DIM), jnp.bfloat16),
            jax.ShapeDtypeStruct((1, PATCH_DIM), jnp.float32),
            jax.ShapeDtypeStruct((1, PATCH_PIX), jnp.float32),
            jax.ShapeDtypeStruct((SEQ, D_DEC), jnp.float32),
        ],
        in_specs=[pl.BlockSpec(memory_space=pltpu.SMEM)] + [vmem] * 5,
        out_specs=[vmem] * 4,
        compiler_params=pltpu.CompilerParams(vmem_limit_bytes=40 * 2**20),
        name="head_step",
    )(inverse, final, w, bias, pix, valid)


class Spread:
    MOVES = {"u": [(0, 0, 1)], "v": [(0, 1, 0)], "z": [(1, 0, 0), (2, 0, 0), (3, 0, 0)]}

    def __init__(self, section, place, block_ref, all_ref, ways, cut, sems, first):
        self.section, self.place, self.at = section, place, neighbours(section, place)
        self.block_ref, self.all_ref, self.ways, self.cut, self.sems = block_ref, all_ref, ways, cut, sems
        self.count = block_ref.shape[0]
        self.copies, self.sides = {}, {}
        self.next_copy = self.next_side = first

    def rows(self, section, holder, way):
        start = (section * 16 + holder) * self.count + self.cut[way]
        return self.all_ref.at[pl.ds(start, self.cut[way + 1] - self.cut[way])]

    def source(self, way, origin):
        if origin == (0, 0, 0):
            return self.block_ref.at[pl.ds(self.cut[way], self.cut[way + 1] - self.cut[way])]
        return self.rows(self.section, self.at(*origin), way)

    def send(self, way, origin, move):
        copy = pltpu.make_async_remote_copy(
            src_ref=self.source(way, origin),
            dst_ref=self.rows(self.section, self.at(*origin), way),
            send_sem=self.sems[0].at[self.next_copy],
            recv_sem=self.sems[1].at[self.next_copy],
            device_id=(self.section, self.at(*move)),
            device_id_type=MESH,
        )
        copy.start()
        self.copies[way, self.moved(origin, move)] = (copy, self.next_copy)
        self.next_copy += 1

    def moved(self, origin, move):
        return tuple((o - m) % s for o, m, s in zip(origin, move, (4, 2, 2)))

    def side(self, way, origin):
        copy = pltpu.make_async_remote_copy(
            src_ref=self.source(way, origin),
            dst_ref=self.rows(self.section, self.at(*origin), way),
            send_sem=self.sems[2].at[self.next_side],
            recv_sem=self.sems[3].at[self.next_side],
            device_id=(1 - self.section, self.place),
            device_id_type=MESH,
        )
        copy.start()
        self.sides[way, origin] = (copy, self.next_side)
        self.next_side += 1

    def arrived(self, target, send_sem, recv_sem):
        pltpu.make_async_remote_copy(
            src_ref=target,
            dst_ref=target,
            send_sem=send_sem,
            recv_sem=recv_sem,
            device_id=(1 - self.section, self.place),
            device_id_type=MESH,
        ).wait_recv()

    def take(self, way, origin, dims):
        index = self.copies[way, origin][1]
        self.arrived(
            self.rows(self.section, self.at(*origin), way), self.sems[0].at[index], self.sems[1].at[index]
        )
        for dim in dims:
            for move in self.MOVES[dim]:
                self.send(way, origin, move)
        self.side(way, origin)

    def start(self):
        zero = (0, 0, 0)
        self.own = pltpu.make_async_copy(
            self.block_ref, self.all_ref.at[pl.ds((self.section * 16 + self.place) * self.count, self.count)], self.sems[4]
        )
        self.own.start()
        for turn in range(3):
            for way, dims in enumerate(self.ways):
                for move in self.MOVES[dims[turn]]:
                    self.send(way, zero, move)
        for way in range(len(self.ways)):
            self.side(way, zero)
        held = {way: [zero] for way in range(len(self.ways))}
        steps = []
        for turn in range(3):
            come = {}
            for way, dims in enumerate(self.ways):
                come[way] = [self.moved(o, m) for m in self.MOVES[dims[turn]] for o in held[way]]
                held[way] = held[way] + come[way]
            for i in range(max(len(v) for v in come.values())):
                for way, dims in enumerate(self.ways):
                    if i < len(come[way]):
                        steps.append(functools.partial(self.take, way, come[way][i], dims[turn + 1 :]))
        return steps

    def finish(self):
        self.own.wait()
        for copy, index in self.copies.values():
            copy.wait_send()
        for (way, origin), (copy, index) in self.sides.items():
            copy.wait_send()
            self.arrived(
                self.rows(1 - self.section, self.at(*origin), way), self.sems[2].at[index], self.sems[3].at[index]
            )


def greet(section, place):
    at = neighbours(section, place)
    barrier = pltpu.get_barrier_semaphore()
    peers = [(1 - section, place)]
    peers += [(section, at(*d)) for d in ((0, 0, 1), (0, 1, 0), (1, 0, 0), (2, 0, 0), (3, 0, 0))]
    for peer in peers:
        pl.semaphore_signal(barrier, inc=1, device_id=peer, device_id_type=MESH)
    pl.semaphore_wait(barrier, len(peers))


def spread_sems(copies, sides):
    return [
        pltpu.SemaphoreType.DMA((copies,)),
        pltpu.SemaphoreType.DMA((copies,)),
        pltpu.SemaphoreType.DMA((sides,)),
        pltpu.SemaphoreType.DMA((sides,)),
        pltpu.SemaphoreType.DMA,
    ]


FOUR_WAYS = (("z", "v", "u"), ("z", "u", "v"), ("v", "z", "u"), ("u", "z", "v"))
ONE_WAY = (("z", "v", "u"),)


def gather_and_encode(early, late, place, xin, positions_kept, cid):
    n_early, n_late = early.shape[0], late.shape[0]
    matrices, vectors = layout(0)
    shapes = {name: (rows, columns) for name, rows, columns in matrices}
    lengths = dict(vectors)
    base = {}
    total = 0
    for name, rows, columns in matrices:
        base[name] = total
        total += rows * columns // (TR * TC)
    kept_weights = ("qkv", "proj", "fc1", "fc2")
    kept_vectors = ("g1", "g2", "gf")
    line = (KEEP, D_ENC)
    hidden = (KEEP, FF_ENC)
    results = [
        (line, F32), (line, BF16), ((KEEP, 3 * D_ENC), BF16), (line, BF16), (line, F32), (line, BF16), (hidden, BF16),
        (hidden, F32), (line, F32), (line, BF16),
    ]

    def kernel(place_ref, early_ref, late_ref, xin_ref, pos_ref, late_all, *refs):
        refs = list(refs)
        out_w = {name: refs.pop(0) for name in kept_weights}
        out_v = {name: refs.pop(0) for name in kept_vectors}
        x, a, qkv, o, h, c, z, slope, y, sent = [refs.pop(0) for _ in results]
        pool = refs.pop(0)
        w = {name: refs.pop(0) for name, rows, columns in matrices}
        v = {name: refs.pop(0) for name, length in vectors}
        left, right = refs.pop(0), refs.pop(0)
        early_sems, late_sems, out_sem = refs[:5], refs[5:10], refs[10]
        section, at_dp = lax.axis_index("section"), lax.axis_index("dp")
        greet(section, at_dp)
        cut = [0, 3, 5, 7, n_early] if n_early == 8 else [0, 1, 2, 3, n_early]
        soon = Spread(section, at_dp, early_ref, pool, FOUR_WAYS, cut, early_sems, 0)
        for step in soon.start():
            step()
        later = Spread(section, at_dp, late_ref, late_all, ONE_WAY, [0, n_late], late_sems, 0)
        steps = later.start()
        soon.finish()

        def pump(count):
            for _ in range(min(count, len(steps))):
                steps.pop(0)()

        def unpack(name):
            rows, columns = shapes[name]
            wide = columns // TC
            many = groups_of(rows, wide)
            count = many * wide

            def group(g, carry):
                for j in range(count):
                    tile = pool[place_ref[base[name] + g * count + j]].astype(F32)
                    left[j * TR : (j + 1) * TR, :] = tile[:, :LANES]
                    right[j * TR : (j + 1) * TR, :] = tile[:, LANES:]
                rows_g = pl.ds(pl.multiple_of(g * many * TR, TR), many * TR)
                for j in range(wide):
                    for n, lines in enumerate((left, right)):
                        start = j * TC + n * LANES
                        w[name][rows_g, start : start + LANES] = lines[pl.ds(j, many * TR, stride=wide), :].astype(BF16)
                return carry

            lax.fori_loop(0, rows // (many * TR), group, 0)
            if name in kept_weights:
                pltpu.make_async_copy(w[name], out_w[name], out_sem.at[kept_weights.index(name)]).start()

        tile = pool[place_ref[total]].astype(F32)
        row = 0
        for name, length in vectors:
            for r in range(length // TC):
                v[name][:, r * TC : (r + 1) * TC] = tile[row : row + 1, :]
                row += 1
        for name in kept_vectors:
            out_v[name][...] = v[name][...]
        unpack("first")
        unpack("qkv")
        pump(1)
        x[...] = project(xin_ref[...], w["first"][...]) + v["first_bias"][...] + pos_ref[...]
        start_block(x, slice(None), (v["g1"], v["b1"], w["qkv"], v["qv_bias"]), a, qkv)
        pump(1)
        for g in range(D_ENC // LANES):
            spans = [slice(part * D_ENC + g * LANES, part * D_ENC + (g + 1) * LANES) for part in range(3)]
            mix_heads(*[qkv.at[:, span] for span in spans], o.at[:, spans[0]], D_ENC // H_ENC)
        pump(2)
        unpack("proj")
        unpack("fc1")
        pump(2)
        unpack("fc2")
        pump(2)
        names = ("proj", "proj_bias", "g2", "b2", "fc1", "fc1_bias", "fc2", "fc2_bias", "gf", "bf")
        finish_body(x, o, *[w[name] if name in w else v[name] for name in names], h, c, z, slope, y, sent, pump)
        pump(len(steps))
        later.finish()
        for name in kept_weights:
            pltpu.make_async_copy(w[name], out_w[name], out_sem.at[kept_weights.index(name)]).wait()

    vmem, hbm = pl.BlockSpec(memory_space=pltpu.VMEM), pl.BlockSpec(memory_space=pltpu.HBM)
    shape = jax.ShapeDtypeStruct
    outs = pl.pallas_call(
        kernel,
        out_shape=[shape((32 * n_late, TR, TC), BF16)]
        + [shape(shapes[name], BF16) for name in kept_weights]
        + [shape((1, lengths[name]), F32) for name in kept_vectors]
        + [shape(*result) for result in results],
        in_specs=[pl.BlockSpec(memory_space=pltpu.SMEM), hbm, hbm, vmem, vmem],
        out_specs=[hbm] * (1 + len(kept_weights)) + [vmem] * (len(kept_vectors) + len(results)),
        scratch_shapes=[pltpu.VMEM((32 * n_early, TR, TC), BF16)]
        + [pltpu.VMEM(shapes[name], BF16) for name, rows, columns in matrices]
        + [pltpu.VMEM((1, length), F32) for name, length in vectors]
        + [pltpu.VMEM((12 * TR, LANES), F32)] * 2
        + spread_sems(60, 64)
        + spread_sems(15, 16)
        + [pltpu.SemaphoreType.DMA((len(kept_weights),))],
        compiler_params=pltpu.CompilerParams(
            collective_id=cid, has_side_effects=True, vmem_limit_bytes=60 * 2**20
        ),
        name="gather_and_encode",
    )(place, early, late, xin, positions_kept)
    late_all, outs = outs[0], outs[1:]
    weights = dict(zip(kept_weights + kept_vectors, outs))
    return late_all, weights, outs[len(weights) :]


def encode(w, xin, positions_kept):
    x, a, qkv = enter_encoder(xin, positions_kept, w)
    o = attention(qkv, H_ENC)
    return x, a, qkv, o, *finish_block(x, o, w, "encoder")


def item_step(enc, dec, encoded, pix, kept, valid, xin, chosen, inverse):
    x0, a0, qkv0, o0, h0, c0, z0, slope0, y0, sent = encoded
    x1, a1, qkv1 = enter_decoder(chosen.T, sent, kept, jnp.asarray(positions(D_DEC)), dec)
    o1 = attention(qkv1, H_DEC)
    h1, c1, z1, slope1, y1, final = finish_block(x1, o1, dec, "decoder")
    pred_low, head_bias, loss_terms, d_final = head_step(
        final, dec["head"], dec["head_bias"], pix, valid, inverse
    )
    two, du, dh, one, do, *sums = back_finish(d_final, y1, slope1, h1, dec, "decoder")
    names = ("gf", "bf", "fc2_bias", "fc1_bias", "g2", "b2", "proj_bias")
    grads_dec = dict(zip(names, sums))
    dqkv = attention_back(qkv1, do, H_DEC)
    low, d_sent, *sums = leave_decoder(dqkv, x1, dh, chosen, kept, dec)
    grads_dec.update(zip(("qv_bias", "g1", "b1", "mask", "first_bias"), sums))
    grads_dec.update(
        head=(final, pred_low),
        head_bias=head_bias,
        fc2=(z1, two),
        fc1=(c1, du),
        proj=(o1, one),
        qkv=(a1, dqkv),
        first=(sent, low),
    )
    two, du, dh, one, do, *sums = back_finish(d_sent, y0, slope0, h0, enc, "encoder")
    grads_enc = dict(zip(names, sums))
    dqkv = attention_back(qkv0, do, H_ENC)
    low, *sums = leave_encoder(dqkv, x0, dh, enc)
    grads_enc.update(zip(("qv_bias", "g1", "b1", "first_bias"), sums))
    grads_enc.update(fc2=(z0, two), fc1=(c0, du), proj=(o0, one), qkv=(a0, dqkv), first=(xin, low))
    return grads_enc, grads_dec, jnp.sum(loss_terms)


def local(pixels, keep_index, clear_mask, slot_tile, master, moment_one, moment_two):
    n_dp = lax.axis_size("dp")
    n_dev = 2 * n_dp
    section, place = lax.axis_index("section"), lax.axis_index("dp")
    me = section * n_dp + place
    slots = master.shape[1]
    turns = [-(-count // n_dev) for count in USED]
    per = sum(turns)
    starts = [0, turns[0] * n_dev]
    rows_each = PARTS_ROWS if n_dp == 16 else 8 * (-(-per // 8))

    pix = lax.dynamic_index_in_dim(pixels, section, 0, keepdims=False)[0]
    keep = lax.dynamic_index_in_dim(keep_index, section, 0, keepdims=False)[0]
    clear = lax.dynamic_index_in_dim(clear_mask, section, 0, keepdims=False)[0]
    kept = jnp.any(keep[:, None] == jnp.arange(SEQ), axis=0).astype(jnp.float32)
    valid = clear.astype(jnp.float32) * (1.0 - kept)
    wide_pix = pix.astype(jnp.float32)
    sums = jnp.concatenate(
        [
            jnp.sum(jnp.sum(wide_pix, 0).reshape(BANDS, PATCH_PIX), 1),
            jnp.sum(jnp.sum(wide_pix * wide_pix, 0).reshape(BANDS, PATCH_PIX), 1),
            jnp.sum(valid)[None],
        ]
    )
    sums = jnp.pad(sums, (0, 1024 - sums.shape[0])).reshape(8, 128)

    def order(table, start):
        used = (table < TILES).astype(jnp.int32)
        count = table.shape[0]
        before = (jnp.arange(count)[:, None] > jnp.arange(count)[None]).astype(jnp.int32)
        return used, jnp.sum(before * used[None], 1) + start

    table_own = slot_tile[0]
    used_own, order_own = order(table_own, starts[1] * section)
    used_mine = lax.dynamic_slice_in_dim(used_own, place * slots, slots)
    order_mine = lax.dynamic_slice_in_dim(order_own, place * slots, slots)
    goes = lax.rem(order_mine, n_dev)
    slot_for = jnp.sum(
        jnp.arange(slots)[None] * used_mine[None] * (goes[None] == jnp.arange(n_dev)[:, None]), 1
    ).astype(jnp.int32)
    dealt = pick_tiles(master[0], slot_for, jnp.bfloat16, "deal_weights")
    table_out = jnp.pad(table_own, (0, 1024 - table_own.shape[0])).reshape(8, 128)
    arrived, all_sums, all_tables = exchange("deal", 1, n_dp, [dealt], [sums, table_out])

    totals = jnp.sum(all_sums, 0).reshape(-1)
    pixel_count = n_dev * SEQ * PATCH_PIX
    band_mean = totals[:BANDS] / pixel_count
    band_scale = lax.rsqrt(totals[BANDS : 2 * BANDS] / pixel_count - band_mean * band_mean + EPS_BAND)
    valid_count = jnp.maximum(totals[2 * BANDS], 1.0)

    chosen = (keep[:, None] == jnp.arange(SEQ)).astype(BF16)
    mean_line = jnp.broadcast_to(band_mean[:, None], (BANDS, PATCH_PIX)).reshape(PATCH_DIM)
    scale_line = jnp.broadcast_to(band_scale[:, None], (BANDS, PATCH_PIX)).reshape(PATCH_DIM)
    xin = ((project(chosen, pix) - mean_line) * scale_line).astype(BF16)

    n_slots = table_own.shape[0]
    tables = jnp.stack([all_tables[s * n_dp].reshape(-1)[:n_slots] for s in range(2)])
    both = [order(tables[s], starts[s]) for s in range(2)]
    used_all = jnp.concatenate([b[0] for b in both])
    order_all = jnp.concatenate([b[1] for b in both])
    owner_all = jnp.arange(2 * n_slots) // slots
    held = jnp.arange(per) * n_dev + me
    match = used_all[None] * (order_all[None] == held[:, None])
    from_owner = jnp.sum(match * owner_all[None], 1).astype(jnp.int32)
    is_held = jnp.sum(match, 1)
    block = pick_tiles(arrived, from_owner, jnp.bfloat16, "hold_weights")
    where_tile = []
    line_tile = []
    source_tile = []
    for s in range(2):
        hit = tables[s][None] == jnp.arange(TILES)[:, None]
        rank = jnp.sum(hit * both[s][1][None], 1)
        device, turn = lax.rem(rank, n_dev), lax.div(rank, n_dev)
        where_tile.append((device * per + turn).astype(jnp.int32))
        source_tile.append((device * turns[s] + turn - (turns[0] if s else 0)).astype(jnp.int32))
        line_tile.append((device * rows_each + line_of(turn, n_dp)).astype(jnp.int32))

    positions_kept = jnp.dot(chosen.astype(F32), jnp.asarray(positions(D_ENC)), precision=lax.Precision.HIGHEST)
    early, late = block[: turns[0]], block[turns[0] :]
    if n_dp == 16:
        late_all, enc, encoded = gather_and_encode(early, late, source_tile[0], xin, positions_kept, 2)
    else:
        early_all, late_all = [lax.all_gather(lax.all_gather(part, "dp"), "section") for part in (early, late)]
        enc = unpack_section(early_all.reshape(-1, TR, TC), source_tile[0], 0)
        encoded = encode(enc, xin, positions_kept)
    dec = unpack_section(late_all.reshape(-1, TR, TC), source_tile[1], 1)

    grads_enc, grads_dec, loss = item_step(
        enc, dec, encoded, pix, kept[:, None], valid[:, None], xin, chosen, (1.0 / valid_count)[None]
    )

    codes = None
    scales = jnp.zeros((n_dev * rows_each, TC), jnp.float32)
    for s, grads in ((1, grads_dec), (0, grads_enc)):
        matrices, vectors = layout(s)
        base = 0
        for name, rows, columns in matrices:
            codes, scales = weight_codes(
                *grads[name], where_tile[s], line_tile[s], base, codes, scales, n_dev * per, f"{name}_{s}"
            )
            base += rows * columns // (TR * TC)
        line = join_vectors([grads[name] for name, length in vectors], str(s))
        codes, scales = weight_codes(
            line, None, where_tile[s], line_tile[s], base, codes, scales, n_dev * per, f"vectors_{s}"
        )

    if n_dp == 16:
        own_codes, own_scales = reduce_all(
            codes.reshape(2, n_dp, per, TR, TC), scales.reshape(2, n_dp, rows_each, TC), 3
        )
    else:
        wide = scales.reshape(n_dev, rows_each, TC)[:, :per]
        values = jnp.where(wide[:, :, None] > 0.0, codes.reshape(n_dev, per, TR, TC).astype(jnp.float32), 0.0)
        values = values * wide[:, :, None]
        values = lax.psum_scatter(values, ("section", "dp"), scatter_dimension=0, tiled=True)[0]
        top = jnp.max(jnp.abs(values), 1, keepdims=True)
        up = jnp.where(top > 0.0, 32766.0 / top, 0.0)
        own_codes = jnp.round(values * up).astype(jnp.int16)
        own_scales = jnp.pad(top[:, 0] * (1.0 / 32766.0), ((0, rows_each - per), (0, 0)))
    own_scale = own_scales[np.array([line_of(t, n_dp) for t in range(per)])]
    own = jnp.where(is_held[:, None, None] > 0, own_codes.astype(jnp.float32) * own_scale[:, None], 0.0)
    tail = jnp.stack([jnp.sum(own * own), loss])
    tail = jnp.pad(tail, (0, 1022)).reshape(8, 128)

    turn_for = jnp.sum(
        jnp.arange(per)[None] * is_held[None] * (from_owner[None] == jnp.arange(n_dev)[:, None]), 1
    ).astype(jnp.int32)
    codes_back = pick_tiles(own_codes, turn_for, jnp.int16, "deal_gradients")
    scales_back = own_scale[turn_for][:, None]
    codes_mine, scales_mine, tails = exchange("return", 4, n_dp, [codes_back, scales_back], [tail])
    totals = jnp.sum(tails, 0)[0]
    grad_norm = jnp.sqrt(totals[0])
    factor = jnp.minimum(1.0, CLIP_NORM / (grad_norm + 1e-06))
    master_new, first_new, second_new = adam(
        codes_mine, scales_mine, goes, used_mine, factor[None], master[0], moment_one[0], moment_two[0]
    )
    return master_new[None], first_new[None], second_new[None], totals[1][None], grad_norm[None]


def solution(mesh):
    return jax.shard_map(
        local,
        mesh=mesh,
        in_specs=(
            P(None, "dp", None, None),
            P(None, "dp", None),
            P(None, "dp", None),
            P("section", None),
            P("section", "dp", None, None),
            P("section", "dp", None, None),
            P("section", "dp", None, None),
        ),
        out_specs=(
            P("section", "dp", None, None),
            P("section", "dp", None, None),
            P("section", "dp", None, None),
            P(),
            P(),
        ),
        check_vma=False,
    )
```

```python
import functools
import math

import jax
import jax.numpy as jnp
import numpy as np
from jax import lax
from jax.experimental import pallas as pl
from jax.experimental.pallas import tpu as pltpu
from jax.sharding import PartitionSpec as P

D_ENC = 768
H_ENC = 12
FF_ENC = 3072
D_DEC = 512
H_DEC = 16
FF_DEC = 2048
BANDS = 6
PATCH_PIX = 256
PATCH_DIM = 1536
SEQ = 588
KEEP = 147
STEP = 5
TILES = 256
USED = (253, 133)

EPS_NORM = 1e-06
EPS_BAND = 1e-05
CLIP_NORM = 0.001
RATE = 0.02
DECAY = 0.05
BETA_ONE = 0.5
BETA_TWO = 0.75
ADAM_EPS = 1e-08

MESH = pl.DeviceIdType.MESH
TR, TC = 128, 256
PARTS = ((0, 6), (6, 11), (11, 13))
PARTS_ROWS = 24


def neighbours(section, place):
    x, y, z = lax.rem(place, 2), lax.rem(lax.div(place, 2), 2), lax.div(place, 4)

    def at(dz, dv, du):
        dx = (1 - section) * du + section * dv
        dy = (1 - section) * dv + section * du
        return lax.rem(z + dz, 4) * 4 + lax.rem(y + dy, 2) * 2 + lax.rem(x + dx, 2)

    return at


def exchange(name, cid, n_dp, dealt, shared):
    n_dev = 2 * n_dp
    n_a, n_s = len(dealt), len(shared)
    n_all = n_a + n_s

    def kernel(*refs):
        sources, targets = refs[:n_all], refs[n_all : 2 * n_all]
        send_sem, recv_sem, own_sem = refs[2 * n_all :]
        section, place = lax.axis_index("section"), lax.axis_index("dp")
        me = section * n_dp + place

        def who(step):
            other = lax.rem(me + step, n_dev)
            return other, (lax.div(other, n_dp), lax.rem(other, n_dp))

        barrier = pltpu.get_barrier_semaphore()

        def greet(step, carry):
            pl.semaphore_signal(barrier, inc=1, device_id=who(step)[1], device_id_type=MESH)
            return carry

        lax.fori_loop(1, n_dev, greet, 0)
        own = []
        for which in range(n_all):
            source = sources[which].at[me] if which < n_a else sources[which]
            copy = pltpu.make_async_copy(source, targets[which].at[me], own_sem.at[which])
            copy.start()
            own.append(copy)
        pl.semaphore_wait(barrier, n_dev - 1)

        def made(which, step):
            other, place_of = who(step)
            source = sources[which].at[other] if which < n_a else sources[which]
            return pltpu.make_async_remote_copy(
                src_ref=source,
                dst_ref=targets[which].at[me],
                send_sem=send_sem.at[which, step],
                recv_sem=recv_sem.at[which, step],
                device_id=place_of,
                device_id_type=MESH,
            )

        def begin(step, carry):
            for which in reversed(range(n_all)):
                made(which, step).start()
            return carry

        def end(step, carry):
            for which in range(n_all):
                made(which, step).wait()
            return carry

        lax.fori_loop(1, n_dev, begin, 0)
        for copy in own:
            copy.wait()
        lax.fori_loop(1, n_dev, end, 0)

    arrays = list(dealt) + list(shared)
    shapes = [jax.ShapeDtypeStruct(a.shape, a.dtype) for a in dealt] + [
        jax.ShapeDtypeStruct((n_dev,) + a.shape, a.dtype) for a in shared
    ]
    any_spec = pl.BlockSpec(memory_space=pltpu.HBM)
    return pl.pallas_call(
        kernel,
        out_shape=shapes,
        in_specs=[any_spec] * n_all,
        out_specs=[any_spec] * n_all,
        scratch_shapes=[
            pltpu.SemaphoreType.DMA((n_all, n_dev)),
            pltpu.SemaphoreType.DMA((n_all, n_dev)),
            pltpu.SemaphoreType.DMA((n_all,)),
        ],
        compiler_params=pltpu.CompilerParams(collective_id=cid, has_side_effects=True),
        name=name,
    )(*arrays)


def line_of(turn, n_dp):
    if n_dp != 16:
        return turn
    return turn + 2 * (turn >= PARTS[0][1]) + 3 * (turn >= PARTS[1][1])


def code(values):
    top = jnp.max(jnp.abs(values), axis=0, keepdims=True)
    up = jnp.where(top > 0.0, 32766.0 / top, 0.0)
    scaled = values * up
    return (scaled + jnp.where(scaled >= 0.0, 0.5, -0.5)).astype(jnp.int32).astype(jnp.int16), top * (1.0 / 32766.0)


def reduce_all(codes, scales, cid, SUMS=True):
    per = codes.shape[2]

    def kernel(codes_ref, scales_ref, out_ref, outs_ref, acc, accs, rc, rcs, r_code, r_scale,
               own_sem, owns_sem, c_send, c_recv, p_send, p_recv):
        section, place = lax.axis_index("section"), lax.axis_index("dp")
        at, at_other = neighbours(section, place), neighbours(1 - section, place)
        sibling = (1 - section, place)
        to_u, to_v = (section, at(0, 0, 1)), (section, at(0, 1, 0))

        def to_z(dz):
            return (section, at(dz, 0, 0))

        barrier = pltpu.get_barrier_semaphore()
        peers = [sibling, to_u, to_v, to_z(1), to_z(2), to_z(3)]
        for peer in peers:
            pl.semaphore_signal(barrier, inc=1, device_id=peer, device_id_type=MESH)
        order = [(dz, dv, du) for dz in (2, 1, 3, 0) for dv in (1, 0) for du in (1, 0)]
        loads = {}
        for n, d in enumerate(order):
            b = at(*d)
            loads[d] = (
                pltpu.make_async_copy(codes_ref.at[section, b], acc.at[b], own_sem.at[n]),
                pltpu.make_async_copy(scales_ref.at[section, b], accs.at[b], owns_sem.at[n]),
            )
            for copy in loads[d]:
                copy.start()
        pl.semaphore_wait(barrier, len(peers))
        crossing = {}
        for n, d in enumerate(order):
            b = at_other(*d)
            pair = []
            for k, (source, target) in enumerate(((codes_ref, rc), (scales_ref, rcs))):
                copy = pltpu.make_async_remote_copy(
                    src_ref=source.at[1 - section, b],
                    dst_ref=target.at[b],
                    send_sem=c_send.at[k, n],
                    recv_sem=c_recv.at[k, n],
                    device_id=sibling,
                    device_id_type=MESH,
                )
                copy.start()
                pair.append(copy)
            crossing[d] = pair

        def add(b, part, from_code, from_first, from_scale, from_row):
            first, count = PARTS[part][0], PARTS[part][1] - PARTS[part][0]

            def one(t, carry):
                line = pl.ds(8 * part + t, 1)
                mine = acc[b, first + t].astype(jnp.float32) * accs[b, line, :]
                theirs = from_code[from_first + t].astype(jnp.float32) * from_scale[pl.ds(from_row + t, 1), :]
                value, scale = code(mine + theirs)
                acc[b, first + t] = value
                accs[b, line, :] = scale
                return carry

            if SUMS:
                lax.fori_loop(0, count, one, 0)

        sends = {}
        used = [0, 0]

        def send(part, key, b, peer):
            t0, t1 = PARTS[part]
            slot, index = used
            used[0] += t1 - t0
            used[1] += 1
            pair = []
            for k, (source, target) in enumerate(
                (
                    (acc.at[b, pl.ds(t0, t1 - t0)], r_code.at[pl.ds(slot, t1 - t0)]),
                    (accs.at[b, pl.ds(8 * part, 8)], r_scale.at[index]),
                )
            ):
                copy = pltpu.make_async_remote_copy(
                    src_ref=source,
                    dst_ref=target,
                    send_sem=p_send.at[k, index],
                    recv_sem=p_recv.at[k, index],
                    device_id=peer,
                    device_id_type=MESH,
                )
                copy.start()
                pair.append(copy)
            sends[part, key] = (pair, slot, index)

        def take(part, key, b):
            pair, slot, index = sends[part, key]
            for copy in pair:
                copy.wait_recv()
            add(b, part, r_code, slot, r_scale.at[index], 0)

        seen = set()

        def ready(d):
            if d not in seen:
                seen.add(d)
                for copy in loads[d]:
                    copy.wait()
                for copy in crossing[d]:
                    copy.wait_recv()

        def first(dz, parts=(0, 1, 2)):
            for dv in (1, 0):
                for du in (1, 0):
                    b = at(dz, dv, du)
                    ready((dz, dv, du))
                    for part in parts:
                        add(b, part, rc.at[b], PARTS[part][0], rcs.at[b], 8 * part)
                        if part == 2 and dz:
                            send(2, ("1", dz, dv, du), b, to_z(dz))
                        if part < 2 and du:
                            send(part, ("1", dz, dv), b, to_u)

        def second(dz):
            for dv in (1, 0):
                for part in (0, 1):
                    b = at(dz, dv, 0)
                    take(part, ("1", dz, dv), b)
                    if dv:
                        send(part, ("2", dz), b, to_v)

        def third(dz):
            for part in (0, 1):
                b = at(dz, 0, 0)
                take(part, ("2", dz), b)
                if dz:
                    send(part, ("3", dz), b, to_z(dz))

        first(2)
        first(1)
        first(3, (2,))
        second(2)
        first(3, (0, 1))
        second(1)
        third(2)
        first(0, (2,))
        second(3)
        first(0, (0, 1))
        third(1)
        for du in (1, 0):
            for dv in (1, 0):
                b = at(0, dv, du)
                for dz in (1, 3, 2):
                    take(2, ("1", dz, dv, du), b)
                if du:
                    send(2, ("2", dv), b, to_u)
        third(3)
        second(0)
        for dv in (1, 0):
            b = at(0, dv, 0)
            take(2, ("2", dv), b)
            if dv:
                send(2, ("3",), b, to_v)
        third(0)
        for dz in (2, 1, 3):
            for part in (0, 1):
                take(part, ("3", dz), place)
        take(2, ("3",), place)
        out_ref[...] = acc[place]
        outs_ref[...] = accs[place]
        for pair in crossing.values():
            for copy in pair:
                copy.wait_send()
        for pair, slot, index in sends.values():
            for copy in pair:
                copy.wait_send()

    n_tiles = 15 * per
    n_copies = 45
    hbm = pl.BlockSpec(memory_space=pltpu.HBM)
    vmem = pl.BlockSpec(memory_space=pltpu.VMEM)
    return pl.pallas_call(
        kernel,
        out_shape=(
            jax.ShapeDtypeStruct((per, TR, TC), jnp.int16),
            jax.ShapeDtypeStruct((PARTS_ROWS, TC), jnp.float32),
        ),
        in_specs=[hbm, hbm],
        out_specs=(vmem, vmem),
        scratch_shapes=[
            pltpu.VMEM((16, per, TR, TC), jnp.int16),
            pltpu.VMEM((16, PARTS_ROWS, TC), jnp.float32),
            pltpu.VMEM((16, per, TR, TC), jnp.int16),
            pltpu.VMEM((16, PARTS_ROWS, TC), jnp.float32),
            pltpu.VMEM((n_tiles, TR, TC), jnp.int16),
            pltpu.VMEM((n_copies, 8, TC), jnp.float32),
            pltpu.SemaphoreType.DMA((16,)),
            pltpu.SemaphoreType.DMA((16,)),
            pltpu.SemaphoreType.DMA((2, 16)),
            pltpu.SemaphoreType.DMA((2, 16)),
            pltpu.SemaphoreType.DMA((2, n_copies)),
            pltpu.SemaphoreType.DMA((2, n_copies)),
        ],
        compiler_params=pltpu.CompilerParams(
            collective_id=cid, has_side_effects=True, vmem_limit_bytes=60 * 2**20
        ),
        name="reduce_tiles",
    )(codes, scales)


def layout(section_id):
    if section_id == 0:
        width, hidden = D_ENC, FF_ENC
        matrices = [("first", PATCH_DIM, D_ENC)]
        vectors = [("first_bias", D_ENC)]
    else:
        width, hidden = D_DEC, FF_DEC
        matrices = [("first", D_ENC, D_DEC)]
        vectors = [("first_bias", D_DEC), ("mask", D_DEC)]
    matrices = matrices + [
        ("qkv", width, 3 * width),
        ("proj", width, width),
        ("fc1", width, hidden),
        ("fc2", hidden, width),
    ]
    vectors = vectors + [
        ("g1", width),
        ("b1", width),
        ("qv_bias", 2 * width),
        ("proj_bias", width),
        ("g2", width),
        ("b2", width),
        ("fc1_bias", hidden),
        ("fc2_bias", width),
        ("gf", width),
        ("bf", width),
    ]
    if section_id == 1:
        matrices = matrices + [("head", D_DEC, PATCH_DIM)]
        vectors = vectors + [("head_bias", PATCH_DIM)]
    return matrices, vectors


def positions(width):
    place = np.arange(SEQ, dtype=np.float32)[:, None]
    rate = np.exp(np.arange(width // 2, dtype=np.float32) * np.float32(-2.0 * math.log(10000.0) / width))
    angle = (place * rate).astype(np.float32)
    return np.concatenate([np.sin(angle), np.cos(angle)], axis=1).astype(np.float32)


LANES = 128
LOG2E = math.log2(math.e)


def pick_tiles(tiles, index, dtype, name):
    count = index.shape[0]

    def kernel(index_ref, tiles_ref, out_ref):
        def one(t, carry):
            out_ref[t] = tiles_ref[index_ref[t]].astype(dtype)
            return carry

        lax.fori_loop(0, count, one, 0)

    return pl.pallas_call(
        kernel,
        out_shape=jax.ShapeDtypeStruct((count, TR, TC), dtype),
        in_specs=[pl.BlockSpec(memory_space=pltpu.SMEM), pl.BlockSpec(memory_space=pltpu.VMEM)],
        out_specs=pl.BlockSpec(memory_space=pltpu.VMEM),
        compiler_params=pltpu.CompilerParams(vmem_limit_bytes=40 * 2**20),
        name=name,
    )(index, tiles)


def groups_of(rows, wide):
    groups = rows // TR
    return max(m for m in range(1, groups + 1) if groups % m == 0 and (m == 1 or m * wide <= 12))


def unpack_matrix(tiles, place, base, rows, columns, name):
    wide = columns // TC
    many = groups_of(rows, wide)
    count = many * wide

    def kernel(place_ref, *refs):
        sources, out_ref, lines = refs[:count], refs[count], refs[count + 1 :]
        for j in range(count):
            for h in range(2):
                lines[h][j * TR : (j + 1) * TR, :] = sources[j][0, :, h * LANES : (h + 1) * LANES].astype(jnp.float32)
        for j in range(wide):
            for h in range(2):
                start = j * TC + h * LANES
                out_ref[:, start : start + LANES] = lines[h][pl.ds(j, many * TR, stride=wide), :].astype(tiles.dtype)

    def spec(j):
        return pl.BlockSpec((1, TR, TC), lambda g, place_ref: (place_ref[base + g * count + j], 0, 0))

    return pl.pallas_call(
        kernel,
        out_shape=jax.ShapeDtypeStruct((rows, columns), tiles.dtype),
        grid_spec=pltpu.PrefetchScalarGridSpec(
            num_scalar_prefetch=1,
            grid=(rows // (many * TR),),
            in_specs=[spec(j) for j in range(count)],
            out_specs=pl.BlockSpec((many * TR, columns), lambda g, place_ref: (g, 0)),
            scratch_shapes=[pltpu.VMEM((count * TR, LANES), jnp.float32)] * 2,
        ),
        compiler_params=pltpu.CompilerParams(vmem_limit_bytes=32 * 2**20),
        name="unpack_" + name,
    )(place, *([tiles] * count))


def unpack_vectors(tiles, place, base, lengths, name):
    def kernel(place_ref, tile_ref, *refs):
        row = 0
        for out_ref, length in zip(refs, lengths):
            for r in range(length // TC):
                out_ref[:, r * TC : (r + 1) * TC] = tile_ref[0, row : row + 1, :].astype(jnp.float32)
                row += 1

    return pl.pallas_call(
        kernel,
        out_shape=[jax.ShapeDtypeStruct((1, length), jnp.float32) for length in lengths],
        grid_spec=pltpu.PrefetchScalarGridSpec(
            num_scalar_prefetch=1,
            grid=(1,),
            in_specs=[pl.BlockSpec((1, TR, TC), lambda g, place_ref: (place_ref[base], 0, 0))],
            out_specs=[pl.BlockSpec((1, length), lambda g, place_ref: (0, 0)) for length in lengths],
        ),
        name="unpack_vectors_" + name,
    )(place, tiles)


def join_vectors(vectors, name):
    def kernel(*refs):
        out_ref = refs[-1]
        row = 0
        for source in refs[:-1]:
            for r in range(source.shape[1] // TC):
                out_ref[row : row + 1, :] = source[:, r * TC : (r + 1) * TC]
                row += 1
        out_ref[row:, :] = jnp.zeros((TR - row, TC), jnp.float32)

    return pl.pallas_call(
        kernel,
        out_shape=jax.ShapeDtypeStruct((TR, TC), jnp.float32),
        name="join_vectors_" + name,
    )(*vectors)


def unpack_section(tiles, place, section_id):
    matrices, vectors = layout(section_id)
    found, base = {}, 0
    for name, rows, columns in matrices:
        found[name] = unpack_matrix(tiles, place, base, rows, columns, f"{name}_{section_id}")
        base += rows * columns // (TR * TC)
    lines = unpack_vectors(tiles, place, base, [length for name, length in vectors], str(section_id))
    found.update({name: line for (name, length), line in zip(vectors, lines)})
    return found


def weight_codes(a, d, place, line, base, codes, scales, total, name):
    length = a.shape[0]
    rows, columns = a.shape if d is None else (a.shape[1], d.shape[1])
    wide = columns // TC
    many = groups_of(rows, wide)
    count = many * wide
    steps = rows // (many * TR)
    fresh = codes is None
    n_in = 1 if d is None else 2

    def kernel(place_ref, line_ref, *refs):
        scales_in = refs[n_in]
        codes_ref, scales_ref, left, right, ready, sem = refs[-6:]
        step = pl.program_id(0)
        slot = lax.rem(step, 2)

        @pl.when(step == 0)
        def _():
            scales_ref[...] = scales_in[...]

        def copies(at_step, at_slot):
            return [
                pltpu.make_async_copy(
                    ready.at[at_slot, j], codes_ref.at[place_ref[base + at_step * count + j]], sem.at[at_slot, j]
                )
                for j in range(count)
            ]

        @pl.when(step >= 2)
        def _():
            for copy in copies(step - 2, slot):
                copy.wait()

        for j in range(wide):
            columns_j = slice(j * TC, (j + 1) * TC)
            if d is None:
                part = refs[0][:, columns_j]
            else:
                part = weight_grad(refs[0][...], refs[1][:, columns_j])
            for h, lines in enumerate((left, right)):
                lines[pl.ds(j, many * TR, stride=wide), :] = part[:, h * LANES : (h + 1) * LANES]
        for j in range(count):
            at = line_ref[base + step * count + j]
            pair = []
            for h, lines in enumerate((left, right)):
                value, scale = code(lines[j * TR : (j + 1) * TR, :])
                ready[slot, j, :, h * LANES : (h + 1) * LANES] = value
                pair.append(scale)
            scales_ref[pl.ds(at, 1), :] = jnp.concatenate(pair, axis=1)
        for copy in copies(step, slot):
            copy.start()

        @pl.when(step == steps - 1)
        def _():
            if steps > 1:
                for copy in copies(step - 1, 1 - slot):
                    copy.wait()
            for copy in copies(step, slot):
                copy.wait()

    whole = pl.BlockSpec(scales.shape, lambda g, a, b: (0, 0))
    hbm = pl.BlockSpec(memory_space=pltpu.HBM)
    if d is None:
        operands, specs = [a], [pl.BlockSpec((many * TR, columns), lambda g, a, b: (g, 0))]
    else:
        operands = [a, d]
        specs = [
            pl.BlockSpec((length, many * TR), lambda g, a, b: (0, g)),
            pl.BlockSpec((length, columns), lambda g, a, b: (0, 0)),
        ]
    aliases = {2 + n_in: 1}
    if not fresh:
        aliases[3 + n_in] = 0
    return pl.pallas_call(
        kernel,
        out_shape=(
            jax.ShapeDtypeStruct((total, TR, TC), jnp.int16),
            jax.ShapeDtypeStruct(scales.shape, jnp.float32),
        ),
        grid_spec=pltpu.PrefetchScalarGridSpec(
            num_scalar_prefetch=2,
            grid=(steps,),
            in_specs=specs + [whole] + ([] if fresh else [hbm]),
            out_specs=(hbm, whole),
            scratch_shapes=[
                pltpu.VMEM((count * TR, LANES), jnp.float32),
                pltpu.VMEM((count * TR, LANES), jnp.float32),
                pltpu.VMEM((2, count, TR, TC), jnp.int16),
                pltpu.SemaphoreType.DMA((2, count)),
            ],
        ),
        input_output_aliases=aliases,
        compiler_params=pltpu.CompilerParams(vmem_limit_bytes=40 * 2**20),
        name="weight_codes_" + name,
    )(place, line, *operands, scales, *([] if fresh else [codes]))


def adam(codes, scales, index, used, factor, master, first, second):
    slots = master.shape[0]
    per = 3 if slots % 3 == 0 else 1

    def kernel(index_ref, used_ref, factor_ref, codes_ref, scales_ref, w_ref, m_ref, v_ref, w_out, m_out, v_out):
        for t in range(per):
            slot = pl.program_id(0) * per + t
            source = index_ref[slot]
            grad = codes_ref[source].astype(jnp.float32) * scales_ref[source]
            grad = jnp.where(used_ref[slot] > 0, grad * factor_ref[0], 0.0)
            first_new = BETA_ONE * m_ref[t] + (1.0 - BETA_ONE) * grad
            second_new = BETA_TWO * v_ref[t] + (1.0 - BETA_TWO) * grad * grad
            ratio = (
                first_new
                / (1.0 - BETA_ONE ** float(STEP))
                / (jnp.sqrt(second_new / (1.0 - BETA_TWO ** float(STEP))) + ADAM_EPS)
            )
            w_out[t] = w_ref[t] - RATE * (ratio + DECAY * w_ref[t])
            m_out[t] = first_new
            v_out[t] = second_new

    smem = pl.BlockSpec(memory_space=pltpu.SMEM)
    block = pl.BlockSpec((per, TR, TC), lambda g: (g, 0, 0))
    return pl.pallas_call(
        kernel,
        out_shape=[jax.ShapeDtypeStruct(master.shape, jnp.float32)] * 3,
        grid=(slots // per,),
        in_specs=[
            smem,
            smem,
            smem,
            pl.BlockSpec(codes.shape, lambda g: (0, 0, 0)),
            pl.BlockSpec(scales.shape, lambda g: (0, 0, 0)),
            block,
            block,
            block,
        ],
        out_specs=[block] * 3,
        compiler_params=pltpu.CompilerParams(vmem_limit_bytes=40 * 2**20),
        name="adam",
    )(index, used, factor, codes, scales, master, first, second)


def project(a, w):
    return jnp.dot(a, w, preferred_element_type=jnp.float32)


def project_back(d, w):
    return lax.dot_general(d, w, (((1,), (1,)), ((), ())), preferred_element_type=jnp.float32)


def weight_grad(a, d):
    return lax.dot_general(a, d, (((0,), (0,)), ((), ())), preferred_element_type=jnp.float32)


def layer_norm(values, gain, offset):
    centre = values - jnp.mean(values, -1, keepdims=True)
    return centre * lax.rsqrt(jnp.mean(centre * centre, -1, keepdims=True) + EPS_NORM) * gain + offset


def norm_back(upstream, values, gain):
    centre = values - jnp.mean(values, -1, keepdims=True)
    spread = lax.rsqrt(jnp.mean(centre * centre, -1, keepdims=True) + EPS_NORM)
    normed = centre * spread
    scaled = upstream * gain
    downstream = spread * (
        scaled - jnp.mean(scaled, -1, keepdims=True) - normed * jnp.mean(scaled * normed, -1, keepdims=True)
    )
    return downstream, line_sum(upstream * normed), line_sum(upstream)


def line_sum(values):
    return jnp.sum(values.astype(jnp.float32), 0, keepdims=True)


ERF_TOP = (
    -2.72614225801306e-10,
    2.77068142495902e-08,
    -2.10102402082508e-06,
    -5.69250639462346e-05,
    -7.34990630326855e-04,
    -2.95459980854025e-03,
    -1.60960333262415e-02,
)
ERF_BOTTOM = (
    -1.45660718464996e-05,
    -2.13374055278905e-04,
    -1.68282697438203e-03,
    -7.37332916720468e-03,
    -1.42647390514189e-02,
)


def erf(x):
    x = jnp.clip(x, -4.0, 4.0)
    square = x * x
    top, bottom = jnp.full_like(x, ERF_TOP[0]), jnp.full_like(x, ERF_BOTTOM[0])
    for coefficient in ERF_TOP[1:]:
        top = top * square + coefficient
    for coefficient in ERF_BOTTOM[1:]:
        bottom = bottom * square + coefficient
    return x * top / bottom


def whole_kernel(kernel, shapes, operands, name, scratch=(), smem=0):
    vmem = pl.BlockSpec(memory_space=pltpu.VMEM)
    return pl.pallas_call(
        kernel,
        out_shape=[jax.ShapeDtypeStruct(shape, dtype) for shape, dtype in shapes],
        in_specs=[pl.BlockSpec(memory_space=pltpu.SMEM)] * smem + [vmem] * (len(operands) - smem),
        out_specs=[vmem] * len(shapes),
        scratch_shapes=scratch,
        compiler_params=pltpu.CompilerParams(vmem_limit_bytes=56 * 2**20),
        name=name,
    )(*operands)


F32, BF16 = jnp.float32, jnp.bfloat16


def start_block(x_ref, rows, w, a_ref, qkv_ref):
    g1, b1, weight, bias = w
    width = x_ref.shape[1]
    a = layer_norm(x_ref[rows, :], g1[...], b1[...]).astype(BF16)
    a_ref[rows, :] = a
    for part in range(3):
        columns = slice(part * width, (part + 1) * width)
        value = project(a, weight[:, columns])
        if part != 1:
            value = value + bias[:, (part // 2) * width : (part // 2 + 1) * width]
        qkv_ref[rows, columns] = value.astype(BF16)


def enter_encoder(xin, place, w):
    def kernel(xin_ref, place_ref, first, bias, g1, b1, weight, qv_bias, x_ref, a_ref, qkv_ref):
        x_ref[...] = project(xin_ref[...], first[...]) + bias[...] + place_ref[...]
        start_block(x_ref, slice(None), (g1, b1, weight, qv_bias), a_ref, qkv_ref)

    shapes = [((KEEP, D_ENC), F32), ((KEEP, D_ENC), BF16), ((KEEP, 3 * D_ENC), BF16)]
    operands = [xin, place] + [w[k] for k in ("first", "first_bias", "g1", "b1", "qkv", "qv_bias")]
    return whole_kernel(kernel, shapes, operands, "enter_encoder")


def enter_decoder_body(chosen_ref, sent_ref, kept_ref, place_ref, first, bias, mask, g1, b1, weight, qv_bias,
                       x_ref, a_ref, qkv_ref):
    for lo, hi in row_cuts(SEQ, 304):
        rows = slice(lo, hi)
        spread = project(chosen_ref[rows, :], sent_ref[...]).astype(BF16)
        placed = project(spread, first[...]) + bias[...]
        x_ref[rows, :] = jnp.where(kept_ref[rows, :] > 0.0, placed, mask[...]) + place_ref[rows, :]
        start_block(x_ref, rows, (g1, b1, weight, qv_bias), a_ref, qkv_ref)


def finish_block(x, attended, w, name):
    length, width = x.shape
    hidden = w["fc1"].shape[1]

    line = (length, width)
    shapes = [(line, F32), (line, BF16), ((length, hidden), BF16), ((length, hidden), F32), (line, F32), (line, BF16)]
    names = ("proj", "proj_bias", "g2", "b2", "fc1", "fc1_bias", "fc2", "fc2_bias", "gf", "bf")
    return whole_kernel(finish_body, shapes, [x, attended] + [w[k] for k in names], "finish_" + name)


def finish_body(x_ref, o_ref, proj, proj_bias, g2, b2, fc1, fc1_bias, fc2, fc2_bias, gf, bf,
                h_ref, c_ref, z_ref, slope_ref, y_ref, out_ref, pump=None):
    length, hidden = z_ref.shape
    for lo, hi in row_cuts(length, 304):
        rows = slice(lo, hi)
        h = x_ref[rows, :] + project(o_ref[rows, :], proj[...]) + proj_bias[...]
        h_ref[rows, :] = h
        c_ref[rows, :] = layer_norm(h, g2[...], b2[...]).astype(BF16)
    for lo in range(0, hidden, 256):
        columns = slice(lo, lo + 256)
        u = project(c_ref[...], fc1[:, columns]) + fc1_bias[:, columns]
        below = 0.5 * (1.0 + erf(u * (1.0 / math.sqrt(2.0))))
        z = (u * below).astype(BF16)
        z_ref[:, columns] = z
        slope_ref[:, columns] = below + u * jnp.exp(-0.5 * u * u) * (1.0 / math.sqrt(2.0 * math.pi))
        y = project(z, fc2[columns, :])
        if lo:
            y_ref[...] += y
        else:
            y_ref[...] = y
        if pump is not None and lo % 512 == 256:
            pump(1)
    for lo, hi in row_cuts(length, 304):
        rows = slice(lo, hi)
        y = h_ref[rows, :] + y_ref[rows, :] + fc2_bias[...]
        y_ref[rows, :] = y
        out_ref[rows, :] = layer_norm(y, gf[...], bf[...]).astype(BF16)


def back_finish_body(d_ref, y_ref, slope_ref, h_ref, gf, fc2, fc1, g2, proj,
                     two_ref, du_ref, dh_ref, one_ref, do_ref, s_gf, s_bf, s_fc2, s_fc1, s_g2, s_b2, s_proj, dc_ref,
                     pump=None):
    length, hidden = slope_ref.shape
    for n, (lo, hi) in enumerate(row_cuts(length, 304)):
        rows = slice(lo, hi)
        dy, gain, shift = norm_back(d_ref[rows, :].astype(F32), y_ref[rows, :], gf[...])
        dh_ref[rows, :] = dy
        two = dy.astype(BF16)
        two_ref[rows, :] = two
        collect(n, (s_gf, gain), (s_bf, shift), (s_fc2, line_sum(two)))
    for lo in range(0, hidden, 256):
        columns = slice(lo, lo + 256)
        du = (project_back(two_ref[...], fc2[columns, :]) * slope_ref[:, columns]).astype(BF16)
        du_ref[:, columns] = du
        s_fc1[:, columns] = line_sum(du)
        dc = project_back(du, fc1[:, columns])
        if lo:
            dc_ref[...] += dc
        else:
            dc_ref[...] = dc
        if pump is not None:
            pump(1)
    for n, (lo, hi) in enumerate(row_cuts(length, 304)):
        rows = slice(lo, hi)
        part, gain, shift = norm_back(dc_ref[rows, :], h_ref[rows, :], g2[...])
        dh = dh_ref[rows, :] + part
        dh_ref[rows, :] = dh
        one = dh.astype(BF16)
        one_ref[rows, :] = one
        collect(n, (s_g2, gain), (s_b2, shift), (s_proj, line_sum(one)))
    do_ref[...] = project_back(one_ref[...], proj[...]).astype(BF16)


def back_finish(d_out, y, slope, h, w, name):
    length, width = y.shape
    hidden = slope.shape[1]
    line = (length, width)
    shapes = [(line, BF16), ((length, hidden), BF16), (line, F32), (line, BF16), (line, BF16)]
    shapes += [((1, n), F32) for n in (width, width, width, hidden, width, width, width)]
    operands = [d_out, y, slope, h] + [w[k] for k in ("gf", "fc2", "fc1", "g2", "proj")]
    return whole_kernel(back_finish_body, shapes, operands, "back_finish_" + name, [pltpu.VMEM(line, F32)])


def collect(n, *pairs):
    for ref, value in pairs:
        ref[...] = ref[...] + value if n else value


def leave_encoder(dqkv, x, dh, w):
    def kernel(d_ref, x_ref, dh_ref, g1, weight, low_ref, s_qv, s_g1, s_b1, s_first):
        d = d_ref[...]
        part, gain, shift = norm_back(project_back(d, weight[...]), x_ref[...], g1[...])
        dx = dh_ref[...] + part
        low_ref[...] = dx.astype(BF16)
        s_qv[:, :D_ENC] = line_sum(d[:, :D_ENC])
        s_qv[:, D_ENC:] = line_sum(d[:, 2 * D_ENC :])
        s_g1[...] = gain
        s_b1[...] = shift
        s_first[...] = line_sum(dx)

    shapes = [((KEEP, D_ENC), BF16)] + [((1, n), F32) for n in (2 * D_ENC, D_ENC, D_ENC, D_ENC)]
    return whole_kernel(kernel, shapes, [dqkv, x, dh, w["g1"], w["qkv"]], "leave_encoder")


def leave_decoder_body(d_ref, x_ref, dh_ref, chosen_ref, kept_ref, g1, weight, first,
                       low_ref, sent_ref, s_qv, s_g1, s_b1, s_mask, s_first, da_ref, dx_ref):
    da_ref[...] = project_back(d_ref[...], weight[...])
    for n, (lo, hi) in enumerate(row_cuts(SEQ, 304)):
        rows = slice(lo, hi)
        part, gain, shift = norm_back(da_ref[rows, :], x_ref[rows, :], g1[...])
        dx = dh_ref[rows, :] + part
        dx_ref[rows, :] = dx.astype(BF16)
        kept_rows = kept_ref[rows, :]
        collect(
            n,
            (s_g1, gain),
            (s_b1, shift),
            (s_mask, line_sum(dx * (1.0 - kept_rows))),
            (s_first, line_sum(dx * kept_rows)),
        )
    s_qv[:, :D_DEC] = line_sum(d_ref[:, :D_DEC])
    s_qv[:, D_DEC:] = line_sum(d_ref[:, 2 * D_DEC :])
    low = project(chosen_ref[...], dx_ref[...]).astype(BF16)
    low_ref[...] = low
    sent_ref[...] = project_back(low, first[...]).astype(BF16)


def head_mask(size, h):
    lane = lax.broadcasted_iota(jnp.int32, (1, LANES), 1)
    return (lane >= h * size) & (lane < (h + 1) * size)


def head_mask(size, h):
    lane = lax.broadcasted_iota(jnp.int32, (1, LANES), 1)
    return (lane >= h * size) & (lane < (h + 1) * size)


def row_cuts(length, step):
    return [(lo, min(lo + step, length)) for lo in range(0, length, step)]


def mix_heads(q_ref, k_ref, v_ref, out_ref, size):
    keys, values = k_ref[...].T, v_ref[...]
    for lo, hi in row_cuts(q_ref.shape[0], 304):
        total = jnp.zeros((hi - lo, LANES), F32)
        for h in range(LANES // size):
            mask = head_mask(size, h)
            query = jnp.where(mask, q_ref[lo:hi, :], jnp.zeros((), BF16))
            scores = project(query, keys)
            power = jnp.exp2((scores - jnp.max(scores, -1, keepdims=True)) * (size ** (-0.5) * LOG2E))
            probs = power * (1.0 / jnp.sum(power, -1, keepdims=True))
            mixed = project(probs.astype(BF16), values)
            total = jnp.where(mask, mixed, total)
        out_ref[lo:hi, :] = total.astype(BF16)


def attention(qkv, heads):
    length, width = qkv.shape[0], qkv.shape[1] // 3
    size = width // heads
    groups = width // LANES

    def kernel(q_ref, k_ref, v_ref, out_ref):
        mix_heads(q_ref, k_ref, v_ref, out_ref, size)

    def spec(offset):
        return pl.BlockSpec((length, LANES), lambda g: (0, g + offset))

    return pl.pallas_call(
        kernel,
        out_shape=jax.ShapeDtypeStruct((length, width), jnp.bfloat16),
        grid=(groups,),
        in_specs=[spec(0), spec(groups), spec(2 * groups)],
        out_specs=spec(0),
        compiler_params=pltpu.CompilerParams(vmem_limit_bytes=40 * 2**20),
        name=f"attention_{heads}",
    )(qkv, qkv, qkv)


def back_heads(q_ref, k_ref, v_ref, g_ref, dq_turned, size, pump=None):
    length, factor = q_ref.shape[0], size ** (-0.5)
    zero = jnp.zeros((), jnp.bfloat16)
    keys, values = k_ref[...], v_ref[...]
    keys_turned = keys.T
    cuts = row_cuts(length, 256)
    for n, (lo, hi) in enumerate(cuts):
        query_all, grad_all = q_ref[lo:hi, :], g_ref[lo:hi, :]
        query_turned, grad_turned = query_all.T, grad_all.T
        dk = dv = None
        for h in range(LANES // size):
            own = slice(h * size, (h + 1) * size)
            row = lax.broadcasted_iota(jnp.int32, (LANES, 1), 0)
            rows = (row >= h * size) & (row < (h + 1) * size)
            mask = head_mask(size, h)
            scores = project(keys, jnp.where(rows, query_turned, zero))
            power = jnp.exp2((scores - jnp.max(scores, 0, keepdims=True)) * (factor * LOG2E))
            probs = power * (1.0 / jnp.sum(power, 0, keepdims=True))
            d_probs = project(values, jnp.where(rows, grad_turned, zero))
            inner = jnp.sum(d_probs * probs, 0, keepdims=True)
            d_scores = (probs * (d_probs - inner)).astype(jnp.bfloat16)
            dv_h = project(probs.astype(jnp.bfloat16), jnp.where(mask, grad_all, zero))
            dk_h = project(d_scores, jnp.where(mask, query_all, zero))
            dv = dv_h if dv is None else dv + dv_h
            dk = dk_h if dk is None else dk + dk_h
            dq_turned[own, lo:hi] = project(keys_turned[own, :], d_scores)
        if n:
            dk_sum, dv_sum = dk_sum + dk, dv_sum + dv
        else:
            dk_sum, dv_sum = dk, dv
    return dq_turned[...].T * factor, dk_sum * factor, dv_sum


def attention_back(qkv, grad, heads):
    length, width = grad.shape
    size = width // heads
    groups = width // LANES

    def kernel(q_ref, k_ref, v_ref, g_ref, out_ref, dq_turned):
        for part, value in enumerate(back_heads(q_ref, k_ref, v_ref, g_ref, dq_turned, size)):
            start = pl.multiple_of(part * width + pl.program_id(0) * LANES, LANES)
            out_ref[:, pl.ds(start, LANES)] = value.astype(BF16)

    def spec(offset):
        return pl.BlockSpec((length, LANES), lambda g: (0, g + offset))

    return pl.pallas_call(
        kernel,
        out_shape=jax.ShapeDtypeStruct((length, 3 * width), jnp.bfloat16),
        grid=(groups,),
        in_specs=[spec(0), spec(groups), spec(2 * groups), spec(0)],
        out_specs=pl.BlockSpec((length, 3 * width), lambda g: (0, 0)),
        scratch_shapes=[pltpu.VMEM((LANES, length), jnp.float32)],
        compiler_params=pltpu.CompilerParams(vmem_limit_bytes=40 * 2**20),
        name=f"attention_back_{heads}",
    )(qkv, qkv, qkv, grad)


def head_body(one, final_ref, w_ref, bias_ref, pix_ref, valid_ref, low_ref, sums_ref, loss_ref, back_ref):
    for band in range(BANDS):
        columns = slice(band * PATCH_PIX, (band + 1) * PATCH_PIX)
        predicted = project(final_ref[...], w_ref[:, columns]) + bias_ref[:, columns]
        values = pix_ref[:, columns].astype(F32)
        centre = values - jnp.mean(values, -1, keepdims=True)
        target = centre * lax.rsqrt(jnp.mean(centre * centre, -1, keepdims=True) + EPS_NORM)
        misfit = predicted - target
        valid_misfit = valid_ref[...] * misfit
        collect(band, (loss_ref, line_sum(valid_misfit * misfit) * (one / (BANDS * PATCH_PIX))))
        grad = valid_misfit * (one * (2.0 / (BANDS * PATCH_PIX)))
        low = grad.astype(BF16)
        low_ref[:, columns] = low
        sums_ref[:, columns] = line_sum(grad)
        collect(band, (back_ref, project_back(low, w_ref[:, columns])))


def decoder_step(tiles, place, inverse, chosen, sent, kept, valid, pix):
    matrices, vectors = layout(1)
    base, total = tile_bases(1)
    line = (SEQ, D_DEC)
    hidden = (SEQ, FF_DEC)
    results = {
        "final": (line, BF16), "pred_low": ((SEQ, PATCH_DIM), BF16), "z": (hidden, BF16), "two": (line, BF16),
        "c": (line, BF16), "du": (hidden, BF16), "o": (line, BF16), "one": (line, BF16), "a": (line, BF16),
        "dqkv": ((SEQ, 3 * D_DEC), BF16), "low": ((KEEP, D_DEC), BF16), "vectors": ((TR, TC), F32),
        "loss": ((1, PATCH_PIX), F32), "d_sent": ((KEEP, D_ENC), BF16),
    }
    inner = {
        "x": (line, F32), "qkv": ((SEQ, 3 * D_DEC), BF16), "h": (line, F32), "slope": (hidden, F32), "y": (line, F32),
        "dh": (line, F32), "d": (line, F32), "dx": (line, BF16), "do": (line, BF16), "turned": ((LANES, SEQ), F32),
    }

    def kernel(place_ref, inverse_ref, tiles_ref, chosen_ref, turned_ref, sent_ref, kept_ref, valid_ref, pix_ref, pos_ref,
               *refs):
        refs = list(refs)
        r = {name: refs.pop(0) for name in results}
        t = {name: refs.pop(0) for name in inner}
        w = {name: refs.pop(0) for name, rows, columns in matrices}
        w.update({name: refs.pop(0) for name, length in vectors})
        g = {name: refs.pop(0) for name, length in vectors}
        left, right, pool, sem = refs
        size = D_DEC // H_DEC

        def fetch(t, carry):
            pltpu.make_async_copy(tiles_ref.at[place_ref[t]], pool.at[t], sem).start()
            return carry

        lax.fori_loop(0, USED[1], fetch, 0)
        pltpu.make_async_copy(tiles_ref.at[pl.ds(0, USED[1])], pool, sem).wait()
        cut_vectors(pool[total].astype(F32), [w[name] for name, length in vectors])
        for name, rows, columns in matrices:
            unpack_into(pool, None, base[name], w[name], left, right)
        names = ("first", "first_bias", "mask", "g1", "b1", "qkv", "qv_bias")
        enter_decoder_body(
            turned_ref, sent_ref, kept_ref, pos_ref, *[w[k] for k in names], t["x"], r["a"], t["qkv"]
        )
        spans = [
            [slice(part * D_DEC + n * LANES, part * D_DEC + (n + 1) * LANES) for part in range(3)]
            for n in range(D_DEC // LANES)
        ]
        for group in spans:
            mix_heads(*[t["qkv"].at[:, span] for span in group], r["o"].at[:, group[0]], size)
        names = ("proj", "proj_bias", "g2", "b2", "fc1", "fc1_bias", "fc2", "fc2_bias", "gf", "bf")
        finish_body(
            t["x"], r["o"], *[w[k] for k in names], t["h"], r["c"], r["z"], t["slope"], t["y"], r["final"]
        )
        head_body(
            inverse_ref[0], r["final"], w["head"], w["head_bias"], pix_ref, valid_ref,
            r["pred_low"], g["head_bias"], r["loss"], t["d"],
        )
        names = ("gf", "bf", "fc2_bias", "fc1_bias", "g2", "b2", "proj_bias")
        back_finish_body(
            t["d"], t["y"], t["slope"], t["h"], *[w[k] for k in ("gf", "fc2", "fc1", "g2", "proj")],
            r["two"], r["du"], t["dh"], r["one"], t["do"], *[g[k] for k in names], t["d"],
        )
        for group in spans:
            parts = back_heads(*[t["qkv"].at[:, span] for span in group], t["do"].at[:, group[0]], t["turned"], size)
            for span, value in zip(group, parts):
                r["dqkv"][:, span] = value.astype(BF16)
        leave_decoder_body(
            r["dqkv"], t["x"], t["dh"], chosen_ref, kept_ref, w["g1"], w["qkv"], w["first"], r["low"], r["d_sent"],
            *[g[k] for k in ("qv_bias", "g1", "b1", "mask", "first_bias")], t["d"], t["dx"],
        )
        join_into(r["vectors"], [g[name] for name, length in vectors])

    vmem = pl.BlockSpec(memory_space=pltpu.VMEM)
    smem = pl.BlockSpec(memory_space=pltpu.SMEM)
    outs = pl.pallas_call(
        kernel,
        out_shape=[jax.ShapeDtypeStruct(*result) for result in results.values()],
        in_specs=[smem, smem, pl.BlockSpec(memory_space=pltpu.HBM)] + [vmem] * 7,
        out_specs=[vmem] * len(results),
        scratch_shapes=[pltpu.VMEM(*value) for value in inner.values()]
        + [pltpu.VMEM((rows, columns), BF16) for name, rows, columns in matrices]
        + [pltpu.VMEM((1, length), F32) for name, length in vectors] * 2
        + [pltpu.VMEM((12 * TR, LANES), F32)] * 2
        + [pltpu.VMEM((USED[1], TR, TC), BF16), pltpu.SemaphoreType.DMA],
        compiler_params=pltpu.CompilerParams(vmem_limit_bytes=60 * 2**20),
        name="decoder_step",
    )(place, inverse, tiles, chosen, chosen.T, sent, kept, valid, pix, jnp.asarray(positions(D_DEC)))
    return dict(zip(results, outs))


class Spread:
    MOVES = {"u": [(0, 0, 1)], "v": [(0, 1, 0)], "z": [(1, 0, 0), (2, 0, 0), (3, 0, 0)]}

    def __init__(self, section, place, block_ref, all_ref, ways, cut, sems, first):
        self.section, self.place, self.at = section, place, neighbours(section, place)
        self.block_ref, self.all_ref, self.ways, self.cut, self.sems = block_ref, all_ref, ways, cut, sems
        self.count = block_ref.shape[0]
        self.copies, self.sides = {}, {}
        self.next_copy = self.next_side = first

    def rows(self, section, holder, way):
        start = (section * 16 + holder) * self.count + self.cut[way]
        return self.all_ref.at[pl.ds(start, self.cut[way + 1] - self.cut[way])]

    def source(self, way, origin):
        if origin == (0, 0, 0):
            return self.block_ref.at[pl.ds(self.cut[way], self.cut[way + 1] - self.cut[way])]
        return self.rows(self.section, self.at(*origin), way)

    def send(self, way, origin, move):
        copy = pltpu.make_async_remote_copy(
            src_ref=self.source(way, origin),
            dst_ref=self.rows(self.section, self.at(*origin), way),
            send_sem=self.sems[0].at[self.next_copy],
            recv_sem=self.sems[1].at[self.next_copy],
            device_id=(self.section, self.at(*move)),
            device_id_type=MESH,
        )
        copy.start()
        self.copies[way, self.moved(origin, move)] = (copy, self.next_copy)
        self.next_copy += 1

    def moved(self, origin, move):
        return tuple((o - m) % s for o, m, s in zip(origin, move, (4, 2, 2)))

    def side(self, way, origin):
        copy = pltpu.make_async_remote_copy(
            src_ref=self.source(way, origin),
            dst_ref=self.rows(self.section, self.at(*origin), way),
            send_sem=self.sems[2].at[self.next_side],
            recv_sem=self.sems[3].at[self.next_side],
            device_id=(1 - self.section, self.place),
            device_id_type=MESH,
        )
        copy.start()
        self.sides[way, origin] = (copy, self.next_side)
        self.next_side += 1

    def arrived(self, target, send_sem, recv_sem):
        pltpu.make_async_remote_copy(
            src_ref=target,
            dst_ref=target,
            send_sem=send_sem,
            recv_sem=recv_sem,
            device_id=(1 - self.section, self.place),
            device_id_type=MESH,
        ).wait_recv()

    def take(self, way, origin, dims):
        index = self.copies[way, origin][1]
        self.arrived(
            self.rows(self.section, self.at(*origin), way), self.sems[0].at[index], self.sems[1].at[index]
        )
        for dim in dims:
            for move in self.MOVES[dim]:
                self.send(way, origin, move)
        self.side(way, origin)

    def start(self):
        zero = (0, 0, 0)
        self.own = pltpu.make_async_copy(
            self.block_ref, self.all_ref.at[pl.ds((self.section * 16 + self.place) * self.count, self.count)], self.sems[4]
        )
        self.own.start()
        for turn in range(3):
            for way, dims in enumerate(self.ways):
                for move in self.MOVES[dims[turn]]:
                    self.send(way, zero, move)
        for way in range(len(self.ways)):
            self.side(way, zero)
        held = {way: [zero] for way in range(len(self.ways))}
        steps = []
        for turn in range(3):
            come = {}
            for way, dims in enumerate(self.ways):
                come[way] = [self.moved(o, m) for m in self.MOVES[dims[turn]] for o in held[way]]
                held[way] = held[way] + come[way]
            for i in range(max(len(v) for v in come.values())):
                for way, dims in enumerate(self.ways):
                    if i < len(come[way]):
                        steps.append(functools.partial(self.take, way, come[way][i], dims[turn + 1 :]))
        return steps

    def finish(self):
        self.own.wait()
        for copy, index in self.copies.values():
            copy.wait_send()
        for (way, origin), (copy, index) in self.sides.items():
            copy.wait_send()
            self.arrived(
                self.rows(1 - self.section, self.at(*origin), way), self.sems[2].at[index], self.sems[3].at[index]
            )


def greet(section, place):
    at = neighbours(section, place)
    barrier = pltpu.get_barrier_semaphore()
    peers = [(1 - section, place)]
    peers += [(section, at(*d)) for d in ((0, 0, 1), (0, 1, 0), (1, 0, 0), (2, 0, 0), (3, 0, 0))]
    for peer in peers:
        pl.semaphore_signal(barrier, inc=1, device_id=peer, device_id_type=MESH)
    pl.semaphore_wait(barrier, len(peers))


def spread_sems(copies, sides):
    return [
        pltpu.SemaphoreType.DMA((copies,)),
        pltpu.SemaphoreType.DMA((copies,)),
        pltpu.SemaphoreType.DMA((sides,)),
        pltpu.SemaphoreType.DMA((sides,)),
        pltpu.SemaphoreType.DMA,
    ]


FOUR_WAYS = (("z", "v", "u"), ("z", "u", "v"), ("v", "z", "u"), ("u", "z", "v"))
ONE_WAY = (("z", "v", "u"),)


def unpack_into(pool, place_ref, base, weight_ref, left, right):
    rows, columns = weight_ref.shape
    wide = columns // TC
    many = groups_of(rows, wide)
    count = many * wide

    def group(g, carry):
        for j in range(count):
            index = base + g * count + j
            tile = pool[index if place_ref is None else place_ref[index]].astype(F32)
            left[j * TR : (j + 1) * TR, :] = tile[:, :LANES]
            right[j * TR : (j + 1) * TR, :] = tile[:, LANES:]
        rows_g = pl.ds(pl.multiple_of(g * many * TR, TR), many * TR)
        for j in range(wide):
            for n, lines in enumerate((left, right)):
                start = j * TC + n * LANES
                weight_ref[rows_g, start : start + LANES] = lines[pl.ds(j, many * TR, stride=wide), :].astype(BF16)
        return carry

    lax.fori_loop(0, rows // (many * TR), group, 0)


def cut_vectors(tile, refs):
    row = 0
    for ref in refs:
        for r in range(ref.shape[1] // TC):
            ref[:, r * TC : (r + 1) * TC] = tile[row : row + 1, :]
            row += 1


def join_into(out_ref, values):
    row = 0
    for value in values:
        for r in range(value.shape[1] // TC):
            out_ref[row : row + 1, :] = value[:, r * TC : (r + 1) * TC]
            row += 1
    out_ref[row:, :] = jnp.zeros((TR - row, TC), F32)


def tile_bases(section_id):
    matrices, vectors = layout(section_id)
    base, total = {}, 0
    for name, rows, columns in matrices:
        base[name] = total
        total += rows * columns // (TR * TC)
    return base, total


def gather_and_encode(early, late, place, xin, positions_kept, cid):
    n_early, n_late = early.shape[0], late.shape[0]
    matrices, vectors = layout(0)
    shapes = {name: (rows, columns) for name, rows, columns in matrices}
    lengths = dict(vectors)
    base, total = tile_bases(0)
    kept_weights = ("qkv", "proj", "fc1", "fc2")
    kept_vectors = ("g1", "g2", "gf")
    line = (KEEP, D_ENC)
    hidden = (KEEP, FF_ENC)
    results = [
        (line, F32), (line, BF16), ((KEEP, 3 * D_ENC), BF16), (line, BF16), (line, F32), (line, BF16), (hidden, BF16),
        (hidden, F32), (line, F32), (line, BF16),
    ]

    def kernel(place_ref, early_ref, late_ref, xin_ref, pos_ref, late_all, *refs):
        refs = list(refs)
        out_w = {name: refs.pop(0) for name in kept_weights}
        out_v = {name: refs.pop(0) for name in kept_vectors}
        x, a, qkv, o, h, c, z, slope, y, sent = [refs.pop(0) for _ in results]
        pool = refs.pop(0)
        w = {name: refs.pop(0) for name, rows, columns in matrices}
        v = {name: refs.pop(0) for name, length in vectors}
        left, right = refs.pop(0), refs.pop(0)
        early_sems, late_sems, out_sem = refs[:5], refs[5:10], refs[10]
        section, at_dp = lax.axis_index("section"), lax.axis_index("dp")
        greet(section, at_dp)
        cut = [0, 3, 5, 7, n_early] if n_early == 8 else [0, 1, 2, 3, n_early]
        soon = Spread(section, at_dp, early_ref, pool, FOUR_WAYS, cut, early_sems, 0)
        for step in soon.start():
            step()
        later = Spread(section, at_dp, late_ref, late_all, ONE_WAY, [0, n_late], late_sems, 0)
        steps = later.start()
        soon.finish()

        def pump(count):
            for _ in range(min(count, len(steps))):
                steps.pop(0)()

        def unpack(name):
            unpack_into(pool, place_ref, base[name], w[name], left, right)
            if name in kept_weights:
                pltpu.make_async_copy(w[name], out_w[name], out_sem.at[kept_weights.index(name)]).start()

        cut_vectors(pool[place_ref[total]].astype(F32), [v[name] for name, length in vectors])
        for name in kept_vectors:
            out_v[name][...] = v[name][...]
        unpack("first")
        unpack("qkv")
        pump(1)
        x[...] = project(xin_ref[...], w["first"][...]) + v["first_bias"][...] + pos_ref[...]
        start_block(x, slice(None), (v["g1"], v["b1"], w["qkv"], v["qv_bias"]), a, qkv)
        pump(1)
        for g in range(D_ENC // LANES):
            spans = [slice(part * D_ENC + g * LANES, part * D_ENC + (g + 1) * LANES) for part in range(3)]
            mix_heads(*[qkv.at[:, span] for span in spans], o.at[:, spans[0]], D_ENC // H_ENC)
        pump(2)
        unpack("proj")
        unpack("fc1")
        pump(2)
        unpack("fc2")
        pump(2)
        names = ("proj", "proj_bias", "g2", "b2", "fc1", "fc1_bias", "fc2", "fc2_bias", "gf", "bf")
        finish_body(x, o, *[w[name] if name in w else v[name] for name in names], h, c, z, slope, y, sent, pump)
        pump(len(steps))
        later.finish()
        for name in kept_weights:
            pltpu.make_async_copy(w[name], out_w[name], out_sem.at[kept_weights.index(name)]).wait()

    vmem, hbm = pl.BlockSpec(memory_space=pltpu.VMEM), pl.BlockSpec(memory_space=pltpu.HBM)
    shape = jax.ShapeDtypeStruct
    outs = pl.pallas_call(
        kernel,
        out_shape=[shape((32 * n_late, TR, TC), BF16)]
        + [shape(shapes[name], BF16) for name in kept_weights]
        + [shape((1, lengths[name]), F32) for name in kept_vectors]
        + [shape(*result) for result in results],
        in_specs=[pl.BlockSpec(memory_space=pltpu.SMEM), hbm, hbm, vmem, vmem],
        out_specs=[hbm] * (1 + len(kept_weights)) + [vmem] * (len(kept_vectors) + len(results)),
        scratch_shapes=[pltpu.VMEM((32 * n_early, TR, TC), BF16)]
        + [pltpu.VMEM(shapes[name], BF16) for name, rows, columns in matrices]
        + [pltpu.VMEM((1, length), F32) for name, length in vectors]
        + [pltpu.VMEM((12 * TR, LANES), F32)] * 2
        + spread_sems(60, 64)
        + spread_sems(15, 16)
        + [pltpu.SemaphoreType.DMA((len(kept_weights),))],
        compiler_params=pltpu.CompilerParams(
            collective_id=cid, has_side_effects=True, vmem_limit_bytes=60 * 2**20
        ),
        name="gather_and_encode",
    )(place, early, late, xin, positions_kept)
    late_all, outs = outs[0], outs[1:]
    weights = dict(zip(kept_weights + kept_vectors, outs))
    return late_all, weights, outs[len(weights) :]


def encode(w, xin, positions_kept):
    x, a, qkv = enter_encoder(xin, positions_kept, w)
    o = attention(qkv, H_ENC)
    return x, a, qkv, o, *finish_block(x, o, w, "encoder")


def encoder_back(w, encoded, d_sent, xin):
    x, a, qkv, o, h, c, z, slope, y, sent = encoded
    two, du, dh, one, do, *sums = back_finish(d_sent, y, slope, h, w, "encoder")
    grads = dict(zip(("gf", "bf", "fc2_bias", "fc1_bias", "g2", "b2", "proj_bias"), sums))
    dqkv = attention_back(qkv, do, H_ENC)
    low, *sums = leave_encoder(dqkv, x, dh, w)
    grads.update(zip(("qv_bias", "g1", "b1", "first_bias"), sums))
    tile = join_vectors([grads[name] for name, length in layout(0)[1]], "0")
    return {"fc2": (z, two), "fc1": (c, du), "proj": (o, one), "qkv": (a, dqkv), "first": (xin, low)}, tile


def local(pixels, keep_index, clear_mask, slot_tile, master, moment_one, moment_two):
    n_dp = lax.axis_size("dp")
    n_dev = 2 * n_dp
    section, place = lax.axis_index("section"), lax.axis_index("dp")
    me = section * n_dp + place
    slots = master.shape[1]
    turns = [-(-count // n_dev) for count in USED]
    per = sum(turns)
    starts = [0, turns[0] * n_dev]
    rows_each = PARTS_ROWS if n_dp == 16 else 8 * (-(-per // 8))

    pix = lax.dynamic_index_in_dim(pixels, section, 0, keepdims=False)[0]
    keep = lax.dynamic_index_in_dim(keep_index, section, 0, keepdims=False)[0]
    clear = lax.dynamic_index_in_dim(clear_mask, section, 0, keepdims=False)[0]
    kept = jnp.any(keep[:, None] == jnp.arange(SEQ), axis=0).astype(jnp.float32)
    valid = clear.astype(jnp.float32) * (1.0 - kept)
    wide_pix = pix.astype(jnp.float32)
    sums = jnp.concatenate(
        [
            jnp.sum(jnp.sum(wide_pix, 0).reshape(BANDS, PATCH_PIX), 1),
            jnp.sum(jnp.sum(wide_pix * wide_pix, 0).reshape(BANDS, PATCH_PIX), 1),
            jnp.sum(valid)[None],
        ]
    )
    sums = jnp.pad(sums, (0, 1024 - sums.shape[0])).reshape(8, 128)

    def order(table, start):
        used = (table < TILES).astype(jnp.int32)
        count = table.shape[0]
        before = (jnp.arange(count)[:, None] > jnp.arange(count)[None]).astype(jnp.int32)
        return used, jnp.sum(before * used[None], 1) + start

    table_own = slot_tile[0]
    used_own, order_own = order(table_own, starts[1] * section)
    used_mine = lax.dynamic_slice_in_dim(used_own, place * slots, slots)
    order_mine = lax.dynamic_slice_in_dim(order_own, place * slots, slots)
    goes = lax.rem(order_mine, n_dev)
    slot_for = jnp.sum(
        jnp.arange(slots)[None] * used_mine[None] * (goes[None] == jnp.arange(n_dev)[:, None]), 1
    ).astype(jnp.int32)
    dealt = pick_tiles(master[0], slot_for, jnp.bfloat16, "deal_weights")
    table_out = jnp.pad(table_own, (0, 1024 - table_own.shape[0])).reshape(8, 128)
    arrived, all_sums, all_tables = exchange("deal", 1, n_dp, [dealt], [sums, table_out])

    totals = jnp.sum(all_sums, 0).reshape(-1)
    pixel_count = n_dev * SEQ * PATCH_PIX
    band_mean = totals[:BANDS] / pixel_count
    band_scale = lax.rsqrt(totals[BANDS : 2 * BANDS] / pixel_count - band_mean * band_mean + EPS_BAND)
    valid_count = jnp.maximum(totals[2 * BANDS], 1.0)

    chosen = (keep[:, None] == jnp.arange(SEQ)).astype(BF16)
    mean_line = jnp.broadcast_to(band_mean[:, None], (BANDS, PATCH_PIX)).reshape(PATCH_DIM)
    scale_line = jnp.broadcast_to(band_scale[:, None], (BANDS, PATCH_PIX)).reshape(PATCH_DIM)
    xin = ((project(chosen, pix) - mean_line) * scale_line).astype(BF16)

    n_slots = table_own.shape[0]
    tables = jnp.stack([all_tables[s * n_dp].reshape(-1)[:n_slots] for s in range(2)])
    both = [order(tables[s], starts[s]) for s in range(2)]
    used_all = jnp.concatenate([b[0] for b in both])
    order_all = jnp.concatenate([b[1] for b in both])
    owner_all = jnp.arange(2 * n_slots) // slots
    held = jnp.arange(per) * n_dev + me
    match = used_all[None] * (order_all[None] == held[:, None])
    from_owner = jnp.sum(match * owner_all[None], 1).astype(jnp.int32)
    is_held = jnp.sum(match, 1)
    block = pick_tiles(arrived, from_owner, jnp.bfloat16, "hold_weights")
    where_tile = []
    line_tile = []
    source_tile = []
    for s in range(2):
        hit = tables[s][None] == jnp.arange(TILES)[:, None]
        rank = jnp.sum(hit * both[s][1][None], 1)
        device, turn = lax.rem(rank, n_dev), lax.div(rank, n_dev)
        where_tile.append((device * per + turn).astype(jnp.int32))
        source_tile.append((device * turns[s] + turn - (turns[0] if s else 0)).astype(jnp.int32))
        line_tile.append((device * rows_each + line_of(turn, n_dp)).astype(jnp.int32))

    positions_kept = jnp.dot(chosen.astype(F32), jnp.asarray(positions(D_ENC)), precision=lax.Precision.HIGHEST)
    early, late = block[: turns[0]], block[turns[0] :]
    if n_dp == 16:
        late_all, enc, encoded = gather_and_encode(early, late, source_tile[0], xin, positions_kept, 2)
    else:
        early_all, late_all = [lax.all_gather(lax.all_gather(part, "dp"), "section") for part in (early, late)]
        enc = unpack_section(early_all.reshape(-1, TR, TC), source_tile[0], 0)
        encoded = encode(enc, xin, positions_kept)
    dec = decoder_step(
        late_all.reshape(-1, TR, TC), source_tile[1], (1.0 / valid_count)[None], chosen, encoded[-1], kept[:, None],
        valid[:, None], pix,
    )
    factors_dec = {
        "head": (dec["final"], dec["pred_low"]),
        "fc2": (dec["z"], dec["two"]),
        "fc1": (dec["c"], dec["du"]),
        "proj": (dec["o"], dec["one"]),
        "qkv": (dec["a"], dec["dqkv"]),
        "first": (encoded[-1], dec["low"]),
    }
    factors_enc, tile_enc = encoder_back(enc, encoded, dec["d_sent"], xin)
    loss = jnp.sum(dec["loss"])

    codes = None
    scales = jnp.zeros((n_dev * rows_each, TC), F32)
    for s, factors, tile in ((1, factors_dec, dec["vectors"]), (0, factors_enc, tile_enc)):
        base, total = tile_bases(s)
        jobs = [(*factors[name], base[name], name) for name in base] + [(tile, None, total, "vectors")]
        for a, d, start, name in jobs:
            codes, scales = weight_codes(
                a, d, where_tile[s], line_tile[s], start, codes, scales, n_dev * per, f"{name}_{s}"
            )

    if n_dp == 16:
        own_codes, own_scales = reduce_all(
            codes.reshape(2, n_dp, per, TR, TC), scales.reshape(2, n_dp, rows_each, TC), 3
        )
    else:
        wide = scales.reshape(n_dev, rows_each, TC)[:, :per]
        values = jnp.where(wide[:, :, None] > 0.0, codes.reshape(n_dev, per, TR, TC).astype(jnp.float32), 0.0)
        values = values * wide[:, :, None]
        values = lax.psum_scatter(values, ("section", "dp"), scatter_dimension=0, tiled=True)[0]
        top = jnp.max(jnp.abs(values), 1, keepdims=True)
        up = jnp.where(top > 0.0, 32766.0 / top, 0.0)
        own_codes = jnp.round(values * up).astype(jnp.int16)
        own_scales = jnp.pad(top[:, 0] * (1.0 / 32766.0), ((0, rows_each - per), (0, 0)))
    own_scale = own_scales[np.array([line_of(t, n_dp) for t in range(per)])]
    own = jnp.where(is_held[:, None, None] > 0, own_codes.astype(jnp.float32) * own_scale[:, None], 0.0)
    tail = jnp.stack([jnp.sum(own * own), loss])
    tail = jnp.pad(tail, (0, 1022)).reshape(8, 128)

    turn_for = jnp.sum(
        jnp.arange(per)[None] * is_held[None] * (from_owner[None] == jnp.arange(n_dev)[:, None]), 1
    ).astype(jnp.int32)
    codes_back = pick_tiles(own_codes, turn_for, jnp.int16, "deal_gradients")
    scales_back = own_scale[turn_for][:, None]
    codes_mine, scales_mine, tails = exchange("return", 4, n_dp, [codes_back, scales_back], [tail])
    totals = jnp.sum(tails, 0)[0]
    grad_norm = jnp.sqrt(totals[0])
    factor = jnp.minimum(1.0, CLIP_NORM / (grad_norm + 1e-06))
    master_new, first_new, second_new = adam(
        codes_mine, scales_mine, goes, used_mine, factor[None], master[0], moment_one[0], moment_two[0]
    )
    return master_new[None], first_new[None], second_new[None], totals[1][None], grad_norm[None]


def solution(mesh):
    return jax.shard_map(
        local,
        mesh=mesh,
        in_specs=(
            P(None, "dp", None, None),
            P(None, "dp", None),
            P(None, "dp", None),
            P("section", None),
            P("section", "dp", None, None),
            P("section", "dp", None, None),
            P("section", "dp", None, None),
        ),
        out_specs=(
            P("section", "dp", None, None),
            P("section", "dp", None, None),
            P("section", "dp", None, None),
            P(),
            P(),
        ),
        check_vma=False,
    )
```

```python
import functools
import math

import jax
import jax.numpy as jnp
import numpy as np
from jax import lax
from jax.experimental import pallas as pl
from jax.experimental.pallas import tpu as pltpu
from jax.sharding import PartitionSpec as P

D_ENC = 768
H_ENC = 12
FF_ENC = 3072
D_DEC = 512
H_DEC = 16
FF_DEC = 2048
BANDS = 6
PATCH_PIX = 256
PATCH_DIM = 1536
SEQ = 588
KEEP = 147
STEP = 5
TILES = 256
USED = (253, 133)

EPS_NORM = 1e-06
EPS_BAND = 1e-05
CLIP_NORM = 0.001
RATE = 0.02
DECAY = 0.05
BETA_ONE = 0.5
BETA_TWO = 0.75
ADAM_EPS = 1e-08

K_SECTION = "section"
K_FIRST_BIAS = "first_bias"
K_PROJ_BIAS = "proj_bias"
K_FC2_BIAS = "fc2_bias"
K_FC1_BIAS = "fc1_bias"
K_FIRST = "first"
K_QV_BIAS = "qv_bias"
K_QKV = "qkv"
K_PROJ = "proj"
K_DP = "dp"
K_FC1 = "fc1"
K_FC2 = "fc2"
K_HEAD_BIAS = "head_bias"
K_GF = "gf"
K_G2 = "g2"
K_G1 = "g1"
K_MASK = "mask"
K_HEAD = "head"
K_BF = "bf"
K_B1 = "b1"
K_B2 = "b2"
K_U = "u"
K_V = "v"
K_Z = "z"

MESH = pl.DeviceIdType.MESH
TR, TC = 128, 256
PARTS = ((0, 6), (6, 11), (11, 13))
PARTS_ROWS = 24


def neighbours(section, place):
    x, y, z = lax.rem(place, 2), lax.rem(lax.div(place, 2), 2), lax.div(place, 4)

    def at(dz, dv, du):
        dx = (1 - section) * du + section * dv
        dy = (1 - section) * dv + section * du
        return lax.rem(z + dz, 4) * 4 + lax.rem(y + dy, 2) * 2 + lax.rem(x + dx, 2)

    return at


def exchange(name, cid, n_dp, dealt, shared):
    n_dev = 2 * n_dp
    n_a, n_s = len(dealt), len(shared)
    n_all = n_a + n_s

    def kernel(*refs):
        sources, targets = refs[:n_all], refs[n_all : 2 * n_all]
        send_sem, recv_sem, own_sem = refs[2 * n_all :]
        section, place = lax.axis_index(K_SECTION), lax.axis_index(K_DP)
        me = section * n_dp + place

        def who(step):
            other = lax.rem(me + step, n_dev)
            return other, (lax.div(other, n_dp), lax.rem(other, n_dp))

        barrier = pltpu.get_barrier_semaphore()

        def greet(step, carry):
            pl.semaphore_signal(barrier, inc=1, device_id=who(step)[1], device_id_type=MESH)
            return carry

        lax.fori_loop(1, n_dev, greet, 0)
        own = []
        for which in range(n_all):
            source = sources[which].at[me] if which < n_a else sources[which]
            copy = pltpu.make_async_copy(source, targets[which].at[me], own_sem.at[which])
            copy.start()
            own.append(copy)
        pl.semaphore_wait(barrier, n_dev - 1)

        def made(which, step):
            other, place_of = who(step)
            source = sources[which].at[other] if which < n_a else sources[which]
            return pltpu.make_async_remote_copy(
                src_ref=source,
                dst_ref=targets[which].at[me],
                send_sem=send_sem.at[which, step],
                recv_sem=recv_sem.at[which, step],
                device_id=place_of,
                device_id_type=MESH,
            )

        def begin(step, carry):
            for which in reversed(range(n_all)):
                made(which, step).start()
            return carry

        def end(step, carry):
            for which in range(n_all):
                made(which, step).wait()
            return carry

        lax.fori_loop(1, n_dev, begin, 0)
        for copy in own:
            copy.wait()
        lax.fori_loop(1, n_dev, end, 0)

    arrays = list(dealt) + list(shared)
    shapes = [jax.ShapeDtypeStruct(a.shape, a.dtype) for a in dealt] + [
        jax.ShapeDtypeStruct((n_dev,) + a.shape, a.dtype) for a in shared
    ]
    any_spec = pl.BlockSpec(memory_space=pltpu.HBM)
    return pl.pallas_call(
        kernel,
        out_shape=shapes,
        in_specs=[any_spec] * n_all,
        out_specs=[any_spec] * n_all,
        scratch_shapes=[
            pltpu.SemaphoreType.DMA((n_all, n_dev)),
            pltpu.SemaphoreType.DMA((n_all, n_dev)),
            pltpu.SemaphoreType.DMA((n_all,)),
        ],
        compiler_params=pltpu.CompilerParams(collective_id=cid, has_side_effects=True),
        name=name,
    )(*arrays)


def line_of(turn, n_dp):
    if n_dp != 16:
        return turn
    return turn + 2 * (turn >= PARTS[0][1]) + 3 * (turn >= PARTS[1][1])


def code(values):
    top = jnp.max(jnp.abs(values), axis=0, keepdims=True)
    up = jnp.where(top > 0.0, 32766.0 / top, 0.0)
    scaled = values * up
    return (scaled + jnp.where(scaled >= 0.0, 0.5, -0.5)).astype(jnp.int32).astype(jnp.int16), top * (1.0 / 32766.0)


def reduce_all(codes, scales, cid, SUMS=True):
    per = codes.shape[2]

    def kernel(codes_ref, scales_ref, out_ref, outs_ref, acc, accs, rc, rcs, r_code, r_scale,
               own_sem, owns_sem, c_send, c_recv, p_send, p_recv):
        section, place = lax.axis_index(K_SECTION), lax.axis_index(K_DP)
        at, at_other = neighbours(section, place), neighbours(1 - section, place)
        sibling = (1 - section, place)
        to_u, to_v = (section, at(0, 0, 1)), (section, at(0, 1, 0))

        def to_z(dz):
            return (section, at(dz, 0, 0))

        barrier = pltpu.get_barrier_semaphore()
        peers = [sibling, to_u, to_v, to_z(1), to_z(2), to_z(3)]
        for peer in peers:
            pl.semaphore_signal(barrier, inc=1, device_id=peer, device_id_type=MESH)
        order = [(dz, dv, du) for dz in (2, 1, 3, 0) for dv in (1, 0) for du in (1, 0)]
        loads = {}
        for n, d in enumerate(order):
            b = at(*d)
            loads[d] = (
                pltpu.make_async_copy(codes_ref.at[section, b], acc.at[b], own_sem.at[n]),
                pltpu.make_async_copy(scales_ref.at[section, b], accs.at[b], owns_sem.at[n]),
            )
            for copy in loads[d]:
                copy.start()
        pl.semaphore_wait(barrier, len(peers))
        crossing = {}
        for n, d in enumerate(order):
            b = at_other(*d)
            pair = []
            for k, (source, target) in enumerate(((codes_ref, rc), (scales_ref, rcs))):
                copy = pltpu.make_async_remote_copy(
                    src_ref=source.at[1 - section, b],
                    dst_ref=target.at[b],
                    send_sem=c_send.at[k, n],
                    recv_sem=c_recv.at[k, n],
                    device_id=sibling,
                    device_id_type=MESH,
                )
                copy.start()
                pair.append(copy)
            crossing[d] = pair

        def add(b, part, from_code, from_first, from_scale, from_row):
            first, count = PARTS[part][0], PARTS[part][1] - PARTS[part][0]

            def one(t, carry):
                line = pl.ds(8 * part + t, 1)
                mine = acc[b, first + t].astype(jnp.float32) * accs[b, line, :]
                theirs = from_code[from_first + t].astype(jnp.float32) * from_scale[pl.ds(from_row + t, 1), :]
                value, scale = code(mine + theirs)
                acc[b, first + t] = value
                accs[b, line, :] = scale
                return carry

            if SUMS:
                lax.fori_loop(0, count, one, 0)

        sends = {}
        used = [0, 0]

        def send(part, key, b, peer):
            t0, t1 = PARTS[part]
            slot, index = used
            used[0] += t1 - t0
            used[1] += 1
            pair = []
            for k, (source, target) in enumerate(
                (
                    (acc.at[b, pl.ds(t0, t1 - t0)], r_code.at[pl.ds(slot, t1 - t0)]),
                    (accs.at[b, pl.ds(8 * part, 8)], r_scale.at[index]),
                )
            ):
                copy = pltpu.make_async_remote_copy(
                    src_ref=source,
                    dst_ref=target,
                    send_sem=p_send.at[k, index],
                    recv_sem=p_recv.at[k, index],
                    device_id=peer,
                    device_id_type=MESH,
                )
                copy.start()
                pair.append(copy)
            sends[part, key] = (pair, slot, index)

        def take(part, key, b):
            pair, slot, index = sends[part, key]
            for copy in pair:
                copy.wait_recv()
            add(b, part, r_code, slot, r_scale.at[index], 0)

        seen = set()

        def ready(d):
            if d not in seen:
                seen.add(d)
                for copy in loads[d]:
                    copy.wait()
                for copy in crossing[d]:
                    copy.wait_recv()

        def first(dz, parts=(0, 1, 2)):
            for dv in (1, 0):
                for du in (1, 0):
                    b = at(dz, dv, du)
                    ready((dz, dv, du))
                    for part in parts:
                        add(b, part, rc.at[b], PARTS[part][0], rcs.at[b], 8 * part)
                        if part == 2 and dz:
                            send(2, ("1", dz, dv, du), b, to_z(dz))
                        if part < 2 and du:
                            send(part, ("1", dz, dv), b, to_u)

        def second(dz):
            for dv in (1, 0):
                for part in (0, 1):
                    b = at(dz, dv, 0)
                    take(part, ("1", dz, dv), b)
                    if dv:
                        send(part, ("2", dz), b, to_v)

        def third(dz):
            for part in (0, 1):
                b = at(dz, 0, 0)
                take(part, ("2", dz), b)
                if dz:
                    send(part, ("3", dz), b, to_z(dz))

        first(2)
        first(1)
        first(3, (2,))
        second(2)
        first(3, (0, 1))
        second(1)
        third(2)
        first(0, (2,))
        second(3)
        first(0, (0, 1))
        third(1)
        for du in (1, 0):
            for dv in (1, 0):
                b = at(0, dv, du)
                for dz in (1, 3, 2):
                    take(2, ("1", dz, dv, du), b)
                if du:
                    send(2, ("2", dv), b, to_u)
        third(3)
        second(0)
        for dv in (1, 0):
            b = at(0, dv, 0)
            take(2, ("2", dv), b)
            if dv:
                send(2, ("3",), b, to_v)
        third(0)
        for dz in (2, 1, 3):
            for part in (0, 1):
                take(part, ("3", dz), place)
        take(2, ("3",), place)
        out_ref[...] = acc[place]
        outs_ref[...] = accs[place]
        for pair in crossing.values():
            for copy in pair:
                copy.wait_send()
        for pair, slot, index in sends.values():
            for copy in pair:
                copy.wait_send()

    n_tiles = 15 * per
    n_copies = 45
    hbm = pl.BlockSpec(memory_space=pltpu.HBM)
    vmem = pl.BlockSpec(memory_space=pltpu.VMEM)
    return pl.pallas_call(
        kernel,
        out_shape=(
            jax.ShapeDtypeStruct((per, TR, TC), jnp.int16),
            jax.ShapeDtypeStruct((PARTS_ROWS, TC), jnp.float32),
        ),
        in_specs=[hbm, hbm],
        out_specs=(vmem, vmem),
        scratch_shapes=[
            pltpu.VMEM((16, per, TR, TC), jnp.int16),
            pltpu.VMEM((16, PARTS_ROWS, TC), jnp.float32),
            pltpu.VMEM((16, per, TR, TC), jnp.int16),
            pltpu.VMEM((16, PARTS_ROWS, TC), jnp.float32),
            pltpu.VMEM((n_tiles, TR, TC), jnp.int16),
            pltpu.VMEM((n_copies, 8, TC), jnp.float32),
            pltpu.SemaphoreType.DMA((16,)),
            pltpu.SemaphoreType.DMA((16,)),
            pltpu.SemaphoreType.DMA((2, 16)),
            pltpu.SemaphoreType.DMA((2, 16)),
            pltpu.SemaphoreType.DMA((2, n_copies)),
            pltpu.SemaphoreType.DMA((2, n_copies)),
        ],
        compiler_params=pltpu.CompilerParams(
            collective_id=cid, has_side_effects=True, vmem_limit_bytes=60 * 2**20
        ),
        name="reduce_tiles",
    )(codes, scales)


def layout(section_id):
    if section_id == 0:
        width, hidden = D_ENC, FF_ENC
        matrices = [(K_FIRST, PATCH_DIM, D_ENC)]
        vectors = [(K_FIRST_BIAS, D_ENC)]
    else:
        width, hidden = D_DEC, FF_DEC
        matrices = [(K_FIRST, D_ENC, D_DEC)]
        vectors = [(K_FIRST_BIAS, D_DEC), (K_MASK, D_DEC)]
    matrices = matrices + [
        (K_QKV, width, 3 * width),
        (K_PROJ, width, width),
        (K_FC1, width, hidden),
        (K_FC2, hidden, width),
    ]
    vectors = vectors + [
        (K_G1, width),
        (K_B1, width),
        (K_QV_BIAS, 2 * width),
        (K_PROJ_BIAS, width),
        (K_G2, width),
        (K_B2, width),
        (K_FC1_BIAS, hidden),
        (K_FC2_BIAS, width),
        (K_GF, width),
        (K_BF, width),
    ]
    if section_id == 1:
        matrices = matrices + [(K_HEAD, D_DEC, PATCH_DIM)]
        vectors = vectors + [(K_HEAD_BIAS, PATCH_DIM)]
    return matrices, vectors


def positions(width):
    place = np.arange(SEQ, dtype=np.float32)[:, None]
    rate = np.exp(np.arange(width // 2, dtype=np.float32) * np.float32(-2.0 * math.log(10000.0) / width))
    angle = (place * rate).astype(np.float32)
    return np.concatenate([np.sin(angle), np.cos(angle)], axis=1).astype(np.float32)


LANES = 128
LOG2E = math.log2(math.e)


def pick_tiles(tiles, index, dtype, name):
    count = index.shape[0]

    def kernel(index_ref, tiles_ref, out_ref):
        def one(t, carry):
            out_ref[t] = tiles_ref[index_ref[t]].astype(dtype)
            return carry

        lax.fori_loop(0, count, one, 0)

    return pl.pallas_call(
        kernel,
        out_shape=jax.ShapeDtypeStruct((count, TR, TC), dtype),
        in_specs=[pl.BlockSpec(memory_space=pltpu.SMEM), pl.BlockSpec(memory_space=pltpu.VMEM)],
        out_specs=pl.BlockSpec(memory_space=pltpu.VMEM),
        compiler_params=pltpu.CompilerParams(vmem_limit_bytes=40 * 2**20),
        name=name,
    )(index, tiles)


def groups_of(rows, wide):
    groups = rows // TR
    return max(m for m in range(1, groups + 1) if groups % m == 0 and (m == 1 or m * wide <= 12))


def unpack_matrix(tiles, place, base, rows, columns, name):
    wide = columns // TC
    many = groups_of(rows, wide)
    count = many * wide

    def kernel(place_ref, *refs):
        sources, out_ref, lines = refs[:count], refs[count], refs[count + 1 :]
        for j in range(count):
            for h in range(2):
                lines[h][j * TR : (j + 1) * TR, :] = sources[j][0, :, h * LANES : (h + 1) * LANES].astype(jnp.float32)
        for j in range(wide):
            for h in range(2):
                start = j * TC + h * LANES
                out_ref[:, start : start + LANES] = lines[h][pl.ds(j, many * TR, stride=wide), :].astype(tiles.dtype)

    def spec(j):
        return pl.BlockSpec((1, TR, TC), lambda g, place_ref: (place_ref[base + g * count + j], 0, 0))

    return pl.pallas_call(
        kernel,
        out_shape=jax.ShapeDtypeStruct((rows, columns), tiles.dtype),
        grid_spec=pltpu.PrefetchScalarGridSpec(
            num_scalar_prefetch=1,
            grid=(rows // (many * TR),),
            in_specs=[spec(j) for j in range(count)],
            out_specs=pl.BlockSpec((many * TR, columns), lambda g, place_ref: (g, 0)),
            scratch_shapes=[pltpu.VMEM((count * TR, LANES), jnp.float32)] * 2,
        ),
        compiler_params=pltpu.CompilerParams(vmem_limit_bytes=32 * 2**20),
        name="unpack_" + name,
    )(place, *([tiles] * count))


def unpack_vectors(tiles, place, base, lengths, name):
    def kernel(place_ref, tile_ref, *refs):
        row = 0
        for out_ref, length in zip(refs, lengths):
            for r in range(length // TC):
                out_ref[:, r * TC : (r + 1) * TC] = tile_ref[0, row : row + 1, :].astype(jnp.float32)
                row += 1

    return pl.pallas_call(
        kernel,
        out_shape=[jax.ShapeDtypeStruct((1, length), jnp.float32) for length in lengths],
        grid_spec=pltpu.PrefetchScalarGridSpec(
            num_scalar_prefetch=1,
            grid=(1,),
            in_specs=[pl.BlockSpec((1, TR, TC), lambda g, place_ref: (place_ref[base], 0, 0))],
            out_specs=[pl.BlockSpec((1, length), lambda g, place_ref: (0, 0)) for length in lengths],
        ),
        name="unpack_vectors_" + name,
    )(place, tiles)


def unpack_section(tiles, place, section_id):
    matrices, vectors = layout(section_id)
    found, base = {}, 0
    for name, rows, columns in matrices:
        found[name] = unpack_matrix(tiles, place, base, rows, columns, f"{name}_{section_id}")
        base += rows * columns // (TR * TC)
    lines = unpack_vectors(tiles, place, base, [length for name, length in vectors], str(section_id))
    found.update({name: line for (name, length), line in zip(vectors, lines)})
    return found


def codes_into(a_ref, d_ref, base, place_ref, line_ref, codes_ref, scales_ref, work):
    left, right, ready, sem = work
    rows, columns = a_ref.shape[1], d_ref.shape[1]
    wide = columns // TC
    many = groups_of(rows, wide)
    count = many * wide
    steps = rows // (many * TR)

    def drain(slot):
        pltpu.make_async_copy(codes_ref.at[pl.ds(0, count)], ready.at[slot, pl.ds(0, count)], sem.at[slot]).wait()

    def group(g, carry):
        slot = lax.rem(g, 2)

        @pl.when(g >= 2)
        def _():
            drain(slot)

        factor = a_ref[:, pl.ds(pl.multiple_of(g * many * TR, TR), many * TR)]
        for j in range(wide):
            part = weight_grad(factor, d_ref[:, j * TC : (j + 1) * TC])
            for h, lines in enumerate((left, right)):
                lines[pl.ds(j, many * TR, stride=wide), :] = part[:, h * LANES : (h + 1) * LANES]
        for j in range(count):
            tile = base + g * count + j
            code_tile(left, right, j, ready, slot, j, scales_ref, line_ref[tile])
            pltpu.make_async_copy(ready.at[slot, j], codes_ref.at[place_ref[tile]], sem.at[slot]).start()
        return carry

    lax.fori_loop(0, steps, group, 0)
    if steps > 1:
        drain(steps % 2)
    drain((steps - 1) % 2)


def code_tile(left, right, j, ready, slot, to, scales_ref, line):
    pair = []
    for h, lines in enumerate((left, right)):
        value, scale = code(lines[j * TR : (j + 1) * TR, :])
        ready[slot, to, :, h * LANES : (h + 1) * LANES] = value
        pair.append(scale)
    scales_ref[pl.ds(line, 1), :] = jnp.concatenate(pair, axis=1)


def vectors_into(values, tile, place_ref, line_ref, codes_ref, scales_ref, work):
    left, right, ready, sem = work
    row = 0
    for value in values:
        for r in range(value.shape[1] // TC):
            left[row : row + 1, :] = value[:, r * TC : r * TC + LANES]
            right[row : row + 1, :] = value[:, r * TC + LANES : (r + 1) * TC]
            row += 1
    for lines in (left, right):
        lines[row:TR, :] = jnp.zeros((TR - row, LANES), F32)
    code_tile(left, right, 0, ready, 0, 0, scales_ref, line_ref[tile])
    copy = pltpu.make_async_copy(ready.at[0, 0], codes_ref.at[place_ref[tile]], sem.at[0])
    copy.start()
    copy.wait()


CODE_WORK = [
    pltpu.VMEM((12 * TR, LANES), jnp.float32),
    pltpu.VMEM((12 * TR, LANES), jnp.float32),
    pltpu.VMEM((2, 12, TR, TC), jnp.int16),
    pltpu.SemaphoreType.DMA((2,)),
]


def unpack_vectors(tiles, place, base, lengths, name):
    def kernel(place_ref, tile_ref, *refs):
        row = 0
        for out_ref, length in zip(refs, lengths):
            for r in range(length // TC):
                out_ref[:, r * TC : (r + 1) * TC] = tile_ref[0, row : row + 1, :].astype(jnp.float32)
                row += 1

    return pl.pallas_call(
        kernel,
        out_shape=[jax.ShapeDtypeStruct((1, length), jnp.float32) for length in lengths],
        grid_spec=pltpu.PrefetchScalarGridSpec(
            num_scalar_prefetch=1,
            grid=(1,),
            in_specs=[pl.BlockSpec((1, TR, TC), lambda g, place_ref: (place_ref[base], 0, 0))],
            out_specs=[pl.BlockSpec((1, length), lambda g, place_ref: (0, 0)) for length in lengths],
        ),
        name="unpack_vectors_" + name,
    )(place, tiles)


def unpack_section(tiles, place, section_id):
    matrices, vectors = layout(section_id)
    found, base = {}, 0
    for name, rows, columns in matrices:
        found[name] = unpack_matrix(tiles, place, base, rows, columns, f"{name}_{section_id}")
        base += rows * columns // (TR * TC)
    lines = unpack_vectors(tiles, place, base, [length for name, length in vectors], str(section_id))
    found.update({name: line for (name, length), line in zip(vectors, lines)})
    return found


def adam(codes, scales, index, used, factor, master, first, second):
    slots = master.shape[0]
    per = 3 if slots % 3 == 0 else 1

    def kernel(index_ref, used_ref, factor_ref, codes_ref, scales_ref, w_ref, m_ref, v_ref, w_out, m_out, v_out):
        for t in range(per):
            slot = pl.program_id(0) * per + t
            source = index_ref[slot]
            grad = codes_ref[source].astype(jnp.float32) * scales_ref[source]
            grad = jnp.where(used_ref[slot] > 0, grad * factor_ref[0], 0.0)
            first_new = BETA_ONE * m_ref[t] + (1.0 - BETA_ONE) * grad
            second_new = BETA_TWO * v_ref[t] + (1.0 - BETA_TWO) * grad * grad
            ratio = (
                first_new
                / (1.0 - BETA_ONE ** float(STEP))
                / (jnp.sqrt(second_new / (1.0 - BETA_TWO ** float(STEP))) + ADAM_EPS)
            )
            w_out[t] = w_ref[t] - RATE * (ratio + DECAY * w_ref[t])
            m_out[t] = first_new
            v_out[t] = second_new

    smem = pl.BlockSpec(memory_space=pltpu.SMEM)
    block = pl.BlockSpec((per, TR, TC), lambda g: (g, 0, 0))
    return pl.pallas_call(
        kernel,
        out_shape=[jax.ShapeDtypeStruct(master.shape, jnp.float32)] * 3,
        grid=(slots // per,),
        in_specs=[
            smem,
            smem,
            smem,
            pl.BlockSpec(codes.shape, lambda g: (0, 0, 0)),
            pl.BlockSpec(scales.shape, lambda g: (0, 0, 0)),
            block,
            block,
            block,
        ],
        out_specs=[block] * 3,
        compiler_params=pltpu.CompilerParams(vmem_limit_bytes=40 * 2**20),
        name="adam",
    )(index, used, factor, codes, scales, master, first, second)


def project(a, w):
    return jnp.dot(a, w, preferred_element_type=jnp.float32)


def project_back(d, w):
    return lax.dot_general(d, w, (((1,), (1,)), ((), ())), preferred_element_type=jnp.float32)


def weight_grad(a, d):
    return lax.dot_general(a, d, (((0,), (0,)), ((), ())), preferred_element_type=jnp.float32)


def layer_norm(values, gain, offset):
    centre = values - jnp.mean(values, -1, keepdims=True)
    return centre * lax.rsqrt(jnp.mean(centre * centre, -1, keepdims=True) + EPS_NORM) * gain + offset


def norm_back(upstream, values, gain):
    centre = values - jnp.mean(values, -1, keepdims=True)
    spread = lax.rsqrt(jnp.mean(centre * centre, -1, keepdims=True) + EPS_NORM)
    normed = centre * spread
    scaled = upstream * gain
    downstream = spread * (
        scaled - jnp.mean(scaled, -1, keepdims=True) - normed * jnp.mean(scaled * normed, -1, keepdims=True)
    )
    return downstream, line_sum(upstream * normed), line_sum(upstream)


def line_sum(values):
    return jnp.sum(values.astype(jnp.float32), 0, keepdims=True)


ERF_TOP = (
    -2.72614225801306e-10,
    2.77068142495902e-08,
    -2.10102402082508e-06,
    -5.69250639462346e-05,
    -7.34990630326855e-04,
    -2.95459980854025e-03,
    -1.60960333262415e-02,
)
ERF_BOTTOM = (
    -1.45660718464996e-05,
    -2.13374055278905e-04,
    -1.68282697438203e-03,
    -7.37332916720468e-03,
    -1.42647390514189e-02,
)


def erf(x):
    x = jnp.clip(x, -4.0, 4.0)
    square = x * x
    top, bottom = jnp.full_like(x, ERF_TOP[0]), jnp.full_like(x, ERF_BOTTOM[0])
    for coefficient in ERF_TOP[1:]:
        top = top * square + coefficient
    for coefficient in ERF_BOTTOM[1:]:
        bottom = bottom * square + coefficient
    return x * top / bottom


def whole_kernel(kernel, shapes, operands, name, scratch=(), smem=0):
    vmem = pl.BlockSpec(memory_space=pltpu.VMEM)
    return pl.pallas_call(
        kernel,
        out_shape=[jax.ShapeDtypeStruct(shape, dtype) for shape, dtype in shapes],
        in_specs=[pl.BlockSpec(memory_space=pltpu.SMEM)] * smem + [vmem] * (len(operands) - smem),
        out_specs=[vmem] * len(shapes),
        scratch_shapes=scratch,
        compiler_params=pltpu.CompilerParams(vmem_limit_bytes=56 * 2**20),
        name=name,
    )(*operands)


F32, BF16 = jnp.float32, jnp.bfloat16


def start_block(x_ref, rows, w, a_ref, qkv_ref):
    g1, b1, weight, bias = w
    width = x_ref.shape[1]
    a = layer_norm(x_ref[rows, :], g1[...], b1[...]).astype(BF16)
    a_ref[rows, :] = a
    for part in range(3):
        columns = slice(part * width, (part + 1) * width)
        value = project(a, weight[:, columns])
        if part != 1:
            value = value + bias[:, (part // 2) * width : (part // 2 + 1) * width]
        qkv_ref[rows, columns] = value.astype(BF16)


def enter_encoder(xin, place, w):
    def kernel(xin_ref, place_ref, first, bias, g1, b1, weight, qv_bias, x_ref, a_ref, qkv_ref):
        x_ref[...] = project(xin_ref[...], first[...]) + bias[...] + place_ref[...]
        start_block(x_ref, slice(None), (g1, b1, weight, qv_bias), a_ref, qkv_ref)

    shapes = [((KEEP, D_ENC), F32), ((KEEP, D_ENC), BF16), ((KEEP, 3 * D_ENC), BF16)]
    operands = [xin, place] + [w[k] for k in (K_FIRST, K_FIRST_BIAS, K_G1, K_B1, K_QKV, K_QV_BIAS)]
    return whole_kernel(kernel, shapes, operands, "enter_encoder")


def enter_decoder_body(chosen_ref, sent_ref, kept_ref, place_ref, first, bias, mask, g1, b1, weight, qv_bias,
                       x_ref, a_ref, qkv_ref):
    for lo, hi in row_cuts(SEQ, 304):
        rows = slice(lo, hi)
        spread = project(chosen_ref[rows, :], sent_ref[...]).astype(BF16)
        placed = project(spread, first[...]) + bias[...]
        x_ref[rows, :] = jnp.where(kept_ref[rows, :] > 0.0, placed, mask[...]) + place_ref[rows, :]
        start_block(x_ref, rows, (g1, b1, weight, qv_bias), a_ref, qkv_ref)


def finish_block(x, attended, w, name):
    length, width = x.shape
    hidden = w[K_FC1].shape[1]

    line = (length, width)
    shapes = [(line, F32), (line, BF16), ((length, hidden), BF16), ((length, hidden), F32), (line, F32), (line, BF16)]
    names = (K_PROJ, K_PROJ_BIAS, K_G2, K_B2, K_FC1, K_FC1_BIAS, K_FC2, K_FC2_BIAS, K_GF, K_BF)
    return whole_kernel(finish_body, shapes, [x, attended] + [w[k] for k in names], "finish_" + name)


def finish_body(x_ref, o_ref, proj, proj_bias, g2, b2, fc1, fc1_bias, fc2, fc2_bias, gf, bf,
                h_ref, c_ref, z_ref, slope_ref, y_ref, out_ref, pump=None):
    length, hidden = z_ref.shape
    for lo, hi in row_cuts(length, 304):
        rows = slice(lo, hi)
        h = x_ref[rows, :] + project(o_ref[rows, :], proj[...]) + proj_bias[...]
        h_ref[rows, :] = h
        c_ref[rows, :] = layer_norm(h, g2[...], b2[...]).astype(BF16)
    for lo in range(0, hidden, 256):
        columns = slice(lo, lo + 256)
        u = project(c_ref[...], fc1[:, columns]) + fc1_bias[:, columns]
        below = 0.5 * (1.0 + erf(u * (1.0 / math.sqrt(2.0))))
        z = (u * below).astype(BF16)
        z_ref[:, columns] = z
        slope_ref[:, columns] = below + u * jnp.exp(-0.5 * u * u) * (1.0 / math.sqrt(2.0 * math.pi))
        y = project(z, fc2[columns, :])
        if lo:
            y_ref[...] += y
        else:
            y_ref[...] = y
        if pump is not None and lo % 512 == 256:
            pump(1)
    for lo, hi in row_cuts(length, 304):
        rows = slice(lo, hi)
        y = h_ref[rows, :] + y_ref[rows, :] + fc2_bias[...]
        y_ref[rows, :] = y
        out_ref[rows, :] = layer_norm(y, gf[...], bf[...]).astype(BF16)


def back_finish_body(d_ref, y_ref, slope_ref, h_ref, gf, fc2, fc1, g2, proj,
                     two_ref, du_ref, dh_ref, one_ref, do_ref, s_gf, s_bf, s_fc2, s_fc1, s_g2, s_b2, s_proj, dc_ref,
                     pump=None):
    length, hidden = slope_ref.shape
    for n, (lo, hi) in enumerate(row_cuts(length, 304)):
        rows = slice(lo, hi)
        dy, gain, shift = norm_back(d_ref[rows, :].astype(F32), y_ref[rows, :], gf[...])
        dh_ref[rows, :] = dy
        two = dy.astype(BF16)
        two_ref[rows, :] = two
        collect(n, (s_gf, gain), (s_bf, shift), (s_fc2, line_sum(two)))
    for lo in range(0, hidden, 256):
        columns = slice(lo, lo + 256)
        du = (project_back(two_ref[...], fc2[columns, :]) * slope_ref[:, columns]).astype(BF16)
        du_ref[:, columns] = du
        s_fc1[:, columns] = line_sum(du)
        dc = project_back(du, fc1[:, columns])
        if lo:
            dc_ref[...] += dc
        else:
            dc_ref[...] = dc
        if pump is not None:
            pump(1)
    for n, (lo, hi) in enumerate(row_cuts(length, 304)):
        rows = slice(lo, hi)
        part, gain, shift = norm_back(dc_ref[rows, :], h_ref[rows, :], g2[...])
        dh = dh_ref[rows, :] + part
        dh_ref[rows, :] = dh
        one = dh.astype(BF16)
        one_ref[rows, :] = one
        collect(n, (s_g2, gain), (s_b2, shift), (s_proj, line_sum(one)))
    do_ref[...] = project_back(one_ref[...], proj[...]).astype(BF16)


def collect(n, *pairs):
    for ref, value in pairs:
        ref[...] = ref[...] + value if n else value


def leave_encoder_body(d_ref, x_ref, dh_ref, g1, weight, low_ref, s_qv, s_g1, s_b1, s_first):
    d = d_ref[...]
    part, gain, shift = norm_back(project_back(d, weight[...]), x_ref[...], g1[...])
    dx = dh_ref[...] + part
    low_ref[...] = dx.astype(BF16)
    s_qv[:, :D_ENC] = line_sum(d[:, :D_ENC])
    s_qv[:, D_ENC:] = line_sum(d[:, 2 * D_ENC :])
    s_g1[...] = gain
    s_b1[...] = shift
    s_first[...] = line_sum(dx)


def leave_decoder_body(d_ref, x_ref, dh_ref, chosen_ref, kept_ref, g1, weight, first,
                       low_ref, sent_ref, s_qv, s_g1, s_b1, s_mask, s_first, da_ref, dx_ref):
    da_ref[...] = project_back(d_ref[...], weight[...])
    for n, (lo, hi) in enumerate(row_cuts(SEQ, 304)):
        rows = slice(lo, hi)
        part, gain, shift = norm_back(da_ref[rows, :], x_ref[rows, :], g1[...])
        dx = dh_ref[rows, :] + part
        dx_ref[rows, :] = dx.astype(BF16)
        kept_rows = kept_ref[rows, :]
        collect(
            n,
            (s_g1, gain),
            (s_b1, shift),
            (s_mask, line_sum(dx * (1.0 - kept_rows))),
            (s_first, line_sum(dx * kept_rows)),
        )
    s_qv[:, :D_DEC] = line_sum(d_ref[:, :D_DEC])
    s_qv[:, D_DEC:] = line_sum(d_ref[:, 2 * D_DEC :])
    low = project(chosen_ref[...], dx_ref[...]).astype(BF16)
    low_ref[...] = low
    sent_ref[...] = project_back(low, first[...]).astype(BF16)


def head_mask(size, h):
    lane = lax.broadcasted_iota(jnp.int32, (1, LANES), 1)
    return (lane >= h * size) & (lane < (h + 1) * size)


def head_mask(size, h):
    lane = lax.broadcasted_iota(jnp.int32, (1, LANES), 1)
    return (lane >= h * size) & (lane < (h + 1) * size)


def row_cuts(length, step):
    return [(lo, min(lo + step, length)) for lo in range(0, length, step)]


def mix_heads(q_ref, k_ref, v_ref, out_ref, size):
    keys, values = k_ref[...].T, v_ref[...]
    for lo, hi in row_cuts(q_ref.shape[0], 304):
        total = jnp.zeros((hi - lo, LANES), F32)
        for h in range(LANES // size):
            mask = head_mask(size, h)
            query = jnp.where(mask, q_ref[lo:hi, :], jnp.zeros((), BF16))
            scores = project(query, keys)
            power = jnp.exp2((scores - jnp.max(scores, -1, keepdims=True)) * (size ** (-0.5) * LOG2E))
            probs = power * (1.0 / jnp.sum(power, -1, keepdims=True))
            mixed = project(probs.astype(BF16), values)
            total = jnp.where(mask, mixed, total)
        out_ref[lo:hi, :] = total.astype(BF16)


def attention(qkv, heads):
    length, width = qkv.shape[0], qkv.shape[1] // 3
    size = width // heads
    groups = width // LANES

    def kernel(q_ref, k_ref, v_ref, out_ref):
        mix_heads(q_ref, k_ref, v_ref, out_ref, size)

    def spec(offset):
        return pl.BlockSpec((length, LANES), lambda g: (0, g + offset))

    return pl.pallas_call(
        kernel,
        out_shape=jax.ShapeDtypeStruct((length, width), jnp.bfloat16),
        grid=(groups,),
        in_specs=[spec(0), spec(groups), spec(2 * groups)],
        out_specs=spec(0),
        compiler_params=pltpu.CompilerParams(vmem_limit_bytes=40 * 2**20),
        name=f"attention_{heads}",
    )(qkv, qkv, qkv)


def back_heads(q_ref, k_ref, v_ref, g_ref, dq_turned, size, pump=None):
    length, factor = q_ref.shape[0], size ** (-0.5)
    zero = jnp.zeros((), jnp.bfloat16)
    keys, values = k_ref[...], v_ref[...]
    keys_turned = keys.T
    cuts = row_cuts(length, 256)
    for n, (lo, hi) in enumerate(cuts):
        query_all, grad_all = q_ref[lo:hi, :], g_ref[lo:hi, :]
        query_turned, grad_turned = query_all.T, grad_all.T
        dk = dv = None
        for h in range(LANES // size):
            own = slice(h * size, (h + 1) * size)
            row = lax.broadcasted_iota(jnp.int32, (LANES, 1), 0)
            rows = (row >= h * size) & (row < (h + 1) * size)
            mask = head_mask(size, h)
            scores = project(keys, jnp.where(rows, query_turned, zero))
            power = jnp.exp2((scores - jnp.max(scores, 0, keepdims=True)) * (factor * LOG2E))
            probs = power * (1.0 / jnp.sum(power, 0, keepdims=True))
            d_probs = project(values, jnp.where(rows, grad_turned, zero))
            inner = jnp.sum(d_probs * probs, 0, keepdims=True)
            d_scores = (probs * (d_probs - inner)).astype(jnp.bfloat16)
            dv_h = project(probs.astype(jnp.bfloat16), jnp.where(mask, grad_all, zero))
            dk_h = project(d_scores, jnp.where(mask, query_all, zero))
            dv = dv_h if dv is None else dv + dv_h
            dk = dk_h if dk is None else dk + dk_h
            dq_turned[own, lo:hi] = project(keys_turned[own, :], d_scores)
        if n:
            dk_sum, dv_sum = dk_sum + dk, dv_sum + dv
        else:
            dk_sum, dv_sum = dk, dv
    return dq_turned[...].T * factor, dk_sum * factor, dv_sum


def head_body(one, final_ref, w_ref, bias_ref, pix_ref, valid_ref, low_ref, sums_ref, loss_ref, back_ref):
    for band in range(BANDS):
        columns = slice(band * PATCH_PIX, (band + 1) * PATCH_PIX)
        predicted = project(final_ref[...], w_ref[:, columns]) + bias_ref[:, columns]
        values = pix_ref[:, columns].astype(F32)
        centre = values - jnp.mean(values, -1, keepdims=True)
        target = centre * lax.rsqrt(jnp.mean(centre * centre, -1, keepdims=True) + EPS_NORM)
        misfit = predicted - target
        valid_misfit = valid_ref[...] * misfit
        collect(band, (loss_ref, line_sum(valid_misfit * misfit) * (one / (BANDS * PATCH_PIX))))
        grad = valid_misfit * (one * (2.0 / (BANDS * PATCH_PIX)))
        low = grad.astype(BF16)
        low_ref[:, columns] = low
        sums_ref[:, columns] = line_sum(grad)
        collect(band, (back_ref, project_back(low, w_ref[:, columns])))


def decoder_step(tiles, place, inverse, chosen, sent, kept, valid, pix, where, line_at, total_tiles, total_lines):
    matrices, vectors = layout(1)
    base, total = tile_bases(1)
    line = (SEQ, D_DEC)
    hidden = (SEQ, FF_DEC)
    inner = [
        ((SEQ, PATCH_DIM), BF16), (hidden, BF16), (hidden, BF16), ((SEQ, 3 * D_DEC), BF16), ((SEQ, 3 * D_DEC), BF16),
        ((KEEP, D_DEC), BF16), (hidden, F32), ((LANES, SEQ), F32),
    ]
    inner += [(line, BF16)] * 8 + [(line, F32)] * 5

    def kernel(place_ref, where_ref, line_ref, inverse_ref, tiles_ref, chosen_ref, turned_ref, sent_ref, kept_ref,
               valid_ref, pix_ref, pos_ref, codes_ref, scales_ref, loss_ref, d_sent, *refs):
        refs = list(refs)
        pred_low, z, du, qkv, dqkv, low, slope, turned = [refs.pop(0) for _ in range(8)]
        final, two, c, o, one, a, dx, do = [refs.pop(0) for _ in range(8)]
        x, h, y, dh, d = [refs.pop(0) for _ in range(5)]
        w = {name: refs.pop(0) for name, rows, columns in matrices}
        w.update({name: refs.pop(0) for name, length in vectors})
        g = {name: refs.pop(0) for name, length in vectors}
        pool, sem = refs.pop(0), refs.pop(0)
        work = refs
        left, right = work[:2]
        scales_ref[...] = jnp.zeros_like(scales_ref)
        size = D_DEC // H_DEC

        def fetch(t, carry):
            pltpu.make_async_copy(tiles_ref.at[place_ref[t]], pool.at[t], sem).start()
            return carry

        lax.fori_loop(0, USED[1], fetch, 0)
        pltpu.make_async_copy(tiles_ref.at[pl.ds(0, USED[1])], pool, sem).wait()
        cut_vectors(pool[total].astype(F32), [w[name] for name, length in vectors])
        for name, rows, columns in matrices:
            unpack_into(pool, None, base[name], w[name], left, right)
        names = (K_FIRST, K_FIRST_BIAS, K_MASK, K_G1, K_B1, K_QKV, K_QV_BIAS)
        enter_decoder_body(
            turned_ref, sent_ref, kept_ref, pos_ref, *[w[k] for k in names], x, a, qkv
        )
        spans = [
            [slice(part * D_DEC + n * LANES, part * D_DEC + (n + 1) * LANES) for part in range(3)]
            for n in range(D_DEC // LANES)
        ]
        for group in spans:
            mix_heads(*[qkv.at[:, span] for span in group], o.at[:, group[0]], size)
        names = (K_PROJ, K_PROJ_BIAS, K_G2, K_B2, K_FC1, K_FC1_BIAS, K_FC2, K_FC2_BIAS, K_GF, K_BF)
        finish_body(
            x, o, *[w[k] for k in names], h, c, z, slope, y, final
        )
        head_body(
            inverse_ref[0], final, w[K_HEAD], w[K_HEAD_BIAS], pix_ref, valid_ref,
            pred_low, g[K_HEAD_BIAS], loss_ref, d,
        )
        names = (K_GF, K_BF, K_FC2_BIAS, K_FC1_BIAS, K_G2, K_B2, K_PROJ_BIAS)
        back_finish_body(
            d, y, slope, h, *[w[k] for k in (K_GF, K_FC2, K_FC1, K_G2, K_PROJ)],
            two, du, dh, one, do, *[g[k] for k in names], d,
        )
        for group in spans:
            parts = back_heads(*[qkv.at[:, span] for span in group], do.at[:, group[0]], turned, size)
            for span, value in zip(group, parts):
                dqkv[:, span] = value.astype(BF16)
        leave_decoder_body(
            dqkv, x, dh, chosen_ref, kept_ref, w[K_G1], w[K_QKV], w[K_FIRST], low, d_sent,
            *[g[k] for k in (K_QV_BIAS, K_G1, K_B1, K_MASK, K_FIRST_BIAS)], d, dx,
        )
        out = (where_ref, line_ref, codes_ref, scales_ref, work)
        factors = ((sent_ref, low), (a, dqkv), (o, one), (c, du), (z, two), (final, pred_low))
        for (name, rows, columns), pair in zip(matrices, factors):
            codes_into(*pair, base[name], *out)
        vectors_into([g[name] for name, length in vectors], total, *out)

    vmem = pl.BlockSpec(memory_space=pltpu.VMEM)
    smem = pl.BlockSpec(memory_space=pltpu.SMEM)
    hbm = pl.BlockSpec(memory_space=pltpu.HBM)
    return pl.pallas_call(
        kernel,
        out_shape=[
            jax.ShapeDtypeStruct((total_tiles, TR, TC), jnp.int16),
            jax.ShapeDtypeStruct((total_lines, TC), F32),
            jax.ShapeDtypeStruct((1, PATCH_PIX), F32),
            jax.ShapeDtypeStruct((KEEP, D_ENC), BF16),
        ],
        in_specs=[smem] * 4 + [hbm] + [vmem] * 7,
        out_specs=[hbm] + [vmem] * 3,
        scratch_shapes=[pltpu.VMEM(*value) for value in inner]
        + [pltpu.VMEM((rows, columns), BF16) for name, rows, columns in matrices]
        + [pltpu.VMEM((1, length), F32) for name, length in vectors] * 2
        + [pltpu.VMEM((USED[1], TR, TC), BF16), pltpu.SemaphoreType.DMA]
        + CODE_WORK,
        compiler_params=pltpu.CompilerParams(vmem_limit_bytes=60 * 2**20),
        name="decoder_step",
    )(place, where, line_at, inverse, tiles, chosen, chosen.T, sent, kept, valid, pix, jnp.asarray(positions(D_DEC)))


def encoder_back(w, encoded, d_sent, xin, where, line_at, codes, scales):
    matrices, vectors = layout(0)
    base, total = tile_bases(0)
    line = (KEEP, D_ENC)
    inner = [((KEEP, FF_ENC), BF16), ((KEEP, 3 * D_ENC), BF16), ((LANES, KEEP), F32)]
    inner += [(line, BF16)] * 4 + [(line, F32)] * 2
    weights = (K_QKV, K_PROJ, K_FC1, K_FC2, K_G1, K_G2, K_GF)

    def kernel(where_ref, line_ref, codes_in, scales_in, x, a, qkv, o, h, c, z, slope, y, d_sent_ref, xin_ref, *refs):
        refs = list(refs)
        v = {name: refs.pop(0) for name in weights}
        codes_ref, scales_ref = refs.pop(0), refs.pop(0)
        du, dqkv, turned, two, one, do, low, dh, d = [refs.pop(0) for _ in range(9)]
        g = {name: refs.pop(0) for name, length in vectors}
        out = (where_ref, line_ref, codes_ref, scales_ref, refs)
        scales_ref[...] = scales_in[...]
        names = (K_GF, K_BF, K_FC2_BIAS, K_FC1_BIAS, K_G2, K_B2, K_PROJ_BIAS)
        back_finish_body(
            d_sent_ref, y, slope, h, *[v[k] for k in (K_GF, K_FC2, K_FC1, K_G2, K_PROJ)],
            two, du, dh, one, do, *[g[k] for k in names], d,
        )
        for n in range(D_ENC // LANES):
            group = [slice(part * D_ENC + n * LANES, part * D_ENC + (n + 1) * LANES) for part in range(3)]
            parts = back_heads(
                *[qkv.at[:, span] for span in group], do.at[:, group[0]], turned, D_ENC // H_ENC
            )
            for span, value in zip(group, parts):
                dqkv[:, span] = value.astype(BF16)
        leave_encoder_body(
            dqkv, x, dh, v[K_G1], v[K_QKV], low, *[g[k] for k in (K_QV_BIAS, K_G1, K_B1, K_FIRST_BIAS)]
        )
        factors = ((xin_ref, low), (a, dqkv), (o, one), (c, du), (z, two))
        for (name, rows, columns), pair in zip(matrices, factors):
            codes_into(*pair, base[name], *out)
        vectors_into([g[name] for name, length in vectors], total, *out)

    vmem = pl.BlockSpec(memory_space=pltpu.VMEM)
    smem = pl.BlockSpec(memory_space=pltpu.SMEM)
    hbm = pl.BlockSpec(memory_space=pltpu.HBM)
    operands = [*encoded[:9], d_sent, xin] + [w[name] for name in weights]
    return pl.pallas_call(
        kernel,
        out_shape=[jax.ShapeDtypeStruct(codes.shape, codes.dtype), jax.ShapeDtypeStruct(scales.shape, F32)],
        in_specs=[smem, smem, hbm] + [vmem] * (1 + len(operands)),
        out_specs=[hbm, vmem],
        scratch_shapes=[pltpu.VMEM(*value) for value in inner]
        + [pltpu.VMEM((1, length), F32) for name, length in vectors]
        + CODE_WORK,
        input_output_aliases={2: 0},
        compiler_params=pltpu.CompilerParams(vmem_limit_bytes=60 * 2**20),
        name="encoder_back",
    )(where, line_at, codes, scales, *operands)


class Spread:
    MOVES = {K_U: [(0, 0, 1)], K_V: [(0, 1, 0)], K_Z: [(1, 0, 0), (2, 0, 0), (3, 0, 0)]}

    def __init__(self, section, place, block_ref, all_ref, ways, cut, sems, first):
        self.section, self.place, self.at = section, place, neighbours(section, place)
        self.block_ref, self.all_ref, self.ways, self.cut, self.sems = block_ref, all_ref, ways, cut, sems
        self.count = block_ref.shape[0]
        self.copies, self.sides = {}, {}
        self.next_copy = self.next_side = first

    def rows(self, section, holder, way):
        start = (section * 16 + holder) * self.count + self.cut[way]
        return self.all_ref.at[pl.ds(start, self.cut[way + 1] - self.cut[way])]

    def source(self, way, origin):
        if origin == (0, 0, 0):
            return self.block_ref.at[pl.ds(self.cut[way], self.cut[way + 1] - self.cut[way])]
        return self.rows(self.section, self.at(*origin), way)

    def send(self, way, origin, move):
        copy = pltpu.make_async_remote_copy(
            src_ref=self.source(way, origin),
            dst_ref=self.rows(self.section, self.at(*origin), way),
            send_sem=self.sems[0].at[self.next_copy],
            recv_sem=self.sems[1].at[self.next_copy],
            device_id=(self.section, self.at(*move)),
            device_id_type=MESH,
        )
        copy.start()
        self.copies[way, self.moved(origin, move)] = (copy, self.next_copy)
        self.next_copy += 1

    def moved(self, origin, move):
        return tuple((o - m) % s for o, m, s in zip(origin, move, (4, 2, 2)))

    def side(self, way, origin):
        copy = pltpu.make_async_remote_copy(
            src_ref=self.source(way, origin),
            dst_ref=self.rows(self.section, self.at(*origin), way),
            send_sem=self.sems[2].at[self.next_side],
            recv_sem=self.sems[3].at[self.next_side],
            device_id=(1 - self.section, self.place),
            device_id_type=MESH,
        )
        copy.start()
        self.sides[way, origin] = (copy, self.next_side)
        self.next_side += 1

    def arrived(self, target, send_sem, recv_sem):
        pltpu.make_async_remote_copy(
            src_ref=target,
            dst_ref=target,
            send_sem=send_sem,
            recv_sem=recv_sem,
            device_id=(1 - self.section, self.place),
            device_id_type=MESH,
        ).wait_recv()

    def take(self, way, origin, dims):
        index = self.copies[way, origin][1]
        self.arrived(
            self.rows(self.section, self.at(*origin), way), self.sems[0].at[index], self.sems[1].at[index]
        )
        for dim in dims:
            for move in self.MOVES[dim]:
                self.send(way, origin, move)
        self.side(way, origin)

    def start(self):
        zero = (0, 0, 0)
        self.own = pltpu.make_async_copy(
            self.block_ref, self.all_ref.at[pl.ds((self.section * 16 + self.place) * self.count, self.count)], self.sems[4]
        )
        self.own.start()
        for turn in range(3):
            for way, dims in enumerate(self.ways):
                for move in self.MOVES[dims[turn]]:
                    self.send(way, zero, move)
        for way in range(len(self.ways)):
            self.side(way, zero)
        held = {way: [zero] for way in range(len(self.ways))}
        steps = []
        for turn in range(3):
            come = {}
            for way, dims in enumerate(self.ways):
                come[way] = [self.moved(o, m) for m in self.MOVES[dims[turn]] for o in held[way]]
                held[way] = held[way] + come[way]
            for i in range(max(len(v) for v in come.values())):
                for way, dims in enumerate(self.ways):
                    if i < len(come[way]):
                        steps.append(functools.partial(self.take, way, come[way][i], dims[turn + 1 :]))
        return steps

    def finish(self):
        self.own.wait()
        for copy, index in self.copies.values():
            copy.wait_send()
        for (way, origin), (copy, index) in self.sides.items():
            copy.wait_send()
            self.arrived(
                self.rows(1 - self.section, self.at(*origin), way), self.sems[2].at[index], self.sems[3].at[index]
            )


def greet(section, place):
    at = neighbours(section, place)
    barrier = pltpu.get_barrier_semaphore()
    peers = [(1 - section, place)]
    peers += [(section, at(*d)) for d in ((0, 0, 1), (0, 1, 0), (1, 0, 0), (2, 0, 0), (3, 0, 0))]
    for peer in peers:
        pl.semaphore_signal(barrier, inc=1, device_id=peer, device_id_type=MESH)
    pl.semaphore_wait(barrier, len(peers))


def spread_sems(copies, sides):
    return [
        pltpu.SemaphoreType.DMA((copies,)),
        pltpu.SemaphoreType.DMA((copies,)),
        pltpu.SemaphoreType.DMA((sides,)),
        pltpu.SemaphoreType.DMA((sides,)),
        pltpu.SemaphoreType.DMA,
    ]


FOUR_WAYS = ((K_Z, K_V, K_U), (K_Z, K_U, K_V), (K_V, K_Z, K_U), (K_U, K_Z, K_V))
ONE_WAY = ((K_Z, K_V, K_U),)


def unpack_into(pool, place_ref, base, weight_ref, left, right):
    rows, columns = weight_ref.shape
    wide = columns // TC
    many = groups_of(rows, wide)
    count = many * wide

    def group(g, carry):
        for j in range(count):
            index = base + g * count + j
            tile = pool[index if place_ref is None else place_ref[index]].astype(F32)
            left[j * TR : (j + 1) * TR, :] = tile[:, :LANES]
            right[j * TR : (j + 1) * TR, :] = tile[:, LANES:]
        rows_g = pl.ds(pl.multiple_of(g * many * TR, TR), many * TR)
        for j in range(wide):
            for n, lines in enumerate((left, right)):
                start = j * TC + n * LANES
                weight_ref[rows_g, start : start + LANES] = lines[pl.ds(j, many * TR, stride=wide), :].astype(BF16)
        return carry

    lax.fori_loop(0, rows // (many * TR), group, 0)


def cut_vectors(tile, refs):
    row = 0
    for ref in refs:
        for r in range(ref.shape[1] // TC):
            ref[:, r * TC : (r + 1) * TC] = tile[row : row + 1, :]
            row += 1


def tile_bases(section_id):
    matrices, vectors = layout(section_id)
    base, total = {}, 0
    for name, rows, columns in matrices:
        base[name] = total
        total += rows * columns // (TR * TC)
    return base, total


def gather_and_encode(early, late, place, xin, positions_kept, cid):
    n_early, n_late = early.shape[0], late.shape[0]
    matrices, vectors = layout(0)
    shapes = {name: (rows, columns) for name, rows, columns in matrices}
    lengths = dict(vectors)
    base, total = tile_bases(0)
    kept_weights = (K_QKV, K_PROJ, K_FC1, K_FC2)
    kept_vectors = (K_G1, K_G2, K_GF)
    line = (KEEP, D_ENC)
    hidden = (KEEP, FF_ENC)
    results = [
        (line, F32), (line, BF16), ((KEEP, 3 * D_ENC), BF16), (line, BF16), (line, F32), (line, BF16), (hidden, BF16),
        (hidden, F32), (line, F32), (line, BF16),
    ]

    def kernel(place_ref, early_ref, late_ref, xin_ref, pos_ref, late_all, *refs):
        refs = list(refs)
        out_w = {name: refs.pop(0) for name in kept_weights}
        out_v = {name: refs.pop(0) for name in kept_vectors}
        x, a, qkv, o, h, c, z, slope, y, sent = [refs.pop(0) for _ in results]
        pool = refs.pop(0)
        w = {name: refs.pop(0) for name, rows, columns in matrices}
        v = {name: refs.pop(0) for name, length in vectors}
        left, right = refs.pop(0), refs.pop(0)
        early_sems, late_sems, out_sem = refs[:5], refs[5:10], refs[10]
        section, at_dp = lax.axis_index(K_SECTION), lax.axis_index(K_DP)
        greet(section, at_dp)
        cut = [0, 3, 5, 7, n_early] if n_early == 8 else [0, 1, 2, 3, n_early]
        soon = Spread(section, at_dp, early_ref, pool, FOUR_WAYS, cut, early_sems, 0)
        for step in soon.start():
            step()
        later = Spread(section, at_dp, late_ref, late_all, ONE_WAY, [0, n_late], late_sems, 0)
        steps = later.start()
        soon.finish()

        def pump(count):
            for _ in range(min(count, len(steps))):
                steps.pop(0)()

        def unpack(name):
            unpack_into(pool, place_ref, base[name], w[name], left, right)
            if name in kept_weights:
                pltpu.make_async_copy(w[name], out_w[name], out_sem.at[kept_weights.index(name)]).start()

        cut_vectors(pool[place_ref[total]].astype(F32), [v[name] for name, length in vectors])
        for name in kept_vectors:
            out_v[name][...] = v[name][...]
        unpack(K_FIRST)
        unpack(K_QKV)
        pump(1)
        x[...] = project(xin_ref[...], w[K_FIRST][...]) + v[K_FIRST_BIAS][...] + pos_ref[...]
        start_block(x, slice(None), (v[K_G1], v[K_B1], w[K_QKV], v[K_QV_BIAS]), a, qkv)
        pump(1)
        for g in range(D_ENC // LANES):
            spans = [slice(part * D_ENC + g * LANES, part * D_ENC + (g + 1) * LANES) for part in range(3)]
            mix_heads(*[qkv.at[:, span] for span in spans], o.at[:, spans[0]], D_ENC // H_ENC)
        pump(2)
        unpack(K_PROJ)
        unpack(K_FC1)
        pump(2)
        unpack(K_FC2)
        pump(2)
        names = (K_PROJ, K_PROJ_BIAS, K_G2, K_B2, K_FC1, K_FC1_BIAS, K_FC2, K_FC2_BIAS, K_GF, K_BF)
        finish_body(x, o, *[w[name] if name in w else v[name] for name in names], h, c, z, slope, y, sent, pump)
        pump(len(steps))
        later.finish()
        for name in kept_weights:
            pltpu.make_async_copy(w[name], out_w[name], out_sem.at[kept_weights.index(name)]).wait()

    vmem, hbm = pl.BlockSpec(memory_space=pltpu.VMEM), pl.BlockSpec(memory_space=pltpu.HBM)
    shape = jax.ShapeDtypeStruct
    outs = pl.pallas_call(
        kernel,
        out_shape=[shape((32 * n_late, TR, TC), BF16)]
        + [shape(shapes[name], BF16) for name in kept_weights]
        + [shape((1, lengths[name]), F32) for name in kept_vectors]
        + [shape(*result) for result in results],
        in_specs=[pl.BlockSpec(memory_space=pltpu.SMEM), hbm, hbm, vmem, vmem],
        out_specs=[hbm] * (1 + len(kept_weights)) + [vmem] * (len(kept_vectors) + len(results)),
        scratch_shapes=[pltpu.VMEM((32 * n_early, TR, TC), BF16)]
        + [pltpu.VMEM(shapes[name], BF16) for name, rows, columns in matrices]
        + [pltpu.VMEM((1, length), F32) for name, length in vectors]
        + [pltpu.VMEM((12 * TR, LANES), F32)] * 2
        + spread_sems(60, 64)
        + spread_sems(15, 16)
        + [pltpu.SemaphoreType.DMA((len(kept_weights),))],
        compiler_params=pltpu.CompilerParams(
            collective_id=cid, has_side_effects=True, vmem_limit_bytes=60 * 2**20
        ),
        name="gather_and_encode",
    )(place, early, late, xin, positions_kept)
    late_all, outs = outs[0], outs[1:]
    weights = dict(zip(kept_weights + kept_vectors, outs))
    return late_all, weights, outs[len(weights) :]


def encode(w, xin, positions_kept):
    x, a, qkv = enter_encoder(xin, positions_kept, w)
    o = attention(qkv, H_ENC)
    return x, a, qkv, o, *finish_block(x, o, w, "encoder")


def local(pixels, keep_index, clear_mask, slot_tile, master, moment_one, moment_two):
    n_dp = lax.axis_size(K_DP)
    n_dev = 2 * n_dp
    section, place = lax.axis_index(K_SECTION), lax.axis_index(K_DP)
    me = section * n_dp + place
    slots = master.shape[1]
    turns = [-(-count // n_dev) for count in USED]
    per = sum(turns)
    starts = [0, turns[0] * n_dev]
    rows_each = PARTS_ROWS if n_dp == 16 else 8 * (-(-per // 8))

    pix = lax.dynamic_index_in_dim(pixels, section, 0, keepdims=False)[0]
    wide_pix = pix.astype(F32)
    keep = lax.dynamic_index_in_dim(keep_index, section, 0, keepdims=False)[0]
    clear = lax.dynamic_index_in_dim(clear_mask, section, 0, keepdims=False)[0]
    kept = jnp.any(keep[:, None] == jnp.arange(SEQ), axis=0).astype(jnp.float32)
    valid = clear.astype(jnp.float32) * (1.0 - kept)
    sums = jnp.concatenate(
        [
            jnp.sum(jnp.sum(wide_pix, 0).reshape(BANDS, PATCH_PIX), 1),
            jnp.sum(jnp.sum(wide_pix * wide_pix, 0).reshape(BANDS, PATCH_PIX), 1),
            jnp.sum(valid)[None],
        ]
    )
    sums = jnp.pad(sums, (0, 1024 - sums.shape[0])).reshape(8, 128)

    def order(table, start):
        used = (table < TILES).astype(jnp.int32)
        count = table.shape[0]
        before = (jnp.arange(count)[:, None] > jnp.arange(count)[None]).astype(jnp.int32)
        return used, jnp.sum(before * used[None], 1) + start

    table_own = slot_tile[0]
    used_own, order_own = order(table_own, starts[1] * section)
    used_mine = lax.dynamic_slice_in_dim(used_own, place * slots, slots)
    order_mine = lax.dynamic_slice_in_dim(order_own, place * slots, slots)
    goes = lax.rem(order_mine, n_dev)
    slot_for = jnp.sum(
        jnp.arange(slots)[None] * used_mine[None] * (goes[None] == jnp.arange(n_dev)[:, None]), 1
    ).astype(jnp.int32)
    dealt = pick_tiles(master[0], slot_for, jnp.bfloat16, "deal_weights")
    table_out = jnp.pad(table_own, (0, 1024 - table_own.shape[0])).reshape(8, 128)
    arrived, all_sums, all_tables = exchange("deal", 1, n_dp, [dealt], [sums, table_out])

    totals = jnp.sum(all_sums, 0).reshape(-1)
    pixel_count = n_dev * SEQ * PATCH_PIX
    band_mean = totals[:BANDS] / pixel_count
    band_scale = lax.rsqrt(totals[BANDS : 2 * BANDS] / pixel_count - band_mean * band_mean + EPS_BAND)
    valid_count = jnp.maximum(totals[2 * BANDS], 1.0)

    chosen = (keep[:, None] == jnp.arange(SEQ)).astype(BF16)
    mean_line = jnp.broadcast_to(band_mean[:, None], (BANDS, PATCH_PIX)).reshape(PATCH_DIM)
    scale_line = jnp.broadcast_to(band_scale[:, None], (BANDS, PATCH_PIX)).reshape(PATCH_DIM)
    xin = ((project(chosen, pix) - mean_line) * scale_line).astype(BF16)

    n_slots = table_own.shape[0]
    tables = jnp.stack([all_tables[s * n_dp].reshape(-1)[:n_slots] for s in range(2)])
    both = [order(tables[s], starts[s]) for s in range(2)]
    used_all = jnp.concatenate([b[0] for b in both])
    order_all = jnp.concatenate([b[1] for b in both])
    owner_all = jnp.arange(2 * n_slots) // slots
    held = jnp.arange(per) * n_dev + me
    match = used_all[None] * (order_all[None] == held[:, None])
    from_owner = jnp.sum(match * owner_all[None], 1).astype(jnp.int32)
    is_held = jnp.sum(match, 1)
    block = pick_tiles(arrived, from_owner, jnp.bfloat16, "hold_weights")
    where_tile = []
    line_tile = []
    source_tile = []
    for s in range(2):
        hit = tables[s][None] == jnp.arange(TILES)[:, None]
        rank = jnp.sum(hit * both[s][1][None], 1)
        device, turn = lax.rem(rank, n_dev), lax.div(rank, n_dev)
        where_tile.append((device * per + turn).astype(jnp.int32))
        source_tile.append((device * turns[s] + turn - (turns[0] if s else 0)).astype(jnp.int32))
        line_tile.append((device * rows_each + line_of(turn, n_dp)).astype(jnp.int32))

    positions_kept = jnp.dot(chosen.astype(F32), jnp.asarray(positions(D_ENC)), precision=lax.Precision.HIGHEST)
    early, late = block[: turns[0]], block[turns[0] :]
    if n_dp == 16:
        late_all, enc, encoded = gather_and_encode(early, late, source_tile[0], xin, positions_kept, 2)
    else:
        early_all, late_all = [lax.all_gather(lax.all_gather(part, K_DP), K_SECTION) for part in (early, late)]
        enc = unpack_section(early_all.reshape(-1, TR, TC), source_tile[0], 0)
        encoded = encode(enc, xin, positions_kept)
    codes, scales, loss_terms, d_sent = decoder_step(
        late_all.reshape(-1, TR, TC), source_tile[1], (1.0 / valid_count)[None], chosen, encoded[-1], kept[:, None],
        valid[:, None], pix, where_tile[1], line_tile[1], n_dev * per, n_dev * rows_each,
    )
    codes, scales = encoder_back(enc, encoded, d_sent, xin, where_tile[0], line_tile[0], codes, scales)
    loss = jnp.sum(loss_terms)

    if n_dp == 16:
        own_codes, own_scales = reduce_all(
            codes.reshape(2, n_dp, per, TR, TC), scales.reshape(2, n_dp, rows_each, TC), 3
        )
    else:
        wide = scales.reshape(n_dev, rows_each, TC)[:, :per]
        values = jnp.where(wide[:, :, None] > 0.0, codes.reshape(n_dev, per, TR, TC).astype(jnp.float32), 0.0)
        values = values * wide[:, :, None]
        values = lax.psum_scatter(values, (K_SECTION, K_DP), scatter_dimension=0, tiled=True)[0]
        top = jnp.max(jnp.abs(values), 1, keepdims=True)
        up = jnp.where(top > 0.0, 32766.0 / top, 0.0)
        own_codes = jnp.round(values * up).astype(jnp.int16)
        own_scales = jnp.pad(top[:, 0] * (1.0 / 32766.0), ((0, rows_each - per), (0, 0)))
    own_scale = own_scales[np.array([line_of(t, n_dp) for t in range(per)])]
    own = jnp.where(is_held[:, None, None] > 0, own_codes.astype(jnp.float32) * own_scale[:, None], 0.0)
    tail = jnp.stack([jnp.sum(own * own), loss])
    tail = jnp.pad(tail, (0, 1022)).reshape(8, 128)

    turn_for = jnp.sum(
        jnp.arange(per)[None] * is_held[None] * (from_owner[None] == jnp.arange(n_dev)[:, None]), 1
    ).astype(jnp.int32)
    codes_back = pick_tiles(own_codes, turn_for, jnp.int16, "deal_gradients")
    scales_back = own_scale[turn_for][:, None]
    codes_mine, scales_mine, tails = exchange("return", 4, n_dp, [codes_back, scales_back], [tail])
    totals = jnp.sum(tails, 0)[0]
    grad_norm = jnp.sqrt(totals[0])
    factor = jnp.minimum(1.0, CLIP_NORM / (grad_norm + 1e-06))
    master_new, first_new, second_new = adam(
        codes_mine, scales_mine, goes, used_mine, factor[None], master[0], moment_one[0], moment_two[0]
    )
    return master_new[None], first_new[None], second_new[None], totals[1][None], grad_norm[None]


def solution(mesh):
    return jax.shard_map(
        local,
        mesh=mesh,
        in_specs=(
            P(None, K_DP, None, None),
            P(None, K_DP, None),
            P(None, K_DP, None),
            P(K_SECTION, None),
            P(K_SECTION, K_DP, None, None),
            P(K_SECTION, K_DP, None, None),
            P(K_SECTION, K_DP, None, None),
        ),
        out_specs=(
            P(K_SECTION, K_DP, None, None),
            P(K_SECTION, K_DP, None, None),
            P(K_SECTION, K_DP, None, None),
            P(),
            P(),
        ),
        check_vma=False,
    )
```

```python
import functools
import math

import jax
import jax.numpy as jnp
import numpy as np
from jax import lax
from jax.experimental import pallas as pl
from jax.experimental.pallas import tpu as pltpu
from jax.sharding import PartitionSpec as P

D_ENC = 768
H_ENC = 12
FF_ENC = 3072
D_DEC = 512
H_DEC = 16
FF_DEC = 2048
BANDS = 6
PATCH_PIX = 256
PATCH_DIM = 1536
SEQ = 588
KEEP = 147
STEP = 5
TILES = 256
USED = (253, 133)

EPS_NORM = 1e-06
EPS_BAND = 1e-05
CLIP_NORM = 0.001
RATE = 0.02
DECAY = 0.05
BETA_ONE = 0.5
BETA_TWO = 0.75
ADAM_EPS = 1e-08

K_SECTION = "section"
K_FIRST_BIAS = "first_bias"
K_PROJ_BIAS = "proj_bias"
K_FC2_BIAS = "fc2_bias"
K_FC1_BIAS = "fc1_bias"
K_FIRST = "first"
K_QV_BIAS = "qv_bias"
K_QKV = "qkv"
K_PROJ = "proj"
K_DP = "dp"
K_FC1 = "fc1"
K_FC2 = "fc2"
K_HEAD_BIAS = "head_bias"
K_GF = "gf"
K_G2 = "g2"
K_G1 = "g1"
K_MASK = "mask"
K_HEAD = "head"
K_BF = "bf"
K_B1 = "b1"
K_B2 = "b2"
K_U = "u"
K_V = "v"
K_Z = "z"

MESH = pl.DeviceIdType.MESH
TR, TC = 128, 256
PARTS = ((0, 6), (6, 11), (11, 13))
PARTS_ROWS = 24


def neighbours(section, place):
    x, y, z = lax.rem(place, 2), lax.rem(lax.div(place, 2), 2), lax.div(place, 4)

    def at(dz, dv, du):
        dx = (1 - section) * du + section * dv
        dy = (1 - section) * dv + section * du
        return lax.rem(z + dz, 4) * 4 + lax.rem(y + dy, 2) * 2 + lax.rem(x + dx, 2)

    return at


class Direct:
    def __init__(self, n_dp, pairs, sems):
        self.section, self.place = lax.axis_index(K_SECTION), lax.axis_index(K_DP)
        self.n_dp, self.n_dev, self.pairs, self.sems = n_dp, 2 * n_dp, pairs, sems
        self.me = self.section * n_dp + self.place

    def who(self, step):
        other = lax.rem(self.me + step, self.n_dev)
        return other, (lax.div(other, self.n_dp), lax.rem(other, self.n_dp))

    def greet(self):
        barrier = pltpu.get_barrier_semaphore()

        def one(step, carry):
            pl.semaphore_signal(barrier, inc=1, device_id=self.who(step)[1], device_id_type=MESH)
            return carry

        lax.fori_loop(1, self.n_dev, one, 0)
        pl.semaphore_wait(barrier, self.n_dev - 1)

    def own(self, which):
        source, dealt, target = self.pairs[which]
        return pltpu.make_async_copy(source.at[self.me] if dealt else source, target.at[self.me], self.sems[2].at[which])

    def copy(self, which, step):
        source, dealt, target = self.pairs[which]
        other, place_of = self.who(step)
        return pltpu.make_async_remote_copy(
            src_ref=source.at[other] if dealt else source,
            dst_ref=target.at[self.me],
            send_sem=self.sems[0].at[which, step],
            recv_sem=self.sems[1].at[which, step],
            device_id=place_of,
            device_id_type=MESH,
        )

    def start(self):
        for which in range(len(self.pairs)):
            self.own(which).start()

        def one(step, carry):
            for which in reversed(range(len(self.pairs))):
                self.copy(which, step).start()
            return carry

        lax.fori_loop(1, self.n_dev, one, 0)

    def finish(self):
        def one(step, carry):
            for which in range(len(self.pairs)):
                self.copy(which, step).wait()
            return carry

        lax.fori_loop(1, self.n_dev, one, 0)
        for which in range(len(self.pairs)):
            self.own(which).wait()


def direct_sems(n_pairs, n_dev):
    return [
        pltpu.SemaphoreType.DMA((n_pairs, n_dev)),
        pltpu.SemaphoreType.DMA((n_pairs, n_dev)),
        pltpu.SemaphoreType.DMA((n_pairs,)),
    ]


def exchange(name, cid, n_dp, dealt, shared):
    n_dev = 2 * n_dp
    arrays = list(dealt) + list(shared)
    count = len(arrays)

    def kernel(*refs):
        pairs = [(refs[n], n < len(dealt), refs[count + n]) for n in range(count)]
        direct = Direct(n_dp, pairs, refs[2 * count :])
        direct.greet()
        direct.start()
        direct.finish()

    shapes = [jax.ShapeDtypeStruct(a.shape, a.dtype) for a in dealt] + [
        jax.ShapeDtypeStruct((n_dev,) + a.shape, a.dtype) for a in shared
    ]
    any_spec = pl.BlockSpec(memory_space=pltpu.HBM)
    return pl.pallas_call(
        kernel,
        out_shape=shapes,
        in_specs=[any_spec] * count,
        out_specs=[any_spec] * count,
        scratch_shapes=direct_sems(count, n_dev),
        compiler_params=pltpu.CompilerParams(collective_id=cid, has_side_effects=True),
        name=name,
    )(*arrays)


def line_of(turn, n_dp):
    if n_dp != 16:
        return turn
    return turn + 2 * (turn >= PARTS[0][1]) + 3 * (turn >= PARTS[1][1])


def code(values):
    top = jnp.max(jnp.abs(values), axis=0, keepdims=True)
    up = jnp.where(top > 0.0, 32766.0 / top, 0.0)
    scaled = values * up
    return (scaled + jnp.where(scaled >= 0.0, 0.5, -0.5)).astype(jnp.int32).astype(jnp.int16), top * (1.0 / 32766.0)


def reduce_and_return(codes, scales, turn_for, held, loss, cid):
    per = codes.shape[2]

    def kernel(turn_ref, held_ref, codes_ref, scales_ref, loss_ref, out_ref, outs_ref, tails_ref, acc, accs, rc, rcs,
               r_code, r_scale, stage, stages, tail, own_sem, owns_sem, c_send, c_recv, p_send, p_recv, *direct_refs):
        section, place = lax.axis_index(K_SECTION), lax.axis_index(K_DP)
        at, at_other = neighbours(section, place), neighbours(1 - section, place)
        sibling = (1 - section, place)
        to_u, to_v = (section, at(0, 0, 1)), (section, at(0, 1, 0))

        def to_z(dz):
            return (section, at(dz, 0, 0))

        direct = Direct(16, [(stage, True, out_ref), (stages, True, outs_ref), (tail, False, tails_ref)], direct_refs)
        order = [(dz, dv, du) for dz in (2, 1, 3, 0) for dv in (1, 0) for du in (1, 0)]
        loads = {}
        for n, d in enumerate(order):
            b = at(*d)
            loads[d] = (
                pltpu.make_async_copy(codes_ref.at[section, b], acc.at[b], own_sem.at[n]),
                pltpu.make_async_copy(scales_ref.at[section, b], accs.at[b], owns_sem.at[n]),
            )
            for copy in loads[d]:
                copy.start()
        direct.greet()
        crossing = {}
        for n, d in enumerate(order):
            b = at_other(*d)
            pair = []
            for k, (source, target) in enumerate(((codes_ref, rc), (scales_ref, rcs))):
                copy = pltpu.make_async_remote_copy(
                    src_ref=source.at[1 - section, b],
                    dst_ref=target.at[b],
                    send_sem=c_send.at[k, n],
                    recv_sem=c_recv.at[k, n],
                    device_id=sibling,
                    device_id_type=MESH,
                )
                copy.start()
                pair.append(copy)
            crossing[d] = pair

        def add(b, part, from_code, from_first, from_scale, from_row):
            first, count = PARTS[part][0], PARTS[part][1] - PARTS[part][0]

            def one(t, carry):
                line = pl.ds(8 * part + t, 1)
                mine = acc[b, first + t].astype(jnp.float32) * accs[b, line, :]
                theirs = from_code[from_first + t].astype(jnp.float32) * from_scale[pl.ds(from_row + t, 1), :]
                value, scale = code(mine + theirs)
                acc[b, first + t] = value
                accs[b, line, :] = scale
                return carry

            lax.fori_loop(0, count, one, 0)

        sends = {}
        used = [0, 0]

        def send(part, key, b, peer):
            t0, t1 = PARTS[part]
            slot, index = used
            used[0] += t1 - t0
            used[1] += 1
            pair = []
            for k, (source, target) in enumerate(
                (
                    (acc.at[b, pl.ds(t0, t1 - t0)], r_code.at[pl.ds(slot, t1 - t0)]),
                    (accs.at[b, pl.ds(8 * part, 8)], r_scale.at[index]),
                )
            ):
                copy = pltpu.make_async_remote_copy(
                    src_ref=source,
                    dst_ref=target,
                    send_sem=p_send.at[k, index],
                    recv_sem=p_recv.at[k, index],
                    device_id=peer,
                    device_id_type=MESH,
                )
                copy.start()
                pair.append(copy)
            sends[part, key] = (pair, slot, index)

        def take(part, key, b):
            pair, slot, index = sends[part, key]
            for copy in pair:
                copy.wait_recv()
            add(b, part, r_code, slot, r_scale.at[index], 0)

        seen = set()

        def ready(d):
            if d not in seen:
                seen.add(d)
                for copy in loads[d]:
                    copy.wait()
                for copy in crossing[d]:
                    copy.wait_recv()

        def first(dz, parts=(0, 1, 2)):
            for dv in (1, 0):
                for du in (1, 0):
                    b = at(dz, dv, du)
                    ready((dz, dv, du))
                    for part in parts:
                        add(b, part, rc.at[b], PARTS[part][0], rcs.at[b], 8 * part)
                        if part == 2 and dz:
                            send(2, ("1", dz, dv, du), b, to_z(dz))
                        if part < 2 and du:
                            send(part, ("1", dz, dv), b, to_u)

        def second(dz):
            for dv in (1, 0):
                for part in (0, 1):
                    b = at(dz, dv, 0)
                    take(part, ("1", dz, dv), b)
                    if dv:
                        send(part, ("2", dz), b, to_v)

        def third(dz):
            for part in (0, 1):
                b = at(dz, 0, 0)
                take(part, ("2", dz), b)
                if dz:
                    send(part, ("3", dz), b, to_z(dz))

        first(2)
        first(1)
        first(3, (2,))
        second(2)
        first(3, (0, 1))
        second(1)
        third(2)
        first(0, (2,))
        second(3)
        first(0, (0, 1))
        third(1)
        for du in (1, 0):
            for dv in (1, 0):
                b = at(0, dv, du)
                for dz in (1, 3, 2):
                    take(2, ("1", dz, dv, du), b)
                if du:
                    send(2, ("2", dv), b, to_u)
        third(3)
        second(0)
        for dv in (1, 0):
            b = at(0, dv, 0)
            take(2, ("2", dv), b)
            if dv:
                send(2, ("3",), b, to_v)
        third(0)
        for dz in (2, 1, 3):
            for part in (0, 1):
                take(part, ("3", dz), place)
        take(2, ("3",), place)
        squares = jnp.zeros((1, TC), jnp.float32)
        for t in range(per):
            value = acc[place, t].astype(jnp.float32) * accs[place, line_of(t, 16) : line_of(t, 16) + 1, :]
            squares = squares + jnp.sum(value * value, 0, keepdims=True) * held_ref[t]
        tail[...] = jnp.zeros_like(tail)
        tail[0:1, :] = squares[:, :128] + squares[:, 128:]
        tail[1:2, :] = loss_ref[:, :128] + loss_ref[:, 128:]

        def deal(e, carry):
            t = turn_ref[e]
            line = t + 2 * (t >= PARTS[0][1]).astype(jnp.int32) + 3 * (t >= PARTS[1][1]).astype(jnp.int32)
            stage[e] = acc[place, t]
            stages[e] = accs[place, pl.ds(line, 1), :]
            return carry

        lax.fori_loop(0, 32, deal, 0)
        direct.start()
        for pair in crossing.values():
            for copy in pair:
                copy.wait_send()
        for pair, slot, index in sends.values():
            for copy in pair:
                copy.wait_send()
        direct.finish()

    n_tiles = 15 * per
    n_copies = 45
    hbm = pl.BlockSpec(memory_space=pltpu.HBM)
    vmem = pl.BlockSpec(memory_space=pltpu.VMEM)
    smem = pl.BlockSpec(memory_space=pltpu.SMEM)
    return pl.pallas_call(
        kernel,
        out_shape=(
            jax.ShapeDtypeStruct((32, TR, TC), jnp.int16),
            jax.ShapeDtypeStruct((32, 1, TC), jnp.float32),
            jax.ShapeDtypeStruct((32, 8, 128), jnp.float32),
        ),
        in_specs=[smem, smem, hbm, hbm, vmem],
        out_specs=(hbm, hbm, hbm),
        scratch_shapes=[
            pltpu.VMEM((16, per, TR, TC), jnp.int16),
            pltpu.VMEM((16, PARTS_ROWS, TC), jnp.float32),
            pltpu.VMEM((16, per, TR, TC), jnp.int16),
            pltpu.VMEM((16, PARTS_ROWS, TC), jnp.float32),
            pltpu.VMEM((n_tiles, TR, TC), jnp.int16),
            pltpu.VMEM((n_copies, 8, TC), jnp.float32),
            pltpu.VMEM((32, TR, TC), jnp.int16),
            pltpu.VMEM((32, 1, TC), jnp.float32),
            pltpu.VMEM((8, 128), jnp.float32),
            pltpu.SemaphoreType.DMA((16,)),
            pltpu.SemaphoreType.DMA((16,)),
            pltpu.SemaphoreType.DMA((2, 16)),
            pltpu.SemaphoreType.DMA((2, 16)),
            pltpu.SemaphoreType.DMA((2, n_copies)),
            pltpu.SemaphoreType.DMA((2, n_copies)),
        ]
        + direct_sems(3, 32),
        compiler_params=pltpu.CompilerParams(
            collective_id=cid, has_side_effects=True, vmem_limit_bytes=60 * 2**20
        ),
        name="reduce_tiles",
    )(turn_for, held, codes, scales, loss)


def layout(section_id):
    if section_id == 0:
        width, hidden = D_ENC, FF_ENC
        matrices = [(K_FIRST, PATCH_DIM, D_ENC)]
        vectors = [(K_FIRST_BIAS, D_ENC)]
    else:
        width, hidden = D_DEC, FF_DEC
        matrices = [(K_FIRST, D_ENC, D_DEC)]
        vectors = [(K_FIRST_BIAS, D_DEC), (K_MASK, D_DEC)]
    matrices = matrices + [
        (K_QKV, width, 3 * width),
        (K_PROJ, width, width),
        (K_FC1, width, hidden),
        (K_FC2, hidden, width),
    ]
    vectors = vectors + [
        (K_G1, width),
        (K_B1, width),
        (K_QV_BIAS, 2 * width),
        (K_PROJ_BIAS, width),
        (K_G2, width),
        (K_B2, width),
        (K_FC1_BIAS, hidden),
        (K_FC2_BIAS, width),
        (K_GF, width),
        (K_BF, width),
    ]
    if section_id == 1:
        matrices = matrices + [(K_HEAD, D_DEC, PATCH_DIM)]
        vectors = vectors + [(K_HEAD_BIAS, PATCH_DIM)]
    return matrices, vectors


def positions(width):
    place = np.arange(SEQ, dtype=np.float32)[:, None]
    rate = np.exp(np.arange(width // 2, dtype=np.float32) * np.float32(-2.0 * math.log(10000.0) / width))
    angle = (place * rate).astype(np.float32)
    return np.concatenate([np.sin(angle), np.cos(angle)], axis=1).astype(np.float32)


LANES = 128
LOG2E = math.log2(math.e)


def pick_tiles(tiles, index, dtype, name):
    count = index.shape[0]

    def kernel(index_ref, tiles_ref, out_ref):
        def one(t, carry):
            out_ref[t] = tiles_ref[index_ref[t]].astype(dtype)
            return carry

        lax.fori_loop(0, count, one, 0)

    return pl.pallas_call(
        kernel,
        out_shape=jax.ShapeDtypeStruct((count, TR, TC), dtype),
        in_specs=[pl.BlockSpec(memory_space=pltpu.SMEM), pl.BlockSpec(memory_space=pltpu.VMEM)],
        out_specs=pl.BlockSpec(memory_space=pltpu.VMEM),
        compiler_params=pltpu.CompilerParams(vmem_limit_bytes=40 * 2**20),
        name=name,
    )(index, tiles)


def groups_of(rows, wide):
    groups = rows // TR
    return max(m for m in range(1, groups + 1) if groups % m == 0 and (m == 1 or m * wide <= 12))


def unpack_matrix(tiles, place, base, rows, columns, name):
    wide = columns // TC
    many = groups_of(rows, wide)
    count = many * wide

    def kernel(place_ref, *refs):
        sources, out_ref, lines = refs[:count], refs[count], refs[count + 1 :]
        for j in range(count):
            for h in range(2):
                lines[h][j * TR : (j + 1) * TR, :] = sources[j][0, :, h * LANES : (h + 1) * LANES].astype(jnp.float32)
        for j in range(wide):
            for h in range(2):
                start = j * TC + h * LANES
                out_ref[:, start : start + LANES] = lines[h][pl.ds(j, many * TR, stride=wide), :].astype(tiles.dtype)

    def spec(j):
        return pl.BlockSpec((1, TR, TC), lambda g, place_ref: (place_ref[base + g * count + j], 0, 0))

    return pl.pallas_call(
        kernel,
        out_shape=jax.ShapeDtypeStruct((rows, columns), tiles.dtype),
        grid_spec=pltpu.PrefetchScalarGridSpec(
            num_scalar_prefetch=1,
            grid=(rows // (many * TR),),
            in_specs=[spec(j) for j in range(count)],
            out_specs=pl.BlockSpec((many * TR, columns), lambda g, place_ref: (g, 0)),
            scratch_shapes=[pltpu.VMEM((count * TR, LANES), jnp.float32)] * 2,
        ),
        compiler_params=pltpu.CompilerParams(vmem_limit_bytes=32 * 2**20),
        name="unpack_" + name,
    )(place, *([tiles] * count))


def codes_into(a_ref, d_ref, base, place_ref, line_ref, codes_ref, scales_ref, work):
    left, right, ready, sem = work
    rows, columns = a_ref.shape[1], d_ref.shape[1]
    wide = columns // TC
    many = groups_of(rows, wide)
    count = many * wide
    steps = rows // (many * TR)

    def drain(slot):
        pltpu.make_async_copy(codes_ref.at[pl.ds(0, count)], ready.at[slot, pl.ds(0, count)], sem.at[slot]).wait()

    def group(g, carry):
        slot = lax.rem(g, 2)

        @pl.when(g >= 2)
        def _():
            drain(slot)

        factor = a_ref[:, pl.ds(pl.multiple_of(g * many * TR, TR), many * TR)]
        for j in range(wide):
            part = weight_grad(factor, d_ref[:, j * TC : (j + 1) * TC])
            for h, lines in enumerate((left, right)):
                lines[pl.ds(j, many * TR, stride=wide), :] = part[:, h * LANES : (h + 1) * LANES]
        for j in range(count):
            tile = base + g * count + j
            code_tile(left, right, j, ready, slot, j, scales_ref, line_ref[tile])
            pltpu.make_async_copy(ready.at[slot, j], codes_ref.at[place_ref[tile]], sem.at[slot]).start()
        return carry

    lax.fori_loop(0, steps, group, 0)
    if steps > 1:
        drain(steps % 2)
    drain((steps - 1) % 2)


def code_tile(left, right, j, ready, slot, to, scales_ref, line):
    pair = []
    for h, lines in enumerate((left, right)):
        value, scale = code(lines[j * TR : (j + 1) * TR, :])
        ready[slot, to, :, h * LANES : (h + 1) * LANES] = value
        pair.append(scale)
    scales_ref[pl.ds(line, 1), :] = jnp.concatenate(pair, axis=1)


def vectors_into(values, tile, place_ref, line_ref, codes_ref, scales_ref, work):
    left, right, ready, sem = work
    row = 0
    for value in values:
        for r in range(value.shape[1] // TC):
            left[row : row + 1, :] = value[:, r * TC : r * TC + LANES]
            right[row : row + 1, :] = value[:, r * TC + LANES : (r + 1) * TC]
            row += 1
    for lines in (left, right):
        lines[row:TR, :] = jnp.zeros((TR - row, LANES), F32)
    code_tile(left, right, 0, ready, 0, 0, scales_ref, line_ref[tile])
    copy = pltpu.make_async_copy(ready.at[0, 0], codes_ref.at[place_ref[tile]], sem.at[0])
    copy.start()
    copy.wait()


CODE_WORK = [
    pltpu.VMEM((12 * TR, LANES), jnp.float32),
    pltpu.VMEM((12 * TR, LANES), jnp.float32),
    pltpu.VMEM((2, 12, TR, TC), jnp.int16),
    pltpu.SemaphoreType.DMA((2,)),
]


def unpack_vectors(tiles, place, base, lengths, name):
    def kernel(place_ref, tile_ref, *refs):
        row = 0
        for out_ref, length in zip(refs, lengths):
            for r in range(length // TC):
                out_ref[:, r * TC : (r + 1) * TC] = tile_ref[0, row : row + 1, :].astype(jnp.float32)
                row += 1

    return pl.pallas_call(
        kernel,
        out_shape=[jax.ShapeDtypeStruct((1, length), jnp.float32) for length in lengths],
        grid_spec=pltpu.PrefetchScalarGridSpec(
            num_scalar_prefetch=1,
            grid=(1,),
            in_specs=[pl.BlockSpec((1, TR, TC), lambda g, place_ref: (place_ref[base], 0, 0))],
            out_specs=[pl.BlockSpec((1, length), lambda g, place_ref: (0, 0)) for length in lengths],
        ),
        name="unpack_vectors_" + name,
    )(place, tiles)


def unpack_section(tiles, place, section_id):
    matrices, vectors = layout(section_id)
    found, base = {}, 0
    for name, rows, columns in matrices:
        found[name] = unpack_matrix(tiles, place, base, rows, columns, f"{name}_{section_id}")
        base += rows * columns // (TR * TC)
    lines = unpack_vectors(tiles, place, base, [length for name, length in vectors], str(section_id))
    found.update({name: line for (name, length), line in zip(vectors, lines)})
    return found


def adam(codes, scales, index, used, factor, master, first, second):
    slots = master.shape[0]
    per = 3 if slots % 3 == 0 else 1

    def kernel(index_ref, used_ref, factor_ref, codes_ref, scales_ref, w_ref, m_ref, v_ref, w_out, m_out, v_out):
        for t in range(per):
            slot = pl.program_id(0) * per + t
            source = index_ref[slot]
            grad = codes_ref[source].astype(jnp.float32) * scales_ref[source]
            grad = jnp.where(used_ref[slot] > 0, grad * factor_ref[0], 0.0)
            first_new = BETA_ONE * m_ref[t] + (1.0 - BETA_ONE) * grad
            second_new = BETA_TWO * v_ref[t] + (1.0 - BETA_TWO) * grad * grad
            ratio = (
                first_new
                / (1.0 - BETA_ONE ** float(STEP))
                / (jnp.sqrt(second_new / (1.0 - BETA_TWO ** float(STEP))) + ADAM_EPS)
            )
            w_out[t] = w_ref[t] - RATE * (ratio + DECAY * w_ref[t])
            m_out[t] = first_new
            v_out[t] = second_new

    smem = pl.BlockSpec(memory_space=pltpu.SMEM)
    block = pl.BlockSpec((per, TR, TC), lambda g: (g, 0, 0))
    return pl.pallas_call(
        kernel,
        out_shape=[jax.ShapeDtypeStruct(master.shape, jnp.float32)] * 3,
        grid=(slots // per,),
        in_specs=[
            smem,
            smem,
            smem,
            pl.BlockSpec(codes.shape, lambda g: (0, 0, 0)),
            pl.BlockSpec(scales.shape, lambda g: (0, 0, 0)),
            block,
            block,
            block,
        ],
        out_specs=[block] * 3,
        compiler_params=pltpu.CompilerParams(vmem_limit_bytes=40 * 2**20),
        name="adam",
    )(index, used, factor, codes, scales, master, first, second)


def project(a, w):
    return jnp.dot(a, w, preferred_element_type=jnp.float32)


def project_back(d, w):
    return lax.dot_general(d, w, (((1,), (1,)), ((), ())), preferred_element_type=jnp.float32)


def weight_grad(a, d):
    return lax.dot_general(a, d, (((0,), (0,)), ((), ())), preferred_element_type=jnp.float32)


def layer_norm(values, gain, offset):
    centre = values - jnp.mean(values, -1, keepdims=True)
    return centre * lax.rsqrt(jnp.mean(centre * centre, -1, keepdims=True) + EPS_NORM) * gain + offset


def norm_back(upstream, values, gain):
    centre = values - jnp.mean(values, -1, keepdims=True)
    spread = lax.rsqrt(jnp.mean(centre * centre, -1, keepdims=True) + EPS_NORM)
    normed = centre * spread
    scaled = upstream * gain
    downstream = spread * (
        scaled - jnp.mean(scaled, -1, keepdims=True) - normed * jnp.mean(scaled * normed, -1, keepdims=True)
    )
    return downstream, line_sum(upstream * normed), line_sum(upstream)


def line_sum(values):
    return jnp.sum(values.astype(jnp.float32), 0, keepdims=True)


ERF_TOP = (
    -2.72614225801306e-10,
    2.77068142495902e-08,
    -2.10102402082508e-06,
    -5.69250639462346e-05,
    -7.34990630326855e-04,
    -2.95459980854025e-03,
    -1.60960333262415e-02,
)
ERF_BOTTOM = (
    -1.45660718464996e-05,
    -2.13374055278905e-04,
    -1.68282697438203e-03,
    -7.37332916720468e-03,
    -1.42647390514189e-02,
)


def erf(x):
    x = jnp.clip(x, -4.0, 4.0)
    square = x * x
    top, bottom = jnp.full_like(x, ERF_TOP[0]), jnp.full_like(x, ERF_BOTTOM[0])
    for coefficient in ERF_TOP[1:]:
        top = top * square + coefficient
    for coefficient in ERF_BOTTOM[1:]:
        bottom = bottom * square + coefficient
    return x * top / bottom


def whole_kernel(kernel, shapes, operands, name, scratch=(), smem=0):
    vmem = pl.BlockSpec(memory_space=pltpu.VMEM)
    return pl.pallas_call(
        kernel,
        out_shape=[jax.ShapeDtypeStruct(shape, dtype) for shape, dtype in shapes],
        in_specs=[pl.BlockSpec(memory_space=pltpu.SMEM)] * smem + [vmem] * (len(operands) - smem),
        out_specs=[vmem] * len(shapes),
        scratch_shapes=scratch,
        compiler_params=pltpu.CompilerParams(vmem_limit_bytes=56 * 2**20),
        name=name,
    )(*operands)


F32, BF16 = jnp.float32, jnp.bfloat16


def start_block(x_ref, rows, w, a_ref, qkv_ref):
    g1, b1, weight, bias = w
    width = x_ref.shape[1]
    a = layer_norm(x_ref[rows, :], g1[...], b1[...]).astype(BF16)
    a_ref[rows, :] = a
    for part in range(3):
        columns = slice(part * width, (part + 1) * width)
        value = project(a, weight[:, columns])
        if part != 1:
            value = value + bias[:, (part // 2) * width : (part // 2 + 1) * width]
        qkv_ref[rows, columns] = value.astype(BF16)


def enter_encoder(xin, place, w):
    def kernel(xin_ref, place_ref, first, bias, g1, b1, weight, qv_bias, x_ref, a_ref, qkv_ref):
        x_ref[...] = project(xin_ref[...], first[...]) + bias[...] + place_ref[...]
        start_block(x_ref, slice(None), (g1, b1, weight, qv_bias), a_ref, qkv_ref)

    shapes = [((KEEP, D_ENC), F32), ((KEEP, D_ENC), BF16), ((KEEP, 3 * D_ENC), BF16)]
    operands = [xin, place] + [w[k] for k in (K_FIRST, K_FIRST_BIAS, K_G1, K_B1, K_QKV, K_QV_BIAS)]
    return whole_kernel(kernel, shapes, operands, "enter_encoder")


def enter_decoder_body(chosen_ref, sent_ref, kept_ref, place_ref, first, bias, mask, g1, b1, weight, qv_bias,
                       x_ref, a_ref, qkv_ref):
    for lo, hi in row_cuts(SEQ, 304):
        rows = slice(lo, hi)
        spread = project(chosen_ref[rows, :], sent_ref[...]).astype(BF16)
        placed = project(spread, first[...]) + bias[...]
        x_ref[rows, :] = jnp.where(kept_ref[rows, :] > 0.0, placed, mask[...]) + place_ref[rows, :]
        start_block(x_ref, rows, (g1, b1, weight, qv_bias), a_ref, qkv_ref)


def finish_block(x, attended, w, name):
    length, width = x.shape
    hidden = w[K_FC1].shape[1]

    line = (length, width)
    shapes = [(line, F32), (line, BF16), ((length, hidden), BF16), ((length, hidden), F32), (line, F32), (line, BF16)]
    names = (K_PROJ, K_PROJ_BIAS, K_G2, K_B2, K_FC1, K_FC1_BIAS, K_FC2, K_FC2_BIAS, K_GF, K_BF)
    return whole_kernel(finish_body, shapes, [x, attended] + [w[k] for k in names], "finish_" + name)


def finish_body(x_ref, o_ref, proj, proj_bias, g2, b2, fc1, fc1_bias, fc2, fc2_bias, gf, bf,
                h_ref, c_ref, z_ref, slope_ref, y_ref, out_ref, pump=None):
    length, hidden = z_ref.shape
    for lo, hi in row_cuts(length, 304):
        rows = slice(lo, hi)
        h = x_ref[rows, :] + project(o_ref[rows, :], proj[...]) + proj_bias[...]
        h_ref[rows, :] = h
        c_ref[rows, :] = layer_norm(h, g2[...], b2[...]).astype(BF16)
    for lo in range(0, hidden, 256):
        columns = slice(lo, lo + 256)
        u = project(c_ref[...], fc1[:, columns]) + fc1_bias[:, columns]
        below = 0.5 * (1.0 + erf(u * (1.0 / math.sqrt(2.0))))
        z = (u * below).astype(BF16)
        z_ref[:, columns] = z
        slope_ref[:, columns] = below + u * jnp.exp(-0.5 * u * u) * (1.0 / math.sqrt(2.0 * math.pi))
        y = project(z, fc2[columns, :])
        if lo:
            y_ref[...] += y
        else:
            y_ref[...] = y
        if pump is not None and lo % 512 == 256:
            pump(1)
    for lo, hi in row_cuts(length, 304):
        rows = slice(lo, hi)
        y = h_ref[rows, :] + y_ref[rows, :] + fc2_bias[...]
        y_ref[rows, :] = y
        out_ref[rows, :] = layer_norm(y, gf[...], bf[...]).astype(BF16)


def back_finish_body(d_ref, y_ref, slope_ref, h_ref, gf, fc2, fc1, g2, proj,
                     two_ref, du_ref, dh_ref, one_ref, do_ref, s_gf, s_bf, s_fc2, s_fc1, s_g2, s_b2, s_proj, dc_ref,
                     pump=None):
    length, hidden = slope_ref.shape
    for n, (lo, hi) in enumerate(row_cuts(length, 304)):
        rows = slice(lo, hi)
        dy, gain, shift = norm_back(d_ref[rows, :].astype(F32), y_ref[rows, :], gf[...])
        dh_ref[rows, :] = dy
        two = dy.astype(BF16)
        two_ref[rows, :] = two
        collect(n, (s_gf, gain), (s_bf, shift), (s_fc2, line_sum(two)))
    for lo in range(0, hidden, 256):
        columns = slice(lo, lo + 256)
        du = (project_back(two_ref[...], fc2[columns, :]) * slope_ref[:, columns]).astype(BF16)
        du_ref[:, columns] = du
        s_fc1[:, columns] = line_sum(du)
        dc = project_back(du, fc1[:, columns])
        if lo:
            dc_ref[...] += dc
        else:
            dc_ref[...] = dc
        if pump is not None:
            pump(1)
    for n, (lo, hi) in enumerate(row_cuts(length, 304)):
        rows = slice(lo, hi)
        part, gain, shift = norm_back(dc_ref[rows, :], h_ref[rows, :], g2[...])
        dh = dh_ref[rows, :] + part
        dh_ref[rows, :] = dh
        one = dh.astype(BF16)
        one_ref[rows, :] = one
        collect(n, (s_g2, gain), (s_b2, shift), (s_proj, line_sum(one)))
    do_ref[...] = project_back(one_ref[...], proj[...]).astype(BF16)


def collect(n, *pairs):
    for ref, value in pairs:
        ref[...] = ref[...] + value if n else value


def leave_encoder_body(d_ref, x_ref, dh_ref, g1, weight, low_ref, s_qv, s_g1, s_b1, s_first):
    d = d_ref[...]
    part, gain, shift = norm_back(project_back(d, weight[...]), x_ref[...], g1[...])
    dx = dh_ref[...] + part
    low_ref[...] = dx.astype(BF16)
    s_qv[:, :D_ENC] = line_sum(d[:, :D_ENC])
    s_qv[:, D_ENC:] = line_sum(d[:, 2 * D_ENC :])
    s_g1[...] = gain
    s_b1[...] = shift
    s_first[...] = line_sum(dx)


def leave_decoder_body(d_ref, x_ref, dh_ref, chosen_ref, kept_ref, g1, weight, first,
                       low_ref, sent_ref, s_qv, s_g1, s_b1, s_mask, s_first, da_ref, dx_ref):
    da_ref[...] = project_back(d_ref[...], weight[...])
    for n, (lo, hi) in enumerate(row_cuts(SEQ, 304)):
        rows = slice(lo, hi)
        part, gain, shift = norm_back(da_ref[rows, :], x_ref[rows, :], g1[...])
        dx = dh_ref[rows, :] + part
        dx_ref[rows, :] = dx.astype(BF16)
        kept_rows = kept_ref[rows, :]
        collect(
            n,
            (s_g1, gain),
            (s_b1, shift),
            (s_mask, line_sum(dx * (1.0 - kept_rows))),
            (s_first, line_sum(dx * kept_rows)),
        )
    s_qv[:, :D_DEC] = line_sum(d_ref[:, :D_DEC])
    s_qv[:, D_DEC:] = line_sum(d_ref[:, 2 * D_DEC :])
    low = project(chosen_ref[...], dx_ref[...]).astype(BF16)
    low_ref[...] = low
    sent_ref[...] = project_back(low, first[...]).astype(BF16)


def head_mask(size, h):
    lane = lax.broadcasted_iota(jnp.int32, (1, LANES), 1)
    return (lane >= h * size) & (lane < (h + 1) * size)


def row_cuts(length, step):
    return [(lo, min(lo + step, length)) for lo in range(0, length, step)]


def mix_heads(q_ref, k_ref, v_ref, out_ref, size):
    keys, values = k_ref[...].T, v_ref[...]
    for lo, hi in row_cuts(q_ref.shape[0], 304):
        total = jnp.zeros((hi - lo, LANES), F32)
        for h in range(LANES // size):
            mask = head_mask(size, h)
            query = jnp.where(mask, q_ref[lo:hi, :], jnp.zeros((), BF16))
            scores = project(query, keys)
            power = jnp.exp2((scores - jnp.max(scores, -1, keepdims=True)) * (size ** (-0.5) * LOG2E))
            probs = power * (1.0 / jnp.sum(power, -1, keepdims=True))
            mixed = project(probs.astype(BF16), values)
            total = jnp.where(mask, mixed, total)
        out_ref[lo:hi, :] = total.astype(BF16)


def attention(qkv, heads):
    length, width = qkv.shape[0], qkv.shape[1] // 3
    size = width // heads
    groups = width // LANES

    def kernel(q_ref, k_ref, v_ref, out_ref):
        mix_heads(q_ref, k_ref, v_ref, out_ref, size)

    def spec(offset):
        return pl.BlockSpec((length, LANES), lambda g: (0, g + offset))

    return pl.pallas_call(
        kernel,
        out_shape=jax.ShapeDtypeStruct((length, width), jnp.bfloat16),
        grid=(groups,),
        in_specs=[spec(0), spec(groups), spec(2 * groups)],
        out_specs=spec(0),
        compiler_params=pltpu.CompilerParams(vmem_limit_bytes=40 * 2**20),
        name=f"attention_{heads}",
    )(qkv, qkv, qkv)


def back_heads(q_ref, k_ref, v_ref, g_ref, dq_turned, size, pump=None):
    length, factor = q_ref.shape[0], size ** (-0.5)
    zero = jnp.zeros((), jnp.bfloat16)
    keys, values = k_ref[...], v_ref[...]
    keys_turned = keys.T
    cuts = row_cuts(length, 256)
    for n, (lo, hi) in enumerate(cuts):
        query_all, grad_all = q_ref[lo:hi, :], g_ref[lo:hi, :]
        query_turned, grad_turned = query_all.T, grad_all.T
        dk = dv = None
        for h in range(LANES // size):
            own = slice(h * size, (h + 1) * size)
            row = lax.broadcasted_iota(jnp.int32, (LANES, 1), 0)
            rows = (row >= h * size) & (row < (h + 1) * size)
            mask = head_mask(size, h)
            scores = project(keys, jnp.where(rows, query_turned, zero))
            power = jnp.exp2((scores - jnp.max(scores, 0, keepdims=True)) * (factor * LOG2E))
            probs = power * (1.0 / jnp.sum(power, 0, keepdims=True))
            d_probs = project(values, jnp.where(rows, grad_turned, zero))
            inner = jnp.sum(d_probs * probs, 0, keepdims=True)
            d_scores = (probs * (d_probs - inner)).astype(jnp.bfloat16)
            dv_h = project(probs.astype(jnp.bfloat16), jnp.where(mask, grad_all, zero))
            dk_h = project(d_scores, jnp.where(mask, query_all, zero))
            dv = dv_h if dv is None else dv + dv_h
            dk = dk_h if dk is None else dk + dk_h
            dq_turned[own, lo:hi] = project(keys_turned[own, :], d_scores)
        if n:
            dk_sum, dv_sum = dk_sum + dk, dv_sum + dv
        else:
            dk_sum, dv_sum = dk, dv
    return dq_turned[...].T * factor, dk_sum * factor, dv_sum


def head_body(one, final_ref, w_ref, bias_ref, pix_ref, valid_ref, low_ref, sums_ref, loss_ref, back_ref):
    for band in range(BANDS):
        columns = slice(band * PATCH_PIX, (band + 1) * PATCH_PIX)
        predicted = project(final_ref[...], w_ref[:, columns]) + bias_ref[:, columns]
        values = pix_ref[:, columns].astype(F32)
        centre = values - jnp.mean(values, -1, keepdims=True)
        target = centre * lax.rsqrt(jnp.mean(centre * centre, -1, keepdims=True) + EPS_NORM)
        misfit = predicted - target
        valid_misfit = valid_ref[...] * misfit
        collect(band, (loss_ref, line_sum(valid_misfit * misfit) * (one / (BANDS * PATCH_PIX))))
        grad = valid_misfit * (one * (2.0 / (BANDS * PATCH_PIX)))
        low = grad.astype(BF16)
        low_ref[:, columns] = low
        sums_ref[:, columns] = line_sum(grad)
        collect(band, (back_ref, project_back(low, w_ref[:, columns])))


def decoder_step(tiles, place, inverse, chosen, sent, kept, valid, pix, where, line_at, total_tiles, total_lines):
    matrices, vectors = layout(1)
    base, total = tile_bases(1)
    line = (SEQ, D_DEC)
    hidden = (SEQ, FF_DEC)
    inner = [
        ((SEQ, PATCH_DIM), BF16), (hidden, BF16), (hidden, BF16), ((SEQ, 3 * D_DEC), BF16), ((SEQ, 3 * D_DEC), BF16),
        ((KEEP, D_DEC), BF16), (hidden, F32), ((LANES, SEQ), F32),
    ]
    inner += [(line, BF16)] * 8 + [(line, F32)] * 5

    def kernel(place_ref, where_ref, line_ref, inverse_ref, tiles_ref, chosen_ref, turned_ref, sent_ref, kept_ref,
               valid_ref, pix_ref, pos_ref, codes_ref, scales_ref, loss_ref, d_sent, *refs):
        refs = list(refs)
        pred_low, z, du, qkv, dqkv, low, slope, turned = [refs.pop(0) for _ in range(8)]
        final, two, c, o, one, a, dx, do = [refs.pop(0) for _ in range(8)]
        x, h, y, dh, d = [refs.pop(0) for _ in range(5)]
        w = {name: refs.pop(0) for name, rows, columns in matrices}
        w.update({name: refs.pop(0) for name, length in vectors})
        g = {name: refs.pop(0) for name, length in vectors}
        pool, sem = refs.pop(0), refs.pop(0)
        work = refs
        left, right = work[:2]
        scales_ref[...] = jnp.zeros_like(scales_ref)
        size = D_DEC // H_DEC

        def fetch(t, carry):
            pltpu.make_async_copy(tiles_ref.at[place_ref[t]], pool.at[t], sem).start()
            return carry

        lax.fori_loop(0, USED[1], fetch, 0)
        pltpu.make_async_copy(tiles_ref.at[pl.ds(0, USED[1])], pool, sem).wait()
        cut_vectors(pool[total].astype(F32), [w[name] for name, length in vectors])
        for name, rows, columns in matrices:
            unpack_into(pool, None, base[name], w[name], left, right)
        names = (K_FIRST, K_FIRST_BIAS, K_MASK, K_G1, K_B1, K_QKV, K_QV_BIAS)
        enter_decoder_body(
            turned_ref, sent_ref, kept_ref, pos_ref, *[w[k] for k in names], x, a, qkv
        )
        spans = [
            [slice(part * D_DEC + n * LANES, part * D_DEC + (n + 1) * LANES) for part in range(3)]
            for n in range(D_DEC // LANES)
        ]
        for group in spans:
            mix_heads(*[qkv.at[:, span] for span in group], o.at[:, group[0]], size)
        names = (K_PROJ, K_PROJ_BIAS, K_G2, K_B2, K_FC1, K_FC1_BIAS, K_FC2, K_FC2_BIAS, K_GF, K_BF)
        finish_body(
            x, o, *[w[k] for k in names], h, c, z, slope, y, final
        )
        head_body(
            inverse_ref[0], final, w[K_HEAD], w[K_HEAD_BIAS], pix_ref, valid_ref,
            pred_low, g[K_HEAD_BIAS], loss_ref, d,
        )
        names = (K_GF, K_BF, K_FC2_BIAS, K_FC1_BIAS, K_G2, K_B2, K_PROJ_BIAS)
        back_finish_body(
            d, y, slope, h, *[w[k] for k in (K_GF, K_FC2, K_FC1, K_G2, K_PROJ)],
            two, du, dh, one, do, *[g[k] for k in names], d,
        )
        for group in spans:
            parts = back_heads(*[qkv.at[:, span] for span in group], do.at[:, group[0]], turned, size)
            for span, value in zip(group, parts):
                dqkv[:, span] = value.astype(BF16)
        leave_decoder_body(
            dqkv, x, dh, chosen_ref, kept_ref, w[K_G1], w[K_QKV], w[K_FIRST], low, d_sent,
            *[g[k] for k in (K_QV_BIAS, K_G1, K_B1, K_MASK, K_FIRST_BIAS)], d, dx,
        )
        out = (where_ref, line_ref, codes_ref, scales_ref, work)
        factors = ((sent_ref, low), (a, dqkv), (o, one), (c, du), (z, two), (final, pred_low))
        for (name, rows, columns), pair in zip(matrices, factors):
            codes_into(*pair, base[name], *out)
        vectors_into([g[name] for name, length in vectors], total, *out)

    vmem = pl.BlockSpec(memory_space=pltpu.VMEM)
    smem = pl.BlockSpec(memory_space=pltpu.SMEM)
    hbm = pl.BlockSpec(memory_space=pltpu.HBM)
    return pl.pallas_call(
        kernel,
        out_shape=[
            jax.ShapeDtypeStruct((total_tiles, TR, TC), jnp.int16),
            jax.ShapeDtypeStruct((total_lines, TC), F32),
            jax.ShapeDtypeStruct((1, PATCH_PIX), F32),
            jax.ShapeDtypeStruct((KEEP, D_ENC), BF16),
        ],
        in_specs=[smem] * 4 + [hbm] + [vmem] * 7,
        out_specs=[hbm] + [vmem] * 3,
        scratch_shapes=[pltpu.VMEM(*value) for value in inner]
        + [pltpu.VMEM((rows, columns), BF16) for name, rows, columns in matrices]
        + [pltpu.VMEM((1, length), F32) for name, length in vectors] * 2
        + [pltpu.VMEM((USED[1], TR, TC), BF16), pltpu.SemaphoreType.DMA]
        + CODE_WORK,
        compiler_params=pltpu.CompilerParams(vmem_limit_bytes=60 * 2**20),
        name="decoder_step",
    )(place, where, line_at, inverse, tiles, chosen, chosen.T, sent, kept, valid, pix, jnp.asarray(positions(D_DEC)))


def encoder_back(w, encoded, d_sent, xin, where, line_at, codes, scales):
    matrices, vectors = layout(0)
    base, total = tile_bases(0)
    line = (KEEP, D_ENC)
    inner = [((KEEP, FF_ENC), BF16), ((KEEP, 3 * D_ENC), BF16), ((LANES, KEEP), F32)]
    inner += [(line, BF16)] * 4 + [(line, F32)] * 2
    weights = (K_QKV, K_PROJ, K_FC1, K_FC2, K_G1, K_G2, K_GF)

    def kernel(where_ref, line_ref, codes_in, scales_in, x, a, qkv, o, h, c, z, slope, y, d_sent_ref, xin_ref, *refs):
        refs = list(refs)
        v = {name: refs.pop(0) for name in weights}
        codes_ref, scales_ref = refs.pop(0), refs.pop(0)
        du, dqkv, turned, two, one, do, low, dh, d = [refs.pop(0) for _ in range(9)]
        g = {name: refs.pop(0) for name, length in vectors}
        out = (where_ref, line_ref, codes_ref, scales_ref, refs)
        scales_ref[...] = scales_in[...]
        names = (K_GF, K_BF, K_FC2_BIAS, K_FC1_BIAS, K_G2, K_B2, K_PROJ_BIAS)
        back_finish_body(
            d_sent_ref, y, slope, h, *[v[k] for k in (K_GF, K_FC2, K_FC1, K_G2, K_PROJ)],
            two, du, dh, one, do, *[g[k] for k in names], d,
        )
        for n in range(D_ENC // LANES):
            group = [slice(part * D_ENC + n * LANES, part * D_ENC + (n + 1) * LANES) for part in range(3)]
            parts = back_heads(
                *[qkv.at[:, span] for span in group], do.at[:, group[0]], turned, D_ENC // H_ENC
            )
            for span, value in zip(group, parts):
                dqkv[:, span] = value.astype(BF16)
        leave_encoder_body(
            dqkv, x, dh, v[K_G1], v[K_QKV], low, *[g[k] for k in (K_QV_BIAS, K_G1, K_B1, K_FIRST_BIAS)]
        )
        factors = ((xin_ref, low), (a, dqkv), (o, one), (c, du), (z, two))
        for (name, rows, columns), pair in zip(matrices, factors):
            codes_into(*pair, base[name], *out)
        vectors_into([g[name] for name, length in vectors], total, *out)

    vmem = pl.BlockSpec(memory_space=pltpu.VMEM)
    smem = pl.BlockSpec(memory_space=pltpu.SMEM)
    hbm = pl.BlockSpec(memory_space=pltpu.HBM)
    operands = [*encoded[:9], d_sent, xin] + [w[name] for name in weights]
    return pl.pallas_call(
        kernel,
        out_shape=[jax.ShapeDtypeStruct(codes.shape, codes.dtype), jax.ShapeDtypeStruct(scales.shape, F32)],
        in_specs=[smem, smem, hbm] + [vmem] * (1 + len(operands)),
        out_specs=[hbm, vmem],
        scratch_shapes=[pltpu.VMEM(*value) for value in inner]
        + [pltpu.VMEM((1, length), F32) for name, length in vectors]
        + CODE_WORK,
        input_output_aliases={2: 0},
        compiler_params=pltpu.CompilerParams(vmem_limit_bytes=60 * 2**20),
        name="encoder_back",
    )(where, line_at, codes, scales, *operands)


class Spread:
    MOVES = {K_U: [(0, 0, 1)], K_V: [(0, 1, 0)], K_Z: [(1, 0, 0), (2, 0, 0), (3, 0, 0)]}

    def __init__(self, section, place, block_ref, all_ref, ways, cut, sems, first):
        self.section, self.place, self.at = section, place, neighbours(section, place)
        self.block_ref, self.all_ref, self.ways, self.cut, self.sems = block_ref, all_ref, ways, cut, sems
        self.count = block_ref.shape[0]
        self.copies, self.sides = {}, {}
        self.next_copy = self.next_side = first

    def rows(self, section, holder, way):
        start = (section * 16 + holder) * self.count + self.cut[way]
        return self.all_ref.at[pl.ds(start, self.cut[way + 1] - self.cut[way])]

    def source(self, way, origin):
        if origin == (0, 0, 0):
            return self.block_ref.at[pl.ds(self.cut[way], self.cut[way + 1] - self.cut[way])]
        return self.rows(self.section, self.at(*origin), way)

    def send(self, way, origin, move):
        copy = pltpu.make_async_remote_copy(
            src_ref=self.source(way, origin),
            dst_ref=self.rows(self.section, self.at(*origin), way),
            send_sem=self.sems[0].at[self.next_copy],
            recv_sem=self.sems[1].at[self.next_copy],
            device_id=(self.section, self.at(*move)),
            device_id_type=MESH,
        )
        copy.start()
        self.copies[way, self.moved(origin, move)] = (copy, self.next_copy)
        self.next_copy += 1

    def moved(self, origin, move):
        return tuple((o - m) % s for o, m, s in zip(origin, move, (4, 2, 2)))

    def side(self, way, origin):
        copy = pltpu.make_async_remote_copy(
            src_ref=self.source(way, origin),
            dst_ref=self.rows(self.section, self.at(*origin), way),
            send_sem=self.sems[2].at[self.next_side],
            recv_sem=self.sems[3].at[self.next_side],
            device_id=(1 - self.section, self.place),
            device_id_type=MESH,
        )
        copy.start()
        self.sides[way, origin] = (copy, self.next_side)
        self.next_side += 1

    def arrived(self, target, send_sem, recv_sem):
        pltpu.make_async_remote_copy(
            src_ref=target,
            dst_ref=target,
            send_sem=send_sem,
            recv_sem=recv_sem,
            device_id=(1 - self.section, self.place),
            device_id_type=MESH,
        ).wait_recv()

    def take(self, way, origin, dims):
        index = self.copies[way, origin][1]
        self.arrived(
            self.rows(self.section, self.at(*origin), way), self.sems[0].at[index], self.sems[1].at[index]
        )
        for dim in dims:
            for move in self.MOVES[dim]:
                self.send(way, origin, move)
        self.side(way, origin)

    def start(self):
        zero = (0, 0, 0)
        self.own = pltpu.make_async_copy(
            self.block_ref, self.all_ref.at[pl.ds((self.section * 16 + self.place) * self.count, self.count)], self.sems[4]
        )
        self.own.start()
        for turn in range(3):
            for way, dims in enumerate(self.ways):
                for move in self.MOVES[dims[turn]]:
                    self.send(way, zero, move)
        for way in range(len(self.ways)):
            self.side(way, zero)
        held = {way: [zero] for way in range(len(self.ways))}
        steps = []
        for turn in range(3):
            come = {}
            for way, dims in enumerate(self.ways):
                come[way] = [self.moved(o, m) for m in self.MOVES[dims[turn]] for o in held[way]]
                held[way] = held[way] + come[way]
            for i in range(max(len(v) for v in come.values())):
                for way, dims in enumerate(self.ways):
                    if i < len(come[way]):
                        steps.append(functools.partial(self.take, way, come[way][i], dims[turn + 1 :]))
        return steps

    def finish(self):
        self.own.wait()
        for copy, index in self.copies.values():
            copy.wait_send()
        for (way, origin), (copy, index) in self.sides.items():
            copy.wait_send()
            self.arrived(
                self.rows(1 - self.section, self.at(*origin), way), self.sems[2].at[index], self.sems[3].at[index]
            )


def spread_sems(copies, sides):
    return [
        pltpu.SemaphoreType.DMA((copies,)),
        pltpu.SemaphoreType.DMA((copies,)),
        pltpu.SemaphoreType.DMA((sides,)),
        pltpu.SemaphoreType.DMA((sides,)),
        pltpu.SemaphoreType.DMA,
    ]


FOUR_WAYS = ((K_Z, K_V, K_U), (K_Z, K_U, K_V), (K_V, K_Z, K_U), (K_U, K_Z, K_V))
ONE_WAY = ((K_Z, K_V, K_U),)


def unpack_into(pool, place_ref, base, weight_ref, left, right):
    rows, columns = weight_ref.shape
    wide = columns // TC
    many = groups_of(rows, wide)
    count = many * wide

    def group(g, carry):
        for j in range(count):
            index = base + g * count + j
            tile = pool[index if place_ref is None else place_ref[index]].astype(F32)
            left[j * TR : (j + 1) * TR, :] = tile[:, :LANES]
            right[j * TR : (j + 1) * TR, :] = tile[:, LANES:]
        rows_g = pl.ds(pl.multiple_of(g * many * TR, TR), many * TR)
        for j in range(wide):
            for n, lines in enumerate((left, right)):
                start = j * TC + n * LANES
                weight_ref[rows_g, start : start + LANES] = lines[pl.ds(j, many * TR, stride=wide), :].astype(BF16)
        return carry

    lax.fori_loop(0, rows // (many * TR), group, 0)


def cut_vectors(tile, refs):
    row = 0
    for ref in refs:
        for r in range(ref.shape[1] // TC):
            ref[:, r * TC : (r + 1) * TC] = tile[row : row + 1, :]
            row += 1


def tile_bases(section_id):
    matrices, vectors = layout(section_id)
    base, total = {}, 0
    for name, rows, columns in matrices:
        base[name] = total
        total += rows * columns // (TR * TC)
    return base, total


def deal_and_encode(master, slot_for, from_owner, sums, chosen, pix, place, positions_kept, turns, cid):
    n_early, n_late = turns
    slots = master.shape[0]
    matrices, vectors = layout(0)
    shapes = {name: (rows, columns) for name, rows, columns in matrices}
    lengths = dict(vectors)
    base, total = tile_bases(0)
    kept_weights = (K_QKV, K_PROJ, K_FC1, K_FC2)
    kept_vectors = (K_G1, K_G2, K_GF)
    line = (KEEP, D_ENC)
    hidden = (KEEP, FF_ENC)
    results = [
        (line, F32), (line, BF16), ((KEEP, 3 * D_ENC), BF16), (line, BF16), (line, F32), (line, BF16), (hidden, BF16),
        (hidden, F32), (line, F32), (line, BF16),
    ]

    def kernel(slot_ref, owner_ref, place_ref, master_ref, sums_ref, chosen_ref, pix_ref, pos_ref,
               late_all, all_sums, xin_ref, *refs):
        refs = list(refs)
        out_w = {name: refs.pop(0) for name in kept_weights}
        out_v = {name: refs.pop(0) for name in kept_vectors}
        x, a, qkv, o, h, c, z, slope, y, sent = [refs.pop(0) for _ in results]
        pool = refs.pop(0)
        w = {name: refs.pop(0) for name, rows, columns in matrices}
        v = {name: refs.pop(0) for name, length in vectors}
        left, right = refs.pop(0), refs.pop(0)
        stage, arrived, early_ref, late_ref = refs[:4]
        early_sems, late_sems, out_sem, direct_refs = refs[4:9], refs[9:14], refs[14], refs[15:]
        section, at_dp = lax.axis_index(K_SECTION), lax.axis_index(K_DP)
        direct = Direct(16, [(stage, True, arrived), (sums_ref, False, all_sums)], direct_refs)

        def pick(e, carry):
            stage[e] = master_ref[slot_ref[e]].astype(BF16)
            return carry

        lax.fori_loop(0, 32, pick, 0)
        direct.greet()
        direct.start()
        seen = project(chosen_ref[...], pix_ref[...])
        direct.finish()
        for t in range(n_early):
            early_ref[t] = arrived[owner_ref[t]]
        for t in range(n_late):
            late_ref[t] = arrived[owner_ref[n_early + t]]
        cut = [0, 3, 5, 7, n_early] if n_early == 8 else [0, 1, 2, 3, n_early]
        soon = Spread(section, at_dp, early_ref, pool, FOUR_WAYS, cut, early_sems, 0)
        soon_steps = soon.start()
        for step in soon_steps:
            step()
        lines = jnp.sum(all_sums[...], 0)[0:1, :]
        lane = lax.broadcasted_iota(jnp.int32, (1, LANES), 1)
        for band in range(BANDS):
            columns = slice(band * PATCH_PIX, (band + 1) * PATCH_PIX)
            mean, square = [
                jnp.sum(jnp.where(lane == n, lines, 0.0), -1, keepdims=True) / (32 * SEQ * PATCH_PIX) for n in (band, BANDS + band)
            ]
            scale = lax.rsqrt(square - mean * mean + EPS_BAND)
            xin_ref[:, columns] = ((seen[:, columns] - mean) * scale).astype(BF16)
        later = Spread(section, at_dp, late_ref, late_all, ONE_WAY, [0, n_late], late_sems, 0)
        steps = later.start()
        soon.finish()

        def pump(count):
            for _ in range(min(count, len(steps))):
                steps.pop(0)()

        def unpack(name):
            unpack_into(pool, place_ref, base[name], w[name], left, right)
            if name in kept_weights:
                pltpu.make_async_copy(w[name], out_w[name], out_sem.at[kept_weights.index(name)]).start()

        cut_vectors(pool[place_ref[total]].astype(F32), [v[name] for name, length in vectors])
        for name in kept_vectors:
            out_v[name][...] = v[name][...]
        unpack(K_FIRST)
        unpack(K_QKV)
        pump(1)
        x[...] = project(xin_ref[...], w[K_FIRST][...]) + v[K_FIRST_BIAS][...] + pos_ref[...]
        start_block(x, slice(None), (v[K_G1], v[K_B1], w[K_QKV], v[K_QV_BIAS]), a, qkv)
        pump(1)
        for g in range(D_ENC // LANES):
            spans = [slice(part * D_ENC + g * LANES, part * D_ENC + (g + 1) * LANES) for part in range(3)]
            mix_heads(*[qkv.at[:, span] for span in spans], o.at[:, spans[0]], D_ENC // H_ENC)
        pump(2)
        unpack(K_PROJ)
        unpack(K_FC1)
        pump(2)
        unpack(K_FC2)
        pump(2)
        names = (K_PROJ, K_PROJ_BIAS, K_G2, K_B2, K_FC1, K_FC1_BIAS, K_FC2, K_FC2_BIAS, K_GF, K_BF)
        finish_body(x, o, *[w[name] if name in w else v[name] for name in names], h, c, z, slope, y, sent, pump)
        pump(len(steps))
        later.finish()
        for name in kept_weights:
            pltpu.make_async_copy(w[name], out_w[name], out_sem.at[kept_weights.index(name)]).wait()

    vmem, hbm = pl.BlockSpec(memory_space=pltpu.VMEM), pl.BlockSpec(memory_space=pltpu.HBM)
    shape = jax.ShapeDtypeStruct
    outs = pl.pallas_call(
        kernel,
        out_shape=[
            shape((32 * n_late, TR, TC), BF16), shape((32, 8, LANES), F32), shape((KEEP, PATCH_DIM), BF16)
        ]
        + [shape(shapes[name], BF16) for name in kept_weights]
        + [shape((1, lengths[name]), F32) for name in kept_vectors]
        + [shape(*result) for result in results],
        in_specs=[pl.BlockSpec(memory_space=pltpu.SMEM)] * 3 + [vmem] * 5,
        out_specs=[hbm] + [vmem] * 2 + [hbm] * len(kept_weights) + [vmem] * (len(kept_vectors) + len(results)),
        scratch_shapes=[pltpu.VMEM((32 * n_early, TR, TC), BF16)]
        + [pltpu.VMEM(shapes[name], BF16) for name, rows, columns in matrices]
        + [pltpu.VMEM((1, length), F32) for name, length in vectors]
        + [pltpu.VMEM((12 * TR, LANES), F32)] * 2
        + [pltpu.VMEM((32, TR, TC), BF16)] * 2
        + [pltpu.VMEM((n_early, TR, TC), BF16), pltpu.VMEM((n_late, TR, TC), BF16)]
        + spread_sems(60, 64)
        + spread_sems(15, 16)
        + [pltpu.SemaphoreType.DMA((len(kept_weights),))]
        + direct_sems(2, 32),
        compiler_params=pltpu.CompilerParams(
            collective_id=cid, has_side_effects=True, vmem_limit_bytes=60 * 2**20
        ),
        name="deal_and_encode",
    )(slot_for, from_owner, place, master, sums, chosen, pix, positions_kept)
    weights = dict(zip(kept_weights + kept_vectors, outs[3:]))
    return outs[0], outs[1], outs[2], weights, outs[3 + len(weights) :]


def encode(w, xin, positions_kept):
    x, a, qkv = enter_encoder(xin, positions_kept, w)
    o = attention(qkv, H_ENC)
    return x, a, qkv, o, *finish_block(x, o, w, "encoder")


def local(pixels, keep_index, clear_mask, slot_tile, master, moment_one, moment_two):
    n_dp = lax.axis_size(K_DP)
    n_dev = 2 * n_dp
    section, place = lax.axis_index(K_SECTION), lax.axis_index(K_DP)
    me = section * n_dp + place
    slots = master.shape[1]
    turns = [-(-count // n_dev) for count in USED]
    per = sum(turns)
    starts = [0, turns[0] * n_dev]
    rows_each = PARTS_ROWS if n_dp == 16 else 8 * (-(-per // 8))

    pix = lax.dynamic_index_in_dim(pixels, section, 0, keepdims=False)[0]
    wide_pix = pix.astype(F32)
    keep = lax.dynamic_index_in_dim(keep_index, section, 0, keepdims=False)[0]
    clear = lax.dynamic_index_in_dim(clear_mask, section, 0, keepdims=False)[0]
    kept = jnp.any(keep[:, None] == jnp.arange(SEQ), axis=0).astype(jnp.float32)
    valid = clear.astype(jnp.float32) * (1.0 - kept)
    sums = jnp.concatenate(
        [
            jnp.sum(jnp.sum(wide_pix, 0).reshape(BANDS, PATCH_PIX), 1),
            jnp.sum(jnp.sum(wide_pix * wide_pix, 0).reshape(BANDS, PATCH_PIX), 1),
            jnp.sum(valid)[None],
        ]
    )
    sums = jnp.pad(sums, (0, 1024 - sums.shape[0])).reshape(8, 128)

    def order(table, start):
        used = (table < TILES).astype(jnp.int32)
        count = table.shape[0]
        before = (jnp.arange(count)[:, None] > jnp.arange(count)[None]).astype(jnp.int32)
        return used, jnp.sum(before * used[None], 1) + start

    table_own = slot_tile[0]
    used_own, order_own = order(table_own, starts[1] * section)
    used_mine = lax.dynamic_slice_in_dim(used_own, place * slots, slots)
    order_mine = lax.dynamic_slice_in_dim(order_own, place * slots, slots)
    goes = lax.rem(order_mine, n_dev)
    slot_for = jnp.sum(
        jnp.arange(slots)[None] * used_mine[None] * (goes[None] == jnp.arange(n_dev)[:, None]), 1
    ).astype(jnp.int32)
    table_other = lax.ppermute(table_own, K_SECTION, [(0, 1), (1, 0)])
    tables = jnp.where(section == 0, jnp.stack([table_own, table_other]), jnp.stack([table_other, table_own]))
    n_slots = table_own.shape[0]
    both = [order(tables[s], starts[s]) for s in range(2)]
    used_all = jnp.concatenate([b[0] for b in both])
    order_all = jnp.concatenate([b[1] for b in both])
    owner_all = jnp.arange(2 * n_slots) // slots
    held = jnp.arange(per) * n_dev + me
    match = used_all[None] * (order_all[None] == held[:, None])
    from_owner = jnp.sum(match * owner_all[None], 1).astype(jnp.int32)
    is_held = jnp.sum(match, 1)
    turn_for = jnp.sum(
        jnp.arange(per)[None] * is_held[None] * (from_owner[None] == jnp.arange(n_dev)[:, None]), 1
    ).astype(jnp.int32)
    chosen = (keep[:, None] == jnp.arange(SEQ)).astype(BF16)

    where_tile = []
    line_tile = []
    source_tile = []
    for s in range(2):
        hit = tables[s][None] == jnp.arange(TILES)[:, None]
        rank = jnp.sum(hit * both[s][1][None], 1)
        device, turn = lax.rem(rank, n_dev), lax.div(rank, n_dev)
        where_tile.append((device * per + turn).astype(jnp.int32))
        source_tile.append((device * turns[s] + turn - (turns[0] if s else 0)).astype(jnp.int32))
        line_tile.append((device * rows_each + line_of(turn, n_dp)).astype(jnp.int32))

    positions_kept = jnp.dot(chosen.astype(F32), jnp.asarray(positions(D_ENC)), precision=lax.Precision.HIGHEST)
    if n_dp == 16:
        late_all, all_sums, xin, enc, encoded = deal_and_encode(
            master[0], slot_for, from_owner, sums, chosen, pix, source_tile[0], positions_kept, turns, 2
        )
        totals = jnp.sum(all_sums, 0).reshape(-1)
    else:
        dealt = pick_tiles(master[0], slot_for, BF16, "deal")
        arrived, all_sums = exchange("exchange", 1, n_dp, [dealt], [sums])
        totals = jnp.sum(all_sums, 0).reshape(-1)
        pixel_count = n_dev * SEQ * PATCH_PIX
        band_mean = totals[:BANDS] / pixel_count
        band_scale = lax.rsqrt(totals[BANDS : 2 * BANDS] / pixel_count - band_mean * band_mean + EPS_BAND)
        mean_line = jnp.broadcast_to(band_mean[:, None], (BANDS, PATCH_PIX)).reshape(PATCH_DIM)
        scale_line = jnp.broadcast_to(band_scale[:, None], (BANDS, PATCH_PIX)).reshape(PATCH_DIM)
        xin = ((project(chosen, pix) - mean_line) * scale_line).astype(BF16)
        block = pick_tiles(arrived, from_owner, BF16, "hold")
        early, late = block[: turns[0]], block[turns[0] :]
        early_all, late_all = [lax.all_gather(lax.all_gather(part, K_DP), K_SECTION) for part in (early, late)]
        enc = unpack_section(early_all.reshape(-1, TR, TC), source_tile[0], 0)
        encoded = encode(enc, xin, positions_kept)
    valid_count = jnp.maximum(totals[2 * BANDS], 1.0)
    codes, scales, loss_terms, d_sent = decoder_step(
        late_all.reshape(-1, TR, TC), source_tile[1], (1.0 / valid_count)[None], chosen, encoded[-1], kept[:, None],
        valid[:, None], pix, where_tile[1], line_tile[1], n_dev * per, n_dev * rows_each,
    )
    codes, scales = encoder_back(enc, encoded, d_sent, xin, where_tile[0], line_tile[0], codes, scales)
    if n_dp == 16:
        codes_mine, scales_mine, tails = reduce_and_return(
            codes.reshape(2, n_dp, per, TR, TC), scales.reshape(2, n_dp, rows_each, TC), turn_for, is_held.astype(F32),
            loss_terms, 3,
        )
    else:
        wide = scales.reshape(n_dev, rows_each, TC)[:, :per]
        values = jnp.where(wide[:, :, None] > 0.0, codes.reshape(n_dev, per, TR, TC).astype(F32), 0.0)
        values = values * wide[:, :, None]
        values = lax.psum_scatter(values, (K_SECTION, K_DP), scatter_dimension=0, tiled=True)[0]
        top = jnp.max(jnp.abs(values), 1, keepdims=True)
        up = jnp.where(top > 0.0, 32766.0 / top, 0.0)
        own_codes = jnp.round(values * up).astype(jnp.int16)
        own_scale = top[:, 0] * (1.0 / 32766.0)
        own = jnp.where(is_held[:, None, None] > 0, own_codes.astype(F32) * own_scale[:, None], 0.0)
        tail = jnp.stack([jnp.sum(own * own), jnp.sum(loss_terms)])
        tail = jnp.pad(tail[:, None], ((0, 6), (0, 127)))
        codes_back = pick_tiles(own_codes, turn_for, jnp.int16, "back")
        scales_back = own_scale[turn_for][:, None]
        codes_mine, scales_mine, tails = exchange("return", 4, n_dp, [codes_back, scales_back], [tail])
    totals = jnp.sum(tails, (0, 2))
    grad_norm = jnp.sqrt(totals[0])
    factor = jnp.minimum(1.0, CLIP_NORM / (grad_norm + 1e-06))
    master_new, first_new, second_new = adam(
        codes_mine, scales_mine, goes, used_mine, factor[None], master[0], moment_one[0], moment_two[0]
    )
    return master_new[None], first_new[None], second_new[None], totals[1][None], grad_norm[None]


def solution(mesh):
    return jax.shard_map(
        local,
        mesh=mesh,
        in_specs=(
            P(None, K_DP, None, None),
            P(None, K_DP, None),
            P(None, K_DP, None),
            P(K_SECTION, None),
            P(K_SECTION, K_DP, None, None),
            P(K_SECTION, K_DP, None, None),
            P(K_SECTION, K_DP, None, None),
        ),
        out_specs=(
            P(K_SECTION, K_DP, None, None),
            P(K_SECTION, K_DP, None, None),
            P(K_SECTION, K_DP, None, None),
            P(),
            P(),
        ),
        check_vma=False,
    )
```

```python
import functools
import math

import jax
import jax.numpy as jnp
import numpy as np
from jax import lax
from jax.experimental import pallas as pl
from jax.experimental.pallas import tpu as pltpu
from jax.sharding import PartitionSpec as P

D_ENC = 768
H_ENC = 12
FF_ENC = 3072
D_DEC = 512
H_DEC = 16
FF_DEC = 2048
BANDS = 6
PATCH_PIX = 256
PATCH_DIM = 1536
SEQ = 588
KEEP = 147
STEP = 5
TILES = 256
USED = (253, 133)

EPS_NORM = 1e-06
EPS_BAND = 1e-05
CLIP_NORM = 0.001
RATE = 0.02
DECAY = 0.05
BETA_ONE = 0.5
BETA_TWO = 0.75
ADAM_EPS = 1e-08

K_SECTION = "section"
K_FIRST_BIAS = "first_bias"
K_PROJ_BIAS = "proj_bias"
K_FC2_BIAS = "fc2_bias"
K_FC1_BIAS = "fc1_bias"
K_FIRST = "first"
K_QV_BIAS = "qv_bias"
K_QKV = "qkv"
K_PROJ = "proj"
K_DP = "dp"
K_FC1 = "fc1"
K_FC2 = "fc2"
K_HEAD_BIAS = "head_bias"
K_GF = "gf"
K_G2 = "g2"
K_G1 = "g1"
K_MASK = "mask"
K_HEAD = "head"
K_BF = "bf"
K_B1 = "b1"
K_B2 = "b2"
K_U = "u"
K_V = "v"
K_Z = "z"

MESH = pl.DeviceIdType.MESH
TR, TC = 128, 256
PARTS = ((0, 6), (6, 11), (11, 13))
PARTS_ROWS = 24
PARTS_SHIFT = (8 - PARTS[0][1], 8 - (PARTS[1][1] - PARTS[0][1]))


def neighbours(section, place):
    x, y, z = lax.rem(place, 2), lax.rem(lax.div(place, 2), 2), lax.div(place, 4)

    def at(dz, dv, du):
        dx = (1 - section) * du + section * dv
        dy = (1 - section) * dv + section * du
        return lax.rem(z + dz, 4) * 4 + lax.rem(y + dy, 2) * 2 + lax.rem(x + dx, 2)

    return at


class Direct:
    def __init__(self, n_dp, pairs, sems):
        self.section, self.place = lax.axis_index(K_SECTION), lax.axis_index(K_DP)
        self.n_dp, self.n_dev, self.pairs, self.sems = n_dp, 2 * n_dp, pairs, sems
        self.me = self.section * n_dp + self.place

    def who(self, step):
        other = lax.rem(self.me + step, self.n_dev)
        return other, (lax.div(other, self.n_dp), lax.rem(other, self.n_dp))

    def greet(self):
        barrier = pltpu.get_barrier_semaphore()

        def one(step, carry):
            pl.semaphore_signal(barrier, inc=1, device_id=self.who(step)[1], device_id_type=MESH)
            return carry

        lax.fori_loop(1, self.n_dev, one, 0)
        pl.semaphore_wait(barrier, self.n_dev - 1)

    def own(self, which):
        source, dealt, target = self.pairs[which]
        return pltpu.make_async_copy(source.at[self.me] if dealt else source, target.at[self.me], self.sems[2].at[which])

    def copy(self, which, step):
        source, dealt, target = self.pairs[which]
        other, place_of = self.who(step)
        return pltpu.make_async_remote_copy(
            src_ref=source.at[other] if dealt else source,
            dst_ref=target.at[self.me],
            send_sem=self.sems[0].at[which, step],
            recv_sem=self.sems[1].at[which, step],
            device_id=place_of,
            device_id_type=MESH,
        )

    def start(self):
        for which in range(len(self.pairs)):
            self.own(which).start()

        def one(step, carry):
            for which in reversed(range(len(self.pairs))):
                self.copy(which, step).start()
            return carry

        lax.fori_loop(1, self.n_dev, one, 0)

    def finish(self):
        def one(step, carry):
            for which in range(len(self.pairs)):
                self.copy(which, step).wait()
            return carry

        lax.fori_loop(1, self.n_dev, one, 0)
        for which in range(len(self.pairs)):
            self.own(which).wait()


def direct_sems(n_pairs, n_dev):
    return [
        pltpu.SemaphoreType.DMA((n_pairs, n_dev)),
        pltpu.SemaphoreType.DMA((n_pairs, n_dev)),
        pltpu.SemaphoreType.DMA((n_pairs,)),
    ]


def exchange(name, cid, n_dp, dealt, shared):
    n_dev = 2 * n_dp
    arrays = list(dealt) + list(shared)
    count = len(arrays)

    def kernel(*refs):
        pairs = [(refs[n], n < len(dealt), refs[count + n]) for n in range(count)]
        direct = Direct(n_dp, pairs, refs[2 * count :])
        direct.greet()
        direct.start()
        direct.finish()

    shapes = [jax.ShapeDtypeStruct(a.shape, a.dtype) for a in dealt] + [
        jax.ShapeDtypeStruct((n_dev,) + a.shape, a.dtype) for a in shared
    ]
    any_spec = pl.BlockSpec(memory_space=pltpu.HBM)
    return pl.pallas_call(
        kernel,
        out_shape=shapes,
        in_specs=[any_spec] * count,
        out_specs=[any_spec] * count,
        scratch_shapes=direct_sems(count, n_dev),
        compiler_params=pltpu.CompilerParams(collective_id=cid, has_side_effects=True),
        name=name,
    )(*arrays)


def line_of(turn, n_dp):
    if n_dp != 16:
        return turn
    return turn + PARTS_SHIFT[0] * (turn >= PARTS[0][1]) + PARTS_SHIFT[1] * (turn >= PARTS[1][1])


def code(values):
    top = jnp.max(jnp.abs(values), axis=0, keepdims=True)
    up = jnp.where(top > 0.0, 32766.0 / top, 0.0)
    scaled = values * up
    return (scaled + jnp.where(scaled >= 0.0, 0.5, -0.5)).astype(jnp.int32).astype(jnp.int16), top * (1.0 / 32766.0)


def reduce_and_return(codes, scales, turn_for, held, loss, cid):
    per = codes.shape[2]

    def kernel(turn_ref, held_ref, codes_ref, scales_ref, loss_ref, out_ref, outs_ref, tails_ref, acc, accs, rc, rcs,
               r_code, r_scale, stage, stages, tail, own_sem, owns_sem, c_send, c_recv, p_send, p_recv, *direct_refs):
        section, place = lax.axis_index(K_SECTION), lax.axis_index(K_DP)
        at, at_other = neighbours(section, place), neighbours(1 - section, place)
        sibling = (1 - section, place)
        to_u, to_v = (section, at(0, 0, 1)), (section, at(0, 1, 0))

        def to_z(dz):
            return (section, at(dz, 0, 0))

        direct = Direct(16, [(stage, True, out_ref), (stages, True, outs_ref), (tail, False, tails_ref)], direct_refs)
        order = [(dz, dv, du) for dz in (2, 1, 3, 0) for dv in (1, 0) for du in (1, 0)]
        loads = {}
        for n, d in enumerate(order):
            b = at(*d)
            loads[d] = (
                pltpu.make_async_copy(codes_ref.at[section, b], acc.at[b], own_sem.at[n]),
                pltpu.make_async_copy(scales_ref.at[section, b], accs.at[b], owns_sem.at[n]),
            )
            for copy in loads[d]:
                copy.start()
        direct.greet()
        crossing = {}
        for n, d in enumerate(order):
            b = at_other(*d)
            pair = []
            for k, (source, target) in enumerate(((codes_ref, rc), (scales_ref, rcs))):
                copy = pltpu.make_async_remote_copy(
                    src_ref=source.at[1 - section, b],
                    dst_ref=target.at[b],
                    send_sem=c_send.at[k, n],
                    recv_sem=c_recv.at[k, n],
                    device_id=sibling,
                    device_id_type=MESH,
                )
                copy.start()
                pair.append(copy)
            crossing[d] = pair

        def add(b, part, from_code, from_first, from_scale, from_row):
            first, count = PARTS[part][0], PARTS[part][1] - PARTS[part][0]

            def one(t, carry):
                line = pl.ds(8 * part + t, 1)
                mine = acc[b, first + t].astype(jnp.float32) * accs[b, line, :]
                theirs = from_code[from_first + t].astype(jnp.float32) * from_scale[pl.ds(from_row + t, 1), :]
                value, scale = code(mine + theirs)
                acc[b, first + t] = value
                accs[b, line, :] = scale
                return carry

            lax.fori_loop(0, count, one, 0)

        sends = {}
        used = [0, 0]

        def send(part, key, b, peer):
            t0, t1 = PARTS[part]
            slot, index = used
            used[0] += t1 - t0
            used[1] += 1
            pair = []
            for k, (source, target) in enumerate(
                (
                    (acc.at[b, pl.ds(t0, t1 - t0)], r_code.at[pl.ds(slot, t1 - t0)]),
                    (accs.at[b, pl.ds(8 * part, 8)], r_scale.at[index]),
                )
            ):
                copy = pltpu.make_async_remote_copy(
                    src_ref=source,
                    dst_ref=target,
                    send_sem=p_send.at[k, index],
                    recv_sem=p_recv.at[k, index],
                    device_id=peer,
                    device_id_type=MESH,
                )
                copy.start()
                pair.append(copy)
            sends[part, key] = (pair, slot, index)

        def take(part, key, b):
            pair, slot, index = sends[part, key]
            for copy in pair:
                copy.wait_recv()
            add(b, part, r_code, slot, r_scale.at[index], 0)

        seen = set()

        def ready(d):
            if d not in seen:
                seen.add(d)
                for copy in loads[d]:
                    copy.wait()
                for copy in crossing[d]:
                    copy.wait_recv()

        def first(dz, parts=(0, 1, 2)):
            for dv in (1, 0):
                for du in (1, 0):
                    b = at(dz, dv, du)
                    ready((dz, dv, du))
                    for part in parts:
                        add(b, part, rc.at[b], PARTS[part][0], rcs.at[b], 8 * part)
                        if part == 2 and dz:
                            send(2, ("1", dz, dv, du), b, to_z(dz))
                        if part < 2 and du:
                            send(part, ("1", dz, dv), b, to_u)

        def second(dz):
            for dv in (1, 0):
                for part in (0, 1):
                    b = at(dz, dv, 0)
                    take(part, ("1", dz, dv), b)
                    if dv:
                        send(part, ("2", dz), b, to_v)

        def third(dz):
            for part in (0, 1):
                b = at(dz, 0, 0)
                take(part, ("2", dz), b)
                if dz:
                    send(part, ("3", dz), b, to_z(dz))

        first(2)
        first(1)
        first(3, (2,))
        second(2)
        first(3, (0, 1))
        second(1)
        third(2)
        first(0, (2,))
        second(3)
        first(0, (0, 1))
        third(1)
        for du in (1, 0):
            for dv in (1, 0):
                b = at(0, dv, du)
                for dz in (1, 3, 2):
                    take(2, ("1", dz, dv, du), b)
                if du:
                    send(2, ("2", dv), b, to_u)
        third(3)
        second(0)
        for dv in (1, 0):
            b = at(0, dv, 0)
            take(2, ("2", dv), b)
            if dv:
                send(2, ("3",), b, to_v)
        third(0)
        for dz in (2, 1, 3):
            for part in (0, 1):
                take(part, ("3", dz), place)
        take(2, ("3",), place)
        squares = jnp.zeros((1, TC), jnp.float32)
        for t in range(per):
            value = acc[place, t].astype(jnp.float32) * accs[place, line_of(t, 16) : line_of(t, 16) + 1, :]
            squares = squares + jnp.sum(value * value, 0, keepdims=True) * held_ref[t]
        tail[...] = jnp.zeros_like(tail)
        tail[0:1, :] = squares[:, :128] + squares[:, 128:]
        tail[1:2, :] = loss_ref[:, :128] + loss_ref[:, 128:]

        def deal(e, carry):
            t = turn_ref[e]
            line = t + sum(s * (t >= p[1]).astype(jnp.int32) for s, p in zip(PARTS_SHIFT, PARTS))
            stage[e] = acc[place, t]
            stages[e] = accs[place, pl.ds(line, 1), :]
            return carry

        lax.fori_loop(0, 32, deal, 0)
        direct.start()
        for pair in crossing.values():
            for copy in pair:
                copy.wait_send()
        for pair, slot, index in sends.values():
            for copy in pair:
                copy.wait_send()
        direct.finish()

    n_tiles = 15 * per
    n_copies = 45
    hbm = pl.BlockSpec(memory_space=pltpu.HBM)
    vmem = pl.BlockSpec(memory_space=pltpu.VMEM)
    smem = pl.BlockSpec(memory_space=pltpu.SMEM)
    return pl.pallas_call(
        kernel,
        out_shape=(
            jax.ShapeDtypeStruct((32, TR, TC), jnp.int16),
            jax.ShapeDtypeStruct((32, 1, TC), jnp.float32),
            jax.ShapeDtypeStruct((32, 8, 128), jnp.float32),
        ),
        in_specs=[smem, smem, hbm, hbm, vmem],
        out_specs=(hbm, hbm, hbm),
        scratch_shapes=[
            pltpu.VMEM((16, per, TR, TC), jnp.int16),
            pltpu.VMEM((16, PARTS_ROWS, TC), jnp.float32),
            pltpu.VMEM((16, per, TR, TC), jnp.int16),
            pltpu.VMEM((16, PARTS_ROWS, TC), jnp.float32),
            pltpu.VMEM((n_tiles, TR, TC), jnp.int16),
            pltpu.VMEM((n_copies, 8, TC), jnp.float32),
            pltpu.VMEM((32, TR, TC), jnp.int16),
            pltpu.VMEM((32, 1, TC), jnp.float32),
            pltpu.VMEM((8, 128), jnp.float32),
            pltpu.SemaphoreType.DMA((16,)),
            pltpu.SemaphoreType.DMA((16,)),
            pltpu.SemaphoreType.DMA((2, 16)),
            pltpu.SemaphoreType.DMA((2, 16)),
            pltpu.SemaphoreType.DMA((2, n_copies)),
            pltpu.SemaphoreType.DMA((2, n_copies)),
        ]
        + direct_sems(3, 32),
        compiler_params=pltpu.CompilerParams(
            collective_id=cid, has_side_effects=True, vmem_limit_bytes=60 * 2**20
        ),
        name="reduce_tiles",
    )(turn_for, held, codes, scales, loss)


def layout(section_id):
    if section_id == 0:
        width, hidden = D_ENC, FF_ENC
        matrices = [(K_FIRST, PATCH_DIM, D_ENC)]
        vectors = [(K_FIRST_BIAS, D_ENC)]
    else:
        width, hidden = D_DEC, FF_DEC
        matrices = [(K_FIRST, D_ENC, D_DEC)]
        vectors = [(K_FIRST_BIAS, D_DEC), (K_MASK, D_DEC)]
    matrices = matrices + [
        (K_QKV, width, 3 * width),
        (K_PROJ, width, width),
        (K_FC1, width, hidden),
        (K_FC2, hidden, width),
    ]
    vectors = vectors + [
        (K_G1, width),
        (K_B1, width),
        (K_QV_BIAS, 2 * width),
        (K_PROJ_BIAS, width),
        (K_G2, width),
        (K_B2, width),
        (K_FC1_BIAS, hidden),
        (K_FC2_BIAS, width),
        (K_GF, width),
        (K_BF, width),
    ]
    if section_id == 1:
        matrices = matrices + [(K_HEAD, D_DEC, PATCH_DIM)]
        vectors = vectors + [(K_HEAD_BIAS, PATCH_DIM)]
    return matrices, vectors


def positions(width):
    place = np.arange(SEQ, dtype=np.float32)[:, None]
    rate = np.exp(np.arange(width // 2, dtype=np.float32) * np.float32(-2.0 * math.log(10000.0) / width))
    angle = (place * rate).astype(np.float32)
    return np.concatenate([np.sin(angle), np.cos(angle)], axis=1).astype(np.float32)


LANES = 128
LOG2E = math.log2(math.e)


def pick_tiles(tiles, index, dtype, name):
    count = index.shape[0]

    def kernel(index_ref, tiles_ref, out_ref):
        def one(t, carry):
            out_ref[t] = tiles_ref[index_ref[t]].astype(dtype)
            return carry

        lax.fori_loop(0, count, one, 0)

    return pl.pallas_call(
        kernel,
        out_shape=jax.ShapeDtypeStruct((count, TR, TC), dtype),
        in_specs=[pl.BlockSpec(memory_space=pltpu.SMEM), pl.BlockSpec(memory_space=pltpu.VMEM)],
        out_specs=pl.BlockSpec(memory_space=pltpu.VMEM),
        compiler_params=pltpu.CompilerParams(vmem_limit_bytes=40 * 2**20),
        name=name,
    )(index, tiles)


def groups_of(rows, wide):
    groups = rows // TR
    return max(m for m in range(1, groups + 1) if groups % m == 0 and (m == 1 or m * wide <= 12))


def unpack_matrix(tiles, place, base, rows, columns, name):
    wide = columns // TC
    many = groups_of(rows, wide)
    count = many * wide

    def kernel(place_ref, *refs):
        sources, out_ref, lines = refs[:count], refs[count], refs[count + 1 :]
        for j in range(count):
            for h in range(2):
                lines[h][j * TR : (j + 1) * TR, :] = sources[j][0, :, h * LANES : (h + 1) * LANES].astype(jnp.float32)
        for j in range(wide):
            for h in range(2):
                start = j * TC + h * LANES
                out_ref[:, start : start + LANES] = lines[h][pl.ds(j, many * TR, stride=wide), :].astype(tiles.dtype)

    def spec(j):
        return pl.BlockSpec((1, TR, TC), lambda g, place_ref: (place_ref[base + g * count + j], 0, 0))

    return pl.pallas_call(
        kernel,
        out_shape=jax.ShapeDtypeStruct((rows, columns), tiles.dtype),
        grid_spec=pltpu.PrefetchScalarGridSpec(
            num_scalar_prefetch=1,
            grid=(rows // (many * TR),),
            in_specs=[spec(j) for j in range(count)],
            out_specs=pl.BlockSpec((many * TR, columns), lambda g, place_ref: (g, 0)),
            scratch_shapes=[pltpu.VMEM((count * TR, LANES), jnp.float32)] * 2,
        ),
        compiler_params=pltpu.CompilerParams(vmem_limit_bytes=32 * 2**20),
        name="unpack_" + name,
    )(place, *([tiles] * count))


def codes_into(a_ref, d_ref, base, place_ref, line_ref, codes_ref, scales_ref, work):
    left, right, ready, sem = work
    rows, columns = a_ref.shape[1], d_ref.shape[1]
    wide = columns // TC
    many = groups_of(rows, wide)
    count = many * wide
    steps = rows // (many * TR)

    def drain(slot):
        pltpu.make_async_copy(codes_ref.at[pl.ds(0, count)], ready.at[slot, pl.ds(0, count)], sem.at[slot]).wait()

    def group(g, carry):
        slot = lax.rem(g, 2)

        @pl.when(g >= 2)
        def _():
            drain(slot)

        factor = a_ref[:, pl.ds(pl.multiple_of(g * many * TR, TR), many * TR)]
        for j in range(wide):
            part = weight_grad(factor, d_ref[:, j * TC : (j + 1) * TC])
            for h, lines in enumerate((left, right)):
                lines[pl.ds(j, many * TR, stride=wide), :] = part[:, h * LANES : (h + 1) * LANES]
        for j in range(count):
            tile = base + g * count + j
            code_tile(left, right, j, ready, slot, j, scales_ref, line_ref[tile])
            pltpu.make_async_copy(ready.at[slot, j], codes_ref.at[place_ref[tile]], sem.at[slot]).start()
        return carry

    lax.fori_loop(0, steps, group, 0)
    if steps > 1:
        drain(steps % 2)
    drain((steps - 1) % 2)


def code_tile(left, right, j, ready, slot, to, scales_ref, line):
    pair = []
    for h, lines in enumerate((left, right)):
        value, scale = code(lines[j * TR : (j + 1) * TR, :])
        ready[slot, to, :, h * LANES : (h + 1) * LANES] = value
        pair.append(scale)
    scales_ref[pl.ds(line, 1), :] = jnp.concatenate(pair, axis=1)


def vectors_into(values, tile, place_ref, line_ref, codes_ref, scales_ref, work):
    left, right, ready, sem = work
    row = 0
    for value in values:
        for r in range(value.shape[1] // TC):
            left[row : row + 1, :] = value[:, r * TC : r * TC + LANES]
            right[row : row + 1, :] = value[:, r * TC + LANES : (r + 1) * TC]
            row += 1
    for lines in (left, right):
        lines[row:TR, :] = jnp.zeros((TR - row, LANES), F32)
    code_tile(left, right, 0, ready, 0, 0, scales_ref, line_ref[tile])
    copy = pltpu.make_async_copy(ready.at[0, 0], codes_ref.at[place_ref[tile]], sem.at[0])
    copy.start()
    copy.wait()


CODE_WORK = [
    pltpu.VMEM((12 * TR, LANES), jnp.float32),
    pltpu.VMEM((12 * TR, LANES), jnp.float32),
    pltpu.VMEM((2, 12, TR, TC), jnp.int16),
    pltpu.SemaphoreType.DMA((2,)),
]


def unpack_vectors(tiles, place, base, lengths, name):
    def kernel(place_ref, tile_ref, *refs):
        row = 0
        for out_ref, length in zip(refs, lengths):
            for r in range(length // TC):
                out_ref[:, r * TC : (r + 1) * TC] = tile_ref[0, row : row + 1, :].astype(jnp.float32)
                row += 1

    return pl.pallas_call(
        kernel,
        out_shape=[jax.ShapeDtypeStruct((1, length), jnp.float32) for length in lengths],
        grid_spec=pltpu.PrefetchScalarGridSpec(
            num_scalar_prefetch=1,
            grid=(1,),
            in_specs=[pl.BlockSpec((1, TR, TC), lambda g, place_ref: (place_ref[base], 0, 0))],
            out_specs=[pl.BlockSpec((1, length), lambda g, place_ref: (0, 0)) for length in lengths],
        ),
        name="unpack_vectors_" + name,
    )(place, tiles)


def unpack_section(tiles, place, section_id):
    matrices, vectors = layout(section_id)
    found, base = {}, 0
    for name, rows, columns in matrices:
        found[name] = unpack_matrix(tiles, place, base, rows, columns, f"{name}_{section_id}")
        base += rows * columns // (TR * TC)
    lines = unpack_vectors(tiles, place, base, [length for name, length in vectors], str(section_id))
    found.update({name: line for (name, length), line in zip(vectors, lines)})
    return found


def adam(codes, scales, index, used, factor, master, first, second):
    slots = master.shape[0]
    per = 4 if slots % 4 == 0 else 2

    def kernel(index_ref, used_ref, factor_ref, *refs):
        codes_refs, scales_refs = refs[:per], refs[per : 2 * per]
        w_ref, m_ref, v_ref, w_out, m_out, v_out = refs[2 * per :]
        for t in range(per):
            slot = pl.program_id(0) * per + t
            grad = codes_refs[t][0].astype(jnp.float32) * scales_refs[t][0]
            grad = jnp.where(used_ref[slot] > 0, grad * factor_ref[0], 0.0)
            first_new = BETA_ONE * m_ref[t] + (1.0 - BETA_ONE) * grad
            second_new = BETA_TWO * v_ref[t] + (1.0 - BETA_TWO) * grad * grad
            ratio = (
                first_new
                / (1.0 - BETA_ONE ** float(STEP))
                / (jnp.sqrt(second_new / (1.0 - BETA_TWO ** float(STEP))) + ADAM_EPS)
            )
            w_out[t] = w_ref[t] - RATE * (ratio + DECAY * w_ref[t])
            m_out[t] = first_new
            v_out[t] = second_new

    def spec(t, rows):
        return pl.BlockSpec((1, rows, TC), lambda g, index_ref, used_ref, factor_ref: (index_ref[g * per + t], 0, 0))

    block = pl.BlockSpec((per, TR, TC), lambda g, index_ref, used_ref, factor_ref: (g, 0, 0))
    held = [pltpu.with_memory_space_constraint(v, pltpu.HBM) for v in (codes, scales, master, first, second)]
    return pl.pallas_call(
        kernel,
        out_shape=[jax.ShapeDtypeStruct(master.shape, jnp.float32)] * 3,
        grid_spec=pltpu.PrefetchScalarGridSpec(
            num_scalar_prefetch=3,
            grid=(slots // per,),
            in_specs=[spec(t, TR) for t in range(per)] + [spec(t, 1) for t in range(per)] + [block] * 3,
            out_specs=[block] * 3,
        ),
        compiler_params=pltpu.CompilerParams(vmem_limit_bytes=40 * 2**20),
        name="adam",
    )(index, used, factor, *[held[0]] * per, *[held[1]] * per, *held[2:])


def project(a, w):
    return jnp.dot(a, w, preferred_element_type=jnp.float32)


def project_back(d, w):
    return lax.dot_general(d, w, (((1,), (1,)), ((), ())), preferred_element_type=jnp.float32)


def weight_grad(a, d):
    return lax.dot_general(a, d, (((0,), (0,)), ((), ())), preferred_element_type=jnp.float32)


def layer_norm(values, gain, offset):
    centre = values - jnp.mean(values, -1, keepdims=True)
    return centre * lax.rsqrt(jnp.mean(centre * centre, -1, keepdims=True) + EPS_NORM) * gain + offset


def norm_back(upstream, values, gain):
    centre = values - jnp.mean(values, -1, keepdims=True)
    spread = lax.rsqrt(jnp.mean(centre * centre, -1, keepdims=True) + EPS_NORM)
    normed = centre * spread
    scaled = upstream * gain
    downstream = spread * (
        scaled - jnp.mean(scaled, -1, keepdims=True) - normed * jnp.mean(scaled * normed, -1, keepdims=True)
    )
    return downstream, line_sum(upstream * normed), line_sum(upstream)


def line_sum(values):
    return jnp.sum(values.astype(jnp.float32), 0, keepdims=True)


ERF_TOP = (
    -2.72614225801306e-10,
    2.77068142495902e-08,
    -2.10102402082508e-06,
    -5.69250639462346e-05,
    -7.34990630326855e-04,
    -2.95459980854025e-03,
    -1.60960333262415e-02,
)
ERF_BOTTOM = (
    -1.45660718464996e-05,
    -2.13374055278905e-04,
    -1.68282697438203e-03,
    -7.37332916720468e-03,
    -1.42647390514189e-02,
)


def erf(x):
    x = jnp.clip(x, -4.0, 4.0)
    square = x * x
    top, bottom = jnp.full_like(x, ERF_TOP[0]), jnp.full_like(x, ERF_BOTTOM[0])
    for coefficient in ERF_TOP[1:]:
        top = top * square + coefficient
    for coefficient in ERF_BOTTOM[1:]:
        bottom = bottom * square + coefficient
    return x * top / bottom


def whole_kernel(kernel, shapes, operands, name, scratch=(), smem=0):
    vmem = pl.BlockSpec(memory_space=pltpu.VMEM)
    return pl.pallas_call(
        kernel,
        out_shape=[jax.ShapeDtypeStruct(shape, dtype) for shape, dtype in shapes],
        in_specs=[pl.BlockSpec(memory_space=pltpu.SMEM)] * smem + [vmem] * (len(operands) - smem),
        out_specs=[vmem] * len(shapes),
        scratch_shapes=scratch,
        compiler_params=pltpu.CompilerParams(vmem_limit_bytes=56 * 2**20),
        name=name,
    )(*operands)


F32, BF16 = jnp.float32, jnp.bfloat16


def start_block(x_ref, rows, w, a_ref, qkv_ref):
    g1, b1, weight, bias = w
    width = x_ref.shape[1]
    a = layer_norm(x_ref[rows, :], g1[...], b1[...]).astype(BF16)
    a_ref[rows, :] = a
    for part in range(3):
        columns = slice(part * width, (part + 1) * width)
        value = project(a, weight[:, columns])
        if part != 1:
            value = value + bias[:, (part // 2) * width : (part // 2 + 1) * width]
        qkv_ref[rows, columns] = value.astype(BF16)


def enter_encoder(xin, place, w):
    def kernel(xin_ref, place_ref, first, bias, g1, b1, weight, qv_bias, x_ref, a_ref, qkv_ref):
        x_ref[...] = project(xin_ref[...], first[...]) + bias[...] + place_ref[...]
        start_block(x_ref, slice(None), (g1, b1, weight, qv_bias), a_ref, qkv_ref)

    shapes = [((KEEP, D_ENC), F32), ((KEEP, D_ENC), BF16), ((KEEP, 3 * D_ENC), BF16)]
    operands = [xin, place] + [w[k] for k in (K_FIRST, K_FIRST_BIAS, K_G1, K_B1, K_QKV, K_QV_BIAS)]
    return whole_kernel(kernel, shapes, operands, "enter_encoder")


def enter_decoder_body(chosen_ref, sent_ref, kept_ref, place_ref, first, bias, mask, g1, b1, weight, qv_bias,
                       x_ref, a_ref, qkv_ref):
    for lo, hi in row_cuts(SEQ, 304):
        rows = slice(lo, hi)
        spread = project(chosen_ref[rows, :], sent_ref[...]).astype(BF16)
        placed = project(spread, first[...]) + bias[...]
        x_ref[rows, :] = jnp.where(kept_ref[rows, :] > 0.0, placed, mask[...]) + place_ref[rows, :]
        start_block(x_ref, rows, (g1, b1, weight, qv_bias), a_ref, qkv_ref)


def finish_block(x, attended, w, name):
    length, width = x.shape
    hidden = w[K_FC1].shape[1]

    line = (length, width)
    shapes = [(line, F32), (line, BF16), ((length, hidden), BF16), ((length, hidden), F32), (line, F32), (line, BF16)]
    names = (K_PROJ, K_PROJ_BIAS, K_G2, K_B2, K_FC1, K_FC1_BIAS, K_FC2, K_FC2_BIAS, K_GF, K_BF)
    return whole_kernel(finish_body, shapes, [x, attended] + [w[k] for k in names], "finish_" + name)


def finish_body(x_ref, o_ref, proj, proj_bias, g2, b2, fc1, fc1_bias, fc2, fc2_bias, gf, bf,
                h_ref, c_ref, z_ref, slope_ref, y_ref, out_ref, pump=None):
    length, hidden = z_ref.shape
    for lo, hi in row_cuts(length, 304):
        rows = slice(lo, hi)
        h = x_ref[rows, :] + project(o_ref[rows, :], proj[...]) + proj_bias[...]
        h_ref[rows, :] = h
        c_ref[rows, :] = layer_norm(h, g2[...], b2[...]).astype(BF16)
    for lo in range(0, hidden, 256):
        columns = slice(lo, lo + 256)
        u = project(c_ref[...], fc1[:, columns]) + fc1_bias[:, columns]
        below = 0.5 * (1.0 + erf(u * (1.0 / math.sqrt(2.0))))
        z = (u * below).astype(BF16)
        z_ref[:, columns] = z
        slope_ref[:, columns] = below + u * jnp.exp(-0.5 * u * u) * (1.0 / math.sqrt(2.0 * math.pi))
        y = project(z, fc2[columns, :])
        if lo:
            y_ref[...] += y
        else:
            y_ref[...] = y
        if pump is not None and lo % 512 == 256:
            pump(1)
    for lo, hi in row_cuts(length, 304):
        rows = slice(lo, hi)
        y = h_ref[rows, :] + y_ref[rows, :] + fc2_bias[...]
        y_ref[rows, :] = y
        out_ref[rows, :] = layer_norm(y, gf[...], bf[...]).astype(BF16)


def back_finish_body(d_ref, y_ref, slope_ref, h_ref, gf, fc2, fc1, g2, proj,
                     two_ref, du_ref, dh_ref, one_ref, do_ref, s_gf, s_bf, s_fc2, s_fc1, s_g2, s_b2, s_proj, dc_ref,
                     pump=None):
    length, hidden = slope_ref.shape
    for n, (lo, hi) in enumerate(row_cuts(length, 304)):
        rows = slice(lo, hi)
        dy, gain, shift = norm_back(d_ref[rows, :].astype(F32), y_ref[rows, :], gf[...])
        dh_ref[rows, :] = dy
        two = dy.astype(BF16)
        two_ref[rows, :] = two
        collect(n, (s_gf, gain), (s_bf, shift), (s_fc2, line_sum(two)))
    for lo in range(0, hidden, 256):
        columns = slice(lo, lo + 256)
        du = (project_back(two_ref[...], fc2[columns, :]) * slope_ref[:, columns]).astype(BF16)
        du_ref[:, columns] = du
        s_fc1[:, columns] = line_sum(du)
        dc = project_back(du, fc1[:, columns])
        if lo:
            dc_ref[...] += dc
        else:
            dc_ref[...] = dc
        if pump is not None:
            pump(1)
    for n, (lo, hi) in enumerate(row_cuts(length, 304)):
        rows = slice(lo, hi)
        part, gain, shift = norm_back(dc_ref[rows, :], h_ref[rows, :], g2[...])
        dh = dh_ref[rows, :] + part
        dh_ref[rows, :] = dh
        one = dh.astype(BF16)
        one_ref[rows, :] = one
        collect(n, (s_g2, gain), (s_b2, shift), (s_proj, line_sum(one)))
    do_ref[...] = project_back(one_ref[...], proj[...]).astype(BF16)


def collect(n, *pairs):
    for ref, value in pairs:
        ref[...] = ref[...] + value if n else value


def leave_encoder_body(d_ref, x_ref, dh_ref, g1, weight, low_ref, s_qv, s_g1, s_b1, s_first):
    d = d_ref[...]
    part, gain, shift = norm_back(project_back(d, weight[...]), x_ref[...], g1[...])
    dx = dh_ref[...] + part
    low_ref[...] = dx.astype(BF16)
    s_qv[:, :D_ENC] = line_sum(d[:, :D_ENC])
    s_qv[:, D_ENC:] = line_sum(d[:, 2 * D_ENC :])
    s_g1[...] = gain
    s_b1[...] = shift
    s_first[...] = line_sum(dx)


def leave_decoder_body(d_ref, x_ref, dh_ref, chosen_ref, kept_ref, g1, weight, first,
                       low_ref, sent_ref, s_qv, s_g1, s_b1, s_mask, s_first, da_ref, dx_ref):
    da_ref[...] = project_back(d_ref[...], weight[...])
    for n, (lo, hi) in enumerate(row_cuts(SEQ, 304)):
        rows = slice(lo, hi)
        part, gain, shift = norm_back(da_ref[rows, :], x_ref[rows, :], g1[...])
        dx = dh_ref[rows, :] + part
        dx_ref[rows, :] = dx.astype(BF16)
        kept_rows = kept_ref[rows, :]
        collect(
            n,
            (s_g1, gain),
            (s_b1, shift),
            (s_mask, line_sum(dx * (1.0 - kept_rows))),
            (s_first, line_sum(dx * kept_rows)),
        )
    s_qv[:, :D_DEC] = line_sum(d_ref[:, :D_DEC])
    s_qv[:, D_DEC:] = line_sum(d_ref[:, 2 * D_DEC :])
    low = project(chosen_ref[...], dx_ref[...]).astype(BF16)
    low_ref[...] = low
    sent_ref[...] = project_back(low, first[...]).astype(BF16)


def head_mask(size, h):
    lane = lax.broadcasted_iota(jnp.int32, (1, LANES), 1)
    return (lane >= h * size) & (lane < (h + 1) * size)


def row_cuts(length, step):
    return [(lo, min(lo + step, length)) for lo in range(0, length, step)]


def mix_heads(q_ref, k_ref, v_ref, out_ref, size):
    keys, values = k_ref[...].T, v_ref[...]
    for lo, hi in row_cuts(q_ref.shape[0], 304):
        total = jnp.zeros((hi - lo, LANES), F32)
        for h in range(LANES // size):
            mask = head_mask(size, h)
            query = jnp.where(mask, q_ref[lo:hi, :], jnp.zeros((), BF16))
            scores = project(query, keys)
            power = jnp.exp2((scores - jnp.max(scores, -1, keepdims=True)) * (size ** (-0.5) * LOG2E))
            probs = power * (1.0 / jnp.sum(power, -1, keepdims=True))
            mixed = project(probs.astype(BF16), values)
            total = jnp.where(mask, mixed, total)
        out_ref[lo:hi, :] = total.astype(BF16)


def attention(qkv, heads):
    length, width = qkv.shape[0], qkv.shape[1] // 3
    size = width // heads
    groups = width // LANES

    def kernel(q_ref, k_ref, v_ref, out_ref):
        mix_heads(q_ref, k_ref, v_ref, out_ref, size)

    def spec(offset):
        return pl.BlockSpec((length, LANES), lambda g: (0, g + offset))

    return pl.pallas_call(
        kernel,
        out_shape=jax.ShapeDtypeStruct((length, width), jnp.bfloat16),
        grid=(groups,),
        in_specs=[spec(0), spec(groups), spec(2 * groups)],
        out_specs=spec(0),
        compiler_params=pltpu.CompilerParams(vmem_limit_bytes=40 * 2**20),
        name=f"attention_{heads}",
    )(qkv, qkv, qkv)


def back_heads(q_ref, k_ref, v_ref, g_ref, dq_turned, size, pump=None):
    length, factor = q_ref.shape[0], size ** (-0.5)
    zero = jnp.zeros((), jnp.bfloat16)
    keys, values = k_ref[...], v_ref[...]
    keys_turned = keys.T
    cuts = row_cuts(length, 256)
    for n, (lo, hi) in enumerate(cuts):
        query_all, grad_all = q_ref[lo:hi, :], g_ref[lo:hi, :]
        query_turned, grad_turned = query_all.T, grad_all.T
        dk = dv = None
        for h in range(LANES // size):
            own = slice(h * size, (h + 1) * size)
            row = lax.broadcasted_iota(jnp.int32, (LANES, 1), 0)
            rows = (row >= h * size) & (row < (h + 1) * size)
            mask = head_mask(size, h)
            scores = project(keys, jnp.where(rows, query_turned, zero))
            power = jnp.exp2((scores - jnp.max(scores, 0, keepdims=True)) * (factor * LOG2E))
            probs = power * (1.0 / jnp.sum(power, 0, keepdims=True))
            d_probs = project(values, jnp.where(rows, grad_turned, zero))
            inner = jnp.sum(d_probs * probs, 0, keepdims=True)
            d_scores = (probs * (d_probs - inner)).astype(jnp.bfloat16)
            dv_h = project(probs.astype(jnp.bfloat16), jnp.where(mask, grad_all, zero))
            dk_h = project(d_scores, jnp.where(mask, query_all, zero))
            dv = dv_h if dv is None else dv + dv_h
            dk = dk_h if dk is None else dk + dk_h
            dq_turned[own, lo:hi] = project(keys_turned[own, :], d_scores)
        if n:
            dk_sum, dv_sum = dk_sum + dk, dv_sum + dv
        else:
            dk_sum, dv_sum = dk, dv
    return dq_turned[...].T * factor, dk_sum * factor, dv_sum


def head_body(one, final_ref, w_ref, bias_ref, pix_ref, valid_ref, low_ref, sums_ref, loss_ref, back_ref):
    for band in range(BANDS):
        columns = slice(band * PATCH_PIX, (band + 1) * PATCH_PIX)
        predicted = project(final_ref[...], w_ref[:, columns]) + bias_ref[:, columns]
        values = pix_ref[:, columns].astype(F32)
        centre = values - jnp.mean(values, -1, keepdims=True)
        target = centre * lax.rsqrt(jnp.mean(centre * centre, -1, keepdims=True) + EPS_NORM)
        misfit = predicted - target
        valid_misfit = valid_ref[...] * misfit
        collect(band, (loss_ref, line_sum(valid_misfit * misfit) * (one / (BANDS * PATCH_PIX))))
        grad = valid_misfit * (one * (2.0 / (BANDS * PATCH_PIX)))
        low = grad.astype(BF16)
        low_ref[:, columns] = low
        sums_ref[:, columns] = line_sum(grad)
        collect(band, (back_ref, project_back(low, w_ref[:, columns])))


def decoder_step(tiles, place, inverse, chosen, sent, kept, valid, pix, where, line_at, total_tiles, total_lines):
    matrices, vectors = layout(1)
    base, total = tile_bases(1)
    line = (SEQ, D_DEC)
    hidden = (SEQ, FF_DEC)
    inner = [
        ((SEQ, PATCH_DIM), BF16), (hidden, BF16), (hidden, BF16), ((SEQ, 3 * D_DEC), BF16), ((SEQ, 3 * D_DEC), BF16),
        ((KEEP, D_DEC), BF16), (hidden, F32), ((LANES, SEQ), F32),
    ]
    inner += [(line, BF16)] * 8 + [(line, F32)] * 5

    def kernel(place_ref, where_ref, line_ref, inverse_ref, tiles_ref, chosen_ref, turned_ref, sent_ref, kept_ref,
               valid_ref, pix_ref, pos_ref, codes_ref, scales_ref, loss_ref, d_sent, *refs):
        refs = list(refs)
        pred_low, z, du, qkv, dqkv, low, slope, turned = [refs.pop(0) for _ in range(8)]
        final, two, c, o, one, a, dx, do = [refs.pop(0) for _ in range(8)]
        x, h, y, dh, d = [refs.pop(0) for _ in range(5)]
        w = {name: refs.pop(0) for name, rows, columns in matrices}
        w.update({name: refs.pop(0) for name, length in vectors})
        g = {name: refs.pop(0) for name, length in vectors}
        pool, sem = refs.pop(0), refs.pop(0)
        work = refs
        left, right = work[:2]
        scales_ref[...] = jnp.zeros_like(scales_ref)
        size = D_DEC // H_DEC

        sizes = {name: rows * columns // (TR * TC) for name, rows, columns in matrices}
        spans = [(total, 1)] + [(base[name], sizes[name]) for name in sizes]
        for n, (start, count) in enumerate(spans):

            def fetch(t, carry, n=n):
                pltpu.make_async_copy(tiles_ref.at[place_ref[t]], pool.at[t], sem.at[n]).start()
                return carry

            lax.fori_loop(start, start + count, fetch, 0)

        def fetched(n):
            start, count = spans[n]
            pltpu.make_async_copy(tiles_ref.at[pl.ds(0, count)], pool.at[pl.ds(start, count)], sem.at[n]).wait()

        fetched(0)
        cut_vectors(pool[total].astype(F32), [w[name] for name, length in vectors])
        for n, (name, rows, columns) in enumerate(matrices):
            fetched(n + 1)
            unpack_into(pool, None, base[name], w[name], left, right)
        names = (K_FIRST, K_FIRST_BIAS, K_MASK, K_G1, K_B1, K_QKV, K_QV_BIAS)
        enter_decoder_body(
            turned_ref, sent_ref, kept_ref, pos_ref, *[w[k] for k in names], x, a, qkv
        )
        spans = [
            [slice(part * D_DEC + n * LANES, part * D_DEC + (n + 1) * LANES) for part in range(3)]
            for n in range(D_DEC // LANES)
        ]
        for group in spans:
            mix_heads(*[qkv.at[:, span] for span in group], o.at[:, group[0]], size)
        names = (K_PROJ, K_PROJ_BIAS, K_G2, K_B2, K_FC1, K_FC1_BIAS, K_FC2, K_FC2_BIAS, K_GF, K_BF)
        finish_body(
            x, o, *[w[k] for k in names], h, c, z, slope, y, final
        )
        head_body(
            inverse_ref[0], final, w[K_HEAD], w[K_HEAD_BIAS], pix_ref, valid_ref,
            pred_low, g[K_HEAD_BIAS], loss_ref, d,
        )
        names = (K_GF, K_BF, K_FC2_BIAS, K_FC1_BIAS, K_G2, K_B2, K_PROJ_BIAS)
        back_finish_body(
            d, y, slope, h, *[w[k] for k in (K_GF, K_FC2, K_FC1, K_G2, K_PROJ)],
            two, du, dh, one, do, *[g[k] for k in names], d,
        )
        for group in spans:
            parts = back_heads(*[qkv.at[:, span] for span in group], do.at[:, group[0]], turned, size)
            for span, value in zip(group, parts):
                dqkv[:, span] = value.astype(BF16)
        leave_decoder_body(
            dqkv, x, dh, chosen_ref, kept_ref, w[K_G1], w[K_QKV], w[K_FIRST], low, d_sent,
            *[g[k] for k in (K_QV_BIAS, K_G1, K_B1, K_MASK, K_FIRST_BIAS)], d, dx,
        )
        out = (where_ref, line_ref, codes_ref, scales_ref, work)
        factors = ((sent_ref, low), (a, dqkv), (o, one), (c, du), (z, two), (final, pred_low))
        for (name, rows, columns), pair in zip(matrices, factors):
            codes_into(*pair, base[name], *out)
        vectors_into([g[name] for name, length in vectors], total, *out)

    vmem = pl.BlockSpec(memory_space=pltpu.VMEM)
    smem = pl.BlockSpec(memory_space=pltpu.SMEM)
    hbm = pl.BlockSpec(memory_space=pltpu.HBM)
    return pl.pallas_call(
        kernel,
        out_shape=[
            jax.ShapeDtypeStruct((total_tiles, TR, TC), jnp.int16),
            jax.ShapeDtypeStruct((total_lines, TC), F32),
            jax.ShapeDtypeStruct((1, PATCH_PIX), F32),
            jax.ShapeDtypeStruct((KEEP, D_ENC), BF16),
        ],
        in_specs=[smem] * 4 + [hbm] + [vmem] * 7,
        out_specs=[hbm] + [vmem] * 3,
        scratch_shapes=[pltpu.VMEM(*value) for value in inner]
        + [pltpu.VMEM((rows, columns), BF16) for name, rows, columns in matrices]
        + [pltpu.VMEM((1, length), F32) for name, length in vectors] * 2
        + [pltpu.VMEM((USED[1], TR, TC), BF16), pltpu.SemaphoreType.DMA((1 + len(matrices),))]
        + CODE_WORK,
        compiler_params=pltpu.CompilerParams(vmem_limit_bytes=60 * 2**20),
        name="decoder_step",
    )(place, where, line_at, inverse, tiles, chosen, chosen.T, sent, kept, valid, pix, jnp.asarray(positions(D_DEC)))


def encoder_back(w, encoded, d_sent, xin, where, line_at, codes, scales):
    matrices, vectors = layout(0)
    base, total = tile_bases(0)
    line = (KEEP, D_ENC)
    inner = [((KEEP, FF_ENC), BF16), ((KEEP, 3 * D_ENC), BF16), ((LANES, KEEP), F32)]
    inner += [(line, BF16)] * 4 + [(line, F32)] * 2
    weights = (K_QKV, K_PROJ, K_FC1, K_FC2, K_G1, K_G2, K_GF)

    def kernel(where_ref, line_ref, codes_in, scales_in, x, a, qkv, o, h, c, z, slope, y, d_sent_ref, xin_ref, *refs):
        refs = list(refs)
        v = {name: refs.pop(0) for name in weights}
        codes_ref, scales_ref = refs.pop(0), refs.pop(0)
        du, dqkv, turned, two, one, do, low, dh, d = [refs.pop(0) for _ in range(9)]
        g = {name: refs.pop(0) for name, length in vectors}
        out = (where_ref, line_ref, codes_ref, scales_ref, refs)
        scales_ref[...] = scales_in[...]
        names = (K_GF, K_BF, K_FC2_BIAS, K_FC1_BIAS, K_G2, K_B2, K_PROJ_BIAS)
        back_finish_body(
            d_sent_ref, y, slope, h, *[v[k] for k in (K_GF, K_FC2, K_FC1, K_G2, K_PROJ)],
            two, du, dh, one, do, *[g[k] for k in names], d,
        )
        for n in range(D_ENC // LANES):
            group = [slice(part * D_ENC + n * LANES, part * D_ENC + (n + 1) * LANES) for part in range(3)]
            parts = back_heads(
                *[qkv.at[:, span] for span in group], do.at[:, group[0]], turned, D_ENC // H_ENC
            )
            for span, value in zip(group, parts):
                dqkv[:, span] = value.astype(BF16)
        leave_encoder_body(
            dqkv, x, dh, v[K_G1], v[K_QKV], low, *[g[k] for k in (K_QV_BIAS, K_G1, K_B1, K_FIRST_BIAS)]
        )
        factors = ((xin_ref, low), (a, dqkv), (o, one), (c, du), (z, two))
        for (name, rows, columns), pair in zip(matrices, factors):
            codes_into(*pair, base[name], *out)
        vectors_into([g[name] for name, length in vectors], total, *out)

    vmem = pl.BlockSpec(memory_space=pltpu.VMEM)
    smem = pl.BlockSpec(memory_space=pltpu.SMEM)
    hbm = pl.BlockSpec(memory_space=pltpu.HBM)
    operands = [*encoded[:9], d_sent, xin] + [w[name] for name in weights]
    return pl.pallas_call(
        kernel,
        out_shape=[jax.ShapeDtypeStruct(codes.shape, codes.dtype), jax.ShapeDtypeStruct(scales.shape, F32)],
        in_specs=[smem, smem, hbm] + [vmem] * (1 + len(operands)),
        out_specs=[hbm, vmem],
        scratch_shapes=[pltpu.VMEM(*value) for value in inner]
        + [pltpu.VMEM((1, length), F32) for name, length in vectors]
        + CODE_WORK,
        input_output_aliases={2: 0},
        compiler_params=pltpu.CompilerParams(vmem_limit_bytes=60 * 2**20),
        name="encoder_back",
    )(where, line_at, codes, scales, *operands)


class Spread:
    MOVES = {K_U: [(0, 0, 1)], K_V: [(0, 1, 0)], K_Z: [(1, 0, 0), (2, 0, 0), (3, 0, 0)]}

    def __init__(self, section, place, block_ref, all_ref, ways, cut, sems, first):
        self.section, self.place, self.at = section, place, neighbours(section, place)
        self.block_ref, self.all_ref, self.ways, self.cut, self.sems = block_ref, all_ref, ways, cut, sems
        self.count = block_ref.shape[0]
        self.copies, self.sides = {}, {}
        self.next_copy = self.next_side = first

    def rows(self, section, holder, way):
        start = (section * 16 + holder) * self.count + self.cut[way]
        return self.all_ref.at[pl.ds(start, self.cut[way + 1] - self.cut[way])]

    def source(self, way, origin):
        if origin == (0, 0, 0):
            return self.block_ref.at[pl.ds(self.cut[way], self.cut[way + 1] - self.cut[way])]
        return self.rows(self.section, self.at(*origin), way)

    def send(self, way, origin, move):
        copy = pltpu.make_async_remote_copy(
            src_ref=self.source(way, origin),
            dst_ref=self.rows(self.section, self.at(*origin), way),
            send_sem=self.sems[0].at[self.next_copy],
            recv_sem=self.sems[1].at[self.next_copy],
            device_id=(self.section, self.at(*move)),
            device_id_type=MESH,
        )
        copy.start()
        self.copies[way, self.moved(origin, move)] = (copy, self.next_copy)
        self.next_copy += 1

    def moved(self, origin, move):
        return tuple((o - m) % s for o, m, s in zip(origin, move, (4, 2, 2)))

    def side(self, way, origin):
        copy = pltpu.make_async_remote_copy(
            src_ref=self.source(way, origin),
            dst_ref=self.rows(self.section, self.at(*origin), way),
            send_sem=self.sems[2].at[self.next_side],
            recv_sem=self.sems[3].at[self.next_side],
            device_id=(1 - self.section, self.place),
            device_id_type=MESH,
        )
        copy.start()
        self.sides[way, origin] = (copy, self.next_side)
        self.next_side += 1

    def arrived(self, target, send_sem, recv_sem):
        pltpu.make_async_remote_copy(
            src_ref=target,
            dst_ref=target,
            send_sem=send_sem,
            recv_sem=recv_sem,
            device_id=(1 - self.section, self.place),
            device_id_type=MESH,
        ).wait_recv()

    def take(self, way, origin, dims):
        index = self.copies[way, origin][1]
        self.arrived(
            self.rows(self.section, self.at(*origin), way), self.sems[0].at[index], self.sems[1].at[index]
        )
        for dim in dims:
            for move in self.MOVES[dim]:
                self.send(way, origin, move)
        self.side(way, origin)

    def start(self):
        zero = (0, 0, 0)
        self.own = pltpu.make_async_copy(
            self.block_ref, self.all_ref.at[pl.ds((self.section * 16 + self.place) * self.count, self.count)], self.sems[4]
        )
        self.own.start()
        for turn in range(3):
            for way, dims in enumerate(self.ways):
                for move in self.MOVES[dims[turn]]:
                    self.send(way, zero, move)
        for way in range(len(self.ways)):
            self.side(way, zero)
        held = {way: [zero] for way in range(len(self.ways))}
        steps = []
        for turn in range(3):
            come = {}
            for way, dims in enumerate(self.ways):
                come[way] = [self.moved(o, m) for m in self.MOVES[dims[turn]] for o in held[way]]
                held[way] = held[way] + come[way]
            for i in range(max(len(v) for v in come.values())):
                for way, dims in enumerate(self.ways):
                    if i < len(come[way]):
                        steps.append(functools.partial(self.take, way, come[way][i], dims[turn + 1 :]))
        return steps

    def finish(self):
        self.own.wait()
        for copy, index in self.copies.values():
            copy.wait_send()
        for (way, origin), (copy, index) in self.sides.items():
            copy.wait_send()
            self.arrived(
                self.rows(1 - self.section, self.at(*origin), way), self.sems[2].at[index], self.sems[3].at[index]
            )


def spread_sems(copies, sides):
    return [
        pltpu.SemaphoreType.DMA((copies,)),
        pltpu.SemaphoreType.DMA((copies,)),
        pltpu.SemaphoreType.DMA((sides,)),
        pltpu.SemaphoreType.DMA((sides,)),
        pltpu.SemaphoreType.DMA,
    ]


FOUR_WAYS = ((K_Z, K_V, K_U), (K_Z, K_U, K_V), (K_V, K_Z, K_U), (K_U, K_Z, K_V))
ONE_WAY = ((K_Z, K_V, K_U),)


def unpack_into(pool, place_ref, base, weight_ref, left, right):
    rows, columns = weight_ref.shape
    wide = columns // TC
    many = groups_of(rows, wide)
    count = many * wide

    def group(g, carry):
        for j in range(count):
            index = base + g * count + j
            tile = pool[index if place_ref is None else place_ref[index]].astype(F32)
            left[j * TR : (j + 1) * TR, :] = tile[:, :LANES]
            right[j * TR : (j + 1) * TR, :] = tile[:, LANES:]
        rows_g = pl.ds(pl.multiple_of(g * many * TR, TR), many * TR)
        for j in range(wide):
            for n, lines in enumerate((left, right)):
                start = j * TC + n * LANES
                weight_ref[rows_g, start : start + LANES] = lines[pl.ds(j, many * TR, stride=wide), :].astype(BF16)
        return carry

    lax.fori_loop(0, rows // (many * TR), group, 0)


def cut_vectors(tile, refs):
    row = 0
    for ref in refs:
        for r in range(ref.shape[1] // TC):
            ref[:, r * TC : (r + 1) * TC] = tile[row : row + 1, :]
            row += 1


def tile_bases(section_id):
    matrices, vectors = layout(section_id)
    base, total = {}, 0
    for name, rows, columns in matrices:
        base[name] = total
        total += rows * columns // (TR * TC)
    return base, total


def deal_and_encode(master, slot_for, from_owner, sums, chosen, pix, place, turns, cid):
    n_early, n_late = turns
    slots = master.shape[0]
    matrices, vectors = layout(0)
    shapes = {name: (rows, columns) for name, rows, columns in matrices}
    lengths = dict(vectors)
    base, total = tile_bases(0)
    kept_weights = (K_QKV, K_PROJ, K_FC1, K_FC2)
    kept_vectors = (K_G1, K_G2, K_GF)
    line = (KEEP, D_ENC)
    hidden = (KEEP, FF_ENC)
    results = [
        (line, F32), (line, BF16), ((KEEP, 3 * D_ENC), BF16), (line, BF16), (line, F32), (line, BF16), (hidden, BF16),
        (hidden, F32), (line, F32), (line, BF16),
    ]

    def kernel(slot_ref, owner_ref, place_ref, master_ref, sums_ref, chosen_ref, pix_ref, pos_ref,
               late_all, all_sums, xin_ref, *refs):
        refs = list(refs)
        out_w = {name: refs.pop(0) for name in kept_weights}
        out_v = {name: refs.pop(0) for name in kept_vectors}
        x, a, qkv, o, h, c, z, slope, y, sent = [refs.pop(0) for _ in results]
        pool = refs.pop(0)
        w = {name: refs.pop(0) for name, rows, columns in matrices}
        v = {name: refs.pop(0) for name, length in vectors}
        left, right = refs.pop(0), refs.pop(0)
        stage, arrived, early_ref, late_ref = refs[:4]
        early_sems, late_sems, out_sem, direct_refs = refs[4:9], refs[9:14], refs[14], refs[15:]
        section, at_dp = lax.axis_index(K_SECTION), lax.axis_index(K_DP)
        direct = Direct(16, [(stage, True, arrived), (sums_ref, False, all_sums)], direct_refs)

        def pick(e, carry):
            stage[e] = master_ref[slot_ref[e]].astype(BF16)
            return carry

        lax.fori_loop(0, 32, pick, 0)
        direct.greet()
        direct.start()
        seen = project(chosen_ref[...], pix_ref[...])
        kept_places = sum(project(chosen_ref[...], pos_ref[part]) for part in range(3))
        direct.finish()
        for t in range(n_early):
            early_ref[t] = arrived[owner_ref[t]]
        for t in range(n_late):
            late_ref[t] = arrived[owner_ref[n_early + t]]
        cut = [0, 3, 5, 7, n_early] if n_early == 8 else [0, 1, 2, 3, n_early]
        soon = Spread(section, at_dp, early_ref, pool, FOUR_WAYS, cut, early_sems, 0)
        soon_steps = soon.start()
        last = 8 * len(FOUR_WAYS)
        for step in soon_steps[:-last]:
            step()
        later = Spread(section, at_dp, late_ref, late_all, ONE_WAY, [0, n_late], late_sems, 0)
        steps = later.start()
        lines = jnp.sum(all_sums[...], 0)[0:1, :]
        lane = lax.broadcasted_iota(jnp.int32, (1, LANES), 1)
        for band in range(BANDS):
            columns = slice(band * PATCH_PIX, (band + 1) * PATCH_PIX)
            mean, square = [
                jnp.sum(jnp.where(lane == n, lines, 0.0), -1, keepdims=True) / (32 * SEQ * PATCH_PIX) for n in (band, BANDS + band)
            ]
            scale = lax.rsqrt(square - mean * mean + EPS_BAND)
            xin_ref[:, columns] = ((seen[:, columns] - mean) * scale).astype(BF16)
        for step in soon_steps[-last:]:
            step()
        soon.finish()

        def pump(count):
            for _ in range(min(count, len(steps))):
                steps.pop(0)()

        def unpack(name):
            unpack_into(pool, place_ref, base[name], w[name], left, right)
            if name in kept_weights:
                pltpu.make_async_copy(w[name], out_w[name], out_sem.at[kept_weights.index(name)]).start()

        cut_vectors(pool[place_ref[total]].astype(F32), [v[name] for name, length in vectors])
        for name in kept_vectors:
            out_v[name][...] = v[name][...]
        unpack(K_FIRST)
        pump(1)
        unpack(K_QKV)
        pump(2)
        x[...] = project(xin_ref[...], w[K_FIRST][...]) + v[K_FIRST_BIAS][...] + kept_places
        start_block(x, slice(None), (v[K_G1], v[K_B1], w[K_QKV], v[K_QV_BIAS]), a, qkv)
        pump(2)
        for g in range(D_ENC // LANES):
            spans = [slice(part * D_ENC + g * LANES, part * D_ENC + (g + 1) * LANES) for part in range(3)]
            mix_heads(*[qkv.at[:, span] for span in spans], o.at[:, spans[0]], D_ENC // H_ENC)
        pump(2)
        unpack(K_PROJ)
        unpack(K_FC1)
        pump(2)
        unpack(K_FC2)
        pump(2)
        names = (K_PROJ, K_PROJ_BIAS, K_G2, K_B2, K_FC1, K_FC1_BIAS, K_FC2, K_FC2_BIAS, K_GF, K_BF)
        finish_body(x, o, *[w[name] if name in w else v[name] for name in names], h, c, z, slope, y, sent, pump)
        pump(len(steps))
        later.finish()
        for name in kept_weights:
            pltpu.make_async_copy(w[name], out_w[name], out_sem.at[kept_weights.index(name)]).wait()

    vmem, hbm = pl.BlockSpec(memory_space=pltpu.VMEM), pl.BlockSpec(memory_space=pltpu.HBM)
    shape = jax.ShapeDtypeStruct
    outs = pl.pallas_call(
        kernel,
        out_shape=[
            shape((32 * n_late, TR, TC), BF16), shape((32, 8, LANES), F32), shape((KEEP, PATCH_DIM), BF16)
        ]
        + [shape(shapes[name], BF16) for name in kept_weights]
        + [shape((1, lengths[name]), F32) for name in kept_vectors]
        + [shape(*result) for result in results],
        in_specs=[pl.BlockSpec(memory_space=pltpu.SMEM)] * 3 + [vmem] * 5,
        out_specs=[hbm] + [vmem] * 2 + [hbm] * len(kept_weights) + [vmem] * (len(kept_vectors) + len(results)),
        scratch_shapes=[pltpu.VMEM((32 * n_early, TR, TC), BF16)]
        + [pltpu.VMEM(shapes[name], BF16) for name, rows, columns in matrices]
        + [pltpu.VMEM((1, length), F32) for name, length in vectors]
        + [pltpu.VMEM((12 * TR, LANES), F32)] * 2
        + [pltpu.VMEM((32, TR, TC), BF16)] * 2
        + [pltpu.VMEM((n_early, TR, TC), BF16), pltpu.VMEM((n_late, TR, TC), BF16)]
        + spread_sems(60, 64)
        + spread_sems(15, 16)
        + [pltpu.SemaphoreType.DMA((len(kept_weights),))]
        + direct_sems(2, 32),
        compiler_params=pltpu.CompilerParams(
            collective_id=cid, has_side_effects=True, vmem_limit_bytes=60 * 2**20
        ),
        name="deal_and_encode",
    )(slot_for, from_owner, place, master, sums, chosen, pix, jnp.asarray(in_three(positions(D_ENC))))
    weights = dict(zip(kept_weights + kept_vectors, outs[3:]))
    return outs[0], outs[1], outs[2], weights, outs[3 + len(weights) :]


def in_three(values):
    parts, rest = [], values
    for _ in range(3):
        parts.append(rest.astype(jnp.bfloat16))
        rest = rest - parts[-1].astype(np.float32)
    return np.stack(parts)


def encode(w, xin, chosen):
    places = jnp.asarray(positions(D_ENC))
    x, a, qkv = enter_encoder(xin, jnp.dot(chosen.astype(F32), places, precision=lax.Precision.HIGHEST), w)
    o = attention(qkv, H_ENC)
    return x, a, qkv, o, *finish_block(x, o, w, "encoder")


def local(pixels, keep_index, clear_mask, slot_tile, master, moment_one, moment_two):
    n_dp = lax.axis_size(K_DP)
    n_dev = 2 * n_dp
    section, place = lax.axis_index(K_SECTION), lax.axis_index(K_DP)
    me = section * n_dp + place
    slots = master.shape[1]
    turns = [-(-count // n_dev) for count in USED]
    per = sum(turns)
    starts = [0, turns[0] * n_dev]
    rows_each = PARTS_ROWS if n_dp == 16 else 8 * (-(-per // 8))

    pix = lax.dynamic_index_in_dim(pixels, section, 0, keepdims=False)[0]
    wide_pix = pix.astype(F32)
    keep = lax.dynamic_index_in_dim(keep_index, section, 0, keepdims=False)[0]
    clear = lax.dynamic_index_in_dim(clear_mask, section, 0, keepdims=False)[0]
    kept = jnp.any(keep[:, None] == jnp.arange(SEQ), axis=0).astype(jnp.float32)
    valid = clear.astype(jnp.float32) * (1.0 - kept)
    sums = jnp.concatenate(
        [
            jnp.sum(jnp.sum(wide_pix, 0).reshape(BANDS, PATCH_PIX), 1),
            jnp.sum(jnp.sum(wide_pix * wide_pix, 0).reshape(BANDS, PATCH_PIX), 1),
            jnp.sum(valid)[None],
        ]
    )
    sums = jnp.pad(sums, (0, 1024 - sums.shape[0])).reshape(8, 128)

    def order(table, start):
        used = (table < TILES).astype(jnp.int32)
        count = table.shape[0]
        before = (jnp.arange(count)[:, None] > jnp.arange(count)[None]).astype(jnp.int32)
        return used, jnp.sum(before * used[None], 1) + start

    table_own = slot_tile[0]
    used_own, order_own = order(table_own, starts[1] * section)
    used_mine = lax.dynamic_slice_in_dim(used_own, place * slots, slots)
    order_mine = lax.dynamic_slice_in_dim(order_own, place * slots, slots)
    goes = lax.rem(order_mine, n_dev)
    slot_for = jnp.sum(
        jnp.arange(slots)[None] * used_mine[None] * (goes[None] == jnp.arange(n_dev)[:, None]), 1
    ).astype(jnp.int32)
    table_other = lax.ppermute(table_own, K_SECTION, [(0, 1), (1, 0)])
    tables = jnp.where(section == 0, jnp.stack([table_own, table_other]), jnp.stack([table_other, table_own]))
    n_slots = table_own.shape[0]
    both = [order(tables[s], starts[s]) for s in range(2)]
    used_all = jnp.concatenate([b[0] for b in both])
    order_all = jnp.concatenate([b[1] for b in both])
    owner_all = jnp.arange(2 * n_slots) // slots
    held = jnp.arange(per) * n_dev + me
    match = used_all[None] * (order_all[None] == held[:, None])
    from_owner = jnp.sum(match * owner_all[None], 1).astype(jnp.int32)
    is_held = jnp.sum(match, 1)
    turn_for = jnp.sum(
        jnp.arange(per)[None] * is_held[None] * (from_owner[None] == jnp.arange(n_dev)[:, None]), 1
    ).astype(jnp.int32)
    chosen = (keep[:, None] == jnp.arange(SEQ)).astype(BF16)

    where_tile = []
    line_tile = []
    source_tile = []
    for s in range(2):
        hit = tables[s][None] == jnp.arange(TILES)[:, None]
        rank = jnp.sum(hit * both[s][1][None], 1)
        device, turn = lax.rem(rank, n_dev), lax.div(rank, n_dev)
        where_tile.append((device * per + turn).astype(jnp.int32))
        source_tile.append((device * turns[s] + turn - (turns[0] if s else 0)).astype(jnp.int32))
        line_tile.append((device * rows_each + line_of(turn, n_dp)).astype(jnp.int32))

    if n_dp == 16:
        late_all, all_sums, xin, enc, encoded = deal_and_encode(
            master[0], slot_for, from_owner, sums, chosen, pix, source_tile[0], turns, 2
        )
        totals = jnp.sum(all_sums, 0).reshape(-1)
    else:
        dealt = pick_tiles(master[0], slot_for, BF16, "deal")
        arrived, all_sums = exchange("exchange", 1, n_dp, [dealt], [sums])
        totals = jnp.sum(all_sums, 0).reshape(-1)
        pixel_count = n_dev * SEQ * PATCH_PIX
        band_mean = totals[:BANDS] / pixel_count
        band_scale = lax.rsqrt(totals[BANDS : 2 * BANDS] / pixel_count - band_mean * band_mean + EPS_BAND)
        mean_line = jnp.broadcast_to(band_mean[:, None], (BANDS, PATCH_PIX)).reshape(PATCH_DIM)
        scale_line = jnp.broadcast_to(band_scale[:, None], (BANDS, PATCH_PIX)).reshape(PATCH_DIM)
        xin = ((project(chosen, pix) - mean_line) * scale_line).astype(BF16)
        block = pick_tiles(arrived, from_owner, BF16, "hold")
        early, late = block[: turns[0]], block[turns[0] :]
        early_all, late_all = [lax.all_gather(lax.all_gather(part, K_DP), K_SECTION) for part in (early, late)]
        enc = unpack_section(early_all.reshape(-1, TR, TC), source_tile[0], 0)
        encoded = encode(enc, xin, chosen)
    valid_count = jnp.maximum(totals[2 * BANDS], 1.0)
    codes, scales, loss_terms, d_sent = decoder_step(
        late_all.reshape(-1, TR, TC), source_tile[1], (1.0 / valid_count)[None], chosen, encoded[-1], kept[:, None],
        valid[:, None], pix, where_tile[1], line_tile[1], n_dev * per, n_dev * rows_each,
    )
    codes, scales = encoder_back(enc, encoded, d_sent, xin, where_tile[0], line_tile[0], codes, scales)
    if n_dp == 16:
        codes_mine, scales_mine, tails = reduce_and_return(
            codes.reshape(2, n_dp, per, TR, TC), scales.reshape(2, n_dp, rows_each, TC), turn_for, is_held.astype(F32),
            loss_terms, 3,
        )
    else:
        wide = scales.reshape(n_dev, rows_each, TC)[:, :per]
        values = jnp.where(wide[:, :, None] > 0.0, codes.reshape(n_dev, per, TR, TC).astype(F32), 0.0)
        values = values * wide[:, :, None]
        values = lax.psum_scatter(values, (K_SECTION, K_DP), scatter_dimension=0, tiled=True)[0]
        top = jnp.max(jnp.abs(values), 1, keepdims=True)
        up = jnp.where(top > 0.0, 32766.0 / top, 0.0)
        own_codes = jnp.round(values * up).astype(jnp.int16)
        own_scale = top[:, 0] * (1.0 / 32766.0)
        own = jnp.where(is_held[:, None, None] > 0, own_codes.astype(F32) * own_scale[:, None], 0.0)
        tail = jnp.stack([jnp.sum(own * own), jnp.sum(loss_terms)])
        tail = jnp.pad(tail[:, None], ((0, 6), (0, 127)))
        codes_back = pick_tiles(own_codes, turn_for, jnp.int16, "back")
        scales_back = own_scale[turn_for][:, None]
        codes_mine, scales_mine, tails = exchange("return", 4, n_dp, [codes_back, scales_back], [tail])
    totals = jnp.sum(tails, (0, 2))
    grad_norm = jnp.sqrt(totals[0])
    factor = jnp.minimum(1.0, CLIP_NORM / (grad_norm + 1e-06))
    master_new, first_new, second_new = adam(
        codes_mine, scales_mine, goes, used_mine, factor[None], master[0], moment_one[0], moment_two[0]
    )
    return master_new[None], first_new[None], second_new[None], totals[1][None], grad_norm[None]


def solution(mesh):
    return jax.shard_map(
        local,
        mesh=mesh,
        in_specs=(
            P(None, K_DP, None, None),
            P(None, K_DP, None),
            P(None, K_DP, None),
            P(K_SECTION, None),
            P(K_SECTION, K_DP, None, None),
            P(K_SECTION, K_DP, None, None),
            P(K_SECTION, K_DP, None, None),
        ),
        out_specs=(
            P(K_SECTION, K_DP, None, None),
            P(K_SECTION, K_DP, None, None),
            P(K_SECTION, K_DP, None, None),
            P(),
            P(),
        ),
        check_vma=False,
    )
```

```python
import functools
import math

import jax
import jax.numpy as jnp
import numpy as np
from jax import lax
from jax.experimental import pallas as pl
from jax.experimental.pallas import tpu as pltpu
from jax.sharding import PartitionSpec as P

D_ENC = 768
H_ENC = 12
FF_ENC = 3072
D_DEC = 512
H_DEC = 16
FF_DEC = 2048
BANDS = 6
PATCH_PIX = 256
PATCH_DIM = 1536
SEQ = 588
KEEP = 147
STEP = 5
TILES = 256
USED = (253, 133)

EPS_NORM = 1e-06
EPS_BAND = 1e-05
CLIP_NORM = 0.001
RATE = 0.02
DECAY = 0.05
BETA_ONE = 0.5
BETA_TWO = 0.75
ADAM_EPS = 1e-08

K_SECTION = "section"
K_FIRST_BIAS = "first_bias"
K_PROJ_BIAS = "proj_bias"
K_FC2_BIAS = "fc2_bias"
K_FC1_BIAS = "fc1_bias"
K_FIRST = "first"
K_QV_BIAS = "qv_bias"
K_QKV = "qkv"
K_PROJ = "proj"
K_DP = "dp"
K_FC1 = "fc1"
K_FC2 = "fc2"
K_HEAD_BIAS = "head_bias"
K_GF = "gf"
K_G2 = "g2"
K_G1 = "g1"
K_MASK = "mask"
K_HEAD = "head"
K_BF = "bf"
K_B1 = "b1"
K_B2 = "b2"
K_U = "u"
K_V = "v"
K_Z = "z"

MESH = pl.DeviceIdType.MESH
TR, TC = 128, 256
PARTS = ((0, 6), (6, 11), (11, 13))
PARTS_ROWS = 24
PARTS_SHIFT = (8 - PARTS[0][1], 8 - (PARTS[1][1] - PARTS[0][1]))


def neighbours(section, place):
    x, y, z = lax.rem(place, 2), lax.rem(lax.div(place, 2), 2), lax.div(place, 4)

    def at(dz, dv, du):
        dx = (1 - section) * du + section * dv
        dy = (1 - section) * dv + section * du
        return lax.rem(z + dz, 4) * 4 + lax.rem(y + dy, 2) * 2 + lax.rem(x + dx, 2)

    return at


class Direct:
    def __init__(self, n_dp, pairs, sems):
        self.section, self.place = lax.axis_index(K_SECTION), lax.axis_index(K_DP)
        self.n_dp, self.n_dev, self.pairs, self.sems = n_dp, 2 * n_dp, pairs, sems
        self.me = self.section * n_dp + self.place

    def who(self, step):
        other = lax.rem(self.me + step, self.n_dev)
        return other, (lax.div(other, self.n_dp), lax.rem(other, self.n_dp))

    def greet(self):
        barrier = pltpu.get_barrier_semaphore()

        def one(step, carry):
            pl.semaphore_signal(barrier, inc=1, device_id=self.who(step)[1], device_id_type=MESH)
            return carry

        lax.fori_loop(1, self.n_dev, one, 0)
        pl.semaphore_wait(barrier, self.n_dev - 1)

    def own(self, which):
        source, dealt, target = self.pairs[which]
        return pltpu.make_async_copy(source.at[self.me] if dealt else source, target.at[self.me], self.sems[2].at[which])

    def copy(self, which, step):
        source, dealt, target = self.pairs[which]
        other, place_of = self.who(step)
        return pltpu.make_async_remote_copy(
            src_ref=source.at[other] if dealt else source,
            dst_ref=target.at[self.me],
            send_sem=self.sems[0].at[which, step],
            recv_sem=self.sems[1].at[which, step],
            device_id=place_of,
            device_id_type=MESH,
        )

    def start(self):
        for which in range(len(self.pairs)):
            self.own(which).start()

        def one(step, carry):
            for which in reversed(range(len(self.pairs))):
                self.copy(which, step).start()
            return carry

        lax.fori_loop(1, self.n_dev, one, 0)

    def finish(self):
        def one(step, carry):
            for which in range(len(self.pairs)):
                self.copy(which, step).wait()
            return carry

        lax.fori_loop(1, self.n_dev, one, 0)
        for which in range(len(self.pairs)):
            self.own(which).wait()


def direct_sems(n_pairs, n_dev):
    return [
        pltpu.SemaphoreType.DMA((n_pairs, n_dev)),
        pltpu.SemaphoreType.DMA((n_pairs, n_dev)),
        pltpu.SemaphoreType.DMA((n_pairs,)),
    ]


def exchange(name, cid, n_dp, dealt, shared):
    n_dev = 2 * n_dp
    arrays = list(dealt) + list(shared)
    count = len(arrays)

    def kernel(*refs):
        pairs = [(refs[n], n < len(dealt), refs[count + n]) for n in range(count)]
        direct = Direct(n_dp, pairs, refs[2 * count :])
        direct.greet()
        direct.start()
        direct.finish()

    shapes = [jax.ShapeDtypeStruct(a.shape, a.dtype) for a in dealt] + [
        jax.ShapeDtypeStruct((n_dev,) + a.shape, a.dtype) for a in shared
    ]
    any_spec = pl.BlockSpec(memory_space=pltpu.HBM)
    return pl.pallas_call(
        kernel,
        out_shape=shapes,
        in_specs=[any_spec] * count,
        out_specs=[any_spec] * count,
        scratch_shapes=direct_sems(count, n_dev),
        compiler_params=pltpu.CompilerParams(collective_id=cid, has_side_effects=True),
        name=name,
    )(*arrays)


def line_of(turn, n_dp):
    if n_dp != 16:
        return turn
    return turn + PARTS_SHIFT[0] * (turn >= PARTS[0][1]) + PARTS_SHIFT[1] * (turn >= PARTS[1][1])


def code(values):
    top = jnp.max(jnp.abs(values), axis=0, keepdims=True)
    up = jnp.where(top > 0.0, 32766.0 / top, 0.0)
    scaled = values * up
    return (scaled + jnp.where(scaled >= 0.0, 0.5, -0.5)).astype(jnp.int32).astype(jnp.int16), top * (1.0 / 32766.0)


def reduce_and_return(codes, scales, turn_for, held, loss, cid):
    per = codes.shape[2]

    def kernel(turn_ref, held_ref, codes_ref, scales_ref, loss_ref, out_ref, outs_ref, tails_ref, acc, accs, rc, rcs,
               r_code, r_scale, stage, stages, tail, own_sem, owns_sem, c_send, c_recv, p_send, p_recv, *direct_refs):
        section, place = lax.axis_index(K_SECTION), lax.axis_index(K_DP)
        at, at_other = neighbours(section, place), neighbours(1 - section, place)
        sibling = (1 - section, place)
        to_u, to_v = (section, at(0, 0, 1)), (section, at(0, 1, 0))

        def to_z(dz):
            return (section, at(dz, 0, 0))

        direct = Direct(16, [(stage, True, out_ref), (stages, True, outs_ref), (tail, False, tails_ref)], direct_refs)
        order = [(dz, dv, du) for dz in (2, 1, 3, 0) for dv in (1, 0) for du in (1, 0)]
        loads = {}
        for n, d in enumerate(order):
            b = at(*d)
            loads[d] = (
                pltpu.make_async_copy(codes_ref.at[section, b], acc.at[b], own_sem.at[n]),
                pltpu.make_async_copy(scales_ref.at[section, b], accs.at[b], owns_sem.at[n]),
            )
            for copy in loads[d]:
                copy.start()
        direct.greet()
        crossing = {}
        for n, d in enumerate(order):
            b = at_other(*d)
            pair = []
            for k, (source, target) in enumerate(((codes_ref, rc), (scales_ref, rcs))):
                copy = pltpu.make_async_remote_copy(
                    src_ref=source.at[1 - section, b],
                    dst_ref=target.at[b],
                    send_sem=c_send.at[k, n],
                    recv_sem=c_recv.at[k, n],
                    device_id=sibling,
                    device_id_type=MESH,
                )
                copy.start()
                pair.append(copy)
            crossing[d] = pair

        def add(b, part, from_code, from_first, from_scale, from_row):
            first, count = PARTS[part][0], PARTS[part][1] - PARTS[part][0]

            def one(t, carry):
                line = pl.ds(8 * part + t, 1)
                mine = acc[b, first + t].astype(jnp.float32) * accs[b, line, :]
                theirs = from_code[from_first + t].astype(jnp.float32) * from_scale[pl.ds(from_row + t, 1), :]
                value, scale = code(mine + theirs)
                acc[b, first + t] = value
                accs[b, line, :] = scale
                return carry

            lax.fori_loop(0, count, one, 0)

        sends = {}
        used = [0, 0]

        def send(part, key, b, peer):
            t0, t1 = PARTS[part]
            slot, index = used
            used[0] += t1 - t0
            used[1] += 1
            pair = []
            for k, (source, target) in enumerate(
                (
                    (acc.at[b, pl.ds(t0, t1 - t0)], r_code.at[pl.ds(slot, t1 - t0)]),
                    (accs.at[b, pl.ds(8 * part, 8)], r_scale.at[index]),
                )
            ):
                copy = pltpu.make_async_remote_copy(
                    src_ref=source,
                    dst_ref=target,
                    send_sem=p_send.at[k, index],
                    recv_sem=p_recv.at[k, index],
                    device_id=peer,
                    device_id_type=MESH,
                )
                copy.start()
                pair.append(copy)
            sends[part, key] = (pair, slot, index)

        def take(part, key, b):
            pair, slot, index = sends[part, key]
            for copy in pair:
                copy.wait_recv()
            add(b, part, r_code, slot, r_scale.at[index], 0)

        seen = set()

        def ready(d):
            if d not in seen:
                seen.add(d)
                for copy in loads[d]:
                    copy.wait()
                for copy in crossing[d]:
                    copy.wait_recv()

        def first(dz, parts=(0, 1, 2)):
            for dv in (1, 0):
                for du in (1, 0):
                    b = at(dz, dv, du)
                    ready((dz, dv, du))
                    for part in parts:
                        add(b, part, rc.at[b], PARTS[part][0], rcs.at[b], 8 * part)
                        if part == 2 and dz:
                            send(2, ("1", dz, dv, du), b, to_z(dz))
                        if part < 2 and du:
                            send(part, ("1", dz, dv), b, to_u)

        def second(dz):
            for dv in (1, 0):
                for part in (0, 1):
                    b = at(dz, dv, 0)
                    take(part, ("1", dz, dv), b)
                    if dv:
                        send(part, ("2", dz), b, to_v)

        def third(dz):
            for part in (0, 1):
                b = at(dz, 0, 0)
                take(part, ("2", dz), b)
                if dz:
                    send(part, ("3", dz), b, to_z(dz))

        first(2)
        first(1)
        first(3, (2,))
        second(2)
        first(3, (0, 1))
        second(1)
        third(2)
        first(0, (2,))
        second(3)
        first(0, (0, 1))
        third(1)
        for du in (1, 0):
            for dv in (1, 0):
                b = at(0, dv, du)
                for dz in (1, 3, 2):
                    take(2, ("1", dz, dv, du), b)
                if du:
                    send(2, ("2", dv), b, to_u)
        third(3)
        second(0)
        for dv in (1, 0):
            b = at(0, dv, 0)
            take(2, ("2", dv), b)
            if dv:
                send(2, ("3",), b, to_v)
        third(0)
        for dz in (2, 1, 3):
            for part in (0, 1):
                take(part, ("3", dz), place)
        take(2, ("3",), place)
        squares = jnp.zeros((1, TC), jnp.float32)
        for t in range(per):
            value = acc[place, t].astype(jnp.float32) * accs[place, line_of(t, 16) : line_of(t, 16) + 1, :]
            squares = squares + jnp.sum(value * value, 0, keepdims=True) * held_ref[t]
        tail[...] = jnp.zeros_like(tail)
        tail[0:1, :] = squares[:, :128] + squares[:, 128:]
        tail[1:2, :] = loss_ref[:, :128] + loss_ref[:, 128:]

        def deal(e, carry):
            t = turn_ref[e]
            line = t + sum(s * (t >= p[1]).astype(jnp.int32) for s, p in zip(PARTS_SHIFT, PARTS))
            stage[e] = acc[place, t]
            stages[e] = accs[place, pl.ds(line, 1), :]
            return carry

        lax.fori_loop(0, 32, deal, 0)
        direct.start()
        for pair in crossing.values():
            for copy in pair:
                copy.wait_send()
        for pair, slot, index in sends.values():
            for copy in pair:
                copy.wait_send()
        direct.finish()

    n_tiles = 15 * per
    n_copies = 45
    hbm = pl.BlockSpec(memory_space=pltpu.HBM)
    vmem = pl.BlockSpec(memory_space=pltpu.VMEM)
    smem = pl.BlockSpec(memory_space=pltpu.SMEM)
    return pl.pallas_call(
        kernel,
        out_shape=(
            jax.ShapeDtypeStruct((32, TR, TC), jnp.int16),
            jax.ShapeDtypeStruct((32, 1, TC), jnp.float32),
            jax.ShapeDtypeStruct((32, 8, 128), jnp.float32),
        ),
        in_specs=[smem, smem, hbm, hbm, vmem],
        out_specs=(hbm, hbm, hbm),
        scratch_shapes=[
            pltpu.VMEM((16, per, TR, TC), jnp.int16),
            pltpu.VMEM((16, PARTS_ROWS, TC), jnp.float32),
            pltpu.VMEM((16, per, TR, TC), jnp.int16),
            pltpu.VMEM((16, PARTS_ROWS, TC), jnp.float32),
            pltpu.VMEM((n_tiles, TR, TC), jnp.int16),
            pltpu.VMEM((n_copies, 8, TC), jnp.float32),
            pltpu.VMEM((32, TR, TC), jnp.int16),
            pltpu.VMEM((32, 1, TC), jnp.float32),
            pltpu.VMEM((8, 128), jnp.float32),
            pltpu.SemaphoreType.DMA((16,)),
            pltpu.SemaphoreType.DMA((16,)),
            pltpu.SemaphoreType.DMA((2, 16)),
            pltpu.SemaphoreType.DMA((2, 16)),
            pltpu.SemaphoreType.DMA((2, n_copies)),
            pltpu.SemaphoreType.DMA((2, n_copies)),
        ]
        + direct_sems(3, 32),
        compiler_params=pltpu.CompilerParams(
            collective_id=cid, has_side_effects=True, vmem_limit_bytes=60 * 2**20
        ),
        name="reduce_tiles",
    )(turn_for, held, codes, scales, loss)


def layout(section_id):
    if section_id == 0:
        width, hidden = D_ENC, FF_ENC
        matrices = [(K_FIRST, PATCH_DIM, D_ENC)]
        vectors = [(K_FIRST_BIAS, D_ENC)]
    else:
        width, hidden = D_DEC, FF_DEC
        matrices = [(K_FIRST, D_ENC, D_DEC)]
        vectors = [(K_FIRST_BIAS, D_DEC), (K_MASK, D_DEC)]
    matrices = matrices + [
        (K_QKV, width, 3 * width),
        (K_PROJ, width, width),
        (K_FC1, width, hidden),
        (K_FC2, hidden, width),
    ]
    vectors = vectors + [
        (K_G1, width),
        (K_B1, width),
        (K_QV_BIAS, 2 * width),
        (K_PROJ_BIAS, width),
        (K_G2, width),
        (K_B2, width),
        (K_FC1_BIAS, hidden),
        (K_FC2_BIAS, width),
        (K_GF, width),
        (K_BF, width),
    ]
    if section_id == 1:
        matrices = matrices + [(K_HEAD, D_DEC, PATCH_DIM)]
        vectors = vectors + [(K_HEAD_BIAS, PATCH_DIM)]
    return matrices, vectors


def positions(width):
    place = np.arange(SEQ, dtype=np.float32)[:, None]
    rate = np.exp(np.arange(width // 2, dtype=np.float32) * np.float32(-2.0 * math.log(10000.0) / width))
    angle = (place * rate).astype(np.float32)
    return np.concatenate([np.sin(angle), np.cos(angle)], axis=1).astype(np.float32)


LANES = 128
LOG2E = math.log2(math.e)


def pick_tiles(tiles, index, dtype, name):
    count = index.shape[0]

    def kernel(index_ref, tiles_ref, out_ref):
        def one(t, carry):
            out_ref[t] = tiles_ref[index_ref[t]].astype(dtype)
            return carry

        lax.fori_loop(0, count, one, 0)

    return pl.pallas_call(
        kernel,
        out_shape=jax.ShapeDtypeStruct((count, TR, TC), dtype),
        in_specs=[pl.BlockSpec(memory_space=pltpu.SMEM), pl.BlockSpec(memory_space=pltpu.VMEM)],
        out_specs=pl.BlockSpec(memory_space=pltpu.VMEM),
        compiler_params=pltpu.CompilerParams(vmem_limit_bytes=40 * 2**20),
        name=name,
    )(index, tiles)


def groups_of(rows, wide):
    groups = rows // TR
    return max(m for m in range(1, groups + 1) if groups % m == 0 and (m == 1 or m * wide <= 12))


def unpack_matrix(tiles, place, base, rows, columns, name):
    wide = columns // TC
    many = groups_of(rows, wide)
    count = many * wide

    def kernel(place_ref, *refs):
        sources, out_ref, lines = refs[:count], refs[count], refs[count + 1 :]
        for j in range(count):
            for h in range(2):
                lines[h][j * TR : (j + 1) * TR, :] = sources[j][0, :, h * LANES : (h + 1) * LANES].astype(jnp.float32)
        for j in range(wide):
            for h in range(2):
                start = j * TC + h * LANES
                out_ref[:, start : start + LANES] = lines[h][pl.ds(j, many * TR, stride=wide), :].astype(tiles.dtype)

    def spec(j):
        return pl.BlockSpec((1, TR, TC), lambda g, place_ref: (place_ref[base + g * count + j], 0, 0))

    return pl.pallas_call(
        kernel,
        out_shape=jax.ShapeDtypeStruct((rows, columns), tiles.dtype),
        grid_spec=pltpu.PrefetchScalarGridSpec(
            num_scalar_prefetch=1,
            grid=(rows // (many * TR),),
            in_specs=[spec(j) for j in range(count)],
            out_specs=pl.BlockSpec((many * TR, columns), lambda g, place_ref: (g, 0)),
            scratch_shapes=[pltpu.VMEM((count * TR, LANES), jnp.float32)] * 2,
        ),
        compiler_params=pltpu.CompilerParams(vmem_limit_bytes=32 * 2**20),
        name="unpack_" + name,
    )(place, *([tiles] * count))


def codes_into(a_ref, d_ref, base, place_ref, line_ref, codes_ref, scales_ref, work):
    left, right, ready, sem = work
    rows, columns = a_ref.shape[1], d_ref.shape[1]
    wide = columns // TC
    many = groups_of(rows, wide)
    count = many * wide
    steps = rows // (many * TR)

    def drain(slot):
        pltpu.make_async_copy(codes_ref.at[pl.ds(0, count)], ready.at[slot, pl.ds(0, count)], sem.at[slot]).wait()

    def group(g, carry):
        slot = lax.rem(g, 2)

        @pl.when(g >= 2)
        def _():
            drain(slot)

        factor = a_ref[:, pl.ds(pl.multiple_of(g * many * TR, TR), many * TR)]
        for j in range(wide):
            part = weight_grad(factor, d_ref[:, j * TC : (j + 1) * TC])
            for h, lines in enumerate((left, right)):
                lines[pl.ds(j, many * TR, stride=wide), :] = part[:, h * LANES : (h + 1) * LANES]
        for j in range(count):
            tile = base + g * count + j
            code_tile(left, right, j, ready, slot, j, scales_ref, line_ref[tile])
            pltpu.make_async_copy(ready.at[slot, j], codes_ref.at[place_ref[tile]], sem.at[slot]).start()
        return carry

    lax.fori_loop(0, steps, group, 0)
    if steps > 1:
        drain(steps % 2)
    drain((steps - 1) % 2)


def code_tile(left, right, j, ready, slot, to, scales_ref, line):
    pair = []
    for h, lines in enumerate((left, right)):
        value, scale = code(lines[j * TR : (j + 1) * TR, :])
        ready[slot, to, :, h * LANES : (h + 1) * LANES] = value
        pair.append(scale)
    scales_ref[pl.ds(line, 1), :] = jnp.concatenate(pair, axis=1)


def vectors_into(values, tile, place_ref, line_ref, codes_ref, scales_ref, work):
    left, right, ready, sem = work
    row = 0
    for value in values:
        for r in range(value.shape[1] // TC):
            left[row : row + 1, :] = value[:, r * TC : r * TC + LANES]
            right[row : row + 1, :] = value[:, r * TC + LANES : (r + 1) * TC]
            row += 1
    for lines in (left, right):
        lines[row:TR, :] = jnp.zeros((TR - row, LANES), F32)
    code_tile(left, right, 0, ready, 0, 0, scales_ref, line_ref[tile])
    copy = pltpu.make_async_copy(ready.at[0, 0], codes_ref.at[place_ref[tile]], sem.at[0])
    copy.start()
    copy.wait()


CODE_WORK = [
    pltpu.VMEM((12 * TR, LANES), jnp.float32),
    pltpu.VMEM((12 * TR, LANES), jnp.float32),
    pltpu.VMEM((2, 12, TR, TC), jnp.int16),
    pltpu.SemaphoreType.DMA((2,)),
]


def unpack_vectors(tiles, place, base, lengths, name):
    def kernel(place_ref, tile_ref, *refs):
        row = 0
        for out_ref, length in zip(refs, lengths):
            for r in range(length // TC):
                out_ref[:, r * TC : (r + 1) * TC] = tile_ref[0, row : row + 1, :].astype(jnp.float32)
                row += 1

    return pl.pallas_call(
        kernel,
        out_shape=[jax.ShapeDtypeStruct((1, length), jnp.float32) for length in lengths],
        grid_spec=pltpu.PrefetchScalarGridSpec(
            num_scalar_prefetch=1,
            grid=(1,),
            in_specs=[pl.BlockSpec((1, TR, TC), lambda g, place_ref: (place_ref[base], 0, 0))],
            out_specs=[pl.BlockSpec((1, length), lambda g, place_ref: (0, 0)) for length in lengths],
        ),
        name="unpack_vectors_" + name,
    )(place, tiles)


def unpack_section(tiles, place, section_id):
    matrices, vectors = layout(section_id)
    found, base = {}, 0
    for name, rows, columns in matrices:
        found[name] = unpack_matrix(tiles, place, base, rows, columns, f"{name}_{section_id}")
        base += rows * columns // (TR * TC)
    lines = unpack_vectors(tiles, place, base, [length for name, length in vectors], str(section_id))
    found.update({name: line for (name, length), line in zip(vectors, lines)})
    return found


def adam(codes, scales, index, used, factor, master, first, second):
    slots = master.shape[0]
    per = 4 if slots % 4 == 0 else 2

    def kernel(index_ref, used_ref, factor_ref, *refs):
        codes_refs, scales_refs = refs[:per], refs[per : 2 * per]
        w_ref, m_ref, v_ref, w_out, m_out, v_out = refs[2 * per :]
        for t in range(per):
            slot = pl.program_id(0) * per + t
            grad = codes_refs[t][0].astype(jnp.float32) * scales_refs[t][0]
            grad = jnp.where(used_ref[slot] > 0, grad * factor_ref[0], 0.0)
            first_new = BETA_ONE * m_ref[t] + (1.0 - BETA_ONE) * grad
            second_new = BETA_TWO * v_ref[t] + (1.0 - BETA_TWO) * grad * grad
            ratio = (
                first_new
                / (1.0 - BETA_ONE ** float(STEP))
                / (jnp.sqrt(second_new / (1.0 - BETA_TWO ** float(STEP))) + ADAM_EPS)
            )
            w_out[t] = w_ref[t] - RATE * (ratio + DECAY * w_ref[t])
            m_out[t] = first_new
            v_out[t] = second_new

    def spec(t, rows):
        return pl.BlockSpec((1, rows, TC), lambda g, index_ref, used_ref, factor_ref: (index_ref[g * per + t], 0, 0))

    block = pl.BlockSpec((per, TR, TC), lambda g, index_ref, used_ref, factor_ref: (g, 0, 0))
    held = [pltpu.with_memory_space_constraint(v, pltpu.HBM) for v in (codes, scales, master, first, second)]
    return pl.pallas_call(
        kernel,
        out_shape=[jax.ShapeDtypeStruct(master.shape, jnp.float32)] * 3,
        grid_spec=pltpu.PrefetchScalarGridSpec(
            num_scalar_prefetch=3,
            grid=(slots // per,),
            in_specs=[spec(t, TR) for t in range(per)] + [spec(t, 1) for t in range(per)] + [block] * 3,
            out_specs=[block] * 3,
        ),
        compiler_params=pltpu.CompilerParams(vmem_limit_bytes=40 * 2**20),
        name="adam",
    )(index, used, factor, *[held[0]] * per, *[held[1]] * per, *held[2:])


def project(a, w):
    return jnp.dot(a, w, preferred_element_type=jnp.float32)


def project_back(d, w):
    return lax.dot_general(d, w, (((1,), (1,)), ((), ())), preferred_element_type=jnp.float32)


def weight_grad(a, d):
    return lax.dot_general(a, d, (((0,), (0,)), ((), ())), preferred_element_type=jnp.float32)


def layer_norm(values, gain, offset):
    centre = values - jnp.mean(values, -1, keepdims=True)
    return centre * lax.rsqrt(jnp.mean(centre * centre, -1, keepdims=True) + EPS_NORM) * gain + offset


def norm_back(upstream, values, gain):
    centre = values - jnp.mean(values, -1, keepdims=True)
    spread = lax.rsqrt(jnp.mean(centre * centre, -1, keepdims=True) + EPS_NORM)
    normed = centre * spread
    scaled = upstream * gain
    downstream = spread * (
        scaled - jnp.mean(scaled, -1, keepdims=True) - normed * jnp.mean(scaled * normed, -1, keepdims=True)
    )
    return downstream, line_sum(upstream * normed), line_sum(upstream)


def line_sum(values):
    return jnp.sum(values.astype(jnp.float32), 0, keepdims=True)


ERF_TOP = (
    -2.72614225801306e-10,
    2.77068142495902e-08,
    -2.10102402082508e-06,
    -5.69250639462346e-05,
    -7.34990630326855e-04,
    -2.95459980854025e-03,
    -1.60960333262415e-02,
)
ERF_BOTTOM = (
    -1.45660718464996e-05,
    -2.13374055278905e-04,
    -1.68282697438203e-03,
    -7.37332916720468e-03,
    -1.42647390514189e-02,
)


def erf(x):
    x = jnp.clip(x, -4.0, 4.0)
    square = x * x
    top, bottom = jnp.full_like(x, ERF_TOP[0]), jnp.full_like(x, ERF_BOTTOM[0])
    for coefficient in ERF_TOP[1:]:
        top = top * square + coefficient
    for coefficient in ERF_BOTTOM[1:]:
        bottom = bottom * square + coefficient
    return x * top / bottom


def whole_kernel(kernel, shapes, operands, name, scratch=(), smem=0):
    vmem = pl.BlockSpec(memory_space=pltpu.VMEM)
    return pl.pallas_call(
        kernel,
        out_shape=[jax.ShapeDtypeStruct(shape, dtype) for shape, dtype in shapes],
        in_specs=[pl.BlockSpec(memory_space=pltpu.SMEM)] * smem + [vmem] * (len(operands) - smem),
        out_specs=[vmem] * len(shapes),
        scratch_shapes=scratch,
        compiler_params=pltpu.CompilerParams(vmem_limit_bytes=56 * 2**20),
        name=name,
    )(*operands)


F32, BF16 = jnp.float32, jnp.bfloat16


def start_block(x_ref, rows, w, a_ref, qkv_ref):
    g1, b1, weight, bias = w
    width = x_ref.shape[1]
    a = layer_norm(x_ref[rows, :], g1[...], b1[...]).astype(BF16)
    a_ref[rows, :] = a
    for part in range(3):
        columns = slice(part * width, (part + 1) * width)
        value = project(a, weight[:, columns])
        if part != 1:
            value = value + bias[:, (part // 2) * width : (part // 2 + 1) * width]
        qkv_ref[rows, columns] = value.astype(BF16)


def enter_encoder(xin, place, w):
    def kernel(xin_ref, place_ref, first, bias, g1, b1, weight, qv_bias, x_ref, a_ref, qkv_ref):
        x_ref[...] = project(xin_ref[...], first[...]) + bias[...] + place_ref[...]
        start_block(x_ref, slice(None), (g1, b1, weight, qv_bias), a_ref, qkv_ref)

    shapes = [((KEEP, D_ENC), F32), ((KEEP, D_ENC), BF16), ((KEEP, 3 * D_ENC), BF16)]
    operands = [xin, place] + [w[k] for k in (K_FIRST, K_FIRST_BIAS, K_G1, K_B1, K_QKV, K_QV_BIAS)]
    return whole_kernel(kernel, shapes, operands, "enter_encoder")


def enter_decoder_body(chosen_ref, sent_ref, kept_ref, place_ref, first, bias, mask, g1, b1, weight, qv_bias,
                       x_ref, a_ref, qkv_ref):
    for lo, hi in row_cuts(SEQ, 304):
        rows = slice(lo, hi)
        spread = project(chosen_ref[rows, :], sent_ref[...]).astype(BF16)
        placed = project(spread, first[...]) + bias[...]
        x_ref[rows, :] = jnp.where(kept_ref[rows, :] > 0.0, placed, mask[...]) + place_ref[rows, :]
        start_block(x_ref, rows, (g1, b1, weight, qv_bias), a_ref, qkv_ref)


def finish_block(x, attended, w, name):
    length, width = x.shape
    hidden = w[K_FC1].shape[1]

    line = (length, width)
    shapes = [(line, F32), (line, BF16), ((length, hidden), BF16), ((length, hidden), F32), (line, F32), (line, BF16)]
    names = (K_PROJ, K_PROJ_BIAS, K_G2, K_B2, K_FC1, K_FC1_BIAS, K_FC2, K_FC2_BIAS, K_GF, K_BF)
    return whole_kernel(finish_body, shapes, [x, attended] + [w[k] for k in names], "finish_" + name)


def finish_body(x_ref, o_ref, proj, proj_bias, g2, b2, fc1, fc1_bias, fc2, fc2_bias, gf, bf,
                h_ref, c_ref, z_ref, slope_ref, y_ref, out_ref, pump=None):
    length, hidden = z_ref.shape
    for lo, hi in row_cuts(length, 304):
        rows = slice(lo, hi)
        h = x_ref[rows, :] + project(o_ref[rows, :], proj[...]) + proj_bias[...]
        h_ref[rows, :] = h
        c_ref[rows, :] = layer_norm(h, g2[...], b2[...]).astype(BF16)
    for lo in range(0, hidden, 256):
        columns = slice(lo, lo + 256)
        u = project(c_ref[...], fc1[:, columns]) + fc1_bias[:, columns]
        below = 0.5 * (1.0 + erf(u * (1.0 / math.sqrt(2.0))))
        z = (u * below).astype(BF16)
        z_ref[:, columns] = z
        slope_ref[:, columns] = below + u * jnp.exp(-0.5 * u * u) * (1.0 / math.sqrt(2.0 * math.pi))
        y = project(z, fc2[columns, :])
        if lo:
            y_ref[...] += y
        else:
            y_ref[...] = y
        if pump is not None and lo % 512 == 256:
            pump(1)
    for lo, hi in row_cuts(length, 304):
        rows = slice(lo, hi)
        y = h_ref[rows, :] + y_ref[rows, :] + fc2_bias[...]
        y_ref[rows, :] = y
        out_ref[rows, :] = layer_norm(y, gf[...], bf[...]).astype(BF16)


def back_finish_body(d_ref, y_ref, slope_ref, h_ref, gf, fc2, fc1, g2, proj,
                     two_ref, du_ref, dh_ref, one_ref, do_ref, s_gf, s_bf, s_fc2, s_fc1, s_g2, s_b2, s_proj, dc_ref,
                     pump=None):
    length, hidden = slope_ref.shape
    for n, (lo, hi) in enumerate(row_cuts(length, 304)):
        rows = slice(lo, hi)
        dy, gain, shift = norm_back(d_ref[rows, :].astype(F32), y_ref[rows, :], gf[...])
        dh_ref[rows, :] = dy
        two = dy.astype(BF16)
        two_ref[rows, :] = two
        collect(n, (s_gf, gain), (s_bf, shift), (s_fc2, line_sum(two)))
    for lo in range(0, hidden, 256):
        columns = slice(lo, lo + 256)
        du = (project_back(two_ref[...], fc2[columns, :]) * slope_ref[:, columns]).astype(BF16)
        du_ref[:, columns] = du
        s_fc1[:, columns] = line_sum(du)
        dc = project_back(du, fc1[:, columns])
        if lo:
            dc_ref[...] += dc
        else:
            dc_ref[...] = dc
        if pump is not None:
            pump(1)
    for n, (lo, hi) in enumerate(row_cuts(length, 304)):
        rows = slice(lo, hi)
        part, gain, shift = norm_back(dc_ref[rows, :], h_ref[rows, :], g2[...])
        dh = dh_ref[rows, :] + part
        dh_ref[rows, :] = dh
        one = dh.astype(BF16)
        one_ref[rows, :] = one
        collect(n, (s_g2, gain), (s_b2, shift), (s_proj, line_sum(one)))
    do_ref[...] = project_back(one_ref[...], proj[...]).astype(BF16)


def collect(n, *pairs):
    for ref, value in pairs:
        ref[...] = ref[...] + value if n else value


def leave_encoder_body(d_ref, x_ref, dh_ref, g1, weight, low_ref, s_qv, s_g1, s_b1, s_first):
    d = d_ref[...]
    part, gain, shift = norm_back(project_back(d, weight[...]), x_ref[...], g1[...])
    dx = dh_ref[...] + part
    low_ref[...] = dx.astype(BF16)
    s_qv[:, :D_ENC] = line_sum(d[:, :D_ENC])
    s_qv[:, D_ENC:] = line_sum(d[:, 2 * D_ENC :])
    s_g1[...] = gain
    s_b1[...] = shift
    s_first[...] = line_sum(dx)


def leave_decoder_body(d_ref, x_ref, dh_ref, chosen_ref, kept_ref, g1, weight, first,
                       low_ref, sent_ref, s_qv, s_g1, s_b1, s_mask, s_first, da_ref, dx_ref):
    da_ref[...] = project_back(d_ref[...], weight[...])
    for n, (lo, hi) in enumerate(row_cuts(SEQ, 304)):
        rows = slice(lo, hi)
        part, gain, shift = norm_back(da_ref[rows, :], x_ref[rows, :], g1[...])
        dx = dh_ref[rows, :] + part
        dx_ref[rows, :] = dx.astype(BF16)
        kept_rows = kept_ref[rows, :]
        collect(
            n,
            (s_g1, gain),
            (s_b1, shift),
            (s_mask, line_sum(dx * (1.0 - kept_rows))),
            (s_first, line_sum(dx * kept_rows)),
        )
    s_qv[:, :D_DEC] = line_sum(d_ref[:, :D_DEC])
    s_qv[:, D_DEC:] = line_sum(d_ref[:, 2 * D_DEC :])
    low = project(chosen_ref[...], dx_ref[...]).astype(BF16)
    low_ref[...] = low
    sent_ref[...] = project_back(low, first[...]).astype(BF16)


def head_mask(size, h):
    lane = lax.broadcasted_iota(jnp.int32, (1, LANES), 1)
    return (lane >= h * size) & (lane < (h + 1) * size)


def row_cuts(length, step):
    return [(lo, min(lo + step, length)) for lo in range(0, length, step)]


def mix_heads(q_ref, k_ref, v_ref, out_ref, size):
    keys, values = k_ref[...].T, v_ref[...]
    for lo, hi in row_cuts(q_ref.shape[0], 304):
        total = jnp.zeros((hi - lo, LANES), F32)
        for h in range(LANES // size):
            mask = head_mask(size, h)
            query = jnp.where(mask, q_ref[lo:hi, :], jnp.zeros((), BF16))
            scores = project(query, keys)
            power = jnp.exp2((scores - jnp.max(scores, -1, keepdims=True)) * (size ** (-0.5) * LOG2E))
            probs = power * (1.0 / jnp.sum(power, -1, keepdims=True))
            mixed = project(probs.astype(BF16), values)
            total = jnp.where(mask, mixed, total)
        out_ref[lo:hi, :] = total.astype(BF16)


def attention(qkv, heads):
    length, width = qkv.shape[0], qkv.shape[1] // 3
    size = width // heads
    groups = width // LANES

    def kernel(q_ref, k_ref, v_ref, out_ref):
        mix_heads(q_ref, k_ref, v_ref, out_ref, size)

    def spec(offset):
        return pl.BlockSpec((length, LANES), lambda g: (0, g + offset))

    return pl.pallas_call(
        kernel,
        out_shape=jax.ShapeDtypeStruct((length, width), jnp.bfloat16),
        grid=(groups,),
        in_specs=[spec(0), spec(groups), spec(2 * groups)],
        out_specs=spec(0),
        compiler_params=pltpu.CompilerParams(vmem_limit_bytes=40 * 2**20),
        name=f"attention_{heads}",
    )(qkv, qkv, qkv)


def back_heads(q_ref, k_ref, v_ref, g_ref, dq_turned, size, pump=None):
    length, factor = q_ref.shape[0], size ** (-0.5)
    zero = jnp.zeros((), jnp.bfloat16)
    keys, values = k_ref[...], v_ref[...]
    keys_turned = keys.T
    cuts = row_cuts(length, 256)
    for n, (lo, hi) in enumerate(cuts):
        query_all, grad_all = q_ref[lo:hi, :], g_ref[lo:hi, :]
        query_turned, grad_turned = query_all.T, grad_all.T
        dk = dv = None
        for h in range(LANES // size):
            own = slice(h * size, (h + 1) * size)
            row = lax.broadcasted_iota(jnp.int32, (LANES, 1), 0)
            rows = (row >= h * size) & (row < (h + 1) * size)
            mask = head_mask(size, h)
            scores = project(keys, jnp.where(rows, query_turned, zero))
            power = jnp.exp2((scores - jnp.max(scores, 0, keepdims=True)) * (factor * LOG2E))
            probs = power * (1.0 / jnp.sum(power, 0, keepdims=True))
            d_probs = project(values, jnp.where(rows, grad_turned, zero))
            inner = jnp.sum(d_probs * probs, 0, keepdims=True)
            d_scores = (probs * (d_probs - inner)).astype(jnp.bfloat16)
            dv_h = project(probs.astype(jnp.bfloat16), jnp.where(mask, grad_all, zero))
            dk_h = project(d_scores, jnp.where(mask, query_all, zero))
            dv = dv_h if dv is None else dv + dv_h
            dk = dk_h if dk is None else dk + dk_h
            dq_turned[own, lo:hi] = project(keys_turned[own, :], d_scores)
        if n:
            dk_sum, dv_sum = dk_sum + dk, dv_sum + dv
        else:
            dk_sum, dv_sum = dk, dv
    return dq_turned[...].T * factor, dk_sum * factor, dv_sum


def head_body(one, final_ref, w_ref, bias_ref, pix_ref, valid_ref, low_ref, sums_ref, loss_ref, back_ref):
    for band in range(BANDS):
        columns = slice(band * PATCH_PIX, (band + 1) * PATCH_PIX)
        predicted = project(final_ref[...], w_ref[:, columns]) + bias_ref[:, columns]
        values = pix_ref[:, columns].astype(F32)
        centre = values - jnp.mean(values, -1, keepdims=True)
        target = centre * lax.rsqrt(jnp.mean(centre * centre, -1, keepdims=True) + EPS_NORM)
        misfit = predicted - target
        valid_misfit = valid_ref[...] * misfit
        collect(band, (loss_ref, line_sum(valid_misfit * misfit) * (one / (BANDS * PATCH_PIX))))
        grad = valid_misfit * (one * (2.0 / (BANDS * PATCH_PIX)))
        low = grad.astype(BF16)
        low_ref[:, columns] = low
        sums_ref[:, columns] = line_sum(grad)
        collect(band, (back_ref, project_back(low, w_ref[:, columns])))


def decoder_step(tiles, place, all_sums, chosen, sent, kept, valid, pix, where, line_at, total_tiles, total_lines):
    matrices, vectors = layout(1)
    base, total = tile_bases(1)
    line = (SEQ, D_DEC)
    hidden = (SEQ, FF_DEC)
    inner = [
        ((SEQ, PATCH_DIM), BF16), (hidden, BF16), (hidden, BF16), ((SEQ, 3 * D_DEC), BF16), ((SEQ, 3 * D_DEC), BF16),
        ((KEEP, D_DEC), BF16), (hidden, F32), ((LANES, SEQ), F32),
    ]
    inner += [(line, BF16)] * 8 + [(line, F32)] * 5

    def kernel(place_ref, where_ref, line_ref, tiles_ref, all_sums, chosen_ref, turned_ref, sent_ref, kept_ref,
               valid_ref, pix_ref, pos_ref, codes_ref, scales_ref, loss_ref, d_sent, *refs):
        refs = list(refs)
        pred_low, z, du, qkv, dqkv, low, slope, turned = [refs.pop(0) for _ in range(8)]
        final, two, c, o, one, a, dx, do = [refs.pop(0) for _ in range(8)]
        x, h, y, dh, d = [refs.pop(0) for _ in range(5)]
        w = {name: refs.pop(0) for name, rows, columns in matrices}
        w.update({name: refs.pop(0) for name, length in vectors})
        g = {name: refs.pop(0) for name, length in vectors}
        pool, sem = refs.pop(0), refs.pop(0)
        work = refs
        left, right = work[:2]
        scales_ref[...] = jnp.zeros_like(scales_ref)
        size = D_DEC // H_DEC

        sizes = {name: rows * columns // (TR * TC) for name, rows, columns in matrices}
        spans = [(total, 1)] + [(base[name], sizes[name]) for name in sizes]
        for n, (start, count) in enumerate(spans):

            def fetch(t, carry, n=n):
                pltpu.make_async_copy(tiles_ref.at[place_ref[t]], pool.at[t], sem.at[n]).start()
                return carry

            lax.fori_loop(start, start + count, fetch, 0)

        def fetched(n):
            start, count = spans[n]
            pltpu.make_async_copy(tiles_ref.at[pl.ds(0, count)], pool.at[pl.ds(start, count)], sem.at[n]).wait()

        fetched(0)
        cut_vectors(pool[total].astype(F32), [w[name] for name, length in vectors])
        for n, (name, rows, columns) in enumerate(matrices):
            fetched(n + 1)
            unpack_into(pool, None, base[name], w[name], left, right)
        names = (K_FIRST, K_FIRST_BIAS, K_MASK, K_G1, K_B1, K_QKV, K_QV_BIAS)
        enter_decoder_body(
            turned_ref, sent_ref, kept_ref, pos_ref, *[w[k] for k in names], x, a, qkv
        )
        spans = [
            [slice(part * D_DEC + n * LANES, part * D_DEC + (n + 1) * LANES) for part in range(3)]
            for n in range(D_DEC // LANES)
        ]
        for group in spans:
            mix_heads(*[qkv.at[:, span] for span in group], o.at[:, group[0]], size)
        names = (K_PROJ, K_PROJ_BIAS, K_G2, K_B2, K_FC1, K_FC1_BIAS, K_FC2, K_FC2_BIAS, K_GF, K_BF)
        finish_body(
            x, o, *[w[k] for k in names], h, c, z, slope, y, final
        )
        lane = lax.broadcasted_iota(jnp.int32, (1, LANES), 1)
        count = jnp.sum(jnp.where(lane == 2 * BANDS, jnp.sum(all_sums[...], 0)[0:1, :], 0.0), -1, keepdims=True)
        head_body(
            1.0 / jnp.maximum(count, 1.0), final, w[K_HEAD], w[K_HEAD_BIAS], pix_ref, valid_ref,
            pred_low, g[K_HEAD_BIAS], loss_ref, d,
        )
        names = (K_GF, K_BF, K_FC2_BIAS, K_FC1_BIAS, K_G2, K_B2, K_PROJ_BIAS)
        back_finish_body(
            d, y, slope, h, *[w[k] for k in (K_GF, K_FC2, K_FC1, K_G2, K_PROJ)],
            two, du, dh, one, do, *[g[k] for k in names], d,
        )
        for group in spans:
            parts = back_heads(*[qkv.at[:, span] for span in group], do.at[:, group[0]], turned, size)
            for span, value in zip(group, parts):
                dqkv[:, span] = value.astype(BF16)
        leave_decoder_body(
            dqkv, x, dh, chosen_ref, kept_ref, w[K_G1], w[K_QKV], w[K_FIRST], low, d_sent,
            *[g[k] for k in (K_QV_BIAS, K_G1, K_B1, K_MASK, K_FIRST_BIAS)], d, dx,
        )
        out = (where_ref, line_ref, codes_ref, scales_ref, work)
        factors = ((sent_ref, low), (a, dqkv), (o, one), (c, du), (z, two), (final, pred_low))
        for (name, rows, columns), pair in zip(matrices, factors):
            codes_into(*pair, base[name], *out)
        vectors_into([g[name] for name, length in vectors], total, *out)

    vmem = pl.BlockSpec(memory_space=pltpu.VMEM)
    smem = pl.BlockSpec(memory_space=pltpu.SMEM)
    hbm = pl.BlockSpec(memory_space=pltpu.HBM)
    return pl.pallas_call(
        kernel,
        out_shape=[
            jax.ShapeDtypeStruct((total_tiles, TR, TC), jnp.int16),
            jax.ShapeDtypeStruct((total_lines, TC), F32),
            jax.ShapeDtypeStruct((1, PATCH_PIX), F32),
            jax.ShapeDtypeStruct((KEEP, D_ENC), BF16),
        ],
        in_specs=[smem] * 3 + [hbm] + [vmem] * 8,
        out_specs=[hbm] + [vmem] * 3,
        scratch_shapes=[pltpu.VMEM(*value) for value in inner]
        + [pltpu.VMEM((rows, columns), BF16) for name, rows, columns in matrices]
        + [pltpu.VMEM((1, length), F32) for name, length in vectors] * 2
        + [pltpu.VMEM((USED[1], TR, TC), BF16), pltpu.SemaphoreType.DMA((1 + len(matrices),))]
        + CODE_WORK,
        compiler_params=pltpu.CompilerParams(vmem_limit_bytes=60 * 2**20),
        name="decoder_step",
    )(place, where, line_at, tiles, all_sums, chosen, chosen.T, sent, kept, valid, pix, jnp.asarray(positions(D_DEC)))


def encoder_back(w, encoded, d_sent, xin, where, line_at, codes, scales):
    matrices, vectors = layout(0)
    base, total = tile_bases(0)
    line = (KEEP, D_ENC)
    inner = [((KEEP, FF_ENC), BF16), ((KEEP, 3 * D_ENC), BF16), ((LANES, KEEP), F32)]
    inner += [(line, BF16)] * 4 + [(line, F32)] * 2
    weights = (K_QKV, K_PROJ, K_FC1, K_FC2, K_G1, K_G2, K_GF)

    def kernel(where_ref, line_ref, codes_in, scales_in, x, a, qkv, o, h, c, z, slope, y, d_sent_ref, xin_ref, *refs):
        refs = list(refs)
        v = {name: refs.pop(0) for name in weights}
        codes_ref, scales_ref = refs.pop(0), refs.pop(0)
        du, dqkv, turned, two, one, do, low, dh, d = [refs.pop(0) for _ in range(9)]
        g = {name: refs.pop(0) for name, length in vectors}
        out = (where_ref, line_ref, codes_ref, scales_ref, refs)
        scales_ref[...] = scales_in[...]
        names = (K_GF, K_BF, K_FC2_BIAS, K_FC1_BIAS, K_G2, K_B2, K_PROJ_BIAS)
        back_finish_body(
            d_sent_ref, y, slope, h, *[v[k] for k in (K_GF, K_FC2, K_FC1, K_G2, K_PROJ)],
            two, du, dh, one, do, *[g[k] for k in names], d,
        )
        for n in range(D_ENC // LANES):
            group = [slice(part * D_ENC + n * LANES, part * D_ENC + (n + 1) * LANES) for part in range(3)]
            parts = back_heads(
                *[qkv.at[:, span] for span in group], do.at[:, group[0]], turned, D_ENC // H_ENC
            )
            for span, value in zip(group, parts):
                dqkv[:, span] = value.astype(BF16)
        leave_encoder_body(
            dqkv, x, dh, v[K_G1], v[K_QKV], low, *[g[k] for k in (K_QV_BIAS, K_G1, K_B1, K_FIRST_BIAS)]
        )
        factors = ((xin_ref, low), (a, dqkv), (o, one), (c, du), (z, two))
        for (name, rows, columns), pair in zip(matrices, factors):
            codes_into(*pair, base[name], *out)
        vectors_into([g[name] for name, length in vectors], total, *out)

    vmem = pl.BlockSpec(memory_space=pltpu.VMEM)
    smem = pl.BlockSpec(memory_space=pltpu.SMEM)
    hbm = pl.BlockSpec(memory_space=pltpu.HBM)
    operands = [*encoded[:9], d_sent, xin] + [w[name] for name in weights]
    return pl.pallas_call(
        kernel,
        out_shape=[jax.ShapeDtypeStruct(codes.shape, codes.dtype), jax.ShapeDtypeStruct(scales.shape, F32)],
        in_specs=[smem, smem, hbm] + [vmem] * (1 + len(operands)),
        out_specs=[hbm, vmem],
        scratch_shapes=[pltpu.VMEM(*value) for value in inner]
        + [pltpu.VMEM((1, length), F32) for name, length in vectors]
        + CODE_WORK,
        input_output_aliases={2: 0},
        compiler_params=pltpu.CompilerParams(vmem_limit_bytes=60 * 2**20),
        name="encoder_back",
    )(where, line_at, codes, scales, *operands)


class Spread:
    MOVES = {K_U: [(0, 0, 1)], K_V: [(0, 1, 0)], K_Z: [(1, 0, 0), (2, 0, 0), (3, 0, 0)]}

    def __init__(self, section, place, block_ref, all_ref, ways, cut, sems, first):
        self.section, self.place, self.at = section, place, neighbours(section, place)
        self.block_ref, self.all_ref, self.ways, self.cut, self.sems = block_ref, all_ref, ways, cut, sems
        self.count = block_ref.shape[0]
        self.copies, self.sides = {}, {}
        self.next_copy = self.next_side = first

    def rows(self, section, holder, way):
        start = (section * 16 + holder) * self.count + self.cut[way]
        return self.all_ref.at[pl.ds(start, self.cut[way + 1] - self.cut[way])]

    def source(self, way, origin):
        if origin == (0, 0, 0):
            return self.block_ref.at[pl.ds(self.cut[way], self.cut[way + 1] - self.cut[way])]
        return self.rows(self.section, self.at(*origin), way)

    def send(self, way, origin, move):
        copy = pltpu.make_async_remote_copy(
            src_ref=self.source(way, origin),
            dst_ref=self.rows(self.section, self.at(*origin), way),
            send_sem=self.sems[0].at[self.next_copy],
            recv_sem=self.sems[1].at[self.next_copy],
            device_id=(self.section, self.at(*move)),
            device_id_type=MESH,
        )
        copy.start()
        self.copies[way, self.moved(origin, move)] = (copy, self.next_copy)
        self.next_copy += 1

    def moved(self, origin, move):
        return tuple((o - m) % s for o, m, s in zip(origin, move, (4, 2, 2)))

    def side(self, way, origin):
        copy = pltpu.make_async_remote_copy(
            src_ref=self.source(way, origin),
            dst_ref=self.rows(self.section, self.at(*origin), way),
            send_sem=self.sems[2].at[self.next_side],
            recv_sem=self.sems[3].at[self.next_side],
            device_id=(1 - self.section, self.place),
            device_id_type=MESH,
        )
        copy.start()
        self.sides[way, origin] = (copy, self.next_side)
        self.next_side += 1

    def arrived(self, target, send_sem, recv_sem):
        pltpu.make_async_remote_copy(
            src_ref=target,
            dst_ref=target,
            send_sem=send_sem,
            recv_sem=recv_sem,
            device_id=(1 - self.section, self.place),
            device_id_type=MESH,
        ).wait_recv()

    def take(self, way, origin, dims):
        index = self.copies[way, origin][1]
        self.arrived(
            self.rows(self.section, self.at(*origin), way), self.sems[0].at[index], self.sems[1].at[index]
        )
        for dim in dims:
            for move in self.MOVES[dim]:
                self.send(way, origin, move)
        self.side(way, origin)

    def start(self):
        zero = (0, 0, 0)
        self.own = pltpu.make_async_copy(
            self.block_ref, self.all_ref.at[pl.ds((self.section * 16 + self.place) * self.count, self.count)], self.sems[4]
        )
        self.own.start()
        for turn in range(3):
            for way, dims in enumerate(self.ways):
                for move in self.MOVES[dims[turn]]:
                    self.send(way, zero, move)
        for way in range(len(self.ways)):
            self.side(way, zero)
        held = {way: [zero] for way in range(len(self.ways))}
        steps = []
        for turn in range(3):
            come = {}
            for way, dims in enumerate(self.ways):
                come[way] = [self.moved(o, m) for m in self.MOVES[dims[turn]] for o in held[way]]
                held[way] = held[way] + come[way]
            for i in range(max(len(v) for v in come.values())):
                for way, dims in enumerate(self.ways):
                    if i < len(come[way]):
                        steps.append(functools.partial(self.take, way, come[way][i], dims[turn + 1 :]))
        return steps

    def finish(self):
        self.own.wait()
        for copy, index in self.copies.values():
            copy.wait_send()
        for (way, origin), (copy, index) in self.sides.items():
            copy.wait_send()
            self.arrived(
                self.rows(1 - self.section, self.at(*origin), way), self.sems[2].at[index], self.sems[3].at[index]
            )


def spread_sems(copies, sides):
    return [
        pltpu.SemaphoreType.DMA((copies,)),
        pltpu.SemaphoreType.DMA((copies,)),
        pltpu.SemaphoreType.DMA((sides,)),
        pltpu.SemaphoreType.DMA((sides,)),
        pltpu.SemaphoreType.DMA,
    ]


FOUR_WAYS = ((K_Z, K_V, K_U), (K_Z, K_U, K_V), (K_V, K_Z, K_U), (K_U, K_Z, K_V))
ONE_WAY = ((K_Z, K_V, K_U),)


def unpack_into(pool, place_ref, base, weight_ref, left, right):
    rows, columns = weight_ref.shape
    wide = columns // TC
    many = groups_of(rows, wide)
    count = many * wide

    def group(g, carry):
        for j in range(count):
            index = base + g * count + j
            tile = pool[index if place_ref is None else place_ref[index]].astype(F32)
            left[j * TR : (j + 1) * TR, :] = tile[:, :LANES]
            right[j * TR : (j + 1) * TR, :] = tile[:, LANES:]
        rows_g = pl.ds(pl.multiple_of(g * many * TR, TR), many * TR)
        for j in range(wide):
            for n, lines in enumerate((left, right)):
                start = j * TC + n * LANES
                weight_ref[rows_g, start : start + LANES] = lines[pl.ds(j, many * TR, stride=wide), :].astype(BF16)
        return carry

    lax.fori_loop(0, rows // (many * TR), group, 0)


def cut_vectors(tile, refs):
    row = 0
    for ref in refs:
        for r in range(ref.shape[1] // TC):
            ref[:, r * TC : (r + 1) * TC] = tile[row : row + 1, :]
            row += 1


def tile_bases(section_id):
    matrices, vectors = layout(section_id)
    base, total = {}, 0
    for name, rows, columns in matrices:
        base[name] = total
        total += rows * columns // (TR * TC)
    return base, total


def deal_and_encode(master, slot_for, from_owner, valid, chosen, pixels, place, turns, cid):
    n_early, n_late = turns
    slots = master.shape[0]
    matrices, vectors = layout(0)
    shapes = {name: (rows, columns) for name, rows, columns in matrices}
    lengths = dict(vectors)
    base, total = tile_bases(0)
    kept_weights = (K_QKV, K_PROJ, K_FC1, K_FC2)
    kept_vectors = (K_G1, K_G2, K_GF)
    line = (KEEP, D_ENC)
    hidden = (KEEP, FF_ENC)
    results = [
        (line, F32), (line, BF16), ((KEEP, 3 * D_ENC), BF16), (line, BF16), (line, F32), (line, BF16), (hidden, BF16),
        (hidden, F32), (line, F32), (line, BF16),
    ]

    def kernel(slot_ref, owner_ref, place_ref, master_ref, valid_ref, chosen_ref, pixels_ref, pos_ref,
               late_all, all_sums, pix_ref, xin_ref, *refs):
        refs = list(refs)
        out_w = {name: refs.pop(0) for name in kept_weights}
        out_v = {name: refs.pop(0) for name in kept_vectors}
        x, a, qkv, o, h, c, z, slope, y, sent = [refs.pop(0) for _ in results]
        pool = refs.pop(0)
        w = {name: refs.pop(0) for name, rows, columns in matrices}
        v = {name: refs.pop(0) for name, length in vectors}
        left, right = refs.pop(0), refs.pop(0)
        stage, arrived, early_ref, late_ref = refs[:4]
        early_sems, late_sems, out_sem, direct_refs = refs[4:9], refs[9:14], refs[14], refs[15:18]
        sums_ref, sums_sems = refs[18], refs[19:]
        section, at_dp = lax.axis_index(K_SECTION), lax.axis_index(K_DP)
        direct = Direct(16, [(stage, True, arrived)], direct_refs)
        direct_sums = Direct(16, [(sums_ref, False, all_sums)], sums_sems)

        def pick(e, carry):
            stage[e] = master_ref[slot_ref[e]].astype(BF16)
            return carry

        lax.fori_loop(0, 32, pick, 0)
        direct.greet()
        direct.start()
        for core in range(2):

            @pl.when(section == core)
            def _(core=core):
                for lo, hi in row_cuts(SEQ, 96):
                    pix_ref[lo:hi, :] = pixels_ref[lo:hi, core, :]

        columns = [jnp.zeros((1, PATCH_DIM), F32)] * 2
        for lo, hi in row_cuts(SEQ, 96):
            values = pix_ref[lo:hi, :].astype(F32)
            columns = [columns[0] + line_sum(values), columns[1] + line_sum(values * values)]
        lane = lax.broadcasted_iota(jnp.int32, (1, LANES), 1)
        line_of_sums = jnp.where(lane == 2 * BANDS, line_sum(valid_ref[...]), 0.0)
        for n in range(2 * BANDS):
            band = n % BANDS
            value = jnp.sum(columns[n // BANDS][:, band * PATCH_PIX : (band + 1) * PATCH_PIX], -1, keepdims=True)
            line_of_sums = jnp.where(lane == n, value, line_of_sums)
        sums_ref[...] = jnp.zeros_like(sums_ref)
        sums_ref[0:1, :] = line_of_sums
        direct_sums.start()
        seen = project(chosen_ref[...], pix_ref[...])
        kept_places = sum(project(chosen_ref[...], pos_ref[part]) for part in range(3))
        direct.finish()
        direct_sums.finish()
        for t in range(n_early):
            early_ref[t] = arrived[owner_ref[t]]
        for t in range(n_late):
            late_ref[t] = arrived[owner_ref[n_early + t]]
        cut = [0, 3, 5, 7, n_early] if n_early == 8 else [0, 1, 2, 3, n_early]
        soon = Spread(section, at_dp, early_ref, pool, FOUR_WAYS, cut, early_sems, 0)
        soon_steps = soon.start()
        last = 8 * len(FOUR_WAYS)
        for step in soon_steps[:-last]:
            step()
        later = Spread(section, at_dp, late_ref, late_all, ONE_WAY, [0, n_late], late_sems, 0)
        steps = later.start()
        lines = jnp.sum(all_sums[...], 0)[0:1, :]
        for band in range(BANDS):
            columns = slice(band * PATCH_PIX, (band + 1) * PATCH_PIX)
            mean, square = [
                jnp.sum(jnp.where(lane == n, lines, 0.0), -1, keepdims=True) / (32 * SEQ * PATCH_PIX) for n in (band, BANDS + band)
            ]
            scale = lax.rsqrt(square - mean * mean + EPS_BAND)
            xin_ref[:, columns] = ((seen[:, columns] - mean) * scale).astype(BF16)
        for step in soon_steps[-last:]:
            step()
        soon.finish()

        def pump(count):
            for _ in range(min(count, len(steps))):
                steps.pop(0)()

        def unpack(name):
            unpack_into(pool, place_ref, base[name], w[name], left, right)
            if name in kept_weights:
                pltpu.make_async_copy(w[name], out_w[name], out_sem.at[kept_weights.index(name)]).start()

        cut_vectors(pool[place_ref[total]].astype(F32), [v[name] for name, length in vectors])
        for name in kept_vectors:
            out_v[name][...] = v[name][...]
        unpack(K_FIRST)
        pump(1)
        unpack(K_QKV)
        pump(2)
        x[...] = project(xin_ref[...], w[K_FIRST][...]) + v[K_FIRST_BIAS][...] + kept_places
        start_block(x, slice(None), (v[K_G1], v[K_B1], w[K_QKV], v[K_QV_BIAS]), a, qkv)
        pump(2)
        for g in range(D_ENC // LANES):
            spans = [slice(part * D_ENC + g * LANES, part * D_ENC + (g + 1) * LANES) for part in range(3)]
            mix_heads(*[qkv.at[:, span] for span in spans], o.at[:, spans[0]], D_ENC // H_ENC)
        pump(2)
        unpack(K_PROJ)
        unpack(K_FC1)
        pump(2)
        unpack(K_FC2)
        pump(2)
        names = (K_PROJ, K_PROJ_BIAS, K_G2, K_B2, K_FC1, K_FC1_BIAS, K_FC2, K_FC2_BIAS, K_GF, K_BF)
        finish_body(x, o, *[w[name] if name in w else v[name] for name in names], h, c, z, slope, y, sent, pump)
        pump(len(steps))
        later.finish()
        for name in kept_weights:
            pltpu.make_async_copy(w[name], out_w[name], out_sem.at[kept_weights.index(name)]).wait()

    vmem, hbm = pl.BlockSpec(memory_space=pltpu.VMEM), pl.BlockSpec(memory_space=pltpu.HBM)
    shape = jax.ShapeDtypeStruct
    outs = pl.pallas_call(
        kernel,
        out_shape=[
            shape((32 * n_late, TR, TC), BF16), shape((32, 8, LANES), F32), shape((SEQ, PATCH_DIM), BF16),
            shape((KEEP, PATCH_DIM), BF16)
        ]
        + [shape(shapes[name], BF16) for name in kept_weights]
        + [shape((1, lengths[name]), F32) for name in kept_vectors]
        + [shape(*result) for result in results],
        in_specs=[pl.BlockSpec(memory_space=pltpu.SMEM)] * 3 + [vmem] * 5,
        out_specs=[hbm] + [vmem] * 3 + [hbm] * len(kept_weights) + [vmem] * (len(kept_vectors) + len(results)),
        scratch_shapes=[pltpu.VMEM((32 * n_early, TR, TC), BF16)]
        + [pltpu.VMEM(shapes[name], BF16) for name, rows, columns in matrices]
        + [pltpu.VMEM((1, length), F32) for name, length in vectors]
        + [pltpu.VMEM((12 * TR, LANES), F32)] * 2
        + [pltpu.VMEM((32, TR, TC), BF16)] * 2
        + [pltpu.VMEM((n_early, TR, TC), BF16), pltpu.VMEM((n_late, TR, TC), BF16)]
        + spread_sems(60, 64)
        + spread_sems(15, 16)
        + [pltpu.SemaphoreType.DMA((len(kept_weights),))]
        + direct_sems(1, 32)
        + [pltpu.VMEM((8, LANES), F32)]
        + direct_sems(1, 32),
        compiler_params=pltpu.CompilerParams(
            collective_id=cid, has_side_effects=True, vmem_limit_bytes=60 * 2**20
        ),
        name="deal_and_encode",
    )(
        slot_for, from_owner, place, master, valid, chosen, pixels.transpose(1, 2, 0, 3).reshape(SEQ, 2, PATCH_DIM),
        jnp.asarray(in_three(positions(D_ENC))),
    )
    weights = dict(zip(kept_weights + kept_vectors, outs[4:]))
    return outs[:4], weights, outs[4 + len(weights) :]


def in_three(values):
    parts, rest = [], values
    for _ in range(3):
        parts.append(rest.astype(jnp.bfloat16))
        rest = rest - parts[-1].astype(np.float32)
    return np.stack(parts)


def encode(w, xin, chosen):
    places = jnp.asarray(positions(D_ENC))
    x, a, qkv = enter_encoder(xin, jnp.dot(chosen.astype(F32), places, precision=lax.Precision.HIGHEST), w)
    o = attention(qkv, H_ENC)
    return x, a, qkv, o, *finish_block(x, o, w, "encoder")


def local(pixels, keep_index, clear_mask, slot_tile, master, moment_one, moment_two):
    n_dp = lax.axis_size(K_DP)
    n_dev = 2 * n_dp
    section, place = lax.axis_index(K_SECTION), lax.axis_index(K_DP)
    me = section * n_dp + place
    slots = master.shape[1]
    turns = [-(-count // n_dev) for count in USED]
    per = sum(turns)
    starts = [0, turns[0] * n_dev]
    rows_each = PARTS_ROWS if n_dp == 16 else 8 * (-(-per // 8))

    keep = lax.dynamic_index_in_dim(keep_index, section, 0, keepdims=False)[0]
    clear = lax.dynamic_index_in_dim(clear_mask, section, 0, keepdims=False)[0]
    kept = jnp.any(keep[:, None] == jnp.arange(SEQ), axis=0).astype(jnp.float32)
    valid = clear.astype(jnp.float32) * (1.0 - kept)
    def order(table, start):
        used = (table < TILES).astype(jnp.int32)
        count = table.shape[0]
        before = (jnp.arange(count)[:, None] > jnp.arange(count)[None]).astype(jnp.int32)
        return used, jnp.sum(before * used[None], 1) + start

    table_own = slot_tile[0]
    used_own, order_own = order(table_own, starts[1] * section)
    used_mine = lax.dynamic_slice_in_dim(used_own, place * slots, slots)
    order_mine = lax.dynamic_slice_in_dim(order_own, place * slots, slots)
    goes = lax.rem(order_mine, n_dev)
    slot_for = jnp.sum(
        jnp.arange(slots)[None] * used_mine[None] * (goes[None] == jnp.arange(n_dev)[:, None]), 1
    ).astype(jnp.int32)
    table_other = lax.ppermute(table_own, K_SECTION, [(0, 1), (1, 0)])
    tables = jnp.where(section == 0, jnp.stack([table_own, table_other]), jnp.stack([table_other, table_own]))
    n_slots = table_own.shape[0]
    both = [order(tables[s], starts[s]) for s in range(2)]
    used_all = jnp.concatenate([b[0] for b in both])
    order_all = jnp.concatenate([b[1] for b in both])
    owner_all = jnp.arange(2 * n_slots) // slots
    held = jnp.arange(per) * n_dev + me
    match = used_all[None] * (order_all[None] == held[:, None])
    from_owner = jnp.sum(match * owner_all[None], 1).astype(jnp.int32)
    is_held = jnp.sum(match, 1)
    turn_for = jnp.sum(
        jnp.arange(per)[None] * is_held[None] * (from_owner[None] == jnp.arange(n_dev)[:, None]), 1
    ).astype(jnp.int32)
    chosen = (keep[:, None] == jnp.arange(SEQ)).astype(BF16)

    where_tile = []
    line_tile = []
    source_tile = []
    for s in range(2):
        hit = tables[s][None] == jnp.arange(TILES)[:, None]
        rank = jnp.sum(hit * both[s][1][None], 1)
        device, turn = lax.rem(rank, n_dev), lax.div(rank, n_dev)
        where_tile.append((device * per + turn).astype(jnp.int32))
        source_tile.append((device * turns[s] + turn - (turns[0] if s else 0)).astype(jnp.int32))
        line_tile.append((device * rows_each + line_of(turn, n_dp)).astype(jnp.int32))

    if n_dp == 16:
        (late_all, all_sums, pix, xin), enc, encoded = deal_and_encode(
            master[0], slot_for, from_owner, valid[:, None], chosen, pixels, source_tile[0], turns, 2
        )
    else:
        pix = lax.dynamic_index_in_dim(pixels, section, 0, keepdims=False)[0]
        wide_pix = pix.astype(F32)
        sums = jnp.concatenate(
            [
                jnp.sum(jnp.sum(wide_pix, 0).reshape(BANDS, PATCH_PIX), 1),
                jnp.sum(jnp.sum(wide_pix * wide_pix, 0).reshape(BANDS, PATCH_PIX), 1),
                jnp.sum(valid)[None],
            ]
        )
        sums = jnp.pad(sums, (0, 1024 - sums.shape[0])).reshape(8, 128)
        dealt = pick_tiles(master[0], slot_for, BF16, "deal")
        arrived, all_sums = exchange("exchange", 1, n_dp, [dealt], [sums])
        totals = jnp.sum(all_sums, 0).reshape(-1)
        pixel_count = n_dev * SEQ * PATCH_PIX
        band_mean = totals[:BANDS] / pixel_count
        band_scale = lax.rsqrt(totals[BANDS : 2 * BANDS] / pixel_count - band_mean * band_mean + EPS_BAND)
        mean_line = jnp.broadcast_to(band_mean[:, None], (BANDS, PATCH_PIX)).reshape(PATCH_DIM)
        scale_line = jnp.broadcast_to(band_scale[:, None], (BANDS, PATCH_PIX)).reshape(PATCH_DIM)
        xin = ((project(chosen, pix) - mean_line) * scale_line).astype(BF16)
        block = pick_tiles(arrived, from_owner, BF16, "hold")
        early, late = block[: turns[0]], block[turns[0] :]
        early_all, late_all = [lax.all_gather(lax.all_gather(part, K_DP), K_SECTION) for part in (early, late)]
        enc = unpack_section(early_all.reshape(-1, TR, TC), source_tile[0], 0)
        encoded = encode(enc, xin, chosen)
    codes, scales, loss_terms, d_sent = decoder_step(
        late_all.reshape(-1, TR, TC), source_tile[1], all_sums, chosen, encoded[-1], kept[:, None],
        valid[:, None], pix, where_tile[1], line_tile[1], n_dev * per, n_dev * rows_each,
    )
    codes, scales = encoder_back(enc, encoded, d_sent, xin, where_tile[0], line_tile[0], codes, scales)
    if n_dp == 16:
        codes_mine, scales_mine, tails = reduce_and_return(
            codes.reshape(2, n_dp, per, TR, TC), scales.reshape(2, n_dp, rows_each, TC), turn_for, is_held.astype(F32),
            loss_terms, 3,
        )
    else:
        wide = scales.reshape(n_dev, rows_each, TC)[:, :per]
        values = jnp.where(wide[:, :, None] > 0.0, codes.reshape(n_dev, per, TR, TC).astype(F32), 0.0)
        values = values * wide[:, :, None]
        values = lax.psum_scatter(values, (K_SECTION, K_DP), scatter_dimension=0, tiled=True)[0]
        top = jnp.max(jnp.abs(values), 1, keepdims=True)
        up = jnp.where(top > 0.0, 32766.0 / top, 0.0)
        own_codes = jnp.round(values * up).astype(jnp.int16)
        own_scale = top[:, 0] * (1.0 / 32766.0)
        own = jnp.where(is_held[:, None, None] > 0, own_codes.astype(F32) * own_scale[:, None], 0.0)
        tail = jnp.stack([jnp.sum(own * own), jnp.sum(loss_terms)])
        tail = jnp.pad(tail[:, None], ((0, 6), (0, 127)))
        codes_back = pick_tiles(own_codes, turn_for, jnp.int16, "back")
        scales_back = own_scale[turn_for][:, None]
        codes_mine, scales_mine, tails = exchange("return", 4, n_dp, [codes_back, scales_back], [tail])
    totals = jnp.sum(tails, (0, 2))
    grad_norm = jnp.sqrt(totals[0])
    factor = jnp.minimum(1.0, CLIP_NORM / (grad_norm + 1e-06))
    master_new, first_new, second_new = adam(
        codes_mine, scales_mine, goes, used_mine, factor[None], master[0], moment_one[0], moment_two[0]
    )
    return master_new[None], first_new[None], second_new[None], totals[1][None], grad_norm[None]


def solution(mesh):
    return jax.shard_map(
        local,
        mesh=mesh,
        in_specs=(
            P(None, K_DP, None, None),
            P(None, K_DP, None),
            P(None, K_DP, None),
            P(K_SECTION, None),
            P(K_SECTION, K_DP, None, None),
            P(K_SECTION, K_DP, None, None),
            P(K_SECTION, K_DP, None, None),
        ),
        out_specs=(
            P(K_SECTION, K_DP, None, None),
            P(K_SECTION, K_DP, None, None),
            P(K_SECTION, K_DP, None, None),
            P(),
            P(),
        ),
        check_vma=False,
    )
```
